128 devices in a mesh: mp: 2 (over core), gx: 8 (over z, y_hi), gy: 8 (over y_lo, x).
Axes of the slice: x: 4, y: 4 (y_hi: 2, y_lo: 2; y = y_hi * 2 + y_lo), z: 4, core: 2. Of those that a mesh axis runs over, the one named last changes fastest.
Arguments:
- states: float32 [2, 64, 1024, 1024], P('mp', None, 'gx', 'gy'), may hold values from -6 to 6
- surface: float32 [2, 8, 1024, 1024], P('mp', None, 'gx', 'gy'), may hold values from -6 to 6
- land_mask: int32 [1024, 1024], P('gx', 'gy'), may hold values 0 or 1
- tile_weights: bfloat16 [2, 8, 8, 256, 128, 128], P('mp', 'gx', 'gy'), may hold values from -0.5 to 0.5
- tile_source: int32 [2, 8, 8, 256], P('mp', 'gx', 'gy'), may hold values from 0 to 127
- tile_target: int32 [2, 8, 8, 256, 1], P('mp', 'gx', 'gy'), may hold values from 0 to 63; in each aligned block of 256 rows (0 to 255, 256 to 511, ..., all dimensions but the last counted through in order) at most 8 rows name the same one
- tile_row: int32 [2, 8, 8, 256], P('mp', 'gx', 'gy'), may hold values from 0 to 127
Outputs:
- new_states: float32 [2, 64, 1024, 1024], P('mp', None, 'gx', 'gy')
- remapped: float32 [2, 8, 1024, 1024], P('mp', None, 'gx', 'gy')
The draws below stay inside these ranges and needn't reach their ends.
Inputs may be any that keep to these rules, and one draw needn't show every extreme that they name: `tile_target`: among the tiles of one device, no destination device is named by more than 8 tiles, and some device is named by exactly 8.
All inputs are finite; a program needn't handle non-finite values. No bound on the sum of `land_mask` on one device may be relied on, other than what follows from the above.
Results may differ from the reference program's by a relative error of at most 0.0029.
Values sent between devices are 32-bit elements; how exact they have to be, the bound alone decides.
A program may use at most 192 MiB of HBM per device.

```python
import math
import jax
import jax.numpy as jnp
import numpy as np
from jax import lax

CX = 128
CY = 128
LEV = 64
KF = 8
CAP = 8
TILES = 256
NX = 1024
NY = 1024
N_GX = 8
N_GY = 8


def set_ends(entries, rng, low, top_value):
    shape = entries.shape
    place = [jax.random.randint(jax.random.fold_in(rng, axis), (), 0, shape[axis]) for axis in range(len(shape))]
    entries = entries.at[tuple(place)].set(low)
    longest = shape.index(max(shape))
    place[longest] = (place[longest] + 1) % shape[longest]
    return entries.at[tuple(place)].set(top_value)


def block_levels(rng, dims, pieces, low, high):
    def one(dim, blocks):
        heights = jax.random.uniform(jax.random.fold_in(jax.random.fold_in(rng, 6), dim), (blocks,), jnp.float32, low / len(pieces), high / len(pieces))
        return jnp.repeat(jnp.exp(heights), dims[dim] // blocks).reshape((-1,) + (1,) * (len(dims) - dim - 1))

    loudness = one(*pieces[0])
    for cut in pieces[1:]:
        loudness = loudness * one(*cut)
    return loudness


def shared_out(rng, own, number, rows, number_of, top, limit, skew):
    sequence = jax.random.permutation(rng, number_of)
    packed, common = shares(number_of, rows * top, limit, skew, True), shares(number_of, rows * top, limit, skew, False)
    places = jnp.arange(number_of)

    def named(sizes, offset_by):
        used = int((sizes > 0).sum())
        fixed = max(1, used // 4)
        passed = fixed + (places - fixed + offset_by * (used - fixed)) % max(1, number_of - fixed)
        return jnp.zeros((number_of,), jnp.int32).at[sequence[jnp.where(places < fixed, places, passed)]].set(jnp.asarray(sizes, jnp.int32))

    sizes = jnp.where(number % 4 == 0, named(packed, number // 4), named(common, number - number // 4 - 1))
    mixed = jax.random.permutation(jax.random.fold_in(own, 3), number_of)
    giver, sink = mixed[0:number_of // 2 * 2:2], mixed[1:number_of // 2 * 2:2]
    room = jnp.minimum(sizes[giver] - 1, limit - sizes[sink]) // 2
    room = jnp.where((giver == sequence[0]) | (sink == sequence[0]) | (sizes[sink] == 0), 0, jnp.maximum(room, 0))
    passed = jax.random.randint(jax.random.fold_in(own, 4), (number_of // 2,), 0, 1 << 20) % (room + 1)
    sizes = sizes.at[giver].add(-passed).at[sink].add(passed)
    labels = jnp.searchsorted(jnp.cumsum(sizes), jnp.arange(rows * top), side="right").astype(jnp.int32)
    listing = labels.reshape(top, rows).T
    listing = listing[jax.random.permutation(jax.random.fold_in(own, 1), rows)]
    offset_by = jax.random.randint(jax.random.fold_in(own, 2), (rows, 1), 0, top)
    return jnp.take_along_axis(listing, (jnp.arange(top)[None, :] + offset_by) % top, axis=1)


def shares(number_of, total, most, skew, full):
    weights = [(1 << 20) // math.isqrt(rank ** skew) + 1 for rank in range(1, number_of + 1)]
    largest = most if full else min(most, max(-(-total // number_of), total * weights[0] // sum(weights)))
    least = 1 if total - largest >= number_of - 1 else 0
    counts, spare = [largest] + [least] * (number_of - 1), total - largest - least * (number_of - 1)
    while spare > 0:
        candidates = [i for i in range(1, number_of) if counts[i] < largest] or [i for i in range(1, number_of) if counts[i] < most]
        mass, remaining = sum([weights[i] for i in candidates]), spare
        for i in candidates:
            addition = min(most - counts[i], max(1, remaining * weights[i] // mass), spare)
            counts[i] = counts[i] + addition
            spare = spare - addition
    return np.array(counts)


def bell_draw(rng, extent, width, reach, pieces=(), held_as=jnp.bfloat16):
    result = width * jax.random.normal(rng, extent, jnp.float32)
    if pieces:
        result = result * block_levels(rng, extent, pieces, -0.22, 0.18)
    return jnp.clip(result, -reach, reach).astype(held_as)


def setup_inputs(seed: int = 0) -> dict:
    key_of = jax.random.split(jax.random.key(seed), 8)
    states = bell_draw(key_of[0], (2, LEV, NX, NY), 1.0, 6.0, ((0, 2), (2, 8), (3, 8)), jnp.float32)
    surface = bell_draw(key_of[1], (2, KF, NX, NY), 1.0, 6.0, ((0, 2), (2, 8), (3, 8)), jnp.float32)
    land_mask = set_ends((jax.random.randint(key_of[2], (NX, NY), 0, 10) < 7).astype(jnp.int32), jax.random.fold_in(key_of[2], 1), 0, 1)
    tile_weights = bell_draw(key_of[3], (2, N_GX, N_GY, TILES, CY, CY), CY ** -0.5, 0.5, ((0, 2), (1, 8), (2, 8)))
    tile_source = set_ends(jax.random.randint(key_of[4], (2, N_GX, N_GY, TILES), 0, CX), jax.random.fold_in(key_of[4], 1), 0, CX - 1).astype(jnp.int32)
    tile_target_keys = jax.random.split(jax.random.fold_in(key_of[5], 1), 2 * N_GX * N_GY * TILES // TILES)
    tile_target_turns = jax.random.permutation(jax.random.fold_in(key_of[5], 3), 2 * N_GX * N_GY * TILES // TILES)
    tile_target = jax.vmap(lambda own, number: shared_out(jax.random.fold_in(key_of[5], 2), own, number, TILES, N_GX * N_GY, 1, CAP, 2))(tile_target_keys, tile_target_turns).reshape((2, N_GX, N_GY, TILES, 1))
    tile_row = set_ends(jax.random.randint(key_of[6], (2, N_GX, N_GY, TILES), 0, CX), jax.random.fold_in(key_of[6], 1), 0, CX - 1).astype(jnp.int32)
    return dict(states=states, surface=surface, land_mask=land_mask, tile_weights=tile_weights, tile_source=tile_source, tile_target=tile_target, tile_row=tile_row)


coef_horiz = (0.15, 0.12)
coef_vert = (0.1, 0.15)
force_gain = 0.5


def stencil(state, wet, horiz, vert):
    weighted = state * wet
    padded = jnp.pad(weighted, ((0, 0), (1, 1), (1, 1)))
    lateral = padded[:, 2:, 1:-1] + padded[:, :-2, 1:-1] + padded[:, 1:-1, 2:] + padded[:, 1:-1, :-2] - 4.0 * weighted
    column = jnp.pad(state, ((1, 1), (0, 0), (0, 0)))
    vertical = column[2:] + column[:-2] - 2.0 * state
    return wet * (state + horiz * lateral + vert * vertical)


def remap_group(surf, wet, weights, source, target, row):
    ndev = N_GX * N_GY
    src = (surf * wet).astype(jnp.bfloat16)
    blocks = src.reshape(KF, N_GX, CX, N_GY, CY).transpose(1, 3, 0, 2, 4).reshape(ndev, KF, CX, CY)

    def one_device(items):
        block, tiles, rows_idx = items
        picked = jnp.take(block, rows_idx, axis=1)
        return jnp.einsum("tji,kti->tkj", tiles.astype(jnp.float32), picked.astype(jnp.float32))

    contrib = lax.map(one_device, (blocks, weights.reshape(ndev, TILES, CY, CY), source.reshape(ndev, TILES).astype(jnp.int32)))
    index = (target.reshape(ndev * TILES) * CX + row.reshape(ndev * TILES)).astype(jnp.int32)
    total = jnp.zeros((ndev * CX, KF, CY), jnp.float32).at[index].add(contrib.reshape(ndev * TILES, KF, CY))
    return total.reshape(N_GX, N_GY, CX, KF, CY).transpose(3, 0, 2, 1, 4).reshape(KF, N_GX * CX, N_GY * CY)


def reference(states, surface, land_mask, tile_weights, tile_source, tile_target, tile_row):
    wets = (jnp.ones((N_GX * CX, N_GY * CY), jnp.float32), land_mask.astype(jnp.float32))
    to_ocean = remap_group(surface[0], wets[0], tile_weights[0], tile_source[0], tile_target[0], tile_row[0])
    to_atmos = remap_group(surface[1], wets[1], tile_weights[1], tile_source[1], tile_target[1], tile_row[1])
    remapped = jnp.stack([to_atmos, to_ocean])
    outputs = []
    for group in range(2):
        first = stencil(states[group], wets[group], coef_horiz[group], coef_vert[group])
        second = stencil(first, wets[group], coef_horiz[group], coef_vert[group])
        second = second.at[0].add(force_gain * wets[group] * remapped[group, 0])
        outputs.append(second)
    return jnp.stack(outputs), remapped
```

```python
import functools

import jax
import jax.numpy as jnp
from jax import lax
from jax.experimental import pallas as pl
from jax.experimental.pallas import tpu as pltpu
from jax.sharding import PartitionSpec as P

CY = 128
KF = 8
CAP = 8
LB = 8

force_gain = 0.5


def shift_pairs(devices, forward):
    up = [(i, i + 1) for i in range(devices - 1)]
    return up if forward else [(j, i) for i, j in up]


def stencil_kernel(with_edges, with_force, coef_ref, wet_ref, u_ref, above_ref, below_ref,
                   hn_ref, hs_ref, hw_ref, he_ref, *rest):
    if with_force:
        force_ref, rest = rest[0], rest[1:]
    out_ref = rest[0]
    i = pl.program_id(0)
    nblk = pl.num_programs(0)
    horiz = coef_ref[0]
    vert = coef_ref[1]
    wet = wet_ref[...]
    rows, cols = wet.shape
    row = lax.broadcasted_iota(jnp.int32, (rows, cols), 0)
    col = lax.broadcasted_iota(jnp.int32, (rows, cols), 1)
    hw_t = jnp.transpose(hw_ref[...])
    he_t = jnp.transpose(he_ref[...])
    above = above_ref[0] * jnp.where(i > 0, 1.0, 0.0)
    below = below_ref[0] * jnp.where(i < nblk - 1, 1.0, 0.0)
    if with_edges:
        en_ref, es_ref, ew_ref, ee_ref, qw_ref, qe_ref = rest[1:]

        @pl.when(i == 0)
        def _():
            qw_ref[...] = jnp.zeros_like(qw_ref)
            qe_ref[...] = jnp.zeros_like(qe_ref)

    for l in range(LB):
        u = u_ref[l]
        prev = u_ref[l - 1] if l > 0 else above
        nxt = u_ref[l + 1] if l < LB - 1 else below
        w = wet * u
        north = jnp.where(row == 0, hn_ref[l:l + 1, :], pltpu.roll(w, 1, 0))
        south = jnp.where(row == rows - 1, hs_ref[l:l + 1, :], pltpu.roll(w, rows - 1, 0))
        west = jnp.where(col == 0, hw_t[:, l:l + 1], pltpu.roll(w, 1, 1))
        east = jnp.where(col == cols - 1, he_t[:, l:l + 1], pltpu.roll(w, cols - 1, 1))
        lateral = north + south + west + east - 4.0 * w
        vertical = prev + nxt - 2.0 * u
        res = wet * (u + horiz * lateral + vert * vertical)
        if with_force and l == 0:
            res = res + jnp.where(i == 0, 1.0, 0.0) * (force_gain * wet * force_ref[...])
        out_ref[l] = res
        if with_edges:
            fw = wet * res
            en_ref[l:l + 1, :] = fw[0:1, :]
            es_ref[l:l + 1, :] = fw[rows - 1:rows, :]
            lane = lax.broadcasted_iota(jnp.int32, qw_ref.shape, 1)
            hit = lane == i * LB + l
            qw_ref[...] = jnp.where(hit, fw[:, 0:1], qw_ref[...])
            qe_ref[...] = jnp.where(hit, fw[:, cols - 1:cols], qe_ref[...])

    if with_edges:
        @pl.when(i == nblk - 1)
        def _():
            lev = ew_ref.shape[0]
            ew_ref[...] = jnp.transpose(qw_ref[...])[0:lev, :]
            ee_ref[...] = jnp.transpose(qe_ref[...])[0:lev, :]


def stencil_step(coef, wet, u, halos, force=None, with_edges=False):
    lev, rows, cols = u.shape
    nblk = lev // LB
    full2 = lambda shape: pl.BlockSpec(shape, lambda i: (0, 0))
    lvl2 = pl.BlockSpec((LB, cols), lambda i: (i, 0))
    in_specs = [
        pl.BlockSpec(memory_space=pltpu.SMEM),
        full2((rows, cols)),
        pl.BlockSpec((LB, rows, cols), lambda i: (i, 0, 0)),
        pl.BlockSpec((1, rows, cols), lambda i: (jnp.maximum(i * LB - 1, 0), 0, 0)),
        pl.BlockSpec((1, rows, cols), lambda i: (jnp.minimum(i * LB + LB, lev - 1), 0, 0)),
        lvl2, lvl2, lvl2, lvl2,
    ]
    args = [coef, wet, u, u, u] + list(halos)
    if force is not None:
        in_specs.append(full2((rows, cols)))
        args.append(force)
    out_shape = [jax.ShapeDtypeStruct((lev, rows, cols), jnp.float32)]
    out_specs = [pl.BlockSpec((LB, rows, cols), lambda i: (i, 0, 0))]
    scratch = []
    if with_edges:
        out_shape += [jax.ShapeDtypeStruct((lev, cols), jnp.float32)] * 2
        out_shape += [jax.ShapeDtypeStruct((lev, rows), jnp.float32)] * 2
        out_specs += [lvl2, lvl2, full2((lev, rows)), full2((lev, rows))]
        scratch = [pltpu.VMEM((rows, 128), jnp.float32)] * 2
    return pl.pallas_call(
        functools.partial(stencil_kernel, with_edges, force is not None),
        grid=(nblk,),
        in_specs=in_specs,
        out_specs=out_specs,
        out_shape=out_shape,
        scratch_shapes=scratch,
        compiler_params=pltpu.CompilerParams(dimension_semantics=("arbitrary",)),
    )(*args)


def exchange(en, es, ew, ee):
    ngx, ngy = lax.axis_size("gx"), lax.axis_size("gy")
    hn = lax.ppermute(es, "gx", shift_pairs(ngx, True))
    hs = lax.ppermute(en, "gx", shift_pairs(ngx, False))
    hw = lax.ppermute(ee, "gy", shift_pairs(ngy, True))
    he = lax.ppermute(ew, "gy", shift_pairs(ngy, False))
    return hn, hs, hw, he


def bucket_kernel(inv_ref, lab_ref, contrib_ref, out_ref):
    ndest = out_ref.shape[0]
    ntiles = contrib_ref.shape[0]
    sub = lax.broadcasted_iota(jnp.int32, (KF, CY), 0)

    def body(d, carry):
        labv = jnp.zeros((KF, CY), jnp.float32)
        for c in range(CAP):
            t = inv_ref[d * CAP + c]
            val = contrib_ref[jnp.minimum(t, ntiles - 1)]
            out_ref[d, c] = jnp.where(t < ntiles, val, 0.0)
            labv = jnp.where(sub == c, lab_ref[d * CAP + c].astype(jnp.float32), labv)
        out_ref[d, CAP] = labv
        return carry

    lax.fori_loop(0, ndest, body, 0)


def recv_kernel(rows_ref, got_ref, acc_ref):
    acc_ref[...] = jnp.zeros_like(acc_ref)
    nslots = got_ref.shape[0] * CAP

    def body(s, carry):
        r = rows_ref[s]
        acc_ref[r] = acc_ref[r] + got_ref[s // CAP, s % CAP]
        return carry

    lax.fori_loop(0, nslots, body, 0)


def local(states, surface, land_mask, tile_weights, tile_source, tile_target, tile_row):
    group = lax.axis_index("mp")
    ndev = lax.axis_size("gx") * lax.axis_size("gy")
    state = states[0]
    lev, rows_here, cols_here = state.shape
    wet = jnp.where(
        group == 0, jnp.ones(land_mask.shape, jnp.float32), land_mask.astype(jnp.float32)
    )
    coef = jnp.stack([jnp.where(group == 0, 0.15, 0.12), jnp.where(group == 0, 0.1, 0.15)]).astype(
        jnp.float32
    )

    src = (surface[0] * wet).astype(jnp.bfloat16)
    source = tile_source[0, 0, 0]
    target = tile_target[0, 0, 0, :, 0]
    dest_row = tile_row[0, 0, 0]
    ntiles = source.shape[0]
    picked = jnp.take(src, source, axis=1)
    contrib = jnp.einsum(
        "tji,kti->tkj", tile_weights[0, 0, 0], picked, preferred_element_type=jnp.float32
    )
    onehot = (target[:, None] == jnp.arange(ndev, dtype=jnp.int32)[None, :]).astype(jnp.int32)
    earlier = jnp.cumsum(onehot, axis=0) - onehot
    rank = jnp.sum(earlier * onehot, axis=1)
    slot = target * CAP + rank
    inv = jnp.full((ndev * CAP,), ntiles, jnp.int32).at[slot].set(jnp.arange(ntiles, dtype=jnp.int32))
    labels = jnp.zeros((ndev * CAP,), jnp.int32).at[slot].set(dest_row)
    buckets = pl.pallas_call(
        bucket_kernel,
        in_specs=[
            pl.BlockSpec(memory_space=pltpu.SMEM),
            pl.BlockSpec(memory_space=pltpu.SMEM),
            pl.BlockSpec(memory_space=pltpu.VMEM),
        ],
        out_specs=pl.BlockSpec(memory_space=pltpu.VMEM),
        out_shape=jax.ShapeDtypeStruct((ndev, CAP + 1, KF, CY), jnp.float32),
    )(inv, labels, contrib)
    arrived = lax.all_to_all(buckets, ("gx", "gy"), split_axis=0, concat_axis=0, tiled=True)
    got_rows = jnp.clip(arrived[:, CAP, :, 0].astype(jnp.int32), 0, rows_here - 1).reshape(-1)
    acc = pl.pallas_call(
        recv_kernel,
        in_specs=[pl.BlockSpec(memory_space=pltpu.SMEM), pl.BlockSpec(memory_space=pltpu.VMEM)],
        out_specs=pl.BlockSpec(memory_space=pltpu.VMEM),
        out_shape=jax.ShapeDtypeStruct((rows_here, KF, CY), jnp.float32),
    )(got_rows, arrived)
    sent = jnp.transpose(acc, (1, 0, 2))
    received = lax.ppermute(sent, "mp", [(0, 1), (1, 0)])

    w0 = state * wet[None]
    halos0 = exchange(
        w0[:, 0, :], w0[:, rows_here - 1, :], w0[:, :, 0], w0[:, :, cols_here - 1]
    )
    first, en, es, ew, ee = stencil_step(coef, wet, state, halos0, with_edges=True)
    halos1 = exchange(en, es, ew, ee)
    (second,) = stencil_step(coef, wet, first, halos1, force=received[0])
    return (second[None], received[None])


def solution(mesh):
    return jax.shard_map(
        local,
        mesh=mesh,
        in_specs=(
            P("mp", None, "gx", "gy"),
            P("mp", None, "gx", "gy"),
            P("gx", "gy"),
            P("mp", "gx", "gy", None, None, None),
            P("mp", "gx", "gy", None),
            P("mp", "gx", "gy", None, None),
            P("mp", "gx", "gy", None),
        ),
        out_specs=(P("mp", None, "gx", "gy"), P("mp", None, "gx", "gy")),
        check_vma=False,
    )
```

```python
import functools

import jax
import jax.numpy as jnp
from jax import lax
from jax.experimental import pallas as pl
from jax.experimental.pallas import tpu as pltpu
from jax.sharding import PartitionSpec as P

CY = 128
KF = 8
CAP = 8
LB = 8

force_gain = 0.5


def shift_pairs(devices, forward):
    up = [(i, i + 1) for i in range(devices - 1)]
    return up if forward else [(j, i) for i, j in up]


def stencil_kernel(with_edges, with_force, coef_ref, wet_ref, u_ref, above_ref, below_ref,
                   hn_ref, hs_ref, hw_ref, he_ref, *rest):
    if with_force:
        force_ref, rest = rest[0], rest[1:]
    out_ref = rest[0]
    i = pl.program_id(0)
    nblk = pl.num_programs(0)
    horiz = coef_ref[0]
    vert = coef_ref[1]
    wet = wet_ref[...]
    rows, cols = wet.shape
    row = lax.broadcasted_iota(jnp.int32, (rows, cols), 0)
    col = lax.broadcasted_iota(jnp.int32, (rows, cols), 1)
    hw_t = jnp.transpose(hw_ref[...])
    he_t = jnp.transpose(he_ref[...])
    above = above_ref[0] * jnp.where(i > 0, 1.0, 0.0)
    below = below_ref[0] * jnp.where(i < nblk - 1, 1.0, 0.0)
    if with_edges:
        en_ref, es_ref, ew_ref, ee_ref, qw_ref, qe_ref = rest[1:]

        @pl.when(i == 0)
        def _():
            qw_ref[...] = jnp.zeros_like(qw_ref)
            qe_ref[...] = jnp.zeros_like(qe_ref)

    if with_edges:
        lane = lax.broadcasted_iota(jnp.int32, qw_ref.shape, 1)
        qw = qw_ref[...]
        qe = qe_ref[...]
    for l in range(LB):
        u = u_ref[l]
        prev = u_ref[l - 1] if l > 0 else above
        nxt = u_ref[l + 1] if l < LB - 1 else below
        w = wet * u
        north = jnp.where(row == 0, hn_ref[l:l + 1, :], pltpu.roll(w, 1, 0))
        south = jnp.where(row == rows - 1, hs_ref[l:l + 1, :], pltpu.roll(w, rows - 1, 0))
        west = jnp.where(col == 0, hw_t[:, l:l + 1], pltpu.roll(w, 1, 1))
        east = jnp.where(col == cols - 1, he_t[:, l:l + 1], pltpu.roll(w, cols - 1, 1))
        lateral = north + south + west + east - 4.0 * w
        vertical = prev + nxt - 2.0 * u
        res = wet * (u + horiz * lateral + vert * vertical)
        if with_force and l == 0:
            res = res + jnp.where(i == 0, 1.0, 0.0) * (force_gain * wet * force_ref[...])
        out_ref[l] = res
        if with_edges:
            fw = wet * res
            en_ref[l:l + 1, :] = fw[0:1, :]
            es_ref[l:l + 1, :] = fw[rows - 1:rows, :]
            hit = lane == i * LB + l
            qw = jnp.where(hit, fw[:, 0:1], qw)
            qe = jnp.where(hit, fw[:, cols - 1:cols], qe)

    if with_edges:
        qw_ref[...] = qw
        qe_ref[...] = qe

        @pl.when(i == nblk - 1)
        def _():
            lev = ew_ref.shape[0]
            ew_ref[...] = jnp.transpose(qw_ref[...])[0:lev, :]
            ee_ref[...] = jnp.transpose(qe_ref[...])[0:lev, :]


def edges_kernel(wet_ref, u_ref, en_ref, es_ref, ew_ref, ee_ref, qw_ref, qe_ref):
    i = pl.program_id(0)
    nblk = pl.num_programs(0)
    wet = wet_ref[...]
    rows, cols = wet.shape

    @pl.when(i == 0)
    def _():
        qw_ref[...] = jnp.zeros_like(qw_ref)
        qe_ref[...] = jnp.zeros_like(qe_ref)

    lane = lax.broadcasted_iota(jnp.int32, qw_ref.shape, 1)
    qw = qw_ref[...]
    qe = qe_ref[...]
    for l in range(LB):
        fw = wet * u_ref[l]
        en_ref[l:l + 1, :] = fw[0:1, :]
        es_ref[l:l + 1, :] = fw[rows - 1:rows, :]
        hit = lane == i * LB + l
        qw = jnp.where(hit, fw[:, 0:1], qw)
        qe = jnp.where(hit, fw[:, cols - 1:cols], qe)
    qw_ref[...] = qw
    qe_ref[...] = qe

    @pl.when(i == nblk - 1)
    def _():
        lev = ew_ref.shape[0]
        ew_ref[...] = jnp.transpose(qw_ref[...])[0:lev, :]
        ee_ref[...] = jnp.transpose(qe_ref[...])[0:lev, :]


def masked_edges(wet, u):
    lev, rows, cols = u.shape
    lvl2 = pl.BlockSpec((LB, cols), lambda i: (i, 0))
    full2 = lambda shape: pl.BlockSpec(shape, lambda i: (0, 0))
    return pl.pallas_call(
        edges_kernel,
        grid=(lev // LB,),
        in_specs=[full2((rows, cols)), pl.BlockSpec((LB, rows, cols), lambda i: (i, 0, 0))],
        out_specs=[lvl2, lvl2, full2((lev, rows)), full2((lev, rows))],
        out_shape=[jax.ShapeDtypeStruct((lev, cols), jnp.float32)] * 2
        + [jax.ShapeDtypeStruct((lev, rows), jnp.float32)] * 2,
        scratch_shapes=[pltpu.VMEM((rows, 128), jnp.float32)] * 2,
        compiler_params=pltpu.CompilerParams(dimension_semantics=("arbitrary",)),
        cost_estimate=pl.CostEstimate(flops=2 * u.size, bytes_accessed=4 * u.size, transcendentals=0),
    )(wet, u)


def force_kernel(x_ref, wet_ref, f_ref, out_ref):
    out_ref[0] = x_ref[0] + force_gain * wet_ref[...] * f_ref[...]


def add_force(x, wet, f):
    lev, rows, cols = x.shape
    plane = pl.BlockSpec((rows, cols), lambda i: (0, 0))
    level0 = pl.BlockSpec((1, rows, cols), lambda i: (0, 0, 0))
    return pl.pallas_call(
        force_kernel,
        grid=(1,),
        in_specs=[level0, plane, plane],
        out_specs=level0,
        out_shape=jax.ShapeDtypeStruct(x.shape, x.dtype),
        input_output_aliases={0: 0},
    )(x, wet, f)


def stencil_step(coef, wet, u, halos, force=None, with_edges=False):
    lev, rows, cols = u.shape
    nblk = lev // LB
    full2 = lambda shape: pl.BlockSpec(shape, lambda i: (0, 0))
    lvl2 = pl.BlockSpec((LB, cols), lambda i: (i, 0))
    in_specs = [
        pl.BlockSpec(memory_space=pltpu.SMEM),
        full2((rows, cols)),
        pl.BlockSpec((LB, rows, cols), lambda i: (i, 0, 0)),
        pl.BlockSpec((1, rows, cols), lambda i: (jnp.maximum(i * LB - 1, 0), 0, 0)),
        pl.BlockSpec((1, rows, cols), lambda i: (jnp.minimum(i * LB + LB, lev - 1), 0, 0)),
        lvl2, lvl2, lvl2, lvl2,
    ]
    args = [coef, wet, u, u, u] + list(halos)
    if force is not None:
        in_specs.append(full2((rows, cols)))
        args.append(force)
    out_shape = [jax.ShapeDtypeStruct((lev, rows, cols), jnp.float32)]
    out_specs = [pl.BlockSpec((LB, rows, cols), lambda i: (i, 0, 0))]
    scratch = []
    if with_edges:
        out_shape += [jax.ShapeDtypeStruct((lev, cols), jnp.float32)] * 2
        out_shape += [jax.ShapeDtypeStruct((lev, rows), jnp.float32)] * 2
        out_specs += [lvl2, lvl2, full2((lev, rows)), full2((lev, rows))]
        scratch = [pltpu.VMEM((rows, 128), jnp.float32)] * 2
    return pl.pallas_call(
        functools.partial(stencil_kernel, with_edges, force is not None),
        grid=(nblk,),
        in_specs=in_specs,
        out_specs=out_specs,
        out_shape=out_shape,
        scratch_shapes=scratch,
        compiler_params=pltpu.CompilerParams(dimension_semantics=("arbitrary",)),
        cost_estimate=pl.CostEstimate(flops=30 * u.size, bytes_accessed=12 * u.size, transcendentals=0),
    )(*args)


def exchange(en, es, ew, ee):
    ngx, ngy = lax.axis_size("gx"), lax.axis_size("gy")
    hn = lax.ppermute(es, "gx", shift_pairs(ngx, True))
    hs = lax.ppermute(en, "gx", shift_pairs(ngx, False))
    hw = lax.ppermute(ee, "gy", shift_pairs(ngy, True))
    he = lax.ppermute(ew, "gy", shift_pairs(ngy, False))
    return hn, hs, hw, he


def bucket_kernel(inv_ref, lab_ref, contrib_ref, out_ref):
    ndest = out_ref.shape[0]
    ntiles = contrib_ref.shape[0]
    sub = lax.broadcasted_iota(jnp.int32, (KF, CY), 0)

    def body(d, carry):
        labv = jnp.zeros((KF, CY), jnp.float32)
        for c in range(CAP):
            t = inv_ref[d * CAP + c]
            val = contrib_ref[jnp.minimum(t, ntiles - 1)]
            out_ref[d, c] = jnp.where(t < ntiles, val, 0.0)
            labv = jnp.where(sub == c, lab_ref[d * CAP + c].astype(jnp.float32), labv)
        out_ref[d, CAP] = labv
        return carry

    lax.fori_loop(0, ndest, body, 0)


def local(states, surface, land_mask, tile_weights, tile_source, tile_target, tile_row):
    group = lax.axis_index("mp")
    ndev = lax.axis_size("gx") * lax.axis_size("gy")
    state = states[0]
    lev, rows_here, cols_here = state.shape
    wet = jnp.where(
        group == 0, jnp.ones(land_mask.shape, jnp.float32), land_mask.astype(jnp.float32)
    )
    coef = jnp.stack([jnp.where(group == 0, 0.15, 0.12), jnp.where(group == 0, 0.1, 0.15)]).astype(
        jnp.float32
    )

    src = (surface[0] * wet).astype(jnp.bfloat16)
    source = tile_source[0, 0, 0]
    target = tile_target[0, 0, 0, :, 0]
    dest_row = tile_row[0, 0, 0]
    ntiles = source.shape[0]
    picked = jnp.take(src, source, axis=1)
    contrib = jnp.einsum(
        "tji,kti->tkj", tile_weights[0, 0, 0], picked, preferred_element_type=jnp.float32
    )
    onehot = (target[:, None] == jnp.arange(ndev, dtype=jnp.int32)[None, :]).astype(jnp.int32)
    earlier = jnp.cumsum(onehot, axis=0) - onehot
    rank = jnp.sum(earlier * onehot, axis=1)
    slot = target * CAP + rank
    inv = jnp.full((ndev * CAP,), ntiles, jnp.int32).at[slot].set(jnp.arange(ntiles, dtype=jnp.int32))
    labels = jnp.zeros((ndev * CAP,), jnp.int32).at[slot].set(dest_row)
    buckets = pl.pallas_call(
        bucket_kernel,
        in_specs=[
            pl.BlockSpec(memory_space=pltpu.SMEM),
            pl.BlockSpec(memory_space=pltpu.SMEM),
            pl.BlockSpec(memory_space=pltpu.VMEM),
        ],
        out_specs=pl.BlockSpec(memory_space=pltpu.VMEM),
        out_shape=jax.ShapeDtypeStruct((ndev, CAP + 1, KF, CY), jnp.float32),
    )(inv, labels, contrib)
    arrived = lax.all_to_all(buckets, ("gx", "gy"), split_axis=0, concat_axis=0, tiled=True)
    got_rows = arrived[:, CAP, :, 0].astype(jnp.int32)
    select = (
        got_rows[:, :, None] == jnp.arange(rows_here, dtype=jnp.int32)[None, None, :]
    ).astype(jnp.float32)
    sent = jnp.einsum(
        "scr,sckj->krj", select, arrived[:, :CAP], precision=lax.Precision.HIGHEST
    )
    received = lax.ppermute(sent, "mp", [(0, 1), (1, 0)])

    halos0 = exchange(*masked_edges(wet, state))
    first, en, es, ew, ee = stencil_step(coef, wet, state, halos0, with_edges=True)
    halos1 = exchange(en, es, ew, ee)
    (second,) = stencil_step(coef, wet, first, halos1)
    second = add_force(second, wet, received[0])
    return (second[None], received[None])


def solution(mesh):
    return jax.shard_map(
        local,
        mesh=mesh,
        in_specs=(
            P("mp", None, "gx", "gy"),
            P("mp", None, "gx", "gy"),
            P("gx", "gy"),
            P("mp", "gx", "gy", None, None, None),
            P("mp", "gx", "gy", None),
            P("mp", "gx", "gy", None, None),
            P("mp", "gx", "gy", None),
        ),
        out_specs=(P("mp", None, "gx", "gy"), P("mp", None, "gx", "gy")),
        check_vma=False,
    )
```

```python
import functools

import jax
import jax.numpy as jnp
from jax import lax
from jax.experimental import pallas as pl
from jax.experimental.pallas import tpu as pltpu
from jax.sharding import PartitionSpec as P

CY = 128
KF = 8
CAP = 8
LB = 8

force_gain = 0.5


def shift_pairs(devices, forward):
    up = [(i, i + 1) for i in range(devices - 1)]
    return up if forward else [(j, i) for i, j in up]


def stencil_kernel(with_edges, with_force, coef_ref, wet_ref, u_ref, above_ref, below_ref,
                   hn_ref, hs_ref, hw_ref, he_ref, *rest):
    if with_force:
        force_ref, rest = rest[0], rest[1:]
    out_ref = rest[0]
    i = pl.program_id(0)
    nblk = pl.num_programs(0)
    horiz = coef_ref[0]
    vert = coef_ref[1]
    wet = wet_ref[...]
    rows, cols = wet.shape
    row = lax.broadcasted_iota(jnp.int32, (rows, cols), 0)
    col = lax.broadcasted_iota(jnp.int32, (rows, cols), 1)
    hw_t = jnp.transpose(hw_ref[...])
    he_t = jnp.transpose(he_ref[...])
    above = above_ref[0] * jnp.where(i > 0, 1.0, 0.0)
    below = below_ref[0] * jnp.where(i < nblk - 1, 1.0, 0.0)
    if with_edges:
        en_ref, es_ref, ew_ref, ee_ref, qw_ref, qe_ref = rest[1:]

        @pl.when(i == 0)
        def _():
            qw_ref[...] = jnp.zeros_like(qw_ref)
            qe_ref[...] = jnp.zeros_like(qe_ref)

    if with_edges:
        lane = lax.broadcasted_iota(jnp.int32, qw_ref.shape, 1)
        qw = qw_ref[...]
        qe = qe_ref[...]
    for l in range(LB):
        u = u_ref[l]
        prev = u_ref[l - 1] if l > 0 else above
        nxt = u_ref[l + 1] if l < LB - 1 else below
        w = wet * u
        north = jnp.where(row == 0, hn_ref[l:l + 1, :], pltpu.roll(w, 1, 0))
        south = jnp.where(row == rows - 1, hs_ref[l:l + 1, :], pltpu.roll(w, rows - 1, 0))
        west = jnp.where(col == 0, hw_t[:, l:l + 1], pltpu.roll(w, 1, 1))
        east = jnp.where(col == cols - 1, he_t[:, l:l + 1], pltpu.roll(w, cols - 1, 1))
        lateral = north + south + west + east - 4.0 * w
        vertical = prev + nxt - 2.0 * u
        res = wet * (u + horiz * lateral + vert * vertical)
        if with_force and l == 0:
            res = res + jnp.where(i == 0, 1.0, 0.0) * (force_gain * wet * force_ref[...])
        out_ref[l] = res
        if with_edges:
            fw = wet * res
            en_ref[l:l + 1, :] = fw[0:1, :]
            es_ref[l:l + 1, :] = fw[rows - 1:rows, :]
            hit = lane == i * LB + l
            qw = jnp.where(hit, fw[:, 0:1], qw)
            qe = jnp.where(hit, fw[:, cols - 1:cols], qe)

    if with_edges:
        qw_ref[...] = qw
        qe_ref[...] = qe

        @pl.when(i == nblk - 1)
        def _():
            lev = ew_ref.shape[0]
            ew_ref[...] = jnp.transpose(qw_ref[...])[0:lev, :]
            ee_ref[...] = jnp.transpose(qe_ref[...])[0:lev, :]


def edges_kernel(wet_ref, u_ref, en_ref, es_ref, ew_ref, ee_ref, qw_ref, qe_ref):
    i = pl.program_id(0)
    nblk = pl.num_programs(0)
    wet = wet_ref[...]
    rows, cols = wet.shape

    @pl.when(i == 0)
    def _():
        qw_ref[...] = jnp.zeros_like(qw_ref)
        qe_ref[...] = jnp.zeros_like(qe_ref)

    lane = lax.broadcasted_iota(jnp.int32, qw_ref.shape, 1)
    qw = qw_ref[...]
    qe = qe_ref[...]
    for l in range(LB):
        fw = wet * u_ref[l]
        en_ref[l:l + 1, :] = fw[0:1, :]
        es_ref[l:l + 1, :] = fw[rows - 1:rows, :]
        hit = lane == i * LB + l
        qw = jnp.where(hit, fw[:, 0:1], qw)
        qe = jnp.where(hit, fw[:, cols - 1:cols], qe)
    qw_ref[...] = qw
    qe_ref[...] = qe

    @pl.when(i == nblk - 1)
    def _():
        lev = ew_ref.shape[0]
        ew_ref[...] = jnp.transpose(qw_ref[...])[0:lev, :]
        ee_ref[...] = jnp.transpose(qe_ref[...])[0:lev, :]


def masked_edges(wet, u):
    lev, rows, cols = u.shape
    lvl2 = pl.BlockSpec((LB, cols), lambda i: (i, 0))
    full2 = lambda shape: pl.BlockSpec(shape, lambda i: (0, 0))
    return pl.pallas_call(
        edges_kernel,
        grid=(lev // LB,),
        in_specs=[full2((rows, cols)), pl.BlockSpec((LB, rows, cols), lambda i: (i, 0, 0))],
        out_specs=[lvl2, lvl2, full2((lev, rows)), full2((lev, rows))],
        out_shape=[jax.ShapeDtypeStruct((lev, cols), jnp.float32)] * 2
        + [jax.ShapeDtypeStruct((lev, rows), jnp.float32)] * 2,
        scratch_shapes=[pltpu.VMEM((rows, 128), jnp.float32)] * 2,
        compiler_params=pltpu.CompilerParams(dimension_semantics=("arbitrary",)),
        cost_estimate=pl.CostEstimate(flops=2 * u.size, bytes_accessed=4 * u.size, transcendentals=0),
    )(wet, u)


def force_kernel(x_ref, wet_ref, f_ref, out_ref):
    out_ref[0] = x_ref[0] + force_gain * wet_ref[...] * f_ref[...]


def add_force(x, wet, f):
    lev, rows, cols = x.shape
    plane = pl.BlockSpec((rows, cols), lambda i: (0, 0))
    level0 = pl.BlockSpec((1, rows, cols), lambda i: (0, 0, 0))
    return pl.pallas_call(
        force_kernel,
        grid=(1,),
        in_specs=[level0, plane, plane],
        out_specs=level0,
        out_shape=jax.ShapeDtypeStruct(x.shape, x.dtype),
        input_output_aliases={0: 0},
    )(x, wet, f)


def stencil_step(coef, wet, u, halos, force=None, with_edges=False):
    lev, rows, cols = u.shape
    nblk = lev // LB
    full2 = lambda shape: pl.BlockSpec(shape, lambda i: (0, 0))
    lvl2 = pl.BlockSpec((LB, cols), lambda i: (i, 0))
    in_specs = [
        pl.BlockSpec(memory_space=pltpu.SMEM),
        full2((rows, cols)),
        pl.BlockSpec((LB, rows, cols), lambda i: (i, 0, 0)),
        pl.BlockSpec((1, rows, cols), lambda i: (jnp.maximum(i * LB - 1, 0), 0, 0)),
        pl.BlockSpec((1, rows, cols), lambda i: (jnp.minimum(i * LB + LB, lev - 1), 0, 0)),
        lvl2, lvl2, lvl2, lvl2,
    ]
    args = [coef, wet, u, u, u] + list(halos)
    if force is not None:
        in_specs.append(full2((rows, cols)))
        args.append(force)
    out_shape = [jax.ShapeDtypeStruct((lev, rows, cols), jnp.float32)]
    out_specs = [pl.BlockSpec((LB, rows, cols), lambda i: (i, 0, 0))]
    scratch = []
    if with_edges:
        out_shape += [jax.ShapeDtypeStruct((lev, cols), jnp.float32)] * 2
        out_shape += [jax.ShapeDtypeStruct((lev, rows), jnp.float32)] * 2
        out_specs += [lvl2, lvl2, full2((lev, rows)), full2((lev, rows))]
        scratch = [pltpu.VMEM((rows, 128), jnp.float32)] * 2
    return pl.pallas_call(
        functools.partial(stencil_kernel, with_edges, force is not None),
        grid=(nblk,),
        in_specs=in_specs,
        out_specs=out_specs,
        out_shape=out_shape,
        scratch_shapes=scratch,
        compiler_params=pltpu.CompilerParams(dimension_semantics=("arbitrary",)),
        cost_estimate=pl.CostEstimate(flops=30 * u.size, bytes_accessed=12 * u.size, transcendentals=0),
    )(*args)


def halo_kernel(en_ref, es_ref, ew_ref, ee_ref, hn_ref, hs_ref, hw_ref, he_ref,
                buf, send_sem, recv_sem):
    mp = lax.axis_index("mp")
    gx = lax.axis_index("gx")
    gy = lax.axis_index("gy")
    ngx = lax.axis_size("gx")
    ngy = lax.axis_size("gy")
    mesh_id = pl.DeviceIdType.MESH
    links = [
        (gx < ngx - 1, (mp, gx + 1, gy), es_ref, 0),
        (gx > 0, (mp, gx - 1, gy), en_ref, 1),
        (gy < ngy - 1, (mp, gx, gy + 1), ee_ref, 2),
        (gy > 0, (mp, gx, gy - 1), ew_ref, 3),
    ]
    barrier = pltpu.get_barrier_semaphore()
    count = jnp.int32(0)
    for present, dev, _, _ in links:
        @pl.when(present)
        def _():
            pl.semaphore_signal(barrier, 1, device_id=dev, device_id_type=mesh_id)

        count = count + present.astype(jnp.int32)
    pl.semaphore_wait(barrier, count)

    copies = []
    for present, dev, src, slot in links:
        copy = pltpu.make_async_remote_copy(
            src_ref=src,
            dst_ref=buf.at[slot],
            send_sem=send_sem.at[slot],
            recv_sem=recv_sem.at[slot],
            device_id=dev,
            device_id_type=mesh_id,
        )
        pl.when(present)(copy.start)
        copies.append((present, copy))
    for present, copy in copies:
        pl.when(present)(copy.wait_send)
    fills = [gx > 0, gx < ngx - 1, gy > 0, gy < ngy - 1]
    outs = [hn_ref, hs_ref, hw_ref, he_ref]
    for slot, (filled, out) in enumerate(zip(fills, outs)):
        _, copy = copies[slot]

        @pl.when(filled)
        def _():
            copy.wait_recv()
            out[...] = buf[slot]

        @pl.when(jnp.logical_not(filled))
        def _():
            out[...] = jnp.zeros_like(out)


def exchange(en, es, ew, ee, call):
    shape = jax.ShapeDtypeStruct(en.shape, en.dtype)
    vmem = pl.BlockSpec(memory_space=pltpu.VMEM)
    return pl.pallas_call(
        halo_kernel,
        in_specs=[vmem] * 4,
        out_specs=[vmem] * 4,
        out_shape=[shape] * 4,
        scratch_shapes=[
            pltpu.VMEM((4,) + en.shape, en.dtype),
            pltpu.SemaphoreType.DMA((4,)),
            pltpu.SemaphoreType.DMA((4,)),
        ],
        compiler_params=pltpu.CompilerParams(collective_id=call, has_side_effects=True),
    )(en, es, ew, ee)


def bucket_kernel(inv_ref, lab_ref, contrib_ref, out_ref):
    ndest = out_ref.shape[0]
    ntiles = contrib_ref.shape[0]
    sub = lax.broadcasted_iota(jnp.int32, (KF, CY), 0)

    def body(d, carry):
        labv = jnp.zeros((KF, CY), jnp.float32)
        for c in range(CAP):
            t = inv_ref[d * CAP + c]
            val = contrib_ref[jnp.minimum(t, ntiles - 1)]
            out_ref[d, c] = jnp.where(t < ntiles, val, 0.0)
            labv = jnp.where(sub == c, lab_ref[d * CAP + c].astype(jnp.float32), labv)
        out_ref[d, CAP] = labv
        return carry

    lax.fori_loop(0, ndest, body, 0)


def local(states, surface, land_mask, tile_weights, tile_source, tile_target, tile_row):
    group = lax.axis_index("mp")
    ndev = lax.axis_size("gx") * lax.axis_size("gy")
    state = states[0]
    lev, rows_here, cols_here = state.shape
    wet = jnp.where(
        group == 0, jnp.ones(land_mask.shape, jnp.float32), land_mask.astype(jnp.float32)
    )
    coef = jnp.stack([jnp.where(group == 0, 0.15, 0.12), jnp.where(group == 0, 0.1, 0.15)]).astype(
        jnp.float32
    )

    src = (surface[0] * wet).astype(jnp.bfloat16)
    source = tile_source[0, 0, 0]
    target = tile_target[0, 0, 0, :, 0]
    dest_row = tile_row[0, 0, 0]
    ntiles = source.shape[0]
    picked = jnp.take(src, source, axis=1)
    contrib = jnp.einsum(
        "tji,kti->tkj", tile_weights[0, 0, 0], picked, preferred_element_type=jnp.float32
    )
    onehot = (target[:, None] == jnp.arange(ndev, dtype=jnp.int32)[None, :]).astype(jnp.int32)
    earlier = jnp.cumsum(onehot, axis=0) - onehot
    rank = jnp.sum(earlier * onehot, axis=1)
    slot = target * CAP + rank
    inv = jnp.full((ndev * CAP,), ntiles, jnp.int32).at[slot].set(jnp.arange(ntiles, dtype=jnp.int32))
    labels = jnp.zeros((ndev * CAP,), jnp.int32).at[slot].set(dest_row)
    buckets = pl.pallas_call(
        bucket_kernel,
        in_specs=[
            pl.BlockSpec(memory_space=pltpu.SMEM),
            pl.BlockSpec(memory_space=pltpu.SMEM),
            pl.BlockSpec(memory_space=pltpu.VMEM),
        ],
        out_specs=pl.BlockSpec(memory_space=pltpu.VMEM),
        out_shape=jax.ShapeDtypeStruct((ndev, CAP + 1, KF, CY), jnp.float32),
    )(inv, labels, contrib)
    arrived = lax.all_to_all(buckets, ("gx", "gy"), split_axis=0, concat_axis=0, tiled=True)
    got_rows = arrived[:, CAP, :, 0].astype(jnp.int32)
    select = (
        got_rows[:, :, None] == jnp.arange(rows_here, dtype=jnp.int32)[None, None, :]
    ).astype(jnp.float32)
    sent = jnp.einsum(
        "scr,sckj->krj", select, arrived[:, :CAP], precision=lax.Precision.HIGHEST
    )
    received = lax.ppermute(sent, "mp", [(0, 1), (1, 0)])

    halos0 = exchange(*masked_edges(wet, state), 0)
    first, en, es, ew, ee = stencil_step(coef, wet, state, halos0, with_edges=True)
    halos1 = exchange(en, es, ew, ee, 1)
    (second,) = stencil_step(coef, wet, first, halos1)
    second = add_force(second, wet, received[0])
    return (second[None], received[None])


def solution(mesh):
    return jax.shard_map(
        local,
        mesh=mesh,
        in_specs=(
            P("mp", None, "gx", "gy"),
            P("mp", None, "gx", "gy"),
            P("gx", "gy"),
            P("mp", "gx", "gy", None, None, None),
            P("mp", "gx", "gy", None),
            P("mp", "gx", "gy", None, None),
            P("mp", "gx", "gy", None),
        ),
        out_specs=(P("mp", None, "gx", "gy"), P("mp", None, "gx", "gy")),
        check_vma=False,
    )
```

```python
import functools

import jax
import jax.numpy as jnp
from jax import lax
from jax.experimental import pallas as pl
from jax.experimental.pallas import tpu as pltpu
from jax.sharding import PartitionSpec as P

CY = 128
KF = 8
CAP = 8
LB = 8

force_gain = 0.5


def shift_pairs(devices, forward):
    up = [(i, i + 1) for i in range(devices - 1)]
    return up if forward else [(j, i) for i, j in up]


def start_spread(buckets_ref, recv, send_sem, recv_sem):
    mp = lax.axis_index("mp")
    ngy = lax.axis_size("gy")
    ndev = lax.axis_size("gx") * ngy
    me = lax.axis_index("gx") * ngy + lax.axis_index("gy")
    mesh_id = pl.DeviceIdType.MESH
    barrier = pltpu.get_barrier_semaphore()

    def greet(d, carry):
        @pl.when(d != me)
        def _():
            pl.semaphore_signal(barrier, 1, device_id=(mp, d // ngy, d % ngy), device_id_type=mesh_id)

        return carry

    lax.fori_loop(0, ndev, greet, 0)
    pl.semaphore_wait(barrier, ndev - 1)
    recv[me] = buckets_ref[me]

    def send(d, carry):
        @pl.when(d != me)
        def _():
            pltpu.make_async_remote_copy(
                src_ref=buckets_ref.at[d],
                dst_ref=recv.at[me],
                send_sem=send_sem.at[d],
                recv_sem=recv_sem.at[me],
                device_id=(mp, d // ngy, d % ngy),
                device_id_type=mesh_id,
            ).start()

        return carry

    lax.fori_loop(0, ndev, send, 0)


def finish_spread(buckets_ref, recv, send_sem, recv_sem, arrived_ref):
    ngy = lax.axis_size("gy")
    ndev = lax.axis_size("gx") * ngy
    me = lax.axis_index("gx") * ngy + lax.axis_index("gy")

    def wait(d, carry):
        @pl.when(d != me)
        def _():
            copy = pltpu.make_async_remote_copy(
                src_ref=buckets_ref.at[d],
                dst_ref=recv.at[d],
                send_sem=send_sem.at[d],
                recv_sem=recv_sem.at[d],
                device_id=(lax.axis_index("mp"), d // ngy, d % ngy),
                device_id_type=pl.DeviceIdType.MESH,
            )
            copy.wait_send()
            copy.wait_recv()

        return carry

    lax.fori_loop(0, ndev, wait, 0)
    arrived_ref[...] = recv[...]


def stencil_kernel(with_edges, with_force, coef_ref, wet_ref, u_ref, above_ref, below_ref,
                   hn_ref, hs_ref, hw_ref, he_ref, *rest):
    if with_force:
        force_ref, rest = rest[0], rest[1:]
    if with_edges:
        buckets_ref, rest = rest[0], rest[1:]
    out_ref = rest[0]
    i = pl.program_id(0)
    nblk = pl.num_programs(0)
    horiz = coef_ref[0]
    vert = coef_ref[1]
    wet = wet_ref[...]
    rows, cols = wet.shape
    row = lax.broadcasted_iota(jnp.int32, (rows, cols), 0)
    col = lax.broadcasted_iota(jnp.int32, (rows, cols), 1)
    hw_t = jnp.transpose(hw_ref[...])
    he_t = jnp.transpose(he_ref[...])
    above = above_ref[0] * jnp.where(i > 0, 1.0, 0.0)
    below = below_ref[0] * jnp.where(i < nblk - 1, 1.0, 0.0)
    if with_edges:
        en_ref, es_ref, ew_ref, ee_ref, arrived_ref, qw_ref, qe_ref, recv, send_sem, recv_sem = rest[1:]

        @pl.when(i == 0)
        def _():
            start_spread(buckets_ref, recv, send_sem, recv_sem)
            qw_ref[...] = jnp.zeros_like(qw_ref)
            qe_ref[...] = jnp.zeros_like(qe_ref)

    if with_edges:
        lane = lax.broadcasted_iota(jnp.int32, qw_ref.shape, 1)
        qw = qw_ref[...]
        qe = qe_ref[...]
    for l in range(LB):
        u = u_ref[l]
        prev = u_ref[l - 1] if l > 0 else above
        nxt = u_ref[l + 1] if l < LB - 1 else below
        w = wet * u
        north = jnp.where(row == 0, hn_ref[l:l + 1, :], pltpu.roll(w, 1, 0))
        south = jnp.where(row == rows - 1, hs_ref[l:l + 1, :], pltpu.roll(w, rows - 1, 0))
        west = jnp.where(col == 0, hw_t[:, l:l + 1], pltpu.roll(w, 1, 1))
        east = jnp.where(col == cols - 1, he_t[:, l:l + 1], pltpu.roll(w, cols - 1, 1))
        lateral = north + south + west + east - 4.0 * w
        vertical = prev + nxt - 2.0 * u
        res = wet * (u + horiz * lateral + vert * vertical)
        if with_force and l == 0:
            res = res + jnp.where(i == 0, 1.0, 0.0) * (force_gain * wet * force_ref[...])
        out_ref[l] = res
        if with_edges:
            fw = wet * res
            en_ref[l:l + 1, :] = fw[0:1, :]
            es_ref[l:l + 1, :] = fw[rows - 1:rows, :]
            hit = lane == i * LB + l
            qw = jnp.where(hit, fw[:, 0:1], qw)
            qe = jnp.where(hit, fw[:, cols - 1:cols], qe)

    if with_edges:
        qw_ref[...] = qw
        qe_ref[...] = qe

        @pl.when(i == nblk - 1)
        def _():
            lev = ew_ref.shape[0]
            ew_ref[...] = jnp.transpose(qw_ref[...])[0:lev, :]
            ee_ref[...] = jnp.transpose(qe_ref[...])[0:lev, :]
            finish_spread(buckets_ref, recv, send_sem, recv_sem, arrived_ref)


def edges_kernel(wet_ref, u_ref, en_ref, es_ref, ew_ref, ee_ref, qw_ref, qe_ref):
    i = pl.program_id(0)
    nblk = pl.num_programs(0)
    wet = wet_ref[...]
    rows, cols = wet.shape

    @pl.when(i == 0)
    def _():
        qw_ref[...] = jnp.zeros_like(qw_ref)
        qe_ref[...] = jnp.zeros_like(qe_ref)

    lane = lax.broadcasted_iota(jnp.int32, qw_ref.shape, 1)
    qw = qw_ref[...]
    qe = qe_ref[...]
    for l in range(LB):
        fw = wet * u_ref[l]
        en_ref[l:l + 1, :] = fw[0:1, :]
        es_ref[l:l + 1, :] = fw[rows - 1:rows, :]
        hit = lane == i * LB + l
        qw = jnp.where(hit, fw[:, 0:1], qw)
        qe = jnp.where(hit, fw[:, cols - 1:cols], qe)
    qw_ref[...] = qw
    qe_ref[...] = qe

    @pl.when(i == nblk - 1)
    def _():
        lev = ew_ref.shape[0]
        ew_ref[...] = jnp.transpose(qw_ref[...])[0:lev, :]
        ee_ref[...] = jnp.transpose(qe_ref[...])[0:lev, :]


def masked_edges(wet, u):
    lev, rows, cols = u.shape
    lvl2 = pl.BlockSpec((LB, cols), lambda i: (i, 0))
    full2 = lambda shape: pl.BlockSpec(shape, lambda i: (0, 0))
    return pl.pallas_call(
        edges_kernel,
        grid=(lev // LB,),
        in_specs=[full2((rows, cols)), pl.BlockSpec((LB, rows, cols), lambda i: (i, 0, 0))],
        out_specs=[lvl2, lvl2, full2((lev, rows)), full2((lev, rows))],
        out_shape=[jax.ShapeDtypeStruct((lev, cols), jnp.float32)] * 2
        + [jax.ShapeDtypeStruct((lev, rows), jnp.float32)] * 2,
        scratch_shapes=[pltpu.VMEM((rows, 128), jnp.float32)] * 2,
        compiler_params=pltpu.CompilerParams(dimension_semantics=("arbitrary",)),
        cost_estimate=pl.CostEstimate(flops=2 * u.size, bytes_accessed=4 * u.size, transcendentals=0),
    )(wet, u)


def force_kernel(x_ref, wet_ref, f_ref, out_ref):
    out_ref[0] = x_ref[0] + force_gain * wet_ref[...] * f_ref[...]


def add_force(x, wet, f):
    lev, rows, cols = x.shape
    plane = pl.BlockSpec((rows, cols), lambda i: (0, 0))
    level0 = pl.BlockSpec((1, rows, cols), lambda i: (0, 0, 0))
    return pl.pallas_call(
        force_kernel,
        grid=(1,),
        in_specs=[level0, plane, plane],
        out_specs=level0,
        out_shape=jax.ShapeDtypeStruct(x.shape, x.dtype),
        input_output_aliases={0: 0},
    )(x, wet, f)


def stencil_step(coef, wet, u, halos, force=None, buckets=None):
    with_edges = buckets is not None
    lev, rows, cols = u.shape
    nblk = lev // LB
    full2 = lambda shape: pl.BlockSpec(shape, lambda i: (0, 0))
    lvl2 = pl.BlockSpec((LB, cols), lambda i: (i, 0))
    in_specs = [
        pl.BlockSpec(memory_space=pltpu.SMEM),
        full2((rows, cols)),
        pl.BlockSpec((LB, rows, cols), lambda i: (i, 0, 0)),
        pl.BlockSpec((1, rows, cols), lambda i: (jnp.maximum(i * LB - 1, 0), 0, 0)),
        pl.BlockSpec((1, rows, cols), lambda i: (jnp.minimum(i * LB + LB, lev - 1), 0, 0)),
        lvl2, lvl2, lvl2, lvl2,
    ]
    args = [coef, wet, u, u, u] + list(halos)
    if force is not None:
        in_specs.append(full2((rows, cols)))
        args.append(force)
    if with_edges:
        in_specs.append(pl.BlockSpec(buckets.shape, lambda i: (0, 0, 0, 0)))
        args.append(buckets)
    out_shape = [jax.ShapeDtypeStruct((lev, rows, cols), jnp.float32)]
    out_specs = [pl.BlockSpec((LB, rows, cols), lambda i: (i, 0, 0))]
    scratch = []
    params = dict(dimension_semantics=("arbitrary",))
    if with_edges:
        out_shape += [jax.ShapeDtypeStruct((lev, cols), jnp.float32)] * 2
        out_shape += [jax.ShapeDtypeStruct((lev, rows), jnp.float32)] * 2
        out_shape += [jax.ShapeDtypeStruct(buckets.shape, buckets.dtype)]
        out_specs += [lvl2, lvl2, full2((lev, rows)), full2((lev, rows))]
        out_specs += [pl.BlockSpec(buckets.shape, lambda i: (0, 0, 0, 0))]
        scratch = [pltpu.VMEM((rows, 128), jnp.float32)] * 2 + [
            pltpu.VMEM(buckets.shape, buckets.dtype),
            pltpu.SemaphoreType.DMA((buckets.shape[0],)),
            pltpu.SemaphoreType.DMA((buckets.shape[0],)),
        ]
        params.update(collective_id=2, has_side_effects=True)
    return pl.pallas_call(
        functools.partial(stencil_kernel, with_edges, force is not None),
        grid=(nblk,),
        in_specs=in_specs,
        out_specs=out_specs,
        out_shape=out_shape,
        scratch_shapes=scratch,
        compiler_params=pltpu.CompilerParams(**params),
        cost_estimate=pl.CostEstimate(flops=30 * u.size, bytes_accessed=12 * u.size, transcendentals=0),
    )(*args)


def halo_kernel(en_ref, es_ref, ew_ref, ee_ref, hn_ref, hs_ref, hw_ref, he_ref,
                buf, send_sem, recv_sem):
    mp = lax.axis_index("mp")
    gx = lax.axis_index("gx")
    gy = lax.axis_index("gy")
    ngx = lax.axis_size("gx")
    ngy = lax.axis_size("gy")
    mesh_id = pl.DeviceIdType.MESH
    links = [
        (gx < ngx - 1, (mp, gx + 1, gy), es_ref, 0),
        (gx > 0, (mp, gx - 1, gy), en_ref, 1),
        (gy < ngy - 1, (mp, gx, gy + 1), ee_ref, 2),
        (gy > 0, (mp, gx, gy - 1), ew_ref, 3),
    ]
    barrier = pltpu.get_barrier_semaphore()
    count = jnp.int32(0)
    for present, dev, _, _ in links:
        @pl.when(present)
        def _():
            pl.semaphore_signal(barrier, 1, device_id=dev, device_id_type=mesh_id)

        count = count + present.astype(jnp.int32)
    pl.semaphore_wait(barrier, count)

    copies = []
    for present, dev, src, slot in links:
        copy = pltpu.make_async_remote_copy(
            src_ref=src,
            dst_ref=buf.at[slot],
            send_sem=send_sem.at[slot],
            recv_sem=recv_sem.at[slot],
            device_id=dev,
            device_id_type=mesh_id,
        )
        pl.when(present)(copy.start)
        copies.append((present, copy))
    for present, copy in copies:
        pl.when(present)(copy.wait_send)
    fills = [gx > 0, gx < ngx - 1, gy > 0, gy < ngy - 1]
    outs = [hn_ref, hs_ref, hw_ref, he_ref]
    for slot, (filled, out) in enumerate(zip(fills, outs)):
        _, copy = copies[slot]

        @pl.when(filled)
        def _():
            copy.wait_recv()
            out[...] = buf[slot]

        @pl.when(jnp.logical_not(filled))
        def _():
            out[...] = jnp.zeros_like(out)


def exchange(en, es, ew, ee, call):
    shape = jax.ShapeDtypeStruct(en.shape, en.dtype)
    vmem = pl.BlockSpec(memory_space=pltpu.VMEM)
    return pl.pallas_call(
        halo_kernel,
        in_specs=[vmem] * 4,
        out_specs=[vmem] * 4,
        out_shape=[shape] * 4,
        scratch_shapes=[
            pltpu.VMEM((4,) + en.shape, en.dtype),
            pltpu.SemaphoreType.DMA((4,)),
            pltpu.SemaphoreType.DMA((4,)),
        ],
        compiler_params=pltpu.CompilerParams(collective_id=call, has_side_effects=True),
    )(en, es, ew, ee)


def bucket_kernel(inv_ref, lab_ref, contrib_ref, out_ref):
    ndest = out_ref.shape[0]
    ntiles = contrib_ref.shape[0]
    sub = lax.broadcasted_iota(jnp.int32, (KF, CY), 0)

    def body(d, carry):
        labv = jnp.zeros((KF, CY), jnp.float32)
        for c in range(CAP):
            t = inv_ref[d * CAP + c]
            val = contrib_ref[jnp.minimum(t, ntiles - 1)]
            out_ref[d, c] = jnp.where(t < ntiles, val, 0.0)
            labv = jnp.where(sub == c, lab_ref[d * CAP + c].astype(jnp.float32), labv)
        out_ref[d, CAP] = labv
        return carry

    lax.fori_loop(0, ndest, body, 0)


def local(states, surface, land_mask, tile_weights, tile_source, tile_target, tile_row):
    group = lax.axis_index("mp")
    ndev = lax.axis_size("gx") * lax.axis_size("gy")
    state = states[0]
    lev, rows_here, cols_here = state.shape
    wet = jnp.where(
        group == 0, jnp.ones(land_mask.shape, jnp.float32), land_mask.astype(jnp.float32)
    )
    coef = jnp.stack([jnp.where(group == 0, 0.15, 0.12), jnp.where(group == 0, 0.1, 0.15)]).astype(
        jnp.float32
    )

    src = (surface[0] * wet).astype(jnp.bfloat16)
    source = tile_source[0, 0, 0]
    target = tile_target[0, 0, 0, :, 0]
    dest_row = tile_row[0, 0, 0]
    ntiles = source.shape[0]
    picked = jnp.take(src, source, axis=1)
    contrib = jnp.einsum(
        "tji,kti->tkj", tile_weights[0, 0, 0], picked, preferred_element_type=jnp.float32
    )
    onehot = (target[:, None] == jnp.arange(ndev, dtype=jnp.int32)[None, :]).astype(jnp.int32)
    earlier = jnp.cumsum(onehot, axis=0) - onehot
    rank = jnp.sum(earlier * onehot, axis=1)
    slot = target * CAP + rank
    inv = jnp.full((ndev * CAP,), ntiles, jnp.int32).at[slot].set(jnp.arange(ntiles, dtype=jnp.int32))
    labels = jnp.zeros((ndev * CAP,), jnp.int32).at[slot].set(dest_row)
    buckets = pl.pallas_call(
        bucket_kernel,
        in_specs=[
            pl.BlockSpec(memory_space=pltpu.SMEM),
            pl.BlockSpec(memory_space=pltpu.SMEM),
            pl.BlockSpec(memory_space=pltpu.VMEM),
        ],
        out_specs=pl.BlockSpec(memory_space=pltpu.VMEM),
        out_shape=jax.ShapeDtypeStruct((ndev, CAP + 1, KF, CY), jnp.float32),
    )(inv, labels, contrib)
    halos0 = exchange(*masked_edges(wet, state), 0)
    first, en, es, ew, ee, arrived = stencil_step(coef, wet, state, halos0, buckets=buckets)
    got_rows = arrived[:, CAP, :, 0].astype(jnp.int32)
    select = (
        got_rows[:, :, None] == jnp.arange(rows_here, dtype=jnp.int32)[None, None, :]
    ).astype(jnp.float32)
    sent = jnp.einsum(
        "scr,sckj->krj", select, arrived[:, :CAP], precision=lax.Precision.HIGHEST
    )
    received = lax.ppermute(sent, "mp", [(0, 1), (1, 0)])

    halos1 = exchange(en, es, ew, ee, 1)
    (second,) = stencil_step(coef, wet, first, halos1)
    second = add_force(second, wet, received[0])
    return (second[None], received[None])


def solution(mesh):
    return jax.shard_map(
        local,
        mesh=mesh,
        in_specs=(
            P("mp", None, "gx", "gy"),
            P("mp", None, "gx", "gy"),
            P("gx", "gy"),
            P("mp", "gx", "gy", None, None, None),
            P("mp", "gx", "gy", None),
            P("mp", "gx", "gy", None, None),
            P("mp", "gx", "gy", None),
        ),
        out_specs=(P("mp", None, "gx", "gy"), P("mp", None, "gx", "gy")),
        check_vma=False,
    )
```

```python
import functools

import jax
import jax.numpy as jnp
from jax import lax
from jax.experimental import pallas as pl
from jax.experimental.pallas import tpu as pltpu
from jax.sharding import PartitionSpec as P

CY = 128
KF = 8
CAP = 8
LB = 8

force_gain = 0.5


def shift_pairs(devices, forward):
    up = [(i, i + 1) for i in range(devices - 1)]
    return up if forward else [(j, i) for i, j in up]


def start_spread(buckets_ref, recv, send_sem, recv_sem):
    mp = lax.axis_index("mp")
    ngy = lax.axis_size("gy")
    ndev = lax.axis_size("gx") * ngy
    me = lax.axis_index("gx") * ngy + lax.axis_index("gy")
    mesh_id = pl.DeviceIdType.MESH
    barrier = pltpu.get_barrier_semaphore()

    def greet(d, carry):
        @pl.when(d != me)
        def _():
            pl.semaphore_signal(barrier, 1, device_id=(mp, d // ngy, d % ngy), device_id_type=mesh_id)

        return carry

    lax.fori_loop(0, ndev, greet, 0)
    pl.semaphore_wait(barrier, ndev - 1)
    recv[me] = buckets_ref[me]

    def send(k, carry):
        d = (me + k) % ndev
        pltpu.make_async_remote_copy(
            src_ref=buckets_ref.at[d],
            dst_ref=recv.at[me],
            send_sem=send_sem.at[d],
            recv_sem=recv_sem.at[me],
            device_id=(mp, d // ngy, d % ngy),
            device_id_type=mesh_id,
        ).start()
        return carry

    lax.fori_loop(1, ndev, send, 0)


def finish_spread(buckets_ref, recv, send_sem, recv_sem, arrived_ref):
    ngy = lax.axis_size("gy")
    ndev = lax.axis_size("gx") * ngy
    me = lax.axis_index("gx") * ngy + lax.axis_index("gy")

    def wait(d, carry):
        @pl.when(d != me)
        def _():
            copy = pltpu.make_async_remote_copy(
                src_ref=buckets_ref.at[d],
                dst_ref=recv.at[d],
                send_sem=send_sem.at[d],
                recv_sem=recv_sem.at[d],
                device_id=(lax.axis_index("mp"), d // ngy, d % ngy),
                device_id_type=pl.DeviceIdType.MESH,
            )
            copy.wait_send()
            copy.wait_recv()

        return carry

    lax.fori_loop(0, ndev, wait, 0)
    arrived_ref[...] = recv[...]


def stencil_kernel(with_edges, with_force, coef_ref, wet_ref, u_ref, above_ref, below_ref,
                   hn_ref, hs_ref, hw_ref, he_ref, *rest):
    if with_force:
        force_ref, rest = rest[0], rest[1:]
    if with_edges:
        buckets_ref, rest = rest[0], rest[1:]
    out_ref = rest[0]
    i = pl.program_id(0)
    nblk = pl.num_programs(0)
    horiz = coef_ref[0]
    vert = coef_ref[1]
    wet = wet_ref[...]
    rows, cols = wet.shape
    row = lax.broadcasted_iota(jnp.int32, (rows, cols), 0)
    col = lax.broadcasted_iota(jnp.int32, (rows, cols), 1)
    hw_t = jnp.transpose(hw_ref[...])
    he_t = jnp.transpose(he_ref[...])
    above = above_ref[0] * jnp.where(i > 0, 1.0, 0.0)
    below = below_ref[0] * jnp.where(i < nblk - 1, 1.0, 0.0)
    if with_edges:
        en_ref, es_ref, ew_ref, ee_ref, arrived_ref, qw_ref, qe_ref, recv, send_sem, recv_sem = rest[1:]

        @pl.when(i == 0)
        def _():
            start_spread(buckets_ref, recv, send_sem, recv_sem)
            qw_ref[...] = jnp.zeros_like(qw_ref)
            qe_ref[...] = jnp.zeros_like(qe_ref)

    if with_edges:
        lane = lax.broadcasted_iota(jnp.int32, qw_ref.shape, 1)
        qw = qw_ref[...]
        qe = qe_ref[...]
    for l in range(LB):
        u = u_ref[l]
        prev = u_ref[l - 1] if l > 0 else above
        nxt = u_ref[l + 1] if l < LB - 1 else below
        w = wet * u
        north = jnp.where(row == 0, hn_ref[l:l + 1, :], pltpu.roll(w, 1, 0))
        south = jnp.where(row == rows - 1, hs_ref[l:l + 1, :], pltpu.roll(w, rows - 1, 0))
        west = jnp.where(col == 0, hw_t[:, l:l + 1], pltpu.roll(w, 1, 1))
        east = jnp.where(col == cols - 1, he_t[:, l:l + 1], pltpu.roll(w, cols - 1, 1))
        lateral = north + south + west + east - 4.0 * w
        vertical = prev + nxt - 2.0 * u
        res = wet * (u + horiz * lateral + vert * vertical)
        if with_force and l == 0:
            res = res + jnp.where(i == 0, 1.0, 0.0) * (force_gain * wet * force_ref[...])
        out_ref[l] = res
        if with_edges:
            fw = wet * res
            en_ref[l:l + 1, :] = fw[0:1, :]
            es_ref[l:l + 1, :] = fw[rows - 1:rows, :]
            hit = lane == i * LB + l
            qw = jnp.where(hit, fw[:, 0:1], qw)
            qe = jnp.where(hit, fw[:, cols - 1:cols], qe)

    if with_edges:
        qw_ref[...] = qw
        qe_ref[...] = qe

        @pl.when(i == nblk - 1)
        def _():
            lev = ew_ref.shape[0]
            ew_ref[...] = jnp.transpose(qw_ref[...])[0:lev, :]
            ee_ref[...] = jnp.transpose(qe_ref[...])[0:lev, :]
            finish_spread(buckets_ref, recv, send_sem, recv_sem, arrived_ref)


def edges_kernel(wet_ref, u_ref, en_ref, es_ref, ew_ref, ee_ref, qw_ref, qe_ref):
    i = pl.program_id(0)
    nblk = pl.num_programs(0)
    wet = wet_ref[...]
    rows, cols = wet.shape

    @pl.when(i == 0)
    def _():
        qw_ref[...] = jnp.zeros_like(qw_ref)
        qe_ref[...] = jnp.zeros_like(qe_ref)

    lane = lax.broadcasted_iota(jnp.int32, qw_ref.shape, 1)
    qw = qw_ref[...]
    qe = qe_ref[...]
    for l in range(LB):
        fw = wet * u_ref[l]
        en_ref[l:l + 1, :] = fw[0:1, :]
        es_ref[l:l + 1, :] = fw[rows - 1:rows, :]
        hit = lane == i * LB + l
        qw = jnp.where(hit, fw[:, 0:1], qw)
        qe = jnp.where(hit, fw[:, cols - 1:cols], qe)
    qw_ref[...] = qw
    qe_ref[...] = qe

    @pl.when(i == nblk - 1)
    def _():
        lev = ew_ref.shape[0]
        ew_ref[...] = jnp.transpose(qw_ref[...])[0:lev, :]
        ee_ref[...] = jnp.transpose(qe_ref[...])[0:lev, :]


def masked_edges(wet, u):
    lev, rows, cols = u.shape
    lvl2 = pl.BlockSpec((LB, cols), lambda i: (i, 0))
    full2 = lambda shape: pl.BlockSpec(shape, lambda i: (0, 0))
    return pl.pallas_call(
        edges_kernel,
        grid=(lev // LB,),
        in_specs=[full2((rows, cols)), pl.BlockSpec((LB, rows, cols), lambda i: (i, 0, 0))],
        out_specs=[lvl2, lvl2, full2((lev, rows)), full2((lev, rows))],
        out_shape=[jax.ShapeDtypeStruct((lev, cols), jnp.float32)] * 2
        + [jax.ShapeDtypeStruct((lev, rows), jnp.float32)] * 2,
        scratch_shapes=[pltpu.VMEM((rows, 128), jnp.float32)] * 2,
        compiler_params=pltpu.CompilerParams(dimension_semantics=("arbitrary",)),
        cost_estimate=pl.CostEstimate(flops=2 * u.size, bytes_accessed=4 * u.size, transcendentals=0),
    )(wet, u)


def force_kernel(x_ref, wet_ref, f_ref, out_ref):
    out_ref[0] = x_ref[0] + force_gain * wet_ref[...] * f_ref[...]


def add_force(x, wet, f):
    lev, rows, cols = x.shape
    plane = pl.BlockSpec((rows, cols), lambda i: (0, 0))
    level0 = pl.BlockSpec((1, rows, cols), lambda i: (0, 0, 0))
    return pl.pallas_call(
        force_kernel,
        grid=(1,),
        in_specs=[level0, plane, plane],
        out_specs=level0,
        out_shape=jax.ShapeDtypeStruct(x.shape, x.dtype),
        input_output_aliases={0: 0},
    )(x, wet, f)


def stencil_step(coef, wet, u, halos, force=None, buckets=None):
    with_edges = buckets is not None
    lev, rows, cols = u.shape
    nblk = lev // LB
    full2 = lambda shape: pl.BlockSpec(shape, lambda i: (0, 0))
    lvl2 = pl.BlockSpec((LB, cols), lambda i: (i, 0))
    in_specs = [
        pl.BlockSpec(memory_space=pltpu.SMEM),
        full2((rows, cols)),
        pl.BlockSpec((LB, rows, cols), lambda i: (i, 0, 0)),
        pl.BlockSpec((1, rows, cols), lambda i: (jnp.maximum(i * LB - 1, 0), 0, 0)),
        pl.BlockSpec((1, rows, cols), lambda i: (jnp.minimum(i * LB + LB, lev - 1), 0, 0)),
        lvl2, lvl2, lvl2, lvl2,
    ]
    args = [coef, wet, u, u, u] + list(halos)
    if force is not None:
        in_specs.append(full2((rows, cols)))
        args.append(force)
    if with_edges:
        in_specs.append(pl.BlockSpec(buckets.shape, lambda i: (0, 0, 0, 0)))
        args.append(buckets)
    out_shape = [jax.ShapeDtypeStruct((lev, rows, cols), jnp.float32)]
    out_specs = [pl.BlockSpec((LB, rows, cols), lambda i: (i, 0, 0))]
    scratch = []
    params = dict(dimension_semantics=("arbitrary",))
    if with_edges:
        out_shape += [jax.ShapeDtypeStruct((lev, cols), jnp.float32)] * 2
        out_shape += [jax.ShapeDtypeStruct((lev, rows), jnp.float32)] * 2
        out_shape += [jax.ShapeDtypeStruct(buckets.shape, buckets.dtype)]
        out_specs += [lvl2, lvl2, full2((lev, rows)), full2((lev, rows))]
        out_specs += [pl.BlockSpec(buckets.shape, lambda i: (0, 0, 0, 0))]
        scratch = [pltpu.VMEM((rows, 128), jnp.float32)] * 2 + [
            pltpu.VMEM(buckets.shape, buckets.dtype),
            pltpu.SemaphoreType.DMA((buckets.shape[0],)),
            pltpu.SemaphoreType.DMA((buckets.shape[0],)),
        ]
        params.update(collective_id=2, has_side_effects=True)
    return pl.pallas_call(
        functools.partial(stencil_kernel, with_edges, force is not None),
        grid=(nblk,),
        in_specs=in_specs,
        out_specs=out_specs,
        out_shape=out_shape,
        scratch_shapes=scratch,
        compiler_params=pltpu.CompilerParams(**params),
        cost_estimate=pl.CostEstimate(flops=30 * u.size, bytes_accessed=12 * u.size, transcendentals=0),
    )(*args)


def halo_kernel(en_ref, es_ref, ew_ref, ee_ref, hn_ref, hs_ref, hw_ref, he_ref,
                buf, send_sem, recv_sem):
    mp = lax.axis_index("mp")
    gx = lax.axis_index("gx")
    gy = lax.axis_index("gy")
    ngx = lax.axis_size("gx")
    ngy = lax.axis_size("gy")
    mesh_id = pl.DeviceIdType.MESH
    links = [
        (gx < ngx - 1, (mp, gx + 1, gy), es_ref, 0),
        (gx > 0, (mp, gx - 1, gy), en_ref, 1),
        (gy < ngy - 1, (mp, gx, gy + 1), ee_ref, 2),
        (gy > 0, (mp, gx, gy - 1), ew_ref, 3),
    ]
    barrier = pltpu.get_barrier_semaphore()
    count = jnp.int32(0)
    for present, dev, _, _ in links:
        @pl.when(present)
        def _():
            pl.semaphore_signal(barrier, 1, device_id=dev, device_id_type=mesh_id)

        count = count + present.astype(jnp.int32)
    pl.semaphore_wait(barrier, count)

    copies = []
    for present, dev, src, slot in links:
        copy = pltpu.make_async_remote_copy(
            src_ref=src,
            dst_ref=buf.at[slot],
            send_sem=send_sem.at[slot],
            recv_sem=recv_sem.at[slot],
            device_id=dev,
            device_id_type=mesh_id,
        )
        pl.when(present)(copy.start)
        copies.append((present, copy))
    for present, copy in copies:
        pl.when(present)(copy.wait_send)
    fills = [gx > 0, gx < ngx - 1, gy > 0, gy < ngy - 1]
    outs = [hn_ref, hs_ref, hw_ref, he_ref]
    for slot, (filled, out) in enumerate(zip(fills, outs)):
        _, copy = copies[slot]

        @pl.when(filled)
        def _():
            copy.wait_recv()
            out[...] = buf[slot]

        @pl.when(jnp.logical_not(filled))
        def _():
            out[...] = jnp.zeros_like(out)


def exchange(en, es, ew, ee, call):
    shape = jax.ShapeDtypeStruct(en.shape, en.dtype)
    vmem = pl.BlockSpec(memory_space=pltpu.VMEM)
    return pl.pallas_call(
        halo_kernel,
        in_specs=[vmem] * 4,
        out_specs=[vmem] * 4,
        out_shape=[shape] * 4,
        scratch_shapes=[
            pltpu.VMEM((4,) + en.shape, en.dtype),
            pltpu.SemaphoreType.DMA((4,)),
            pltpu.SemaphoreType.DMA((4,)),
        ],
        compiler_params=pltpu.CompilerParams(collective_id=call, has_side_effects=True),
    )(en, es, ew, ee)


def bucket_kernel(inv_ref, lab_ref, contrib_ref, out_ref):
    ndest = out_ref.shape[0]
    ntiles = contrib_ref.shape[0]
    sub = lax.broadcasted_iota(jnp.int32, (KF, CY), 0)

    def body(d, carry):
        labv = jnp.zeros((KF, CY), jnp.float32)
        for c in range(CAP):
            t = inv_ref[d * CAP + c]
            val = contrib_ref[jnp.minimum(t, ntiles - 1)]
            out_ref[d, c] = jnp.where(t < ntiles, val, 0.0)
            labv = jnp.where(sub == c, lab_ref[d * CAP + c].astype(jnp.float32), labv)
        out_ref[d, CAP] = labv
        return carry

    lax.fori_loop(0, ndest, body, 0)


def local(states, surface, land_mask, tile_weights, tile_source, tile_target, tile_row):
    group = lax.axis_index("mp")
    ndev = lax.axis_size("gx") * lax.axis_size("gy")
    state = states[0]
    lev, rows_here, cols_here = state.shape
    wet = jnp.where(
        group == 0, jnp.ones(land_mask.shape, jnp.float32), land_mask.astype(jnp.float32)
    )
    coef = jnp.stack([jnp.where(group == 0, 0.15, 0.12), jnp.where(group == 0, 0.1, 0.15)]).astype(
        jnp.float32
    )

    src = (surface[0] * wet).astype(jnp.bfloat16)
    source = tile_source[0, 0, 0]
    target = tile_target[0, 0, 0, :, 0]
    dest_row = tile_row[0, 0, 0]
    ntiles = source.shape[0]
    picked = jnp.take(src, source, axis=1)
    contrib = jnp.einsum(
        "tji,kti->tkj", tile_weights[0, 0, 0], picked, preferred_element_type=jnp.float32
    )
    onehot = (target[:, None] == jnp.arange(ndev, dtype=jnp.int32)[None, :]).astype(jnp.int32)
    earlier = jnp.cumsum(onehot, axis=0) - onehot
    rank = jnp.sum(earlier * onehot, axis=1)
    slot = target * CAP + rank
    inv = jnp.full((ndev * CAP,), ntiles, jnp.int32).at[slot].set(jnp.arange(ntiles, dtype=jnp.int32))
    labels = jnp.zeros((ndev * CAP,), jnp.int32).at[slot].set(dest_row)
    buckets = pl.pallas_call(
        bucket_kernel,
        in_specs=[
            pl.BlockSpec(memory_space=pltpu.SMEM),
            pl.BlockSpec(memory_space=pltpu.SMEM),
            pl.BlockSpec(memory_space=pltpu.VMEM),
        ],
        out_specs=pl.BlockSpec(memory_space=pltpu.VMEM),
        out_shape=jax.ShapeDtypeStruct((ndev, CAP + 1, KF, CY), jnp.float32),
    )(inv, labels, contrib)
    halos0 = exchange(*masked_edges(wet, state), 0)
    first, en, es, ew, ee, arrived = stencil_step(coef, wet, state, halos0, buckets=buckets)
    got_rows = arrived[:, CAP, :, 0].astype(jnp.int32)
    select = (
        got_rows[:, :, None] == jnp.arange(rows_here, dtype=jnp.int32)[None, None, :]
    ).astype(jnp.float32)
    sent = jnp.einsum(
        "scr,sckj->krj", select, arrived[:, :CAP], precision=lax.Precision.HIGHEST
    )
    received = lax.ppermute(sent, "mp", [(0, 1), (1, 0)])

    halos1 = exchange(en, es, ew, ee, 1)
    (second,) = stencil_step(coef, wet, first, halos1)
    second = add_force(second, wet, received[0])
    return (second[None], received[None])


def solution(mesh):
    return jax.shard_map(
        local,
        mesh=mesh,
        in_specs=(
            P("mp", None, "gx", "gy"),
            P("mp", None, "gx", "gy"),
            P("gx", "gy"),
            P("mp", "gx", "gy", None, None, None),
            P("mp", "gx", "gy", None),
            P("mp", "gx", "gy", None, None),
            P("mp", "gx", "gy", None),
        ),
        out_specs=(P("mp", None, "gx", "gy"), P("mp", None, "gx", "gy")),
        check_vma=False,
    )
```

```python
import functools

import jax
import jax.numpy as jnp
from jax import lax
from jax.experimental import pallas as pl
from jax.experimental.pallas import tpu as pltpu
from jax.sharding import PartitionSpec as P

CY = 128
KF = 8
CAP = 8
LB = 8

force_gain = 0.5


def shift_pairs(devices, forward):
    up = [(i, i + 1) for i in range(devices - 1)]
    return up if forward else [(j, i) for i, j in up]


def start_spread(buckets_ref, recv, send_sem, recv_sem):
    mp = lax.axis_index("mp")
    ngy = lax.axis_size("gy")
    ndev = lax.axis_size("gx") * ngy
    me = lax.axis_index("gx") * ngy + lax.axis_index("gy")
    mesh_id = pl.DeviceIdType.MESH
    barrier = pltpu.get_barrier_semaphore()

    def greet(d, carry):
        @pl.when(d != me)
        def _():
            pl.semaphore_signal(barrier, 1, device_id=(mp, d // ngy, d % ngy), device_id_type=mesh_id)

        return carry

    lax.fori_loop(0, ndev, greet, 0)
    pl.semaphore_wait(barrier, ndev - 1)
    recv[me] = buckets_ref[me]

    def send(k, carry):
        d = (me + k) % ndev
        pltpu.make_async_remote_copy(
            src_ref=buckets_ref.at[d],
            dst_ref=recv.at[me],
            send_sem=send_sem.at[d],
            recv_sem=recv_sem.at[me],
            device_id=(mp, d // ngy, d % ngy),
            device_id_type=mesh_id,
        ).start()
        return carry

    lax.fori_loop(1, ndev, send, 0)


def finish_spread(buckets_ref, recv, send_sem, recv_sem, arrived_ref):
    ngy = lax.axis_size("gy")
    ndev = lax.axis_size("gx") * ngy
    me = lax.axis_index("gx") * ngy + lax.axis_index("gy")

    def wait(d, carry):
        @pl.when(d != me)
        def _():
            copy = pltpu.make_async_remote_copy(
                src_ref=buckets_ref.at[d],
                dst_ref=recv.at[d],
                send_sem=send_sem.at[d],
                recv_sem=recv_sem.at[d],
                device_id=(lax.axis_index("mp"), d // ngy, d % ngy),
                device_id_type=pl.DeviceIdType.MESH,
            )
            copy.wait_send()
            copy.wait_recv()

        return carry

    lax.fori_loop(0, ndev, wait, 0)
    arrived_ref[...] = recv[...]


def first_kernel(coef_ref, wet_ref, u_ref, above_ref, below_ref, buckets_ref,
                 out_ref, en_ref, es_ref, ew_ref, ee_ref, arrived_ref,
                 edge0, halo, qw_ref, qe_ref, recv, send_sem, recv_sem, hsend, hrecv):
    p = pl.program_id(0)
    i = pl.program_id(1)
    nblk = pl.num_programs(1)
    wet = wet_ref[...]
    rows, cols = wet.shape
    lev = ew_ref.shape[0]
    mp = lax.axis_index("mp")
    gx = lax.axis_index("gx")
    gy = lax.axis_index("gy")
    ngx = lax.axis_size("gx")
    ngy = lax.axis_size("gy")
    mesh_id = pl.DeviceIdType.MESH
    links = [
        (gx < ngx - 1, (mp, gx + 1, gy), 1, 0),
        (gx > 0, (mp, gx - 1, gy), 0, 1),
        (gy < ngy - 1, (mp, gx, gy + 1), 3, 2),
        (gy > 0, (mp, gx, gy - 1), 2, 3),
    ]
    fills = [gx > 0, gx < ngx - 1, gy > 0, gy < ngy - 1]
    copies = [
        pltpu.make_async_remote_copy(
            src_ref=edge0.at[src],
            dst_ref=halo.at[slot],
            send_sem=hsend.at[slot],
            recv_sem=hrecv.at[slot],
            device_id=dev,
            device_id_type=mesh_id,
        )
        for _, dev, src, slot in links
    ]
    lane = lax.broadcasted_iota(jnp.int32, qw_ref.shape, 1)

    @pl.when((p == 0) & (i == 0))
    def _():
        start_spread(buckets_ref, recv, send_sem, recv_sem)
        qw_ref[...] = jnp.zeros_like(qw_ref)
        qe_ref[...] = jnp.zeros_like(qe_ref)

    @pl.when(p == 0)
    def _():
        qw = qw_ref[...]
        qe = qe_ref[...]
        for l in range(LB):
            fw = wet * u_ref[l]
            edge0[0, i, l:l + 1, :] = fw[0:1, :]
            edge0[1, i, l:l + 1, :] = fw[rows - 1:rows, :]
            hit = lane == i * LB + l
            qw = jnp.where(hit, fw[:, 0:1], qw)
            qe = jnp.where(hit, fw[:, cols - 1:cols], qe)
        qw_ref[...] = qw
        qe_ref[...] = qe

    @pl.when((p == 0) & (i == nblk - 1))
    def _():
        edge0[2] = jnp.transpose(qw_ref[...])[0:lev, :].reshape(nblk, LB, rows)
        edge0[3] = jnp.transpose(qe_ref[...])[0:lev, :].reshape(nblk, LB, rows)
        for (present, _, _, _), copy in zip(links, copies):
            pl.when(present)(copy.start)

    @pl.when((p == 1) & (i == 0))
    def _():
        for (present, _, _, _), copy in zip(links, copies):
            pl.when(present)(copy.wait_send)
        for slot, filled in enumerate(fills):
            pl.when(filled)(copies[slot].wait_recv)

            @pl.when(jnp.logical_not(filled))
            def _():
                halo[slot] = jnp.zeros_like(halo[slot])

        qw_ref[...] = jnp.zeros_like(qw_ref)
        qe_ref[...] = jnp.zeros_like(qe_ref)

    @pl.when(p == 1)
    def _():
        horiz = coef_ref[0]
        vert = coef_ref[1]
        row = lax.broadcasted_iota(jnp.int32, (rows, cols), 0)
        col = lax.broadcasted_iota(jnp.int32, (rows, cols), 1)
        hn = halo[0, i]
        hs = halo[1, i]
        hw_t = jnp.transpose(halo[2, i])
        he_t = jnp.transpose(halo[3, i])
        above = above_ref[0] * jnp.where(i > 0, 1.0, 0.0)
        below = below_ref[0] * jnp.where(i < nblk - 1, 1.0, 0.0)
        qw = qw_ref[...]
        qe = qe_ref[...]
        for l in range(LB):
            u = u_ref[l]
            prev = u_ref[l - 1] if l > 0 else above
            nxt = u_ref[l + 1] if l < LB - 1 else below
            w = wet * u
            north = jnp.where(row == 0, hn[l:l + 1, :], pltpu.roll(w, 1, 0))
            south = jnp.where(row == rows - 1, hs[l:l + 1, :], pltpu.roll(w, rows - 1, 0))
            west = jnp.where(col == 0, hw_t[:, l:l + 1], pltpu.roll(w, 1, 1))
            east = jnp.where(col == cols - 1, he_t[:, l:l + 1], pltpu.roll(w, cols - 1, 1))
            lateral = north + south + west + east - 4.0 * w
            vertical = prev + nxt - 2.0 * u
            res = wet * (u + horiz * lateral + vert * vertical)
            out_ref[l] = res
            fw = wet * res
            en_ref[l:l + 1, :] = fw[0:1, :]
            es_ref[l:l + 1, :] = fw[rows - 1:rows, :]
            hit = lane == i * LB + l
            qw = jnp.where(hit, fw[:, 0:1], qw)
            qe = jnp.where(hit, fw[:, cols - 1:cols], qe)
        qw_ref[...] = qw
        qe_ref[...] = qe

    @pl.when((p == 1) & (i == nblk - 1))
    def _():
        ew_ref[...] = jnp.transpose(qw_ref[...])[0:lev, :]
        ee_ref[...] = jnp.transpose(qe_ref[...])[0:lev, :]
        finish_spread(buckets_ref, recv, send_sem, recv_sem, arrived_ref)


def first_step(coef, wet, u, buckets):
    lev, rows, cols = u.shape
    nblk = lev // LB
    full2 = lambda shape: pl.BlockSpec(shape, lambda p, i: (0, 0))
    lvl2 = pl.BlockSpec((LB, cols), lambda p, i: (i * p, 0))
    whole = pl.BlockSpec(buckets.shape, lambda p, i: (0, 0, 0, 0))
    in_specs = [
        pl.BlockSpec(memory_space=pltpu.SMEM),
        full2((rows, cols)),
        pl.BlockSpec((LB, rows, cols), lambda p, i: (i, 0, 0)),
        pl.BlockSpec((1, rows, cols), lambda p, i: (jnp.maximum(i * LB - 1, 0), 0, 0)),
        pl.BlockSpec((1, rows, cols), lambda p, i: (jnp.minimum(i * LB + LB, lev - 1), 0, 0)),
        whole,
    ]
    out_shape = [
        jax.ShapeDtypeStruct((lev, rows, cols), jnp.float32),
        jax.ShapeDtypeStruct((lev, cols), jnp.float32),
        jax.ShapeDtypeStruct((lev, cols), jnp.float32),
        jax.ShapeDtypeStruct((lev, rows), jnp.float32),
        jax.ShapeDtypeStruct((lev, rows), jnp.float32),
        jax.ShapeDtypeStruct(buckets.shape, buckets.dtype),
    ]
    out_specs = [
        pl.BlockSpec((LB, rows, cols), lambda p, i: (i * p, 0, 0)),
        lvl2, lvl2, full2((lev, rows)), full2((lev, rows)), whole,
    ]
    scratch = [
        pltpu.VMEM((4, nblk, LB, cols), jnp.float32),
        pltpu.VMEM((4, nblk, LB, cols), jnp.float32),
        pltpu.VMEM((rows, 128), jnp.float32),
        pltpu.VMEM((rows, 128), jnp.float32),
        pltpu.VMEM(buckets.shape, buckets.dtype),
        pltpu.SemaphoreType.DMA((buckets.shape[0],)),
        pltpu.SemaphoreType.DMA((buckets.shape[0],)),
        pltpu.SemaphoreType.DMA((4,)),
        pltpu.SemaphoreType.DMA((4,)),
    ]
    return pl.pallas_call(
        first_kernel,
        grid=(2, nblk),
        in_specs=in_specs,
        out_specs=out_specs,
        out_shape=out_shape,
        scratch_shapes=scratch,
        compiler_params=pltpu.CompilerParams(
            dimension_semantics=("arbitrary", "arbitrary"), collective_id=2, has_side_effects=True
        ),
        cost_estimate=pl.CostEstimate(flops=32 * u.size, bytes_accessed=16 * u.size, transcendentals=0),
    )(coef, wet, u, u, u, buckets)


def stencil_kernel(with_edges, with_force, coef_ref, wet_ref, u_ref, above_ref, below_ref,
                   hn_ref, hs_ref, hw_ref, he_ref, *rest):
    if with_force:
        force_ref, rest = rest[0], rest[1:]
    if with_edges:
        buckets_ref, rest = rest[0], rest[1:]
    out_ref = rest[0]
    i = pl.program_id(0)
    nblk = pl.num_programs(0)
    horiz = coef_ref[0]
    vert = coef_ref[1]
    wet = wet_ref[...]
    rows, cols = wet.shape
    row = lax.broadcasted_iota(jnp.int32, (rows, cols), 0)
    col = lax.broadcasted_iota(jnp.int32, (rows, cols), 1)
    hw_t = jnp.transpose(hw_ref[...])
    he_t = jnp.transpose(he_ref[...])
    above = above_ref[0] * jnp.where(i > 0, 1.0, 0.0)
    below = below_ref[0] * jnp.where(i < nblk - 1, 1.0, 0.0)
    if with_edges:
        en_ref, es_ref, ew_ref, ee_ref, arrived_ref, qw_ref, qe_ref, recv, send_sem, recv_sem = rest[1:]

        @pl.when(i == 0)
        def _():
            start_spread(buckets_ref, recv, send_sem, recv_sem)
            qw_ref[...] = jnp.zeros_like(qw_ref)
            qe_ref[...] = jnp.zeros_like(qe_ref)

    if with_edges:
        lane = lax.broadcasted_iota(jnp.int32, qw_ref.shape, 1)
        qw = qw_ref[...]
        qe = qe_ref[...]
    for l in range(LB):
        u = u_ref[l]
        prev = u_ref[l - 1] if l > 0 else above
        nxt = u_ref[l + 1] if l < LB - 1 else below
        w = wet * u
        north = jnp.where(row == 0, hn_ref[l:l + 1, :], pltpu.roll(w, 1, 0))
        south = jnp.where(row == rows - 1, hs_ref[l:l + 1, :], pltpu.roll(w, rows - 1, 0))
        west = jnp.where(col == 0, hw_t[:, l:l + 1], pltpu.roll(w, 1, 1))
        east = jnp.where(col == cols - 1, he_t[:, l:l + 1], pltpu.roll(w, cols - 1, 1))
        lateral = north + south + west + east - 4.0 * w
        vertical = prev + nxt - 2.0 * u
        res = wet * (u + horiz * lateral + vert * vertical)
        if with_force and l == 0:
            res = res + jnp.where(i == 0, 1.0, 0.0) * (force_gain * wet * force_ref[...])
        out_ref[l] = res
        if with_edges:
            fw = wet * res
            en_ref[l:l + 1, :] = fw[0:1, :]
            es_ref[l:l + 1, :] = fw[rows - 1:rows, :]
            hit = lane == i * LB + l
            qw = jnp.where(hit, fw[:, 0:1], qw)
            qe = jnp.where(hit, fw[:, cols - 1:cols], qe)

    if with_edges:
        qw_ref[...] = qw
        qe_ref[...] = qe

        @pl.when(i == nblk - 1)
        def _():
            lev = ew_ref.shape[0]
            ew_ref[...] = jnp.transpose(qw_ref[...])[0:lev, :]
            ee_ref[...] = jnp.transpose(qe_ref[...])[0:lev, :]
            finish_spread(buckets_ref, recv, send_sem, recv_sem, arrived_ref)


def edges_kernel(wet_ref, u_ref, en_ref, es_ref, ew_ref, ee_ref, qw_ref, qe_ref):
    i = pl.program_id(0)
    nblk = pl.num_programs(0)
    wet = wet_ref[...]
    rows, cols = wet.shape

    @pl.when(i == 0)
    def _():
        qw_ref[...] = jnp.zeros_like(qw_ref)
        qe_ref[...] = jnp.zeros_like(qe_ref)

    lane = lax.broadcasted_iota(jnp.int32, qw_ref.shape, 1)
    qw = qw_ref[...]
    qe = qe_ref[...]
    for l in range(LB):
        fw = wet * u_ref[l]
        en_ref[l:l + 1, :] = fw[0:1, :]
        es_ref[l:l + 1, :] = fw[rows - 1:rows, :]
        hit = lane == i * LB + l
        qw = jnp.where(hit, fw[:, 0:1], qw)
        qe = jnp.where(hit, fw[:, cols - 1:cols], qe)
    qw_ref[...] = qw
    qe_ref[...] = qe

    @pl.when(i == nblk - 1)
    def _():
        lev = ew_ref.shape[0]
        ew_ref[...] = jnp.transpose(qw_ref[...])[0:lev, :]
        ee_ref[...] = jnp.transpose(qe_ref[...])[0:lev, :]


def masked_edges(wet, u):
    lev, rows, cols = u.shape
    lvl2 = pl.BlockSpec((LB, cols), lambda i: (i, 0))
    full2 = lambda shape: pl.BlockSpec(shape, lambda i: (0, 0))
    return pl.pallas_call(
        edges_kernel,
        grid=(lev // LB,),
        in_specs=[full2((rows, cols)), pl.BlockSpec((LB, rows, cols), lambda i: (i, 0, 0))],
        out_specs=[lvl2, lvl2, full2((lev, rows)), full2((lev, rows))],
        out_shape=[jax.ShapeDtypeStruct((lev, cols), jnp.float32)] * 2
        + [jax.ShapeDtypeStruct((lev, rows), jnp.float32)] * 2,
        scratch_shapes=[pltpu.VMEM((rows, 128), jnp.float32)] * 2,
        compiler_params=pltpu.CompilerParams(dimension_semantics=("arbitrary",)),
        cost_estimate=pl.CostEstimate(flops=2 * u.size, bytes_accessed=4 * u.size, transcendentals=0),
    )(wet, u)


def force_kernel(x_ref, wet_ref, f_ref, out_ref):
    out_ref[0] = x_ref[0] + force_gain * wet_ref[...] * f_ref[...]


def add_force(x, wet, f):
    lev, rows, cols = x.shape
    plane = pl.BlockSpec((rows, cols), lambda i: (0, 0))
    level0 = pl.BlockSpec((1, rows, cols), lambda i: (0, 0, 0))
    return pl.pallas_call(
        force_kernel,
        grid=(1,),
        in_specs=[level0, plane, plane],
        out_specs=level0,
        out_shape=jax.ShapeDtypeStruct(x.shape, x.dtype),
        input_output_aliases={0: 0},
    )(x, wet, f)


def stencil_step(coef, wet, u, halos, force=None, buckets=None):
    with_edges = buckets is not None
    lev, rows, cols = u.shape
    nblk = lev // LB
    full2 = lambda shape: pl.BlockSpec(shape, lambda i: (0, 0))
    lvl2 = pl.BlockSpec((LB, cols), lambda i: (i, 0))
    in_specs = [
        pl.BlockSpec(memory_space=pltpu.SMEM),
        full2((rows, cols)),
        pl.BlockSpec((LB, rows, cols), lambda i: (i, 0, 0)),
        pl.BlockSpec((1, rows, cols), lambda i: (jnp.maximum(i * LB - 1, 0), 0, 0)),
        pl.BlockSpec((1, rows, cols), lambda i: (jnp.minimum(i * LB + LB, lev - 1), 0, 0)),
        lvl2, lvl2, lvl2, lvl2,
    ]
    args = [coef, wet, u, u, u] + list(halos)
    if force is not None:
        in_specs.append(full2((rows, cols)))
        args.append(force)
    if with_edges:
        in_specs.append(pl.BlockSpec(buckets.shape, lambda i: (0, 0, 0, 0)))
        args.append(buckets)
    out_shape = [jax.ShapeDtypeStruct((lev, rows, cols), jnp.float32)]
    out_specs = [pl.BlockSpec((LB, rows, cols), lambda i: (i, 0, 0))]
    scratch = []
    params = dict(dimension_semantics=("arbitrary",))
    if with_edges:
        out_shape += [jax.ShapeDtypeStruct((lev, cols), jnp.float32)] * 2
        out_shape += [jax.ShapeDtypeStruct((lev, rows), jnp.float32)] * 2
        out_shape += [jax.ShapeDtypeStruct(buckets.shape, buckets.dtype)]
        out_specs += [lvl2, lvl2, full2((lev, rows)), full2((lev, rows))]
        out_specs += [pl.BlockSpec(buckets.shape, lambda i: (0, 0, 0, 0))]
        scratch = [pltpu.VMEM((rows, 128), jnp.float32)] * 2 + [
            pltpu.VMEM(buckets.shape, buckets.dtype),
            pltpu.SemaphoreType.DMA((buckets.shape[0],)),
            pltpu.SemaphoreType.DMA((buckets.shape[0],)),
        ]
        params.update(collective_id=2, has_side_effects=True)
    return pl.pallas_call(
        functools.partial(stencil_kernel, with_edges, force is not None),
        grid=(nblk,),
        in_specs=in_specs,
        out_specs=out_specs,
        out_shape=out_shape,
        scratch_shapes=scratch,
        compiler_params=pltpu.CompilerParams(**params),
        cost_estimate=pl.CostEstimate(flops=30 * u.size, bytes_accessed=12 * u.size, transcendentals=0),
    )(*args)


def halo_kernel(en_ref, es_ref, ew_ref, ee_ref, hn_ref, hs_ref, hw_ref, he_ref,
                buf, send_sem, recv_sem):
    mp = lax.axis_index("mp")
    gx = lax.axis_index("gx")
    gy = lax.axis_index("gy")
    ngx = lax.axis_size("gx")
    ngy = lax.axis_size("gy")
    mesh_id = pl.DeviceIdType.MESH
    links = [
        (gx < ngx - 1, (mp, gx + 1, gy), es_ref, 0),
        (gx > 0, (mp, gx - 1, gy), en_ref, 1),
        (gy < ngy - 1, (mp, gx, gy + 1), ee_ref, 2),
        (gy > 0, (mp, gx, gy - 1), ew_ref, 3),
    ]
    barrier = pltpu.get_barrier_semaphore()
    count = jnp.int32(0)
    for present, dev, _, _ in links:
        @pl.when(present)
        def _():
            pl.semaphore_signal(barrier, 1, device_id=dev, device_id_type=mesh_id)

        count = count + present.astype(jnp.int32)
    pl.semaphore_wait(barrier, count)

    copies = []
    for present, dev, src, slot in links:
        copy = pltpu.make_async_remote_copy(
            src_ref=src,
            dst_ref=buf.at[slot],
            send_sem=send_sem.at[slot],
            recv_sem=recv_sem.at[slot],
            device_id=dev,
            device_id_type=mesh_id,
        )
        pl.when(present)(copy.start)
        copies.append((present, copy))
    for present, copy in copies:
        pl.when(present)(copy.wait_send)
    fills = [gx > 0, gx < ngx - 1, gy > 0, gy < ngy - 1]
    outs = [hn_ref, hs_ref, hw_ref, he_ref]
    for slot, (filled, out) in enumerate(zip(fills, outs)):
        _, copy = copies[slot]

        @pl.when(filled)
        def _():
            copy.wait_recv()
            out[...] = buf[slot]

        @pl.when(jnp.logical_not(filled))
        def _():
            out[...] = jnp.zeros_like(out)


def exchange(en, es, ew, ee, call):
    shape = jax.ShapeDtypeStruct(en.shape, en.dtype)
    vmem = pl.BlockSpec(memory_space=pltpu.VMEM)
    return pl.pallas_call(
        halo_kernel,
        in_specs=[vmem] * 4,
        out_specs=[vmem] * 4,
        out_shape=[shape] * 4,
        scratch_shapes=[
            pltpu.VMEM((4,) + en.shape, en.dtype),
            pltpu.SemaphoreType.DMA((4,)),
            pltpu.SemaphoreType.DMA((4,)),
        ],
        compiler_params=pltpu.CompilerParams(collective_id=call, has_side_effects=True),
    )(en, es, ew, ee)


def bucket_kernel(inv_ref, lab_ref, contrib_ref, out_ref):
    ndest = out_ref.shape[0]
    ntiles = contrib_ref.shape[0]
    sub = lax.broadcasted_iota(jnp.int32, (KF, CY), 0)

    def body(d, carry):
        labv = jnp.zeros((KF, CY), jnp.float32)
        for c in range(CAP):
            t = inv_ref[d * CAP + c]
            val = contrib_ref[jnp.minimum(t, ntiles - 1)]
            out_ref[d, c] = jnp.where(t < ntiles, val, 0.0)
            labv = jnp.where(sub == c, lab_ref[d * CAP + c].astype(jnp.float32), labv)
        out_ref[d, CAP] = labv
        return carry

    lax.fori_loop(0, ndest, body, 0)


def local(states, surface, land_mask, tile_weights, tile_source, tile_target, tile_row):
    group = lax.axis_index("mp")
    ndev = lax.axis_size("gx") * lax.axis_size("gy")
    state = states[0]
    lev, rows_here, cols_here = state.shape
    wet = jnp.where(
        group == 0, jnp.ones(land_mask.shape, jnp.float32), land_mask.astype(jnp.float32)
    )
    coef = jnp.stack([jnp.where(group == 0, 0.15, 0.12), jnp.where(group == 0, 0.1, 0.15)]).astype(
        jnp.float32
    )

    src = (surface[0] * wet).astype(jnp.bfloat16)
    source = tile_source[0, 0, 0]
    target = tile_target[0, 0, 0, :, 0]
    dest_row = tile_row[0, 0, 0]
    ntiles = source.shape[0]
    picked = jnp.take(src, source, axis=1)
    contrib = jnp.einsum(
        "tji,kti->tkj", tile_weights[0, 0, 0], picked, preferred_element_type=jnp.float32
    )
    onehot = (target[:, None] == jnp.arange(ndev, dtype=jnp.int32)[None, :]).astype(jnp.int32)
    earlier = jnp.cumsum(onehot, axis=0) - onehot
    rank = jnp.sum(earlier * onehot, axis=1)
    slot = target * CAP + rank
    inv = jnp.full((ndev * CAP,), ntiles, jnp.int32).at[slot].set(jnp.arange(ntiles, dtype=jnp.int32))
    labels = jnp.zeros((ndev * CAP,), jnp.int32).at[slot].set(dest_row)
    buckets = pl.pallas_call(
        bucket_kernel,
        in_specs=[
            pl.BlockSpec(memory_space=pltpu.SMEM),
            pl.BlockSpec(memory_space=pltpu.SMEM),
            pl.BlockSpec(memory_space=pltpu.VMEM),
        ],
        out_specs=pl.BlockSpec(memory_space=pltpu.VMEM),
        out_shape=jax.ShapeDtypeStruct((ndev, CAP + 1, KF, CY), jnp.float32),
    )(inv, labels, contrib)
    first, en, es, ew, ee, arrived = first_step(coef, wet, state, buckets)
    got_rows = arrived[:, CAP, :, 0].astype(jnp.int32)
    select = (
        got_rows[:, :, None] == jnp.arange(rows_here, dtype=jnp.int32)[None, None, :]
    ).astype(jnp.float32)
    sent = jnp.einsum(
        "scr,sckj->krj", select, arrived[:, :CAP], precision=lax.Precision.HIGHEST
    )
    received = lax.ppermute(sent, "mp", [(0, 1), (1, 0)])

    halos1 = exchange(en, es, ew, ee, 1)
    (second,) = stencil_step(coef, wet, first, halos1)
    second = add_force(second, wet, received[0])
    return (second[None], received[None])


def solution(mesh):
    return jax.shard_map(
        local,
        mesh=mesh,
        in_specs=(
            P("mp", None, "gx", "gy"),
            P("mp", None, "gx", "gy"),
            P("gx", "gy"),
            P("mp", "gx", "gy", None, None, None),
            P("mp", "gx", "gy", None),
            P("mp", "gx", "gy", None, None),
            P("mp", "gx", "gy", None),
        ),
        out_specs=(P("mp", None, "gx", "gy"), P("mp", None, "gx", "gy")),
        check_vma=False,
    )
```

```python
import functools

import jax
import jax.numpy as jnp
from jax import lax
from jax.experimental import pallas as pl
from jax.experimental.pallas import tpu as pltpu
from jax.sharding import PartitionSpec as P

CY = 128
KF = 8
CAP = 8
LB = 8

force_gain = 0.5


def shift_pairs(devices, forward):
    up = [(i, i + 1) for i in range(devices - 1)]
    return up if forward else [(j, i) for i, j in up]


def start_spread(buckets_ref, recv, send_sem, recv_sem, first_out=None):
    mp = lax.axis_index("mp")
    ngy = lax.axis_size("gy")
    ndev = lax.axis_size("gx") * ngy
    me = lax.axis_index("gx") * ngy + lax.axis_index("gy")
    mesh_id = pl.DeviceIdType.MESH
    barrier = pltpu.get_barrier_semaphore()

    def greet(d, carry):
        @pl.when(d != me)
        def _():
            pl.semaphore_signal(barrier, 1, device_id=(mp, d // ngy, d % ngy), device_id_type=mesh_id)

        return carry

    lax.fori_loop(0, ndev, greet, 0)
    pl.semaphore_wait(barrier, ndev - 1)
    if first_out is not None:
        first_out()
    recv[me] = buckets_ref[me]

    def send(k, carry):
        d = (me + k) % ndev
        pltpu.make_async_remote_copy(
            src_ref=buckets_ref.at[d],
            dst_ref=recv.at[me],
            send_sem=send_sem.at[d],
            recv_sem=recv_sem.at[me],
            device_id=(mp, d // ngy, d % ngy),
            device_id_type=mesh_id,
        ).start()
        return carry

    lax.fori_loop(1, ndev, send, 0)


def finish_spread(buckets_ref, recv, send_sem, recv_sem, arrived_ref):
    ngy = lax.axis_size("gy")
    ndev = lax.axis_size("gx") * ngy
    me = lax.axis_index("gx") * ngy + lax.axis_index("gy")

    def wait(d, carry):
        @pl.when(d != me)
        def _():
            copy = pltpu.make_async_remote_copy(
                src_ref=buckets_ref.at[d],
                dst_ref=recv.at[d],
                send_sem=send_sem.at[d],
                recv_sem=recv_sem.at[d],
                device_id=(lax.axis_index("mp"), d // ngy, d % ngy),
                device_id_type=pl.DeviceIdType.MESH,
            )
            copy.wait_send()
            copy.wait_recv()

        return carry

    lax.fori_loop(0, ndev, wait, 0)
    arrived_ref[...] = recv[...]


def first_kernel(coef_ref, wet_ref, u_ref, above_ref, below_ref, buckets_ref,
                 e0n, e0s, e0w, e0e,
                 out_ref, en_ref, es_ref, ew_ref, ee_ref, arrived_ref,
                 halo, qw_ref, qe_ref, recv, send_sem, recv_sem, hsend, hrecv):
    i = pl.program_id(0)
    nblk = pl.num_programs(0)
    edge0 = [e0n, e0s, e0w, e0e]
    wet = wet_ref[...]
    rows, cols = wet.shape
    lev = ew_ref.shape[0]
    mp = lax.axis_index("mp")
    gx = lax.axis_index("gx")
    gy = lax.axis_index("gy")
    ngx = lax.axis_size("gx")
    ngy = lax.axis_size("gy")
    mesh_id = pl.DeviceIdType.MESH
    links = [
        (gx < ngx - 1, (mp, gx + 1, gy), 1, 0),
        (gx > 0, (mp, gx - 1, gy), 0, 1),
        (gy < ngy - 1, (mp, gx, gy + 1), 3, 2),
        (gy > 0, (mp, gx, gy - 1), 2, 3),
    ]
    fills = [gx > 0, gx < ngx - 1, gy > 0, gy < ngy - 1]
    copies = [
        pltpu.make_async_remote_copy(
            src_ref=edge0[src],
            dst_ref=halo.at[slot],
            send_sem=hsend.at[slot],
            recv_sem=hrecv.at[slot],
            device_id=dev,
            device_id_type=mesh_id,
        )
        for _, dev, src, slot in links
    ]
    lane = lax.broadcasted_iota(jnp.int32, qw_ref.shape, 1)

    def send_halos():
        for (present, _, _, _), copy in zip(links, copies):
            pl.when(present)(copy.start)

    @pl.when(i == 0)
    def _():
        start_spread(buckets_ref, recv, send_sem, recv_sem, send_halos)
        for (present, _, _, _), copy in zip(links, copies):
            pl.when(present)(copy.wait_send)
        for slot, filled in enumerate(fills):
            pl.when(filled)(copies[slot].wait_recv)

            @pl.when(jnp.logical_not(filled))
            def _():
                halo[slot] = jnp.zeros_like(halo[slot])

        qw_ref[...] = jnp.zeros_like(qw_ref)
        qe_ref[...] = jnp.zeros_like(qe_ref)

    def _():
        horiz = coef_ref[0]
        vert = coef_ref[1]
        row = lax.broadcasted_iota(jnp.int32, (rows, cols), 0)
        col = lax.broadcasted_iota(jnp.int32, (rows, cols), 1)
        hn = halo[0, pl.ds(i * LB, LB)]
        hs = halo[1, pl.ds(i * LB, LB)]
        hw_t = jnp.transpose(halo[2, pl.ds(i * LB, LB)])
        he_t = jnp.transpose(halo[3, pl.ds(i * LB, LB)])
        above = above_ref[0] * jnp.where(i > 0, 1.0, 0.0)
        below = below_ref[0] * jnp.where(i < nblk - 1, 1.0, 0.0)
        qw = qw_ref[...]
        qe = qe_ref[...]
        for l in range(LB):
            u = u_ref[l]
            prev = u_ref[l - 1] if l > 0 else above
            nxt = u_ref[l + 1] if l < LB - 1 else below
            w = wet * u
            north = jnp.where(row == 0, hn[l:l + 1, :], pltpu.roll(w, 1, 0))
            south = jnp.where(row == rows - 1, hs[l:l + 1, :], pltpu.roll(w, rows - 1, 0))
            west = jnp.where(col == 0, hw_t[:, l:l + 1], pltpu.roll(w, 1, 1))
            east = jnp.where(col == cols - 1, he_t[:, l:l + 1], pltpu.roll(w, cols - 1, 1))
            lateral = north + south + west + east - 4.0 * w
            vertical = prev + nxt - 2.0 * u
            res = wet * (u + horiz * lateral + vert * vertical)
            out_ref[l] = res
            fw = wet * res
            en_ref[l:l + 1, :] = fw[0:1, :]
            es_ref[l:l + 1, :] = fw[rows - 1:rows, :]
            hit = lane == i * LB + l
            qw = jnp.where(hit, fw[:, 0:1], qw)
            qe = jnp.where(hit, fw[:, cols - 1:cols], qe)
        qw_ref[...] = qw
        qe_ref[...] = qe

    _()

    @pl.when(i == nblk - 1)
    def _():
        ew_ref[...] = jnp.transpose(qw_ref[...])[0:lev, :]
        ee_ref[...] = jnp.transpose(qe_ref[...])[0:lev, :]
        finish_spread(buckets_ref, recv, send_sem, recv_sem, arrived_ref)


def first_step(coef, wet, u, buckets, edges):
    lev, rows, cols = u.shape
    nblk = lev // LB
    full2 = lambda shape: pl.BlockSpec(shape, lambda i: (0, 0))
    lvl2 = pl.BlockSpec((LB, cols), lambda i: (i, 0))
    whole = pl.BlockSpec(buckets.shape, lambda i: (0, 0, 0, 0))
    in_specs = [
        pl.BlockSpec(memory_space=pltpu.SMEM),
        full2((rows, cols)),
        pl.BlockSpec((LB, rows, cols), lambda i: (i, 0, 0)),
        pl.BlockSpec((1, rows, cols), lambda i: (jnp.maximum(i * LB - 1, 0), 0, 0)),
        pl.BlockSpec((1, rows, cols), lambda i: (jnp.minimum(i * LB + LB, lev - 1), 0, 0)),
        whole,
    ] + [full2((lev, cols))] * 4
    out_shape = [
        jax.ShapeDtypeStruct((lev, rows, cols), jnp.float32),
        jax.ShapeDtypeStruct((lev, cols), jnp.float32),
        jax.ShapeDtypeStruct((lev, cols), jnp.float32),
        jax.ShapeDtypeStruct((lev, rows), jnp.float32),
        jax.ShapeDtypeStruct((lev, rows), jnp.float32),
        jax.ShapeDtypeStruct(buckets.shape, buckets.dtype),
    ]
    out_specs = [
        pl.BlockSpec((LB, rows, cols), lambda i: (i, 0, 0)),
        lvl2, lvl2, full2((lev, rows)), full2((lev, rows)), whole,
    ]
    scratch = [
        pltpu.VMEM((4, lev, cols), jnp.float32),
        pltpu.VMEM((rows, 128), jnp.float32),
        pltpu.VMEM((rows, 128), jnp.float32),
        pltpu.VMEM(buckets.shape, buckets.dtype),
        pltpu.SemaphoreType.DMA((buckets.shape[0],)),
        pltpu.SemaphoreType.DMA((buckets.shape[0],)),
        pltpu.SemaphoreType.DMA((4,)),
        pltpu.SemaphoreType.DMA((4,)),
    ]
    return pl.pallas_call(
        first_kernel,
        grid=(nblk,),
        in_specs=in_specs,
        out_specs=out_specs,
        out_shape=out_shape,
        scratch_shapes=scratch,
        compiler_params=pltpu.CompilerParams(
            dimension_semantics=("arbitrary",), collective_id=2, has_side_effects=True
        ),
        cost_estimate=pl.CostEstimate(flops=30 * u.size, bytes_accessed=12 * u.size, transcendentals=0),
    )(coef, wet, u, u, u, buckets, *edges)


def stencil_kernel(with_edges, with_force, coef_ref, wet_ref, u_ref, above_ref, below_ref,
                   hn_ref, hs_ref, hw_ref, he_ref, *rest):
    if with_force:
        force_ref, rest = rest[0], rest[1:]
    if with_edges:
        buckets_ref, rest = rest[0], rest[1:]
    out_ref = rest[0]
    i = pl.program_id(0)
    nblk = pl.num_programs(0)
    horiz = coef_ref[0]
    vert = coef_ref[1]
    wet = wet_ref[...]
    rows, cols = wet.shape
    row = lax.broadcasted_iota(jnp.int32, (rows, cols), 0)
    col = lax.broadcasted_iota(jnp.int32, (rows, cols), 1)
    hw_t = jnp.transpose(hw_ref[...])
    he_t = jnp.transpose(he_ref[...])
    above = above_ref[0] * jnp.where(i > 0, 1.0, 0.0)
    below = below_ref[0] * jnp.where(i < nblk - 1, 1.0, 0.0)
    if with_edges:
        en_ref, es_ref, ew_ref, ee_ref, arrived_ref, qw_ref, qe_ref, recv, send_sem, recv_sem = rest[1:]

        @pl.when(i == 0)
        def _():
            start_spread(buckets_ref, recv, send_sem, recv_sem)
            qw_ref[...] = jnp.zeros_like(qw_ref)
            qe_ref[...] = jnp.zeros_like(qe_ref)

    if with_edges:
        lane = lax.broadcasted_iota(jnp.int32, qw_ref.shape, 1)
        qw = qw_ref[...]
        qe = qe_ref[...]
    for l in range(LB):
        u = u_ref[l]
        prev = u_ref[l - 1] if l > 0 else above
        nxt = u_ref[l + 1] if l < LB - 1 else below
        w = wet * u
        north = jnp.where(row == 0, hn_ref[l:l + 1, :], pltpu.roll(w, 1, 0))
        south = jnp.where(row == rows - 1, hs_ref[l:l + 1, :], pltpu.roll(w, rows - 1, 0))
        west = jnp.where(col == 0, hw_t[:, l:l + 1], pltpu.roll(w, 1, 1))
        east = jnp.where(col == cols - 1, he_t[:, l:l + 1], pltpu.roll(w, cols - 1, 1))
        lateral = north + south + west + east - 4.0 * w
        vertical = prev + nxt - 2.0 * u
        res = wet * (u + horiz * lateral + vert * vertical)
        if with_force and l == 0:
            res = res + jnp.where(i == 0, 1.0, 0.0) * (force_gain * wet * force_ref[...])
        out_ref[l] = res
        if with_edges:
            fw = wet * res
            en_ref[l:l + 1, :] = fw[0:1, :]
            es_ref[l:l + 1, :] = fw[rows - 1:rows, :]
            hit = lane == i * LB + l
            qw = jnp.where(hit, fw[:, 0:1], qw)
            qe = jnp.where(hit, fw[:, cols - 1:cols], qe)

    if with_edges:
        qw_ref[...] = qw
        qe_ref[...] = qe

        @pl.when(i == nblk - 1)
        def _():
            lev = ew_ref.shape[0]
            ew_ref[...] = jnp.transpose(qw_ref[...])[0:lev, :]
            ee_ref[...] = jnp.transpose(qe_ref[...])[0:lev, :]
            finish_spread(buckets_ref, recv, send_sem, recv_sem, arrived_ref)


def edges_kernel(wet_ref, u_ref, en_ref, es_ref, ew_ref, ee_ref, qw_ref, qe_ref):
    i = pl.program_id(0)
    nblk = pl.num_programs(0)
    wet = wet_ref[...]
    rows, cols = wet.shape

    @pl.when(i == 0)
    def _():
        qw_ref[...] = jnp.zeros_like(qw_ref)
        qe_ref[...] = jnp.zeros_like(qe_ref)

    lane = lax.broadcasted_iota(jnp.int32, qw_ref.shape, 1)
    qw = qw_ref[...]
    qe = qe_ref[...]
    for l in range(LB):
        fw = wet * u_ref[l]
        en_ref[l:l + 1, :] = fw[0:1, :]
        es_ref[l:l + 1, :] = fw[rows - 1:rows, :]
        hit = lane == i * LB + l
        qw = jnp.where(hit, fw[:, 0:1], qw)
        qe = jnp.where(hit, fw[:, cols - 1:cols], qe)
    qw_ref[...] = qw
    qe_ref[...] = qe

    @pl.when(i == nblk - 1)
    def _():
        lev = ew_ref.shape[0]
        ew_ref[...] = jnp.transpose(qw_ref[...])[0:lev, :]
        ee_ref[...] = jnp.transpose(qe_ref[...])[0:lev, :]


def masked_edges(wet, u):
    lev, rows, cols = u.shape
    lvl2 = pl.BlockSpec((LB, cols), lambda i: (i, 0))
    full2 = lambda shape: pl.BlockSpec(shape, lambda i: (0, 0))
    return pl.pallas_call(
        edges_kernel,
        grid=(lev // LB,),
        in_specs=[full2((rows, cols)), pl.BlockSpec((LB, rows, cols), lambda i: (i, 0, 0))],
        out_specs=[lvl2, lvl2, full2((lev, rows)), full2((lev, rows))],
        out_shape=[jax.ShapeDtypeStruct((lev, cols), jnp.float32)] * 2
        + [jax.ShapeDtypeStruct((lev, rows), jnp.float32)] * 2,
        scratch_shapes=[pltpu.VMEM((rows, 128), jnp.float32)] * 2,
        compiler_params=pltpu.CompilerParams(dimension_semantics=("arbitrary",)),
        cost_estimate=pl.CostEstimate(flops=2 * u.size, bytes_accessed=4 * u.size, transcendentals=0),
    )(wet, u)


def force_kernel(x_ref, wet_ref, f_ref, out_ref):
    out_ref[0] = x_ref[0] + force_gain * wet_ref[...] * f_ref[...]


def add_force(x, wet, f):
    lev, rows, cols = x.shape
    plane = pl.BlockSpec((rows, cols), lambda i: (0, 0))
    level0 = pl.BlockSpec((1, rows, cols), lambda i: (0, 0, 0))
    return pl.pallas_call(
        force_kernel,
        grid=(1,),
        in_specs=[level0, plane, plane],
        out_specs=level0,
        out_shape=jax.ShapeDtypeStruct(x.shape, x.dtype),
        input_output_aliases={0: 0},
    )(x, wet, f)


def stencil_step(coef, wet, u, halos, force=None, buckets=None):
    with_edges = buckets is not None
    lev, rows, cols = u.shape
    nblk = lev // LB
    full2 = lambda shape: pl.BlockSpec(shape, lambda i: (0, 0))
    lvl2 = pl.BlockSpec((LB, cols), lambda i: (i, 0))
    in_specs = [
        pl.BlockSpec(memory_space=pltpu.SMEM),
        full2((rows, cols)),
        pl.BlockSpec((LB, rows, cols), lambda i: (i, 0, 0)),
        pl.BlockSpec((1, rows, cols), lambda i: (jnp.maximum(i * LB - 1, 0), 0, 0)),
        pl.BlockSpec((1, rows, cols), lambda i: (jnp.minimum(i * LB + LB, lev - 1), 0, 0)),
        lvl2, lvl2, lvl2, lvl2,
    ]
    args = [coef, wet, u, u, u] + list(halos)
    if force is not None:
        in_specs.append(full2((rows, cols)))
        args.append(force)
    if with_edges:
        in_specs.append(pl.BlockSpec(buckets.shape, lambda i: (0, 0, 0, 0)))
        args.append(buckets)
    out_shape = [jax.ShapeDtypeStruct((lev, rows, cols), jnp.float32)]
    out_specs = [pl.BlockSpec((LB, rows, cols), lambda i: (i, 0, 0))]
    scratch = []
    params = dict(dimension_semantics=("arbitrary",))
    if with_edges:
        out_shape += [jax.ShapeDtypeStruct((lev, cols), jnp.float32)] * 2
        out_shape += [jax.ShapeDtypeStruct((lev, rows), jnp.float32)] * 2
        out_shape += [jax.ShapeDtypeStruct(buckets.shape, buckets.dtype)]
        out_specs += [lvl2, lvl2, full2((lev, rows)), full2((lev, rows))]
        out_specs += [pl.BlockSpec(buckets.shape, lambda i: (0, 0, 0, 0))]
        scratch = [pltpu.VMEM((rows, 128), jnp.float32)] * 2 + [
            pltpu.VMEM(buckets.shape, buckets.dtype),
            pltpu.SemaphoreType.DMA((buckets.shape[0],)),
            pltpu.SemaphoreType.DMA((buckets.shape[0],)),
        ]
        params.update(collective_id=2, has_side_effects=True)
    return pl.pallas_call(
        functools.partial(stencil_kernel, with_edges, force is not None),
        grid=(nblk,),
        in_specs=in_specs,
        out_specs=out_specs,
        out_shape=out_shape,
        scratch_shapes=scratch,
        compiler_params=pltpu.CompilerParams(**params),
        cost_estimate=pl.CostEstimate(flops=30 * u.size, bytes_accessed=12 * u.size, transcendentals=0),
    )(*args)


def halo_kernel(en_ref, es_ref, ew_ref, ee_ref, hn_ref, hs_ref, hw_ref, he_ref,
                buf, send_sem, recv_sem):
    mp = lax.axis_index("mp")
    gx = lax.axis_index("gx")
    gy = lax.axis_index("gy")
    ngx = lax.axis_size("gx")
    ngy = lax.axis_size("gy")
    mesh_id = pl.DeviceIdType.MESH
    links = [
        (gx < ngx - 1, (mp, gx + 1, gy), es_ref, 0),
        (gx > 0, (mp, gx - 1, gy), en_ref, 1),
        (gy < ngy - 1, (mp, gx, gy + 1), ee_ref, 2),
        (gy > 0, (mp, gx, gy - 1), ew_ref, 3),
    ]
    barrier = pltpu.get_barrier_semaphore()
    count = jnp.int32(0)
    for present, dev, _, _ in links:
        @pl.when(present)
        def _():
            pl.semaphore_signal(barrier, 1, device_id=dev, device_id_type=mesh_id)

        count = count + present.astype(jnp.int32)
    pl.semaphore_wait(barrier, count)

    copies = []
    for present, dev, src, slot in links:
        copy = pltpu.make_async_remote_copy(
            src_ref=src,
            dst_ref=buf.at[slot],
            send_sem=send_sem.at[slot],
            recv_sem=recv_sem.at[slot],
            device_id=dev,
            device_id_type=mesh_id,
        )
        pl.when(present)(copy.start)
        copies.append((present, copy))
    for present, copy in copies:
        pl.when(present)(copy.wait_send)
    fills = [gx > 0, gx < ngx - 1, gy > 0, gy < ngy - 1]
    outs = [hn_ref, hs_ref, hw_ref, he_ref]
    for slot, (filled, out) in enumerate(zip(fills, outs)):
        _, copy = copies[slot]

        @pl.when(filled)
        def _():
            copy.wait_recv()
            out[...] = buf[slot]

        @pl.when(jnp.logical_not(filled))
        def _():
            out[...] = jnp.zeros_like(out)


def exchange(en, es, ew, ee, call):
    shape = jax.ShapeDtypeStruct(en.shape, en.dtype)
    vmem = pl.BlockSpec(memory_space=pltpu.VMEM)
    return pl.pallas_call(
        halo_kernel,
        in_specs=[vmem] * 4,
        out_specs=[vmem] * 4,
        out_shape=[shape] * 4,
        scratch_shapes=[
            pltpu.VMEM((4,) + en.shape, en.dtype),
            pltpu.SemaphoreType.DMA((4,)),
            pltpu.SemaphoreType.DMA((4,)),
        ],
        compiler_params=pltpu.CompilerParams(collective_id=call, has_side_effects=True),
    )(en, es, ew, ee)


def bucket_kernel(inv_ref, lab_ref, contrib_ref, out_ref):
    ndest = out_ref.shape[0]
    ntiles = contrib_ref.shape[0]
    sub = lax.broadcasted_iota(jnp.int32, (KF, CY), 0)

    def body(d, carry):
        labv = jnp.zeros((KF, CY), jnp.float32)
        for c in range(CAP):
            t = inv_ref[d * CAP + c]
            val = contrib_ref[jnp.minimum(t, ntiles - 1)]
            out_ref[d, c] = jnp.where(t < ntiles, val, 0.0)
            labv = jnp.where(sub == c, lab_ref[d * CAP + c].astype(jnp.float32), labv)
        out_ref[d, CAP] = labv
        return carry

    lax.fori_loop(0, ndest, body, 0)


def local(states, surface, land_mask, tile_weights, tile_source, tile_target, tile_row):
    group = lax.axis_index("mp")
    ndev = lax.axis_size("gx") * lax.axis_size("gy")
    state = states[0]
    lev, rows_here, cols_here = state.shape
    wet = jnp.where(
        group == 0, jnp.ones(land_mask.shape, jnp.float32), land_mask.astype(jnp.float32)
    )
    coef = jnp.stack([jnp.where(group == 0, 0.15, 0.12), jnp.where(group == 0, 0.1, 0.15)]).astype(
        jnp.float32
    )

    src = (surface[0] * wet).astype(jnp.bfloat16)
    source = tile_source[0, 0, 0]
    target = tile_target[0, 0, 0, :, 0]
    dest_row = tile_row[0, 0, 0]
    ntiles = source.shape[0]
    picked = jnp.take(src, source, axis=1)
    contrib = jnp.einsum(
        "tji,kti->tkj", tile_weights[0, 0, 0], picked, preferred_element_type=jnp.float32
    )
    onehot = (target[:, None] == jnp.arange(ndev, dtype=jnp.int32)[None, :]).astype(jnp.int32)
    earlier = jnp.cumsum(onehot, axis=0) - onehot
    rank = jnp.sum(earlier * onehot, axis=1)
    slot = target * CAP + rank
    inv = jnp.full((ndev * CAP,), ntiles, jnp.int32).at[slot].set(jnp.arange(ntiles, dtype=jnp.int32))
    labels = jnp.zeros((ndev * CAP,), jnp.int32).at[slot].set(dest_row)
    buckets = pl.pallas_call(
        bucket_kernel,
        in_specs=[
            pl.BlockSpec(memory_space=pltpu.SMEM),
            pl.BlockSpec(memory_space=pltpu.SMEM),
            pl.BlockSpec(memory_space=pltpu.VMEM),
        ],
        out_specs=pl.BlockSpec(memory_space=pltpu.VMEM),
        out_shape=jax.ShapeDtypeStruct((ndev, CAP + 1, KF, CY), jnp.float32),
    )(inv, labels, contrib)
    first, en, es, ew, ee, arrived = first_step(coef, wet, state, buckets, masked_edges(wet, state))
    got_rows = arrived[:, CAP, :, 0].astype(jnp.int32)
    select = (
        got_rows[:, :, None] == jnp.arange(rows_here, dtype=jnp.int32)[None, None, :]
    ).astype(jnp.float32)
    sent = jnp.einsum(
        "scr,sckj->krj", select, arrived[:, :CAP], precision=lax.Precision.HIGHEST
    )
    received = lax.ppermute(sent, "mp", [(0, 1), (1, 0)])

    halos1 = exchange(en, es, ew, ee, 1)
    (second,) = stencil_step(coef, wet, first, halos1)
    second = add_force(second, wet, received[0])
    return (second[None], received[None])


def solution(mesh):
    return jax.shard_map(
        local,
        mesh=mesh,
        in_specs=(
            P("mp", None, "gx", "gy"),
            P("mp", None, "gx", "gy"),
            P("gx", "gy"),
            P("mp", "gx", "gy", None, None, None),
            P("mp", "gx", "gy", None),
            P("mp", "gx", "gy", None, None),
            P("mp", "gx", "gy", None),
        ),
        out_specs=(P("mp", None, "gx", "gy"), P("mp", None, "gx", "gy")),
        check_vma=False,
    )
```

```python
import functools

import jax
import jax.numpy as jnp
from jax import lax
from jax.experimental import pallas as pl
from jax.experimental.pallas import tpu as pltpu
from jax.sharding import PartitionSpec as P

CY = 128
KF = 8
CAP = 8
LB = 8

force_gain = 0.5


def shift_pairs(devices, forward):
    up = [(i, i + 1) for i in range(devices - 1)]
    return up if forward else [(j, i) for i, j in up]


def start_spread(buckets_ref, recv, send_sem, recv_sem, first_out=None):
    mp = lax.axis_index("mp")
    ngy = lax.axis_size("gy")
    ndev = lax.axis_size("gx") * ngy
    me = lax.axis_index("gx") * ngy + lax.axis_index("gy")
    mesh_id = pl.DeviceIdType.MESH
    barrier = pltpu.get_barrier_semaphore()

    def greet(d, carry):
        @pl.when(d != me)
        def _():
            pl.semaphore_signal(barrier, 1, device_id=(mp, d // ngy, d % ngy), device_id_type=mesh_id)

        return carry

    lax.fori_loop(0, ndev, greet, 0)
    pl.semaphore_wait(barrier, ndev - 1)
    if first_out is not None:
        first_out()
    recv[me] = buckets_ref[me]

    def send(k, carry):
        d = (me + k) % ndev
        pltpu.make_async_remote_copy(
            src_ref=buckets_ref.at[d],
            dst_ref=recv.at[me],
            send_sem=send_sem.at[d],
            recv_sem=recv_sem.at[me],
            device_id=(mp, d // ngy, d % ngy),
            device_id_type=mesh_id,
        ).start()
        return carry

    lax.fori_loop(1, ndev, send, 0)


def finish_spread(buckets_ref, recv, send_sem, recv_sem, arrived_ref):
    ngy = lax.axis_size("gy")
    ndev = lax.axis_size("gx") * ngy
    me = lax.axis_index("gx") * ngy + lax.axis_index("gy")

    def wait(d, carry):
        @pl.when(d != me)
        def _():
            copy = pltpu.make_async_remote_copy(
                src_ref=buckets_ref.at[d],
                dst_ref=recv.at[d],
                send_sem=send_sem.at[d],
                recv_sem=recv_sem.at[d],
                device_id=(lax.axis_index("mp"), d // ngy, d % ngy),
                device_id_type=pl.DeviceIdType.MESH,
            )
            copy.wait_send()
            copy.wait_recv()

        return carry

    lax.fori_loop(0, ndev, wait, 0)
    arrived_ref[...] = recv[...]


def interval_kernel(coef_ref, wet_ref, u_ref, above_ref, below_ref, buckets_ref,
                    e0n, e0s, e0w, e0e,
                    out_ref, arrived_ref,
                    first, edge1, halo0, halo1, qw_ref, qe_ref, recv,
                    send_sem, recv_sem, hsend, hrecv):
    p = pl.program_id(0)
    i = pl.program_id(1)
    nblk = pl.num_programs(1)
    wet = wet_ref[...]
    rows, cols = wet.shape
    lev = first.shape[0]
    mp = lax.axis_index("mp")
    gx = lax.axis_index("gx")
    gy = lax.axis_index("gy")
    ngx = lax.axis_size("gx")
    ngy = lax.axis_size("gy")
    ndev = ngx * ngy
    me = gx * ngy + gy
    mesh_id = pl.DeviceIdType.MESH
    links = [
        (gx < ngx - 1, (mp, gx + 1, gy), 1, 0),
        (gx > 0, (mp, gx - 1, gy), 0, 1),
        (gy < ngy - 1, (mp, gx, gy + 1), 3, 2),
        (gy > 0, (mp, gx, gy - 1), 2, 3),
    ]
    fills = [gx > 0, gx < ngx - 1, gy > 0, gy < ngy - 1]
    edge0 = [e0n, e0s, e0w, e0e]

    def halo_copy(stage, src, slot, dev):
        srcs = edge0[src] if stage == 0 else edge1.at[src]
        dsts = halo0.at[slot] if stage == 0 else halo1.at[slot]
        return pltpu.make_async_remote_copy(
            src_ref=srcs,
            dst_ref=dsts,
            send_sem=hsend.at[stage, slot],
            recv_sem=hrecv.at[stage, slot],
            device_id=dev,
            device_id_type=mesh_id,
        )

    def send_halos(stage):
        for present, dev, src, slot in links:
            pl.when(present)(halo_copy(stage, src, slot, dev).start)

    def take_halos(stage, dst):
        for present, dev, src, slot in links:
            pl.when(present)(halo_copy(stage, src, slot, dev).wait_send)
        for slot, filled in enumerate(fills):
            _, dev, src, _ = links[slot]
            pl.when(filled)(halo_copy(stage, src, slot, dev).wait_recv)

            @pl.when(jnp.logical_not(filled))
            def _():
                dst[slot] = jnp.zeros_like(dst[slot])

    def bucket_copy(d):
        return pltpu.make_async_remote_copy(
            src_ref=buckets_ref.at[d],
            dst_ref=recv.at[me],
            send_sem=send_sem.at[d],
            recv_sem=recv_sem.at[me],
            device_id=(mp, d // ngy, d % ngy),
            device_id_type=mesh_id,
        )

    def issue(k0, count):
        for n in range(count):
            k = k0 + n

            @pl.when(k < ndev)
            def _():
                bucket_copy((me + k) % ndev).start()

    lane = lax.broadcasted_iota(jnp.int32, qw_ref.shape, 1)
    row = lax.broadcasted_iota(jnp.int32, (rows, cols), 0)
    col = lax.broadcasted_iota(jnp.int32, (rows, cols), 1)
    horiz = coef_ref[0]
    vert = coef_ref[1]

    def step(load, above, below, hn, hs, hw_t, he_t, store):
        for l in range(LB):
            u = load(l)
            prev = load(l - 1) if l > 0 else above
            nxt = load(l + 1) if l < LB - 1 else below
            w = wet * u
            north = jnp.where(row == 0, hn[l:l + 1, :], pltpu.roll(w, 1, 0))
            south = jnp.where(row == rows - 1, hs[l:l + 1, :], pltpu.roll(w, rows - 1, 0))
            west = jnp.where(col == 0, hw_t[:, l:l + 1], pltpu.roll(w, 1, 1))
            east = jnp.where(col == cols - 1, he_t[:, l:l + 1], pltpu.roll(w, cols - 1, 1))
            lateral = north + south + west + east - 4.0 * w
            vertical = prev + nxt - 2.0 * u
            store(l, wet * (u + horiz * lateral + vert * vertical))

    @pl.when((p == 0) & (i == 0))
    def _():
        barrier = pltpu.get_barrier_semaphore()

        def greet(d, carry):
            @pl.when(d != me)
            def _():
                pl.semaphore_signal(barrier, 1, device_id=(mp, d // ngy, d % ngy), device_id_type=mesh_id)

            return carry

        lax.fori_loop(0, ndev, greet, 0)
        pl.semaphore_wait(barrier, ndev - 1)
        send_halos(0)
        recv[me] = buckets_ref[me]
        take_halos(0, halo0)
        qw_ref[...] = jnp.zeros_like(qw_ref)
        qe_ref[...] = jnp.zeros_like(qe_ref)

    @pl.when(p == 0)
    def _():
        issue(1 + 2 * i, 2)
        blk = pl.ds(pl.multiple_of(i * LB, LB), LB)
        hn = halo0[0, blk]
        hs = halo0[1, blk]
        hw_t = jnp.transpose(halo0[2, blk])
        he_t = jnp.transpose(halo0[3, blk])
        above = above_ref[0] * jnp.where(i > 0, 1.0, 0.0)
        below = below_ref[0] * jnp.where(i < nblk - 1, 1.0, 0.0)
        qs = [qw_ref[...], qe_ref[...]]

        def store(l, res):
            first[i * LB + l] = res
            fw = wet * res
            edge1[0, i, l:l + 1, :] = fw[0:1, :]
            edge1[1, i, l:l + 1, :] = fw[rows - 1:rows, :]
            hit = lane == i * LB + l
            qs[0] = jnp.where(hit, fw[:, 0:1], qs[0])
            qs[1] = jnp.where(hit, fw[:, cols - 1:cols], qs[1])

        step(lambda l: u_ref[l], above, below, hn, hs, hw_t, he_t, store)
        qw_ref[...] = qs[0]
        qe_ref[...] = qs[1]

    @pl.when((p == 0) & (i == nblk - 1))
    def _():
        edge1[2] = jnp.transpose(qw_ref[...])[0:lev, :].reshape(nblk, LB, rows)
        edge1[3] = jnp.transpose(qe_ref[...])[0:lev, :].reshape(nblk, LB, rows)
        send_halos(1)

    @pl.when((p == 1) & (i == 0))
    def _():
        take_halos(1, halo1)

    @pl.when(p == 1)
    def _():
        issue(1 + 2 * nblk + 6 * i, 6)
        base = i * LB
        above = first[jnp.maximum(base - 1, 0)] * jnp.where(i > 0, 1.0, 0.0)
        below = first[jnp.minimum(base + LB, lev - 1)] * jnp.where(i < nblk - 1, 1.0, 0.0)
        hw_t = jnp.transpose(halo1[2, i])
        he_t = jnp.transpose(halo1[3, i])

        def store(l, res):
            out_ref[l] = res

        step(lambda l: first[base + l], above, below, halo1[0, i], halo1[1, i], hw_t, he_t, store)

    @pl.when((p == 1) & (i == nblk - 1))
    def _():
        def wait(d, carry):
            @pl.when(d != me)
            def _():
                copy = pltpu.make_async_remote_copy(
                    src_ref=buckets_ref.at[d],
                    dst_ref=recv.at[d],
                    send_sem=send_sem.at[d],
                    recv_sem=recv_sem.at[d],
                    device_id=(mp, d // ngy, d % ngy),
                    device_id_type=mesh_id,
                )
                copy.wait_send()
                copy.wait_recv()

            return carry

        lax.fori_loop(0, ndev, wait, 0)
        arrived_ref[...] = recv[...]


def interval(coef, wet, u, buckets, edges):
    lev, rows, cols = u.shape
    nblk = lev // LB
    assert 1 + 2 * nblk + 6 * nblk >= buckets.shape[0]
    full2 = lambda shape: pl.BlockSpec(shape, lambda p, i: (0, 0))
    whole = pl.BlockSpec(buckets.shape, lambda p, i: (0, 0, 0, 0))
    held = lambda p, i: i + p * (nblk - 1 - i)
    in_specs = [
        pl.BlockSpec(memory_space=pltpu.SMEM),
        full2((rows, cols)),
        pl.BlockSpec((LB, rows, cols), lambda p, i: (held(p, i), 0, 0)),
        pl.BlockSpec((1, rows, cols), lambda p, i: (jnp.maximum(held(p, i) * LB - 1, 0), 0, 0)),
        pl.BlockSpec((1, rows, cols), lambda p, i: (jnp.minimum(held(p, i) * LB + LB, lev - 1), 0, 0)),
        whole,
    ] + [full2((lev, cols))] * 4
    out_shape = [
        jax.ShapeDtypeStruct((lev, rows, cols), jnp.float32),
        jax.ShapeDtypeStruct(buckets.shape, buckets.dtype),
    ]
    out_specs = [pl.BlockSpec((LB, rows, cols), lambda p, i: (i * p, 0, 0)), whole]
    scratch = [
        pltpu.VMEM((lev, rows, cols), jnp.float32),
        pltpu.VMEM((4, nblk, LB, cols), jnp.float32),
        pltpu.VMEM((4, lev, cols), jnp.float32),
        pltpu.VMEM((4, nblk, LB, cols), jnp.float32),
        pltpu.VMEM((rows, 128), jnp.float32),
        pltpu.VMEM((rows, 128), jnp.float32),
        pltpu.VMEM(buckets.shape, buckets.dtype),
        pltpu.SemaphoreType.DMA((buckets.shape[0],)),
        pltpu.SemaphoreType.DMA((buckets.shape[0],)),
        pltpu.SemaphoreType.DMA((2, 4)),
        pltpu.SemaphoreType.DMA((2, 4)),
    ]
    return pl.pallas_call(
        interval_kernel,
        grid=(2, nblk),
        in_specs=in_specs,
        out_specs=out_specs,
        out_shape=out_shape,
        scratch_shapes=scratch,
        compiler_params=pltpu.CompilerParams(
            dimension_semantics=("arbitrary", "arbitrary"), collective_id=3, has_side_effects=True,
            vmem_limit_bytes=48 * 1024 * 1024,
        ),
        cost_estimate=pl.CostEstimate(flops=60 * u.size, bytes_accessed=12 * u.size, transcendentals=0),
    )(coef, wet, u, u, u, buckets, *edges)


def first_kernel(coef_ref, wet_ref, u_ref, above_ref, below_ref, buckets_ref,
                 e0n, e0s, e0w, e0e,
                 out_ref, en_ref, es_ref, ew_ref, ee_ref, arrived_ref,
                 halo, qw_ref, qe_ref, recv, send_sem, recv_sem, hsend, hrecv):
    i = pl.program_id(0)
    nblk = pl.num_programs(0)
    edge0 = [e0n, e0s, e0w, e0e]
    wet = wet_ref[...]
    rows, cols = wet.shape
    lev = ew_ref.shape[0]
    mp = lax.axis_index("mp")
    gx = lax.axis_index("gx")
    gy = lax.axis_index("gy")
    ngx = lax.axis_size("gx")
    ngy = lax.axis_size("gy")
    mesh_id = pl.DeviceIdType.MESH
    links = [
        (gx < ngx - 1, (mp, gx + 1, gy), 1, 0),
        (gx > 0, (mp, gx - 1, gy), 0, 1),
        (gy < ngy - 1, (mp, gx, gy + 1), 3, 2),
        (gy > 0, (mp, gx, gy - 1), 2, 3),
    ]
    fills = [gx > 0, gx < ngx - 1, gy > 0, gy < ngy - 1]
    copies = [
        pltpu.make_async_remote_copy(
            src_ref=edge0[src],
            dst_ref=halo.at[slot],
            send_sem=hsend.at[slot],
            recv_sem=hrecv.at[slot],
            device_id=dev,
            device_id_type=mesh_id,
        )
        for _, dev, src, slot in links
    ]
    lane = lax.broadcasted_iota(jnp.int32, qw_ref.shape, 1)

    def send_halos():
        for (present, _, _, _), copy in zip(links, copies):
            pl.when(present)(copy.start)

    @pl.when(i == 0)
    def _():
        start_spread(buckets_ref, recv, send_sem, recv_sem, send_halos)
        for (present, _, _, _), copy in zip(links, copies):
            pl.when(present)(copy.wait_send)
        for slot, filled in enumerate(fills):
            pl.when(filled)(copies[slot].wait_recv)

            @pl.when(jnp.logical_not(filled))
            def _():
                halo[slot] = jnp.zeros_like(halo[slot])

        qw_ref[...] = jnp.zeros_like(qw_ref)
        qe_ref[...] = jnp.zeros_like(qe_ref)

    def _():
        horiz = coef_ref[0]
        vert = coef_ref[1]
        row = lax.broadcasted_iota(jnp.int32, (rows, cols), 0)
        col = lax.broadcasted_iota(jnp.int32, (rows, cols), 1)
        hn = halo[0, pl.ds(i * LB, LB)]
        hs = halo[1, pl.ds(i * LB, LB)]
        hw_t = jnp.transpose(halo[2, pl.ds(i * LB, LB)])
        he_t = jnp.transpose(halo[3, pl.ds(i * LB, LB)])
        above = above_ref[0] * jnp.where(i > 0, 1.0, 0.0)
        below = below_ref[0] * jnp.where(i < nblk - 1, 1.0, 0.0)
        qw = qw_ref[...]
        qe = qe_ref[...]
        for l in range(LB):
            u = u_ref[l]
            prev = u_ref[l - 1] if l > 0 else above
            nxt = u_ref[l + 1] if l < LB - 1 else below
            w = wet * u
            north = jnp.where(row == 0, hn[l:l + 1, :], pltpu.roll(w, 1, 0))
            south = jnp.where(row == rows - 1, hs[l:l + 1, :], pltpu.roll(w, rows - 1, 0))
            west = jnp.where(col == 0, hw_t[:, l:l + 1], pltpu.roll(w, 1, 1))
            east = jnp.where(col == cols - 1, he_t[:, l:l + 1], pltpu.roll(w, cols - 1, 1))
            lateral = north + south + west + east - 4.0 * w
            vertical = prev + nxt - 2.0 * u
            res = wet * (u + horiz * lateral + vert * vertical)
            out_ref[l] = res
            fw = wet * res
            en_ref[l:l + 1, :] = fw[0:1, :]
            es_ref[l:l + 1, :] = fw[rows - 1:rows, :]
            hit = lane == i * LB + l
            qw = jnp.where(hit, fw[:, 0:1], qw)
            qe = jnp.where(hit, fw[:, cols - 1:cols], qe)
        qw_ref[...] = qw
        qe_ref[...] = qe

    _()

    @pl.when(i == nblk - 1)
    def _():
        ew_ref[...] = jnp.transpose(qw_ref[...])[0:lev, :]
        ee_ref[...] = jnp.transpose(qe_ref[...])[0:lev, :]
        finish_spread(buckets_ref, recv, send_sem, recv_sem, arrived_ref)


def first_step(coef, wet, u, buckets, edges):
    lev, rows, cols = u.shape
    nblk = lev // LB
    full2 = lambda shape: pl.BlockSpec(shape, lambda i: (0, 0))
    lvl2 = pl.BlockSpec((LB, cols), lambda i: (i, 0))
    whole = pl.BlockSpec(buckets.shape, lambda i: (0, 0, 0, 0))
    in_specs = [
        pl.BlockSpec(memory_space=pltpu.SMEM),
        full2((rows, cols)),
        pl.BlockSpec((LB, rows, cols), lambda i: (i, 0, 0)),
        pl.BlockSpec((1, rows, cols), lambda i: (jnp.maximum(i * LB - 1, 0), 0, 0)),
        pl.BlockSpec((1, rows, cols), lambda i: (jnp.minimum(i * LB + LB, lev - 1), 0, 0)),
        whole,
    ] + [full2((lev, cols))] * 4
    out_shape = [
        jax.ShapeDtypeStruct((lev, rows, cols), jnp.float32),
        jax.ShapeDtypeStruct((lev, cols), jnp.float32),
        jax.ShapeDtypeStruct((lev, cols), jnp.float32),
        jax.ShapeDtypeStruct((lev, rows), jnp.float32),
        jax.ShapeDtypeStruct((lev, rows), jnp.float32),
        jax.ShapeDtypeStruct(buckets.shape, buckets.dtype),
    ]
    out_specs = [
        pl.BlockSpec((LB, rows, cols), lambda i: (i, 0, 0)),
        lvl2, lvl2, full2((lev, rows)), full2((lev, rows)), whole,
    ]
    scratch = [
        pltpu.VMEM((4, lev, cols), jnp.float32),
        pltpu.VMEM((rows, 128), jnp.float32),
        pltpu.VMEM((rows, 128), jnp.float32),
        pltpu.VMEM(buckets.shape, buckets.dtype),
        pltpu.SemaphoreType.DMA((buckets.shape[0],)),
        pltpu.SemaphoreType.DMA((buckets.shape[0],)),
        pltpu.SemaphoreType.DMA((4,)),
        pltpu.SemaphoreType.DMA((4,)),
    ]
    return pl.pallas_call(
        first_kernel,
        grid=(nblk,),
        in_specs=in_specs,
        out_specs=out_specs,
        out_shape=out_shape,
        scratch_shapes=scratch,
        compiler_params=pltpu.CompilerParams(
            dimension_semantics=("arbitrary",), collective_id=2, has_side_effects=True
        ),
        cost_estimate=pl.CostEstimate(flops=30 * u.size, bytes_accessed=12 * u.size, transcendentals=0),
    )(coef, wet, u, u, u, buckets, *edges)


def stencil_kernel(with_edges, with_force, coef_ref, wet_ref, u_ref, above_ref, below_ref,
                   hn_ref, hs_ref, hw_ref, he_ref, *rest):
    if with_force:
        force_ref, rest = rest[0], rest[1:]
    if with_edges:
        buckets_ref, rest = rest[0], rest[1:]
    out_ref = rest[0]
    i = pl.program_id(0)
    nblk = pl.num_programs(0)
    horiz = coef_ref[0]
    vert = coef_ref[1]
    wet = wet_ref[...]
    rows, cols = wet.shape
    row = lax.broadcasted_iota(jnp.int32, (rows, cols), 0)
    col = lax.broadcasted_iota(jnp.int32, (rows, cols), 1)
    hw_t = jnp.transpose(hw_ref[...])
    he_t = jnp.transpose(he_ref[...])
    above = above_ref[0] * jnp.where(i > 0, 1.0, 0.0)
    below = below_ref[0] * jnp.where(i < nblk - 1, 1.0, 0.0)
    if with_edges:
        en_ref, es_ref, ew_ref, ee_ref, arrived_ref, qw_ref, qe_ref, recv, send_sem, recv_sem = rest[1:]

        @pl.when(i == 0)
        def _():
            start_spread(buckets_ref, recv, send_sem, recv_sem)
            qw_ref[...] = jnp.zeros_like(qw_ref)
            qe_ref[...] = jnp.zeros_like(qe_ref)

    if with_edges:
        lane = lax.broadcasted_iota(jnp.int32, qw_ref.shape, 1)
        qw = qw_ref[...]
        qe = qe_ref[...]
    for l in range(LB):
        u = u_ref[l]
        prev = u_ref[l - 1] if l > 0 else above
        nxt = u_ref[l + 1] if l < LB - 1 else below
        w = wet * u
        north = jnp.where(row == 0, hn_ref[l:l + 1, :], pltpu.roll(w, 1, 0))
        south = jnp.where(row == rows - 1, hs_ref[l:l + 1, :], pltpu.roll(w, rows - 1, 0))
        west = jnp.where(col == 0, hw_t[:, l:l + 1], pltpu.roll(w, 1, 1))
        east = jnp.where(col == cols - 1, he_t[:, l:l + 1], pltpu.roll(w, cols - 1, 1))
        lateral = north + south + west + east - 4.0 * w
        vertical = prev + nxt - 2.0 * u
        res = wet * (u + horiz * lateral + vert * vertical)
        if with_force and l == 0:
            res = res + jnp.where(i == 0, 1.0, 0.0) * (force_gain * wet * force_ref[...])
        out_ref[l] = res
        if with_edges:
            fw = wet * res
            en_ref[l:l + 1, :] = fw[0:1, :]
            es_ref[l:l + 1, :] = fw[rows - 1:rows, :]
            hit = lane == i * LB + l
            qw = jnp.where(hit, fw[:, 0:1], qw)
            qe = jnp.where(hit, fw[:, cols - 1:cols], qe)

    if with_edges:
        qw_ref[...] = qw
        qe_ref[...] = qe

        @pl.when(i == nblk - 1)
        def _():
            lev = ew_ref.shape[0]
            ew_ref[...] = jnp.transpose(qw_ref[...])[0:lev, :]
            ee_ref[...] = jnp.transpose(qe_ref[...])[0:lev, :]
            finish_spread(buckets_ref, recv, send_sem, recv_sem, arrived_ref)


def edges_kernel(wet_ref, u_ref, en_ref, es_ref, ew_ref, ee_ref, qw_ref, qe_ref):
    i = pl.program_id(0)
    nblk = pl.num_programs(0)
    wet = wet_ref[...]
    rows, cols = wet.shape

    @pl.when(i == 0)
    def _():
        qw_ref[...] = jnp.zeros_like(qw_ref)
        qe_ref[...] = jnp.zeros_like(qe_ref)

    lane = lax.broadcasted_iota(jnp.int32, qw_ref.shape, 1)
    qw = qw_ref[...]
    qe = qe_ref[...]
    for l in range(LB):
        fw = wet * u_ref[l]
        en_ref[l:l + 1, :] = fw[0:1, :]
        es_ref[l:l + 1, :] = fw[rows - 1:rows, :]
        hit = lane == i * LB + l
        qw = jnp.where(hit, fw[:, 0:1], qw)
        qe = jnp.where(hit, fw[:, cols - 1:cols], qe)
    qw_ref[...] = qw
    qe_ref[...] = qe

    @pl.when(i == nblk - 1)
    def _():
        lev = ew_ref.shape[0]
        ew_ref[...] = jnp.transpose(qw_ref[...])[0:lev, :]
        ee_ref[...] = jnp.transpose(qe_ref[...])[0:lev, :]


def masked_edges(wet, u):
    lev, rows, cols = u.shape
    lvl2 = pl.BlockSpec((LB, cols), lambda i: (i, 0))
    full2 = lambda shape: pl.BlockSpec(shape, lambda i: (0, 0))
    return pl.pallas_call(
        edges_kernel,
        grid=(lev // LB,),
        in_specs=[full2((rows, cols)), pl.BlockSpec((LB, rows, cols), lambda i: (i, 0, 0))],
        out_specs=[lvl2, lvl2, full2((lev, rows)), full2((lev, rows))],
        out_shape=[jax.ShapeDtypeStruct((lev, cols), jnp.float32)] * 2
        + [jax.ShapeDtypeStruct((lev, rows), jnp.float32)] * 2,
        scratch_shapes=[pltpu.VMEM((rows, 128), jnp.float32)] * 2,
        compiler_params=pltpu.CompilerParams(dimension_semantics=("arbitrary",)),
        cost_estimate=pl.CostEstimate(flops=2 * u.size, bytes_accessed=4 * u.size, transcendentals=0),
    )(wet, u)


def force_kernel(x_ref, wet_ref, f_ref, out_ref):
    out_ref[0] = x_ref[0] + force_gain * wet_ref[...] * f_ref[...]


def add_force(x, wet, f):
    lev, rows, cols = x.shape
    plane = pl.BlockSpec((rows, cols), lambda i: (0, 0))
    level0 = pl.BlockSpec((1, rows, cols), lambda i: (0, 0, 0))
    return pl.pallas_call(
        force_kernel,
        grid=(1,),
        in_specs=[level0, plane, plane],
        out_specs=level0,
        out_shape=jax.ShapeDtypeStruct(x.shape, x.dtype),
        input_output_aliases={0: 0},
    )(x, wet, f)


def stencil_step(coef, wet, u, halos, force=None, buckets=None):
    with_edges = buckets is not None
    lev, rows, cols = u.shape
    nblk = lev // LB
    full2 = lambda shape: pl.BlockSpec(shape, lambda i: (0, 0))
    lvl2 = pl.BlockSpec((LB, cols), lambda i: (i, 0))
    in_specs = [
        pl.BlockSpec(memory_space=pltpu.SMEM),
        full2((rows, cols)),
        pl.BlockSpec((LB, rows, cols), lambda i: (i, 0, 0)),
        pl.BlockSpec((1, rows, cols), lambda i: (jnp.maximum(i * LB - 1, 0), 0, 0)),
        pl.BlockSpec((1, rows, cols), lambda i: (jnp.minimum(i * LB + LB, lev - 1), 0, 0)),
        lvl2, lvl2, lvl2, lvl2,
    ]
    args = [coef, wet, u, u, u] + list(halos)
    if force is not None:
        in_specs.append(full2((rows, cols)))
        args.append(force)
    if with_edges:
        in_specs.append(pl.BlockSpec(buckets.shape, lambda i: (0, 0, 0, 0)))
        args.append(buckets)
    out_shape = [jax.ShapeDtypeStruct((lev, rows, cols), jnp.float32)]
    out_specs = [pl.BlockSpec((LB, rows, cols), lambda i: (i, 0, 0))]
    scratch = []
    params = dict(dimension_semantics=("arbitrary",))
    if with_edges:
        out_shape += [jax.ShapeDtypeStruct((lev, cols), jnp.float32)] * 2
        out_shape += [jax.ShapeDtypeStruct((lev, rows), jnp.float32)] * 2
        out_shape += [jax.ShapeDtypeStruct(buckets.shape, buckets.dtype)]
        out_specs += [lvl2, lvl2, full2((lev, rows)), full2((lev, rows))]
        out_specs += [pl.BlockSpec(buckets.shape, lambda i: (0, 0, 0, 0))]
        scratch = [pltpu.VMEM((rows, 128), jnp.float32)] * 2 + [
            pltpu.VMEM(buckets.shape, buckets.dtype),
            pltpu.SemaphoreType.DMA((buckets.shape[0],)),
            pltpu.SemaphoreType.DMA((buckets.shape[0],)),
        ]
        params.update(collective_id=2, has_side_effects=True)
    return pl.pallas_call(
        functools.partial(stencil_kernel, with_edges, force is not None),
        grid=(nblk,),
        in_specs=in_specs,
        out_specs=out_specs,
        out_shape=out_shape,
        scratch_shapes=scratch,
        compiler_params=pltpu.CompilerParams(**params),
        cost_estimate=pl.CostEstimate(flops=30 * u.size, bytes_accessed=12 * u.size, transcendentals=0),
    )(*args)


def halo_kernel(en_ref, es_ref, ew_ref, ee_ref, hn_ref, hs_ref, hw_ref, he_ref,
                buf, send_sem, recv_sem):
    mp = lax.axis_index("mp")
    gx = lax.axis_index("gx")
    gy = lax.axis_index("gy")
    ngx = lax.axis_size("gx")
    ngy = lax.axis_size("gy")
    mesh_id = pl.DeviceIdType.MESH
    links = [
        (gx < ngx - 1, (mp, gx + 1, gy), es_ref, 0),
        (gx > 0, (mp, gx - 1, gy), en_ref, 1),
        (gy < ngy - 1, (mp, gx, gy + 1), ee_ref, 2),
        (gy > 0, (mp, gx, gy - 1), ew_ref, 3),
    ]
    barrier = pltpu.get_barrier_semaphore()
    count = jnp.int32(0)
    for present, dev, _, _ in links:
        @pl.when(present)
        def _():
            pl.semaphore_signal(barrier, 1, device_id=dev, device_id_type=mesh_id)

        count = count + present.astype(jnp.int32)
    pl.semaphore_wait(barrier, count)

    copies = []
    for present, dev, src, slot in links:
        copy = pltpu.make_async_remote_copy(
            src_ref=src,
            dst_ref=buf.at[slot],
            send_sem=send_sem.at[slot],
            recv_sem=recv_sem.at[slot],
            device_id=dev,
            device_id_type=mesh_id,
        )
        pl.when(present)(copy.start)
        copies.append((present, copy))
    for present, copy in copies:
        pl.when(present)(copy.wait_send)
    fills = [gx > 0, gx < ngx - 1, gy > 0, gy < ngy - 1]
    outs = [hn_ref, hs_ref, hw_ref, he_ref]
    for slot, (filled, out) in enumerate(zip(fills, outs)):
        _, copy = copies[slot]

        @pl.when(filled)
        def _():
            copy.wait_recv()
            out[...] = buf[slot]

        @pl.when(jnp.logical_not(filled))
        def _():
            out[...] = jnp.zeros_like(out)


def exchange(en, es, ew, ee, call):
    shape = jax.ShapeDtypeStruct(en.shape, en.dtype)
    vmem = pl.BlockSpec(memory_space=pltpu.VMEM)
    return pl.pallas_call(
        halo_kernel,
        in_specs=[vmem] * 4,
        out_specs=[vmem] * 4,
        out_shape=[shape] * 4,
        scratch_shapes=[
            pltpu.VMEM((4,) + en.shape, en.dtype),
            pltpu.SemaphoreType.DMA((4,)),
            pltpu.SemaphoreType.DMA((4,)),
        ],
        compiler_params=pltpu.CompilerParams(collective_id=call, has_side_effects=True),
    )(en, es, ew, ee)


def bucket_kernel(inv_ref, lab_ref, contrib_ref, out_ref):
    ndest = out_ref.shape[0]
    ntiles = contrib_ref.shape[0]
    sub = lax.broadcasted_iota(jnp.int32, (KF, CY), 0)

    def body(d, carry):
        labv = jnp.zeros((KF, CY), jnp.float32)
        for c in range(CAP):
            t = inv_ref[d * CAP + c]
            val = contrib_ref[jnp.minimum(t, ntiles - 1)]
            out_ref[d, c] = jnp.where(t < ntiles, val, 0.0)
            labv = jnp.where(sub == c, lab_ref[d * CAP + c].astype(jnp.float32), labv)
        out_ref[d, CAP] = labv
        return carry

    lax.fori_loop(0, ndest, body, 0)


def local(states, surface, land_mask, tile_weights, tile_source, tile_target, tile_row):
    group = lax.axis_index("mp")
    ndev = lax.axis_size("gx") * lax.axis_size("gy")
    state = states[0]
    lev, rows_here, cols_here = state.shape
    wet = jnp.where(
        group == 0, jnp.ones(land_mask.shape, jnp.float32), land_mask.astype(jnp.float32)
    )
    coef = jnp.stack([jnp.where(group == 0, 0.15, 0.12), jnp.where(group == 0, 0.1, 0.15)]).astype(
        jnp.float32
    )

    src = (surface[0] * wet).astype(jnp.bfloat16)
    source = tile_source[0, 0, 0]
    target = tile_target[0, 0, 0, :, 0]
    dest_row = tile_row[0, 0, 0]
    ntiles = source.shape[0]
    picked = jnp.take(src, source, axis=1)
    contrib = jnp.einsum(
        "tji,kti->tkj", tile_weights[0, 0, 0], picked, preferred_element_type=jnp.float32
    )
    onehot = (target[:, None] == jnp.arange(ndev, dtype=jnp.int32)[None, :]).astype(jnp.int32)
    earlier = jnp.cumsum(onehot, axis=0) - onehot
    rank = jnp.sum(earlier * onehot, axis=1)
    slot = target * CAP + rank
    inv = jnp.full((ndev * CAP,), ntiles, jnp.int32).at[slot].set(jnp.arange(ntiles, dtype=jnp.int32))
    labels = jnp.zeros((ndev * CAP,), jnp.int32).at[slot].set(dest_row)
    buckets = pl.pallas_call(
        bucket_kernel,
        in_specs=[
            pl.BlockSpec(memory_space=pltpu.SMEM),
            pl.BlockSpec(memory_space=pltpu.SMEM),
            pl.BlockSpec(memory_space=pltpu.VMEM),
        ],
        out_specs=pl.BlockSpec(memory_space=pltpu.VMEM),
        out_shape=jax.ShapeDtypeStruct((ndev, CAP + 1, KF, CY), jnp.float32),
    )(inv, labels, contrib)
    second, arrived = interval(coef, wet, state, buckets, masked_edges(wet, state))
    got_rows = arrived[:, CAP, :, 0].astype(jnp.int32)
    select = (
        got_rows[:, :, None] == jnp.arange(rows_here, dtype=jnp.int32)[None, None, :]
    ).astype(jnp.float32)
    sent = jnp.einsum(
        "scr,sckj->krj", select, arrived[:, :CAP], precision=lax.Precision.HIGHEST
    )
    received = lax.ppermute(sent, "mp", [(0, 1), (1, 0)])

    second = add_force(second, wet, received[0])
    return (second[None], received[None])


def solution(mesh):
    return jax.shard_map(
        local,
        mesh=mesh,
        in_specs=(
            P("mp", None, "gx", "gy"),
            P("mp", None, "gx", "gy"),
            P("gx", "gy"),
            P("mp", "gx", "gy", None, None, None),
            P("mp", "gx", "gy", None),
            P("mp", "gx", "gy", None, None),
            P("mp", "gx", "gy", None),
        ),
        out_specs=(P("mp", None, "gx", "gy"), P("mp", None, "gx", "gy")),
        check_vma=False,
    )
```

```python
import functools

import jax
import jax.numpy as jnp
from jax import lax
from jax.experimental import pallas as pl
from jax.experimental.pallas import tpu as pltpu
from jax.sharding import PartitionSpec as P

CY = 128
KF = 8
CAP = 8
LB = 8

force_gain = 0.5


def shift_pairs(devices, forward):
    up = [(i, i + 1) for i in range(devices - 1)]
    return up if forward else [(j, i) for i, j in up]


def start_spread(buckets_ref, recv, send_sem, recv_sem, first_out=None):
    mp = lax.axis_index("mp")
    ngy = lax.axis_size("gy")
    ndev = lax.axis_size("gx") * ngy
    me = lax.axis_index("gx") * ngy + lax.axis_index("gy")
    mesh_id = pl.DeviceIdType.MESH
    barrier = pltpu.get_barrier_semaphore()

    def greet(d, carry):
        @pl.when(d != me)
        def _():
            pl.semaphore_signal(barrier, 1, device_id=(mp, d // ngy, d % ngy), device_id_type=mesh_id)

        return carry

    lax.fori_loop(0, ndev, greet, 0)
    pl.semaphore_wait(barrier, ndev - 1)
    if first_out is not None:
        first_out()
    recv[me] = buckets_ref[me]

    def send(k, carry):
        d = (me + k) % ndev
        pltpu.make_async_remote_copy(
            src_ref=buckets_ref.at[d],
            dst_ref=recv.at[me],
            send_sem=send_sem.at[d],
            recv_sem=recv_sem.at[me],
            device_id=(mp, d // ngy, d % ngy),
            device_id_type=mesh_id,
        ).start()
        return carry

    lax.fori_loop(1, ndev, send, 0)


def finish_spread(buckets_ref, recv, send_sem, recv_sem, arrived_ref):
    ngy = lax.axis_size("gy")
    ndev = lax.axis_size("gx") * ngy
    me = lax.axis_index("gx") * ngy + lax.axis_index("gy")

    def wait(d, carry):
        @pl.when(d != me)
        def _():
            copy = pltpu.make_async_remote_copy(
                src_ref=buckets_ref.at[d],
                dst_ref=recv.at[d],
                send_sem=send_sem.at[d],
                recv_sem=recv_sem.at[d],
                device_id=(lax.axis_index("mp"), d // ngy, d % ngy),
                device_id_type=pl.DeviceIdType.MESH,
            )
            copy.wait_send()
            copy.wait_recv()

        return carry

    lax.fori_loop(0, ndev, wait, 0)
    arrived_ref[...] = recv[...]


def interval_kernel(coef_ref, wet_ref, u_ref, above_ref, below_ref, buckets_ref,
                    e0n, e0s, e0w, e0e,
                    out_ref, arrived_ref,
                    first, edge1, halo0, halo1, qw_ref, qe_ref, recv,
                    send_sem, recv_sem, hsend, hrecv):
    p = pl.program_id(0)
    i = pl.program_id(1)
    nblk = pl.num_programs(1)
    wet = wet_ref[...]
    rows, cols = wet.shape
    lev = first.shape[0]
    mp = lax.axis_index("mp")
    gx = lax.axis_index("gx")
    gy = lax.axis_index("gy")
    ngx = lax.axis_size("gx")
    ngy = lax.axis_size("gy")
    ndev = ngx * ngy
    me = gx * ngy + gy
    mesh_id = pl.DeviceIdType.MESH
    links = [
        (gx < ngx - 1, (mp, gx + 1, gy), 1, 0),
        (gx > 0, (mp, gx - 1, gy), 0, 1),
        (gy < ngy - 1, (mp, gx, gy + 1), 3, 2),
        (gy > 0, (mp, gx, gy - 1), 2, 3),
    ]
    fills = [gx > 0, gx < ngx - 1, gy > 0, gy < ngy - 1]
    edge0 = [e0n, e0s, e0w, e0e]

    def halo_copy(stage, src, slot, dev):
        srcs = edge0[src] if stage == 0 else edge1.at[src]
        dsts = halo0.at[slot] if stage == 0 else halo1.at[slot]
        return pltpu.make_async_remote_copy(
            src_ref=srcs,
            dst_ref=dsts,
            send_sem=hsend.at[stage, slot],
            recv_sem=hrecv.at[stage, slot],
            device_id=dev,
            device_id_type=mesh_id,
        )

    def send_halos(stage):
        for present, dev, src, slot in links:
            pl.when(present)(halo_copy(stage, src, slot, dev).start)

    def take_halos(stage, dst):
        for present, dev, src, slot in links:
            pl.when(present)(halo_copy(stage, src, slot, dev).wait_send)
        for slot, filled in enumerate(fills):
            _, dev, src, _ = links[slot]
            pl.when(filled)(halo_copy(stage, src, slot, dev).wait_recv)

            @pl.when(jnp.logical_not(filled))
            def _():
                dst[slot] = jnp.zeros_like(dst[slot])

    def bucket_copy(d):
        return pltpu.make_async_remote_copy(
            src_ref=buckets_ref.at[d],
            dst_ref=recv.at[me],
            send_sem=send_sem.at[d],
            recv_sem=recv_sem.at[me],
            device_id=(mp, d // ngy, d % ngy),
            device_id_type=mesh_id,
        )

    def issue(k0, count):
        for n in range(count):
            k = k0 + n

            @pl.when(k < ndev)
            def _():
                bucket_copy((me + k) % ndev).start()

    lane = lax.broadcasted_iota(jnp.int32, qw_ref.shape, 1)
    row = lax.broadcasted_iota(jnp.int32, (rows, cols), 0)
    col = lax.broadcasted_iota(jnp.int32, (rows, cols), 1)
    horiz = coef_ref[0]
    vert = coef_ref[1]

    def step(load, above, below, hn, hs, hw_t, he_t, store):
        for l in range(LB):
            u = load(l)
            prev = load(l - 1) if l > 0 else above
            nxt = load(l + 1) if l < LB - 1 else below
            w = wet * u
            north = jnp.where(row == 0, hn[l:l + 1, :], pltpu.roll(w, 1, 0))
            south = jnp.where(row == rows - 1, hs[l:l + 1, :], pltpu.roll(w, rows - 1, 0))
            west = jnp.where(col == 0, hw_t[:, l:l + 1], pltpu.roll(w, 1, 1))
            east = jnp.where(col == cols - 1, he_t[:, l:l + 1], pltpu.roll(w, cols - 1, 1))
            lateral = north + south + west + east - 4.0 * w
            vertical = prev + nxt - 2.0 * u
            store(l, wet * (u + horiz * lateral + vert * vertical))

    @pl.when((p == 0) & (i == 0))
    def _():
        barrier = pltpu.get_barrier_semaphore()

        def greet(d, carry):
            @pl.when(d != me)
            def _():
                pl.semaphore_signal(barrier, 1, device_id=(mp, d // ngy, d % ngy), device_id_type=mesh_id)

            return carry

        lax.fori_loop(0, ndev, greet, 0)
        pl.semaphore_wait(barrier, ndev - 1)
        send_halos(0)
        recv[me] = buckets_ref[me]
        take_halos(0, halo0)
        qw_ref[...] = jnp.zeros_like(qw_ref)
        qe_ref[...] = jnp.zeros_like(qe_ref)

    @pl.when(p == 0)
    def _():
        issue(1 + 3 * i, 3)
        blk = pl.ds(pl.multiple_of(i * LB, LB), LB)
        hn = halo0[0, blk]
        hs = halo0[1, blk]
        hw_t = jnp.transpose(halo0[2, blk])
        he_t = jnp.transpose(halo0[3, blk])
        above = above_ref[0] * jnp.where(i > 0, 1.0, 0.0)
        below = below_ref[0] * jnp.where(i < nblk - 1, 1.0, 0.0)
        qs = [qw_ref[...], qe_ref[...]]

        def store(l, res):
            first[i * LB + l] = res
            fw = wet * res
            edge1[0, i, l:l + 1, :] = fw[0:1, :]
            edge1[1, i, l:l + 1, :] = fw[rows - 1:rows, :]
            hit = lane == i * LB + l
            qs[0] = jnp.where(hit, fw[:, 0:1], qs[0])
            qs[1] = jnp.where(hit, fw[:, cols - 1:cols], qs[1])

        step(lambda l: u_ref[l], above, below, hn, hs, hw_t, he_t, store)
        qw_ref[...] = qs[0]
        qe_ref[...] = qs[1]

    @pl.when((p == 0) & (i == nblk - 1))
    def _():
        edge1[2] = jnp.transpose(qw_ref[...])[0:lev, :].reshape(nblk, LB, rows)
        edge1[3] = jnp.transpose(qe_ref[...])[0:lev, :].reshape(nblk, LB, rows)
        send_halos(1)

    @pl.when((p == 1) & (i == 0))
    def _():
        take_halos(1, halo1)

        def late(k, carry):
            bucket_copy((me + k) % ndev).start()
            return carry

        lax.fori_loop(min(1 + 3 * nblk, ndev), ndev, late, 0)

    @pl.when(p == 1)
    def _():
        base = i * LB
        above = first[jnp.maximum(base - 1, 0)] * jnp.where(i > 0, 1.0, 0.0)
        below = first[jnp.minimum(base + LB, lev - 1)] * jnp.where(i < nblk - 1, 1.0, 0.0)
        hw_t = jnp.transpose(halo1[2, i])
        he_t = jnp.transpose(halo1[3, i])

        def store(l, res):
            out_ref[l] = res

        step(lambda l: first[base + l], above, below, halo1[0, i], halo1[1, i], hw_t, he_t, store)

    @pl.when((p == 1) & (i == nblk - 1))
    def _():
        def wait(d, carry):
            @pl.when(d != me)
            def _():
                copy = pltpu.make_async_remote_copy(
                    src_ref=buckets_ref.at[d],
                    dst_ref=recv.at[d],
                    send_sem=send_sem.at[d],
                    recv_sem=recv_sem.at[d],
                    device_id=(mp, d // ngy, d % ngy),
                    device_id_type=mesh_id,
                )
                copy.wait_send()
                copy.wait_recv()

            return carry

        lax.fori_loop(0, ndev, wait, 0)
        arrived_ref[...] = recv[...]


def interval(coef, wet, u, buckets, edges):
    lev, rows, cols = u.shape
    nblk = lev // LB
    full2 = lambda shape: pl.BlockSpec(shape, lambda p, i: (0, 0))
    whole = pl.BlockSpec(buckets.shape, lambda p, i: (0, 0, 0, 0))
    held = lambda p, i: i + p * (nblk - 1 - i)
    in_specs = [
        pl.BlockSpec(memory_space=pltpu.SMEM),
        full2((rows, cols)),
        pl.BlockSpec((LB, rows, cols), lambda p, i: (held(p, i), 0, 0)),
        pl.BlockSpec((1, rows, cols), lambda p, i: (jnp.maximum(held(p, i) * LB - 1, 0), 0, 0)),
        pl.BlockSpec((1, rows, cols), lambda p, i: (jnp.minimum(held(p, i) * LB + LB, lev - 1), 0, 0)),
        whole,
    ] + [full2((lev, cols))] * 4
    out_shape = [
        jax.ShapeDtypeStruct((lev, rows, cols), jnp.float32),
        jax.ShapeDtypeStruct(buckets.shape, buckets.dtype),
    ]
    out_specs = [pl.BlockSpec((LB, rows, cols), lambda p, i: (i * p, 0, 0)), whole]
    scratch = [
        pltpu.VMEM((lev, rows, cols), jnp.float32),
        pltpu.VMEM((4, nblk, LB, cols), jnp.float32),
        pltpu.VMEM((4, lev, cols), jnp.float32),
        pltpu.VMEM((4, nblk, LB, cols), jnp.float32),
        pltpu.VMEM((rows, 128), jnp.float32),
        pltpu.VMEM((rows, 128), jnp.float32),
        pltpu.VMEM(buckets.shape, buckets.dtype),
        pltpu.SemaphoreType.DMA((buckets.shape[0],)),
        pltpu.SemaphoreType.DMA((buckets.shape[0],)),
        pltpu.SemaphoreType.DMA((2, 4)),
        pltpu.SemaphoreType.DMA((2, 4)),
    ]
    return pl.pallas_call(
        interval_kernel,
        grid=(2, nblk),
        in_specs=in_specs,
        out_specs=out_specs,
        out_shape=out_shape,
        scratch_shapes=scratch,
        compiler_params=pltpu.CompilerParams(
            dimension_semantics=("arbitrary", "arbitrary"), collective_id=3, has_side_effects=True,
            vmem_limit_bytes=48 * 1024 * 1024,
        ),
        cost_estimate=pl.CostEstimate(flops=60 * u.size, bytes_accessed=12 * u.size, transcendentals=0),
    )(coef, wet, u, u, u, buckets, *edges)


def first_kernel(coef_ref, wet_ref, u_ref, above_ref, below_ref, buckets_ref,
                 e0n, e0s, e0w, e0e,
                 out_ref, en_ref, es_ref, ew_ref, ee_ref, arrived_ref,
                 halo, qw_ref, qe_ref, recv, send_sem, recv_sem, hsend, hrecv):
    i = pl.program_id(0)
    nblk = pl.num_programs(0)
    edge0 = [e0n, e0s, e0w, e0e]
    wet = wet_ref[...]
    rows, cols = wet.shape
    lev = ew_ref.shape[0]
    mp = lax.axis_index("mp")
    gx = lax.axis_index("gx")
    gy = lax.axis_index("gy")
    ngx = lax.axis_size("gx")
    ngy = lax.axis_size("gy")
    mesh_id = pl.DeviceIdType.MESH
    links = [
        (gx < ngx - 1, (mp, gx + 1, gy), 1, 0),
        (gx > 0, (mp, gx - 1, gy), 0, 1),
        (gy < ngy - 1, (mp, gx, gy + 1), 3, 2),
        (gy > 0, (mp, gx, gy - 1), 2, 3),
    ]
    fills = [gx > 0, gx < ngx - 1, gy > 0, gy < ngy - 1]
    copies = [
        pltpu.make_async_remote_copy(
            src_ref=edge0[src],
            dst_ref=halo.at[slot],
            send_sem=hsend.at[slot],
            recv_sem=hrecv.at[slot],
            device_id=dev,
            device_id_type=mesh_id,
        )
        for _, dev, src, slot in links
    ]
    lane = lax.broadcasted_iota(jnp.int32, qw_ref.shape, 1)

    def send_halos():
        for (present, _, _, _), copy in zip(links, copies):
            pl.when(present)(copy.start)

    @pl.when(i == 0)
    def _():
        start_spread(buckets_ref, recv, send_sem, recv_sem, send_halos)
        for (present, _, _, _), copy in zip(links, copies):
            pl.when(present)(copy.wait_send)
        for slot, filled in enumerate(fills):
            pl.when(filled)(copies[slot].wait_recv)

            @pl.when(jnp.logical_not(filled))
            def _():
                halo[slot] = jnp.zeros_like(halo[slot])

        qw_ref[...] = jnp.zeros_like(qw_ref)
        qe_ref[...] = jnp.zeros_like(qe_ref)

    def _():
        horiz = coef_ref[0]
        vert = coef_ref[1]
        row = lax.broadcasted_iota(jnp.int32, (rows, cols), 0)
        col = lax.broadcasted_iota(jnp.int32, (rows, cols), 1)
        hn = halo[0, pl.ds(i * LB, LB)]
        hs = halo[1, pl.ds(i * LB, LB)]
        hw_t = jnp.transpose(halo[2, pl.ds(i * LB, LB)])
        he_t = jnp.transpose(halo[3, pl.ds(i * LB, LB)])
        above = above_ref[0] * jnp.where(i > 0, 1.0, 0.0)
        below = below_ref[0] * jnp.where(i < nblk - 1, 1.0, 0.0)
        qw = qw_ref[...]
        qe = qe_ref[...]
        for l in range(LB):
            u = u_ref[l]
            prev = u_ref[l - 1] if l > 0 else above
            nxt = u_ref[l + 1] if l < LB - 1 else below
            w = wet * u
            north = jnp.where(row == 0, hn[l:l + 1, :], pltpu.roll(w, 1, 0))
            south = jnp.where(row == rows - 1, hs[l:l + 1, :], pltpu.roll(w, rows - 1, 0))
            west = jnp.where(col == 0, hw_t[:, l:l + 1], pltpu.roll(w, 1, 1))
            east = jnp.where(col == cols - 1, he_t[:, l:l + 1], pltpu.roll(w, cols - 1, 1))
            lateral = north + south + west + east - 4.0 * w
            vertical = prev + nxt - 2.0 * u
            res = wet * (u + horiz * lateral + vert * vertical)
            out_ref[l] = res
            fw = wet * res
            en_ref[l:l + 1, :] = fw[0:1, :]
            es_ref[l:l + 1, :] = fw[rows - 1:rows, :]
            hit = lane == i * LB + l
            qw = jnp.where(hit, fw[:, 0:1], qw)
            qe = jnp.where(hit, fw[:, cols - 1:cols], qe)
        qw_ref[...] = qw
        qe_ref[...] = qe

    _()

    @pl.when(i == nblk - 1)
    def _():
        ew_ref[...] = jnp.transpose(qw_ref[...])[0:lev, :]
        ee_ref[...] = jnp.transpose(qe_ref[...])[0:lev, :]
        finish_spread(buckets_ref, recv, send_sem, recv_sem, arrived_ref)


def first_step(coef, wet, u, buckets, edges):
    lev, rows, cols = u.shape
    nblk = lev // LB
    full2 = lambda shape: pl.BlockSpec(shape, lambda i: (0, 0))
    lvl2 = pl.BlockSpec((LB, cols), lambda i: (i, 0))
    whole = pl.BlockSpec(buckets.shape, lambda i: (0, 0, 0, 0))
    in_specs = [
        pl.BlockSpec(memory_space=pltpu.SMEM),
        full2((rows, cols)),
        pl.BlockSpec((LB, rows, cols), lambda i: (i, 0, 0)),
        pl.BlockSpec((1, rows, cols), lambda i: (jnp.maximum(i * LB - 1, 0), 0, 0)),
        pl.BlockSpec((1, rows, cols), lambda i: (jnp.minimum(i * LB + LB, lev - 1), 0, 0)),
        whole,
    ] + [full2((lev, cols))] * 4
    out_shape = [
        jax.ShapeDtypeStruct((lev, rows, cols), jnp.float32),
        jax.ShapeDtypeStruct((lev, cols), jnp.float32),
        jax.ShapeDtypeStruct((lev, cols), jnp.float32),
        jax.ShapeDtypeStruct((lev, rows), jnp.float32),
        jax.ShapeDtypeStruct((lev, rows), jnp.float32),
        jax.ShapeDtypeStruct(buckets.shape, buckets.dtype),
    ]
    out_specs = [
        pl.BlockSpec((LB, rows, cols), lambda i: (i, 0, 0)),
        lvl2, lvl2, full2((lev, rows)), full2((lev, rows)), whole,
    ]
    scratch = [
        pltpu.VMEM((4, lev, cols), jnp.float32),
        pltpu.VMEM((rows, 128), jnp.float32),
        pltpu.VMEM((rows, 128), jnp.float32),
        pltpu.VMEM(buckets.shape, buckets.dtype),
        pltpu.SemaphoreType.DMA((buckets.shape[0],)),
        pltpu.SemaphoreType.DMA((buckets.shape[0],)),
        pltpu.SemaphoreType.DMA((4,)),
        pltpu.SemaphoreType.DMA((4,)),
    ]
    return pl.pallas_call(
        first_kernel,
        grid=(nblk,),
        in_specs=in_specs,
        out_specs=out_specs,
        out_shape=out_shape,
        scratch_shapes=scratch,
        compiler_params=pltpu.CompilerParams(
            dimension_semantics=("arbitrary",), collective_id=2, has_side_effects=True
        ),
        cost_estimate=pl.CostEstimate(flops=30 * u.size, bytes_accessed=12 * u.size, transcendentals=0),
    )(coef, wet, u, u, u, buckets, *edges)


def stencil_kernel(with_edges, with_force, coef_ref, wet_ref, u_ref, above_ref, below_ref,
                   hn_ref, hs_ref, hw_ref, he_ref, *rest):
    if with_force:
        force_ref, rest = rest[0], rest[1:]
    if with_edges:
        buckets_ref, rest = rest[0], rest[1:]
    out_ref = rest[0]
    i = pl.program_id(0)
    nblk = pl.num_programs(0)
    horiz = coef_ref[0]
    vert = coef_ref[1]
    wet = wet_ref[...]
    rows, cols = wet.shape
    row = lax.broadcasted_iota(jnp.int32, (rows, cols), 0)
    col = lax.broadcasted_iota(jnp.int32, (rows, cols), 1)
    hw_t = jnp.transpose(hw_ref[...])
    he_t = jnp.transpose(he_ref[...])
    above = above_ref[0] * jnp.where(i > 0, 1.0, 0.0)
    below = below_ref[0] * jnp.where(i < nblk - 1, 1.0, 0.0)
    if with_edges:
        en_ref, es_ref, ew_ref, ee_ref, arrived_ref, qw_ref, qe_ref, recv, send_sem, recv_sem = rest[1:]

        @pl.when(i == 0)
        def _():
            start_spread(buckets_ref, recv, send_sem, recv_sem)
            qw_ref[...] = jnp.zeros_like(qw_ref)
            qe_ref[...] = jnp.zeros_like(qe_ref)

    if with_edges:
        lane = lax.broadcasted_iota(jnp.int32, qw_ref.shape, 1)
        qw = qw_ref[...]
        qe = qe_ref[...]
    for l in range(LB):
        u = u_ref[l]
        prev = u_ref[l - 1] if l > 0 else above
        nxt = u_ref[l + 1] if l < LB - 1 else below
        w = wet * u
        north = jnp.where(row == 0, hn_ref[l:l + 1, :], pltpu.roll(w, 1, 0))
        south = jnp.where(row == rows - 1, hs_ref[l:l + 1, :], pltpu.roll(w, rows - 1, 0))
        west = jnp.where(col == 0, hw_t[:, l:l + 1], pltpu.roll(w, 1, 1))
        east = jnp.where(col == cols - 1, he_t[:, l:l + 1], pltpu.roll(w, cols - 1, 1))
        lateral = north + south + west + east - 4.0 * w
        vertical = prev + nxt - 2.0 * u
        res = wet * (u + horiz * lateral + vert * vertical)
        if with_force and l == 0:
            res = res + jnp.where(i == 0, 1.0, 0.0) * (force_gain * wet * force_ref[...])
        out_ref[l] = res
        if with_edges:
            fw = wet * res
            en_ref[l:l + 1, :] = fw[0:1, :]
            es_ref[l:l + 1, :] = fw[rows - 1:rows, :]
            hit = lane == i * LB + l
            qw = jnp.where(hit, fw[:, 0:1], qw)
            qe = jnp.where(hit, fw[:, cols - 1:cols], qe)

    if with_edges:
        qw_ref[...] = qw
        qe_ref[...] = qe

        @pl.when(i == nblk - 1)
        def _():
            lev = ew_ref.shape[0]
            ew_ref[...] = jnp.transpose(qw_ref[...])[0:lev, :]
            ee_ref[...] = jnp.transpose(qe_ref[...])[0:lev, :]
            finish_spread(buckets_ref, recv, send_sem, recv_sem, arrived_ref)


def edges_kernel(wet_ref, u_ref, en_ref, es_ref, ew_ref, ee_ref, qw_ref, qe_ref):
    i = pl.program_id(0)
    nblk = pl.num_programs(0)
    wet = wet_ref[...]
    rows, cols = wet.shape

    @pl.when(i == 0)
    def _():
        qw_ref[...] = jnp.zeros_like(qw_ref)
        qe_ref[...] = jnp.zeros_like(qe_ref)

    lane = lax.broadcasted_iota(jnp.int32, qw_ref.shape, 1)
    qw = qw_ref[...]
    qe = qe_ref[...]
    for l in range(LB):
        fw = wet * u_ref[l]
        en_ref[l:l + 1, :] = fw[0:1, :]
        es_ref[l:l + 1, :] = fw[rows - 1:rows, :]
        hit = lane == i * LB + l
        qw = jnp.where(hit, fw[:, 0:1], qw)
        qe = jnp.where(hit, fw[:, cols - 1:cols], qe)
    qw_ref[...] = qw
    qe_ref[...] = qe

    @pl.when(i == nblk - 1)
    def _():
        lev = ew_ref.shape[0]
        ew_ref[...] = jnp.transpose(qw_ref[...])[0:lev, :]
        ee_ref[...] = jnp.transpose(qe_ref[...])[0:lev, :]


def masked_edges(wet, u):
    lev, rows, cols = u.shape
    lvl2 = pl.BlockSpec((LB, cols), lambda i: (i, 0))
    full2 = lambda shape: pl.BlockSpec(shape, lambda i: (0, 0))
    return pl.pallas_call(
        edges_kernel,
        grid=(lev // LB,),
        in_specs=[full2((rows, cols)), pl.BlockSpec((LB, rows, cols), lambda i: (i, 0, 0))],
        out_specs=[lvl2, lvl2, full2((lev, rows)), full2((lev, rows))],
        out_shape=[jax.ShapeDtypeStruct((lev, cols), jnp.float32)] * 2
        + [jax.ShapeDtypeStruct((lev, rows), jnp.float32)] * 2,
        scratch_shapes=[pltpu.VMEM((rows, 128), jnp.float32)] * 2,
        compiler_params=pltpu.CompilerParams(dimension_semantics=("arbitrary",)),
        cost_estimate=pl.CostEstimate(flops=2 * u.size, bytes_accessed=4 * u.size, transcendentals=0),
    )(wet, u)


def force_kernel(x_ref, wet_ref, f_ref, out_ref):
    out_ref[0] = x_ref[0] + force_gain * wet_ref[...] * f_ref[...]


def add_force(x, wet, f):
    lev, rows, cols = x.shape
    plane = pl.BlockSpec((rows, cols), lambda i: (0, 0))
    level0 = pl.BlockSpec((1, rows, cols), lambda i: (0, 0, 0))
    return pl.pallas_call(
        force_kernel,
        grid=(1,),
        in_specs=[level0, plane, plane],
        out_specs=level0,
        out_shape=jax.ShapeDtypeStruct(x.shape, x.dtype),
        input_output_aliases={0: 0},
    )(x, wet, f)


def stencil_step(coef, wet, u, halos, force=None, buckets=None):
    with_edges = buckets is not None
    lev, rows, cols = u.shape
    nblk = lev // LB
    full2 = lambda shape: pl.BlockSpec(shape, lambda i: (0, 0))
    lvl2 = pl.BlockSpec((LB, cols), lambda i: (i, 0))
    in_specs = [
        pl.BlockSpec(memory_space=pltpu.SMEM),
        full2((rows, cols)),
        pl.BlockSpec((LB, rows, cols), lambda i: (i, 0, 0)),
        pl.BlockSpec((1, rows, cols), lambda i: (jnp.maximum(i * LB - 1, 0), 0, 0)),
        pl.BlockSpec((1, rows, cols), lambda i: (jnp.minimum(i * LB + LB, lev - 1), 0, 0)),
        lvl2, lvl2, lvl2, lvl2,
    ]
    args = [coef, wet, u, u, u] + list(halos)
    if force is not None:
        in_specs.append(full2((rows, cols)))
        args.append(force)
    if with_edges:
        in_specs.append(pl.BlockSpec(buckets.shape, lambda i: (0, 0, 0, 0)))
        args.append(buckets)
    out_shape = [jax.ShapeDtypeStruct((lev, rows, cols), jnp.float32)]
    out_specs = [pl.BlockSpec((LB, rows, cols), lambda i: (i, 0, 0))]
    scratch = []
    params = dict(dimension_semantics=("arbitrary",))
    if with_edges:
        out_shape += [jax.ShapeDtypeStruct((lev, cols), jnp.float32)] * 2
        out_shape += [jax.ShapeDtypeStruct((lev, rows), jnp.float32)] * 2
        out_shape += [jax.ShapeDtypeStruct(buckets.shape, buckets.dtype)]
        out_specs += [lvl2, lvl2, full2((lev, rows)), full2((lev, rows))]
        out_specs += [pl.BlockSpec(buckets.shape, lambda i: (0, 0, 0, 0))]
        scratch = [pltpu.VMEM((rows, 128), jnp.float32)] * 2 + [
            pltpu.VMEM(buckets.shape, buckets.dtype),
            pltpu.SemaphoreType.DMA((buckets.shape[0],)),
            pltpu.SemaphoreType.DMA((buckets.shape[0],)),
        ]
        params.update(collective_id=2, has_side_effects=True)
    return pl.pallas_call(
        functools.partial(stencil_kernel, with_edges, force is not None),
        grid=(nblk,),
        in_specs=in_specs,
        out_specs=out_specs,
        out_shape=out_shape,
        scratch_shapes=scratch,
        compiler_params=pltpu.CompilerParams(**params),
        cost_estimate=pl.CostEstimate(flops=30 * u.size, bytes_accessed=12 * u.size, transcendentals=0),
    )(*args)


def halo_kernel(en_ref, es_ref, ew_ref, ee_ref, hn_ref, hs_ref, hw_ref, he_ref,
                buf, send_sem, recv_sem):
    mp = lax.axis_index("mp")
    gx = lax.axis_index("gx")
    gy = lax.axis_index("gy")
    ngx = lax.axis_size("gx")
    ngy = lax.axis_size("gy")
    mesh_id = pl.DeviceIdType.MESH
    links = [
        (gx < ngx - 1, (mp, gx + 1, gy), es_ref, 0),
        (gx > 0, (mp, gx - 1, gy), en_ref, 1),
        (gy < ngy - 1, (mp, gx, gy + 1), ee_ref, 2),
        (gy > 0, (mp, gx, gy - 1), ew_ref, 3),
    ]
    barrier = pltpu.get_barrier_semaphore()
    count = jnp.int32(0)
    for present, dev, _, _ in links:
        @pl.when(present)
        def _():
            pl.semaphore_signal(barrier, 1, device_id=dev, device_id_type=mesh_id)

        count = count + present.astype(jnp.int32)
    pl.semaphore_wait(barrier, count)

    copies = []
    for present, dev, src, slot in links:
        copy = pltpu.make_async_remote_copy(
            src_ref=src,
            dst_ref=buf.at[slot],
            send_sem=send_sem.at[slot],
            recv_sem=recv_sem.at[slot],
            device_id=dev,
            device_id_type=mesh_id,
        )
        pl.when(present)(copy.start)
        copies.append((present, copy))
    for present, copy in copies:
        pl.when(present)(copy.wait_send)
    fills = [gx > 0, gx < ngx - 1, gy > 0, gy < ngy - 1]
    outs = [hn_ref, hs_ref, hw_ref, he_ref]
    for slot, (filled, out) in enumerate(zip(fills, outs)):
        _, copy = copies[slot]

        @pl.when(filled)
        def _():
            copy.wait_recv()
            out[...] = buf[slot]

        @pl.when(jnp.logical_not(filled))
        def _():
            out[...] = jnp.zeros_like(out)


def exchange(en, es, ew, ee, call):
    shape = jax.ShapeDtypeStruct(en.shape, en.dtype)
    vmem = pl.BlockSpec(memory_space=pltpu.VMEM)
    return pl.pallas_call(
        halo_kernel,
        in_specs=[vmem] * 4,
        out_specs=[vmem] * 4,
        out_shape=[shape] * 4,
        scratch_shapes=[
            pltpu.VMEM((4,) + en.shape, en.dtype),
            pltpu.SemaphoreType.DMA((4,)),
            pltpu.SemaphoreType.DMA((4,)),
        ],
        compiler_params=pltpu.CompilerParams(collective_id=call, has_side_effects=True),
    )(en, es, ew, ee)


def bucket_kernel(inv_ref, lab_ref, contrib_ref, out_ref):
    ndest = out_ref.shape[0]
    ntiles = contrib_ref.shape[0]
    sub = lax.broadcasted_iota(jnp.int32, (KF, CY), 0)

    def body(d, carry):
        labv = jnp.zeros((KF, CY), jnp.float32)
        for c in range(CAP):
            t = inv_ref[d * CAP + c]
            val = contrib_ref[jnp.minimum(t, ntiles - 1)]
            out_ref[d, c] = jnp.where(t < ntiles, val, 0.0)
            labv = jnp.where(sub == c, lab_ref[d * CAP + c].astype(jnp.float32), labv)
        out_ref[d, CAP] = labv
        return carry

    lax.fori_loop(0, ndest, body, 0)


def local(states, surface, land_mask, tile_weights, tile_source, tile_target, tile_row):
    group = lax.axis_index("mp")
    ndev = lax.axis_size("gx") * lax.axis_size("gy")
    state = states[0]
    lev, rows_here, cols_here = state.shape
    wet = jnp.where(
        group == 0, jnp.ones(land_mask.shape, jnp.float32), land_mask.astype(jnp.float32)
    )
    coef = jnp.stack([jnp.where(group == 0, 0.15, 0.12), jnp.where(group == 0, 0.1, 0.15)]).astype(
        jnp.float32
    )

    src = (surface[0] * wet).astype(jnp.bfloat16)
    source = tile_source[0, 0, 0]
    target = tile_target[0, 0, 0, :, 0]
    dest_row = tile_row[0, 0, 0]
    ntiles = source.shape[0]
    picked = jnp.take(src, source, axis=1)
    contrib = jnp.einsum(
        "tji,kti->tkj", tile_weights[0, 0, 0], picked, preferred_element_type=jnp.float32
    )
    onehot = (target[:, None] == jnp.arange(ndev, dtype=jnp.int32)[None, :]).astype(jnp.int32)
    earlier = jnp.cumsum(onehot, axis=0) - onehot
    rank = jnp.sum(earlier * onehot, axis=1)
    slot = target * CAP + rank
    inv = jnp.full((ndev * CAP,), ntiles, jnp.int32).at[slot].set(jnp.arange(ntiles, dtype=jnp.int32))
    labels = jnp.zeros((ndev * CAP,), jnp.int32).at[slot].set(dest_row)
    buckets = pl.pallas_call(
        bucket_kernel,
        in_specs=[
            pl.BlockSpec(memory_space=pltpu.SMEM),
            pl.BlockSpec(memory_space=pltpu.SMEM),
            pl.BlockSpec(memory_space=pltpu.VMEM),
        ],
        out_specs=pl.BlockSpec(memory_space=pltpu.VMEM),
        out_shape=jax.ShapeDtypeStruct((ndev, CAP + 1, KF, CY), jnp.float32),
    )(inv, labels, contrib)
    second, arrived = interval(coef, wet, state, buckets, masked_edges(wet, state))
    got_rows = arrived[:, CAP, :, 0].astype(jnp.int32)
    select = (
        got_rows[:, :, None] == jnp.arange(rows_here, dtype=jnp.int32)[None, None, :]
    ).astype(jnp.float32)
    sent = jnp.einsum(
        "scr,sckj->krj", select, arrived[:, :CAP], precision=lax.Precision.HIGHEST
    )
    received = lax.ppermute(sent, "mp", [(0, 1), (1, 0)])

    second = add_force(second, wet, received[0])
    return (second[None], received[None])


def solution(mesh):
    return jax.shard_map(
        local,
        mesh=mesh,
        in_specs=(
            P("mp", None, "gx", "gy"),
            P("mp", None, "gx", "gy"),
            P("gx", "gy"),
            P("mp", "gx", "gy", None, None, None),
            P("mp", "gx", "gy", None),
            P("mp", "gx", "gy", None, None),
            P("mp", "gx", "gy", None),
        ),
        out_specs=(P("mp", None, "gx", "gy"), P("mp", None, "gx", "gy")),
        check_vma=False,
    )
```

```python
import functools

import jax
import jax.numpy as jnp
from jax import lax
from jax.experimental import pallas as pl
from jax.experimental.pallas import tpu as pltpu
from jax.sharding import PartitionSpec as P

CY = 128
KF = 8
CAP = 8
LB = 8

force_gain = 0.5


def shift_pairs(devices, forward):
    up = [(i, i + 1) for i in range(devices - 1)]
    return up if forward else [(j, i) for i, j in up]


def start_spread(buckets_ref, recv, send_sem, recv_sem, first_out=None):
    mp = lax.axis_index("mp")
    ngy = lax.axis_size("gy")
    ndev = lax.axis_size("gx") * ngy
    me = lax.axis_index("gx") * ngy + lax.axis_index("gy")
    mesh_id = pl.DeviceIdType.MESH
    barrier = pltpu.get_barrier_semaphore()

    def greet(d, carry):
        @pl.when(d != me)
        def _():
            pl.semaphore_signal(barrier, 1, device_id=(mp, d // ngy, d % ngy), device_id_type=mesh_id)

        return carry

    lax.fori_loop(0, ndev, greet, 0)
    pl.semaphore_wait(barrier, ndev - 1)
    if first_out is not None:
        first_out()
    recv[me] = buckets_ref[me]

    def send(k, carry):
        d = (me + k) % ndev
        pltpu.make_async_remote_copy(
            src_ref=buckets_ref.at[d],
            dst_ref=recv.at[me],
            send_sem=send_sem.at[d],
            recv_sem=recv_sem.at[me],
            device_id=(mp, d // ngy, d % ngy),
            device_id_type=mesh_id,
        ).start()
        return carry

    lax.fori_loop(1, ndev, send, 0)


def finish_spread(buckets_ref, recv, send_sem, recv_sem, arrived_ref):
    ngy = lax.axis_size("gy")
    ndev = lax.axis_size("gx") * ngy
    me = lax.axis_index("gx") * ngy + lax.axis_index("gy")

    def wait(d, carry):
        @pl.when(d != me)
        def _():
            copy = pltpu.make_async_remote_copy(
                src_ref=buckets_ref.at[d],
                dst_ref=recv.at[d],
                send_sem=send_sem.at[d],
                recv_sem=recv_sem.at[d],
                device_id=(lax.axis_index("mp"), d // ngy, d % ngy),
                device_id_type=pl.DeviceIdType.MESH,
            )
            copy.wait_send()
            copy.wait_recv()

        return carry

    lax.fori_loop(0, ndev, wait, 0)
    arrived_ref[...] = recv[...]


def interval_kernel(coef_ref, wet_ref, u_ref, above_ref, below_ref, buckets_ref,
                    e0n, e0s, e0w, e0e,
                    out_ref, arrived_ref,
                    first, edge1, halo0, halo1, qw_ref, qe_ref, recv,
                    send_sem, recv_sem, hsend, hrecv):
    p = pl.program_id(0)
    i = pl.program_id(1)
    nblk = pl.num_programs(1)
    wet = wet_ref[...]
    rows, cols = wet.shape
    lev = first.shape[0]
    mp = lax.axis_index("mp")
    gx = lax.axis_index("gx")
    gy = lax.axis_index("gy")
    ngx = lax.axis_size("gx")
    ngy = lax.axis_size("gy")
    ndev = ngx * ngy
    me = gx * ngy + gy
    mesh_id = pl.DeviceIdType.MESH
    links = [
        (gx < ngx - 1, (mp, gx + 1, gy), 1, 0),
        (gx > 0, (mp, gx - 1, gy), 0, 1),
        (gy < ngy - 1, (mp, gx, gy + 1), 3, 2),
        (gy > 0, (mp, gx, gy - 1), 2, 3),
    ]
    fills = [gx > 0, gx < ngx - 1, gy > 0, gy < ngy - 1]
    edge0 = [e0n, e0s, e0w, e0e]

    def halo_copy(stage, src, slot, dev):
        srcs = edge0[src] if stage == 0 else edge1.at[src]
        dsts = halo0.at[slot] if stage == 0 else halo1.at[slot]
        return pltpu.make_async_remote_copy(
            src_ref=srcs,
            dst_ref=dsts,
            send_sem=hsend.at[stage, slot],
            recv_sem=hrecv.at[stage, slot],
            device_id=dev,
            device_id_type=mesh_id,
        )

    def send_halos(stage):
        for present, dev, src, slot in links:
            pl.when(present)(halo_copy(stage, src, slot, dev).start)

    def take_halos(stage, dst):
        for present, dev, src, slot in links:
            pl.when(present)(halo_copy(stage, src, slot, dev).wait_send)
        for slot, filled in enumerate(fills):
            _, dev, src, _ = links[slot]
            pl.when(filled)(halo_copy(stage, src, slot, dev).wait_recv)

            @pl.when(jnp.logical_not(filled))
            def _():
                dst[slot] = jnp.zeros_like(dst[slot])

    def bucket_copy(d):
        return pltpu.make_async_remote_copy(
            src_ref=buckets_ref.at[d],
            dst_ref=recv.at[me],
            send_sem=send_sem.at[d],
            recv_sem=recv_sem.at[me],
            device_id=(mp, d // ngy, d % ngy),
            device_id_type=mesh_id,
        )

    def issue(k0, count):
        for n in range(count):
            k = k0 + n

            @pl.when(k < ndev)
            def _():
                bucket_copy((me + k) % ndev).start()

    lane = lax.broadcasted_iota(jnp.int32, qw_ref.shape, 1)
    row = lax.broadcasted_iota(jnp.int32, (rows, cols), 0)
    col = lax.broadcasted_iota(jnp.int32, (rows, cols), 1)
    horiz = coef_ref[0]
    vert = coef_ref[1]

    def step(load, above, below, hn, hs, hw_t, he_t, store):
        for l in range(LB):
            u = load(l)
            prev = load(l - 1) if l > 0 else above
            nxt = load(l + 1) if l < LB - 1 else below
            w = wet * u
            north = jnp.where(row == 0, hn[l:l + 1, :], pltpu.roll(w, 1, 0))
            south = jnp.where(row == rows - 1, hs[l:l + 1, :], pltpu.roll(w, rows - 1, 0))
            west = jnp.where(col == 0, hw_t[:, l:l + 1], pltpu.roll(w, 1, 1))
            east = jnp.where(col == cols - 1, he_t[:, l:l + 1], pltpu.roll(w, cols - 1, 1))
            lateral = north + south + west + east - 4.0 * w
            vertical = prev + nxt - 2.0 * u
            store(l, wet * (u + horiz * lateral + vert * vertical))

    @pl.when((p == 0) & (i == 0))
    def _():
        barrier = pltpu.get_barrier_semaphore()

        def greet(d, carry):
            @pl.when(d != me)
            def _():
                pl.semaphore_signal(barrier, 1, device_id=(mp, d // ngy, d % ngy), device_id_type=mesh_id)

            return carry

        lax.fori_loop(0, ndev, greet, 0)
        pl.semaphore_wait(barrier, ndev - 1)
        send_halos(0)
        recv[me] = buckets_ref[me]
        take_halos(0, halo0)
        qw_ref[...] = jnp.zeros_like(qw_ref)
        qe_ref[...] = jnp.zeros_like(qe_ref)

    @pl.when(p == 0)
    def _():
        issue(1 + 3 * i, 3)
        blk = pl.ds(pl.multiple_of(i * LB, LB), LB)
        hn = halo0[0, blk]
        hs = halo0[1, blk]
        hw_t = jnp.transpose(halo0[2, blk])
        he_t = jnp.transpose(halo0[3, blk])
        above = above_ref[0] * jnp.where(i > 0, 1.0, 0.0)
        below = below_ref[0] * jnp.where(i < nblk - 1, 1.0, 0.0)
        qs = [qw_ref[...], qe_ref[...]]

        def store(l, res):
            first[i * LB + l] = res
            fw = wet * res
            edge1[0, i, l:l + 1, :] = fw[0:1, :]
            edge1[1, i, l:l + 1, :] = fw[rows - 1:rows, :]
            hit = lane == i * LB + l
            qs[0] = jnp.where(hit, fw[:, 0:1], qs[0])
            qs[1] = jnp.where(hit, fw[:, cols - 1:cols], qs[1])

        step(lambda l: u_ref[l], above, below, hn, hs, hw_t, he_t, store)
        qw_ref[...] = qs[0]
        qe_ref[...] = qs[1]

    @pl.when((p == 0) & (i == nblk - 1))
    def _():
        edge1[2] = jnp.transpose(qw_ref[...])[0:lev, :].reshape(nblk, LB, rows)
        edge1[3] = jnp.transpose(qe_ref[...])[0:lev, :].reshape(nblk, LB, rows)
        send_halos(1)

    @pl.when((p == 1) & (i == 0))
    def _():
        take_halos(1, halo1)

        def late(k, carry):
            bucket_copy((me + k) % ndev).start()
            return carry

        lax.fori_loop(min(1 + 3 * nblk, ndev), ndev, late, 0)

    @pl.when(p == 1)
    def _():
        base = i * LB
        above = first[jnp.maximum(base - 1, 0)] * jnp.where(i > 0, 1.0, 0.0)
        below = first[jnp.minimum(base + LB, lev - 1)] * jnp.where(i < nblk - 1, 1.0, 0.0)
        hw_t = jnp.transpose(halo1[2, i])
        he_t = jnp.transpose(halo1[3, i])

        def store(l, res):
            out_ref[l] = res

        step(lambda l: first[base + l], above, below, halo1[0, i], halo1[1, i], hw_t, he_t, store)

    @pl.when((p == 1) & (i == nblk - 1))
    def _():
        def wait(d, carry):
            @pl.when(d != me)
            def _():
                copy = pltpu.make_async_remote_copy(
                    src_ref=buckets_ref.at[d],
                    dst_ref=recv.at[d],
                    send_sem=send_sem.at[d],
                    recv_sem=recv_sem.at[d],
                    device_id=(mp, d // ngy, d % ngy),
                    device_id_type=mesh_id,
                )
                copy.wait_send()
                copy.wait_recv()

            return carry

        lax.fori_loop(0, ndev, wait, 0)
        arrived_ref[...] = recv[...]


def interval(coef, wet, u, buckets, edges):
    lev, rows, cols = u.shape
    nblk = lev // LB
    full2 = lambda shape: pl.BlockSpec(shape, lambda p, i: (0, 0))
    whole = pl.BlockSpec(buckets.shape, lambda p, i: (0, 0, 0, 0))
    held = lambda p, i: i + p * (nblk - 1 - i)
    in_specs = [
        pl.BlockSpec(memory_space=pltpu.SMEM),
        full2((rows, cols)),
        pl.BlockSpec((LB, rows, cols), lambda p, i: (held(p, i), 0, 0)),
        pl.BlockSpec((1, rows, cols), lambda p, i: (jnp.maximum(held(p, i) * LB - 1, 0), 0, 0)),
        pl.BlockSpec((1, rows, cols), lambda p, i: (jnp.minimum(held(p, i) * LB + LB, lev - 1), 0, 0)),
        whole,
    ] + [full2((lev, cols))] * 4
    out_shape = [
        jax.ShapeDtypeStruct((lev, rows, cols), jnp.float32),
        jax.ShapeDtypeStruct(buckets.shape, buckets.dtype),
    ]
    out_specs = [pl.BlockSpec((LB, rows, cols), lambda p, i: (i * p, 0, 0)), whole]
    scratch = [
        pltpu.VMEM((lev, rows, cols), jnp.float32),
        pltpu.VMEM((4, nblk, LB, cols), jnp.float32),
        pltpu.VMEM((4, lev, cols), jnp.float32),
        pltpu.VMEM((4, nblk, LB, cols), jnp.float32),
        pltpu.VMEM((rows, 128), jnp.float32),
        pltpu.VMEM((rows, 128), jnp.float32),
        pltpu.VMEM(buckets.shape, buckets.dtype),
        pltpu.SemaphoreType.DMA((buckets.shape[0],)),
        pltpu.SemaphoreType.DMA((buckets.shape[0],)),
        pltpu.SemaphoreType.DMA((2, 4)),
        pltpu.SemaphoreType.DMA((2, 4)),
    ]
    return pl.pallas_call(
        interval_kernel,
        grid=(2, nblk),
        in_specs=in_specs,
        out_specs=out_specs,
        out_shape=out_shape,
        scratch_shapes=scratch,
        compiler_params=pltpu.CompilerParams(
            dimension_semantics=("arbitrary", "arbitrary"), collective_id=3, has_side_effects=True,
            vmem_limit_bytes=48 * 1024 * 1024,
        ),
        cost_estimate=pl.CostEstimate(flops=60 * u.size, bytes_accessed=12 * u.size, transcendentals=0),
    )(coef, wet, u, u, u, buckets, *edges)


def first_kernel(coef_ref, wet_ref, u_ref, above_ref, below_ref, buckets_ref,
                 e0n, e0s, e0w, e0e,
                 out_ref, en_ref, es_ref, ew_ref, ee_ref, arrived_ref,
                 halo, qw_ref, qe_ref, recv, send_sem, recv_sem, hsend, hrecv):
    i = pl.program_id(0)
    nblk = pl.num_programs(0)
    edge0 = [e0n, e0s, e0w, e0e]
    wet = wet_ref[...]
    rows, cols = wet.shape
    lev = ew_ref.shape[0]
    mp = lax.axis_index("mp")
    gx = lax.axis_index("gx")
    gy = lax.axis_index("gy")
    ngx = lax.axis_size("gx")
    ngy = lax.axis_size("gy")
    mesh_id = pl.DeviceIdType.MESH
    links = [
        (gx < ngx - 1, (mp, gx + 1, gy), 1, 0),
        (gx > 0, (mp, gx - 1, gy), 0, 1),
        (gy < ngy - 1, (mp, gx, gy + 1), 3, 2),
        (gy > 0, (mp, gx, gy - 1), 2, 3),
    ]
    fills = [gx > 0, gx < ngx - 1, gy > 0, gy < ngy - 1]
    copies = [
        pltpu.make_async_remote_copy(
            src_ref=edge0[src],
            dst_ref=halo.at[slot],
            send_sem=hsend.at[slot],
            recv_sem=hrecv.at[slot],
            device_id=dev,
            device_id_type=mesh_id,
        )
        for _, dev, src, slot in links
    ]
    lane = lax.broadcasted_iota(jnp.int32, qw_ref.shape, 1)

    def send_halos():
        for (present, _, _, _), copy in zip(links, copies):
            pl.when(present)(copy.start)

    @pl.when(i == 0)
    def _():
        start_spread(buckets_ref, recv, send_sem, recv_sem, send_halos)
        for (present, _, _, _), copy in zip(links, copies):
            pl.when(present)(copy.wait_send)
        for slot, filled in enumerate(fills):
            pl.when(filled)(copies[slot].wait_recv)

            @pl.when(jnp.logical_not(filled))
            def _():
                halo[slot] = jnp.zeros_like(halo[slot])

        qw_ref[...] = jnp.zeros_like(qw_ref)
        qe_ref[...] = jnp.zeros_like(qe_ref)

    def _():
        horiz = coef_ref[0]
        vert = coef_ref[1]
        row = lax.broadcasted_iota(jnp.int32, (rows, cols), 0)
        col = lax.broadcasted_iota(jnp.int32, (rows, cols), 1)
        hn = halo[0, pl.ds(i * LB, LB)]
        hs = halo[1, pl.ds(i * LB, LB)]
        hw_t = jnp.transpose(halo[2, pl.ds(i * LB, LB)])
        he_t = jnp.transpose(halo[3, pl.ds(i * LB, LB)])
        above = above_ref[0] * jnp.where(i > 0, 1.0, 0.0)
        below = below_ref[0] * jnp.where(i < nblk - 1, 1.0, 0.0)
        qw = qw_ref[...]
        qe = qe_ref[...]
        for l in range(LB):
            u = u_ref[l]
            prev = u_ref[l - 1] if l > 0 else above
            nxt = u_ref[l + 1] if l < LB - 1 else below
            w = wet * u
            north = jnp.where(row == 0, hn[l:l + 1, :], pltpu.roll(w, 1, 0))
            south = jnp.where(row == rows - 1, hs[l:l + 1, :], pltpu.roll(w, rows - 1, 0))
            west = jnp.where(col == 0, hw_t[:, l:l + 1], pltpu.roll(w, 1, 1))
            east = jnp.where(col == cols - 1, he_t[:, l:l + 1], pltpu.roll(w, cols - 1, 1))
            lateral = north + south + west + east - 4.0 * w
            vertical = prev + nxt - 2.0 * u
            res = wet * (u + horiz * lateral + vert * vertical)
            out_ref[l] = res
            fw = wet * res
            en_ref[l:l + 1, :] = fw[0:1, :]
            es_ref[l:l + 1, :] = fw[rows - 1:rows, :]
            hit = lane == i * LB + l
            qw = jnp.where(hit, fw[:, 0:1], qw)
            qe = jnp.where(hit, fw[:, cols - 1:cols], qe)
        qw_ref[...] = qw
        qe_ref[...] = qe

    _()

    @pl.when(i == nblk - 1)
    def _():
        ew_ref[...] = jnp.transpose(qw_ref[...])[0:lev, :]
        ee_ref[...] = jnp.transpose(qe_ref[...])[0:lev, :]
        finish_spread(buckets_ref, recv, send_sem, recv_sem, arrived_ref)


def first_step(coef, wet, u, buckets, edges):
    lev, rows, cols = u.shape
    nblk = lev // LB
    full2 = lambda shape: pl.BlockSpec(shape, lambda i: (0, 0))
    lvl2 = pl.BlockSpec((LB, cols), lambda i: (i, 0))
    whole = pl.BlockSpec(buckets.shape, lambda i: (0, 0, 0, 0))
    in_specs = [
        pl.BlockSpec(memory_space=pltpu.SMEM),
        full2((rows, cols)),
        pl.BlockSpec((LB, rows, cols), lambda i: (i, 0, 0)),
        pl.BlockSpec((1, rows, cols), lambda i: (jnp.maximum(i * LB - 1, 0), 0, 0)),
        pl.BlockSpec((1, rows, cols), lambda i: (jnp.minimum(i * LB + LB, lev - 1), 0, 0)),
        whole,
    ] + [full2((lev, cols))] * 4
    out_shape = [
        jax.ShapeDtypeStruct((lev, rows, cols), jnp.float32),
        jax.ShapeDtypeStruct((lev, cols), jnp.float32),
        jax.ShapeDtypeStruct((lev, cols), jnp.float32),
        jax.ShapeDtypeStruct((lev, rows), jnp.float32),
        jax.ShapeDtypeStruct((lev, rows), jnp.float32),
        jax.ShapeDtypeStruct(buckets.shape, buckets.dtype),
    ]
    out_specs = [
        pl.BlockSpec((LB, rows, cols), lambda i: (i, 0, 0)),
        lvl2, lvl2, full2((lev, rows)), full2((lev, rows)), whole,
    ]
    scratch = [
        pltpu.VMEM((4, lev, cols), jnp.float32),
        pltpu.VMEM((rows, 128), jnp.float32),
        pltpu.VMEM((rows, 128), jnp.float32),
        pltpu.VMEM(buckets.shape, buckets.dtype),
        pltpu.SemaphoreType.DMA((buckets.shape[0],)),
        pltpu.SemaphoreType.DMA((buckets.shape[0],)),
        pltpu.SemaphoreType.DMA((4,)),
        pltpu.SemaphoreType.DMA((4,)),
    ]
    return pl.pallas_call(
        first_kernel,
        grid=(nblk,),
        in_specs=in_specs,
        out_specs=out_specs,
        out_shape=out_shape,
        scratch_shapes=scratch,
        compiler_params=pltpu.CompilerParams(
            dimension_semantics=("arbitrary",), collective_id=2, has_side_effects=True
        ),
        cost_estimate=pl.CostEstimate(flops=30 * u.size, bytes_accessed=12 * u.size, transcendentals=0),
    )(coef, wet, u, u, u, buckets, *edges)


def stencil_kernel(with_edges, with_force, coef_ref, wet_ref, u_ref, above_ref, below_ref,
                   hn_ref, hs_ref, hw_ref, he_ref, *rest):
    if with_force:
        force_ref, rest = rest[0], rest[1:]
    if with_edges:
        buckets_ref, rest = rest[0], rest[1:]
    out_ref = rest[0]
    i = pl.program_id(0)
    nblk = pl.num_programs(0)
    horiz = coef_ref[0]
    vert = coef_ref[1]
    wet = wet_ref[...]
    rows, cols = wet.shape
    row = lax.broadcasted_iota(jnp.int32, (rows, cols), 0)
    col = lax.broadcasted_iota(jnp.int32, (rows, cols), 1)
    hw_t = jnp.transpose(hw_ref[...])
    he_t = jnp.transpose(he_ref[...])
    above = above_ref[0] * jnp.where(i > 0, 1.0, 0.0)
    below = below_ref[0] * jnp.where(i < nblk - 1, 1.0, 0.0)
    if with_edges:
        en_ref, es_ref, ew_ref, ee_ref, arrived_ref, qw_ref, qe_ref, recv, send_sem, recv_sem = rest[1:]

        @pl.when(i == 0)
        def _():
            start_spread(buckets_ref, recv, send_sem, recv_sem)
            qw_ref[...] = jnp.zeros_like(qw_ref)
            qe_ref[...] = jnp.zeros_like(qe_ref)

    if with_edges:
        lane = lax.broadcasted_iota(jnp.int32, qw_ref.shape, 1)
        qw = qw_ref[...]
        qe = qe_ref[...]
    for l in range(LB):
        u = u_ref[l]
        prev = u_ref[l - 1] if l > 0 else above
        nxt = u_ref[l + 1] if l < LB - 1 else below
        w = wet * u
        north = jnp.where(row == 0, hn_ref[l:l + 1, :], pltpu.roll(w, 1, 0))
        south = jnp.where(row == rows - 1, hs_ref[l:l + 1, :], pltpu.roll(w, rows - 1, 0))
        west = jnp.where(col == 0, hw_t[:, l:l + 1], pltpu.roll(w, 1, 1))
        east = jnp.where(col == cols - 1, he_t[:, l:l + 1], pltpu.roll(w, cols - 1, 1))
        lateral = north + south + west + east - 4.0 * w
        vertical = prev + nxt - 2.0 * u
        res = wet * (u + horiz * lateral + vert * vertical)
        if with_force and l == 0:
            res = res + jnp.where(i == 0, 1.0, 0.0) * (force_gain * wet * force_ref[...])
        out_ref[l] = res
        if with_edges:
            fw = wet * res
            en_ref[l:l + 1, :] = fw[0:1, :]
            es_ref[l:l + 1, :] = fw[rows - 1:rows, :]
            hit = lane == i * LB + l
            qw = jnp.where(hit, fw[:, 0:1], qw)
            qe = jnp.where(hit, fw[:, cols - 1:cols], qe)

    if with_edges:
        qw_ref[...] = qw
        qe_ref[...] = qe

        @pl.when(i == nblk - 1)
        def _():
            lev = ew_ref.shape[0]
            ew_ref[...] = jnp.transpose(qw_ref[...])[0:lev, :]
            ee_ref[...] = jnp.transpose(qe_ref[...])[0:lev, :]
            finish_spread(buckets_ref, recv, send_sem, recv_sem, arrived_ref)


def edges_kernel(wet_ref, u_ref, en_ref, es_ref, ew_ref, ee_ref, qw_ref, qe_ref):
    i = pl.program_id(0)
    nblk = pl.num_programs(0)
    wet = wet_ref[...]
    rows, cols = wet.shape

    @pl.when(i == 0)
    def _():
        qw_ref[...] = jnp.zeros_like(qw_ref)
        qe_ref[...] = jnp.zeros_like(qe_ref)

    lane = lax.broadcasted_iota(jnp.int32, qw_ref.shape, 1)
    qw = qw_ref[...]
    qe = qe_ref[...]
    for l in range(LB):
        fw = wet * u_ref[l]
        en_ref[l:l + 1, :] = fw[0:1, :]
        es_ref[l:l + 1, :] = fw[rows - 1:rows, :]
        hit = lane == i * LB + l
        qw = jnp.where(hit, fw[:, 0:1], qw)
        qe = jnp.where(hit, fw[:, cols - 1:cols], qe)
    qw_ref[...] = qw
    qe_ref[...] = qe

    @pl.when(i == nblk - 1)
    def _():
        lev = ew_ref.shape[0]
        ew_ref[...] = jnp.transpose(qw_ref[...])[0:lev, :]
        ee_ref[...] = jnp.transpose(qe_ref[...])[0:lev, :]


def masked_edges(wet, u):
    lev, rows, cols = u.shape
    lvl2 = pl.BlockSpec((LB, cols), lambda i: (i, 0))
    full2 = lambda shape: pl.BlockSpec(shape, lambda i: (0, 0))
    return pl.pallas_call(
        edges_kernel,
        grid=(lev // LB,),
        in_specs=[full2((rows, cols)), pl.BlockSpec((LB, rows, cols), lambda i: (i, 0, 0))],
        out_specs=[lvl2, lvl2, full2((lev, rows)), full2((lev, rows))],
        out_shape=[jax.ShapeDtypeStruct((lev, cols), jnp.float32)] * 2
        + [jax.ShapeDtypeStruct((lev, rows), jnp.float32)] * 2,
        scratch_shapes=[pltpu.VMEM((rows, 128), jnp.float32)] * 2,
        compiler_params=pltpu.CompilerParams(dimension_semantics=("arbitrary",)),
        cost_estimate=pl.CostEstimate(flops=2 * u.size, bytes_accessed=4 * u.size, transcendentals=0),
    )(wet, u)


def force_kernel(x_ref, wet_ref, f_ref, out_ref):
    out_ref[...] = x_ref[...]

    @pl.when(pl.program_id(0) == 0)
    def _():
        out_ref[0] = x_ref[0] + force_gain * wet_ref[...] * f_ref[...]


def add_force(x, wet, f):
    lev, rows, cols = x.shape
    plane = pl.BlockSpec((rows, cols), lambda i: (0, 0))
    blocks = pl.BlockSpec((LB, rows, cols), lambda i: (i, 0, 0))
    return pl.pallas_call(
        force_kernel,
        grid=(lev // LB,),
        in_specs=[blocks, plane, plane],
        out_specs=blocks,
        out_shape=jax.ShapeDtypeStruct(x.shape, x.dtype),
        cost_estimate=pl.CostEstimate(flops=x.size, bytes_accessed=8 * x.size, transcendentals=0),
    )(x, wet, f)


def stencil_step(coef, wet, u, halos, force=None, buckets=None):
    with_edges = buckets is not None
    lev, rows, cols = u.shape
    nblk = lev // LB
    full2 = lambda shape: pl.BlockSpec(shape, lambda i: (0, 0))
    lvl2 = pl.BlockSpec((LB, cols), lambda i: (i, 0))
    in_specs = [
        pl.BlockSpec(memory_space=pltpu.SMEM),
        full2((rows, cols)),
        pl.BlockSpec((LB, rows, cols), lambda i: (i, 0, 0)),
        pl.BlockSpec((1, rows, cols), lambda i: (jnp.maximum(i * LB - 1, 0), 0, 0)),
        pl.BlockSpec((1, rows, cols), lambda i: (jnp.minimum(i * LB + LB, lev - 1), 0, 0)),
        lvl2, lvl2, lvl2, lvl2,
    ]
    args = [coef, wet, u, u, u] + list(halos)
    if force is not None:
        in_specs.append(full2((rows, cols)))
        args.append(force)
    if with_edges:
        in_specs.append(pl.BlockSpec(buckets.shape, lambda i: (0, 0, 0, 0)))
        args.append(buckets)
    out_shape = [jax.ShapeDtypeStruct((lev, rows, cols), jnp.float32)]
    out_specs = [pl.BlockSpec((LB, rows, cols), lambda i: (i, 0, 0))]
    scratch = []
    params = dict(dimension_semantics=("arbitrary",))
    if with_edges:
        out_shape += [jax.ShapeDtypeStruct((lev, cols), jnp.float32)] * 2
        out_shape += [jax.ShapeDtypeStruct((lev, rows), jnp.float32)] * 2
        out_shape += [jax.ShapeDtypeStruct(buckets.shape, buckets.dtype)]
        out_specs += [lvl2, lvl2, full2((lev, rows)), full2((lev, rows))]
        out_specs += [pl.BlockSpec(buckets.shape, lambda i: (0, 0, 0, 0))]
        scratch = [pltpu.VMEM((rows, 128), jnp.float32)] * 2 + [
            pltpu.VMEM(buckets.shape, buckets.dtype),
            pltpu.SemaphoreType.DMA((buckets.shape[0],)),
            pltpu.SemaphoreType.DMA((buckets.shape[0],)),
        ]
        params.update(collective_id=2, has_side_effects=True)
    return pl.pallas_call(
        functools.partial(stencil_kernel, with_edges, force is not None),
        grid=(nblk,),
        in_specs=in_specs,
        out_specs=out_specs,
        out_shape=out_shape,
        scratch_shapes=scratch,
        compiler_params=pltpu.CompilerParams(**params),
        cost_estimate=pl.CostEstimate(flops=30 * u.size, bytes_accessed=12 * u.size, transcendentals=0),
    )(*args)


def halo_kernel(en_ref, es_ref, ew_ref, ee_ref, hn_ref, hs_ref, hw_ref, he_ref,
                buf, send_sem, recv_sem):
    mp = lax.axis_index("mp")
    gx = lax.axis_index("gx")
    gy = lax.axis_index("gy")
    ngx = lax.axis_size("gx")
    ngy = lax.axis_size("gy")
    mesh_id = pl.DeviceIdType.MESH
    links = [
        (gx < ngx - 1, (mp, gx + 1, gy), es_ref, 0),
        (gx > 0, (mp, gx - 1, gy), en_ref, 1),
        (gy < ngy - 1, (mp, gx, gy + 1), ee_ref, 2),
        (gy > 0, (mp, gx, gy - 1), ew_ref, 3),
    ]
    barrier = pltpu.get_barrier_semaphore()
    count = jnp.int32(0)
    for present, dev, _, _ in links:
        @pl.when(present)
        def _():
            pl.semaphore_signal(barrier, 1, device_id=dev, device_id_type=mesh_id)

        count = count + present.astype(jnp.int32)
    pl.semaphore_wait(barrier, count)

    copies = []
    for present, dev, src, slot in links:
        copy = pltpu.make_async_remote_copy(
            src_ref=src,
            dst_ref=buf.at[slot],
            send_sem=send_sem.at[slot],
            recv_sem=recv_sem.at[slot],
            device_id=dev,
            device_id_type=mesh_id,
        )
        pl.when(present)(copy.start)
        copies.append((present, copy))
    for present, copy in copies:
        pl.when(present)(copy.wait_send)
    fills = [gx > 0, gx < ngx - 1, gy > 0, gy < ngy - 1]
    outs = [hn_ref, hs_ref, hw_ref, he_ref]
    for slot, (filled, out) in enumerate(zip(fills, outs)):
        _, copy = copies[slot]

        @pl.when(filled)
        def _():
            copy.wait_recv()
            out[...] = buf[slot]

        @pl.when(jnp.logical_not(filled))
        def _():
            out[...] = jnp.zeros_like(out)


def exchange(en, es, ew, ee, call):
    shape = jax.ShapeDtypeStruct(en.shape, en.dtype)
    vmem = pl.BlockSpec(memory_space=pltpu.VMEM)
    return pl.pallas_call(
        halo_kernel,
        in_specs=[vmem] * 4,
        out_specs=[vmem] * 4,
        out_shape=[shape] * 4,
        scratch_shapes=[
            pltpu.VMEM((4,) + en.shape, en.dtype),
            pltpu.SemaphoreType.DMA((4,)),
            pltpu.SemaphoreType.DMA((4,)),
        ],
        compiler_params=pltpu.CompilerParams(collective_id=call, has_side_effects=True),
    )(en, es, ew, ee)


def bucket_kernel(inv_ref, lab_ref, contrib_ref, out_ref):
    ndest = out_ref.shape[0]
    ntiles = contrib_ref.shape[0]
    sub = lax.broadcasted_iota(jnp.int32, (KF, CY), 0)

    def body(d, carry):
        labv = jnp.zeros((KF, CY), jnp.float32)
        for c in range(CAP):
            t = inv_ref[d * CAP + c]
            val = contrib_ref[jnp.minimum(t, ntiles - 1)]
            out_ref[d, c] = jnp.where(t < ntiles, val, 0.0)
            labv = jnp.where(sub == c, lab_ref[d * CAP + c].astype(jnp.float32), labv)
        out_ref[d, CAP] = labv
        return carry

    lax.fori_loop(0, ndest, body, 0)


def local(states, surface, land_mask, tile_weights, tile_source, tile_target, tile_row):
    group = lax.axis_index("mp")
    ndev = lax.axis_size("gx") * lax.axis_size("gy")
    state = states[0]
    lev, rows_here, cols_here = state.shape
    wet = jnp.where(
        group == 0, jnp.ones(land_mask.shape, jnp.float32), land_mask.astype(jnp.float32)
    )
    coef = jnp.stack([jnp.where(group == 0, 0.15, 0.12), jnp.where(group == 0, 0.1, 0.15)]).astype(
        jnp.float32
    )

    src = (surface[0] * wet).astype(jnp.bfloat16)
    source = tile_source[0, 0, 0]
    target = tile_target[0, 0, 0, :, 0]
    dest_row = tile_row[0, 0, 0]
    ntiles = source.shape[0]
    picked = jnp.take(src, source, axis=1)
    contrib = jnp.einsum(
        "tji,kti->tkj", tile_weights[0, 0, 0], picked, preferred_element_type=jnp.float32
    )
    onehot = (target[:, None] == jnp.arange(ndev, dtype=jnp.int32)[None, :]).astype(jnp.int32)
    earlier = jnp.cumsum(onehot, axis=0) - onehot
    rank = jnp.sum(earlier * onehot, axis=1)
    slot = target * CAP + rank
    inv = jnp.full((ndev * CAP,), ntiles, jnp.int32).at[slot].set(jnp.arange(ntiles, dtype=jnp.int32))
    labels = jnp.zeros((ndev * CAP,), jnp.int32).at[slot].set(dest_row)
    buckets = pl.pallas_call(
        bucket_kernel,
        in_specs=[
            pl.BlockSpec(memory_space=pltpu.SMEM),
            pl.BlockSpec(memory_space=pltpu.SMEM),
            pl.BlockSpec(memory_space=pltpu.VMEM),
        ],
        out_specs=pl.BlockSpec(memory_space=pltpu.VMEM),
        out_shape=jax.ShapeDtypeStruct((ndev, CAP + 1, KF, CY), jnp.float32),
    )(inv, labels, contrib)
    second, arrived = interval(coef, wet, state, buckets, masked_edges(wet, state))
    got_rows = arrived[:, CAP, :, 0].astype(jnp.int32)
    select = (
        got_rows[:, :, None] == jnp.arange(rows_here, dtype=jnp.int32)[None, None, :]
    ).astype(jnp.float32)
    sent = jnp.einsum(
        "scr,sckj->krj", select, arrived[:, :CAP], precision=lax.Precision.HIGHEST
    )
    received = lax.ppermute(sent, "mp", [(0, 1), (1, 0)])

    second = add_force(second, wet, received[0])
    return (second[None], received[None])


def solution(mesh):
    return jax.shard_map(
        local,
        mesh=mesh,
        in_specs=(
            P("mp", None, "gx", "gy"),
            P("mp", None, "gx", "gy"),
            P("gx", "gy"),
            P("mp", "gx", "gy", None, None, None),
            P("mp", "gx", "gy", None),
            P("mp", "gx", "gy", None, None),
            P("mp", "gx", "gy", None),
        ),
        out_specs=(P("mp", None, "gx", "gy"), P("mp", None, "gx", "gy")),
        check_vma=False,
    )
```

```python
import functools

import jax
import jax.numpy as jnp
from jax import lax
from jax.experimental import pallas as pl
from jax.experimental.pallas import tpu as pltpu
from jax.sharding import PartitionSpec as P

CY = 128
KF = 8
CAP = 8
LB = 8

force_gain = 0.5


def shift_pairs(devices, forward):
    up = [(i, i + 1) for i in range(devices - 1)]
    return up if forward else [(j, i) for i, j in up]


def start_spread(buckets_ref, recv, send_sem, recv_sem, first_out=None):
    mp = lax.axis_index("mp")
    ngy = lax.axis_size("gy")
    ndev = lax.axis_size("gx") * ngy
    me = lax.axis_index("gx") * ngy + lax.axis_index("gy")
    mesh_id = pl.DeviceIdType.MESH
    barrier = pltpu.get_barrier_semaphore()

    def greet(d, carry):
        @pl.when(d != me)
        def _():
            pl.semaphore_signal(barrier, 1, device_id=(mp, d // ngy, d % ngy), device_id_type=mesh_id)

        return carry

    lax.fori_loop(0, ndev, greet, 0)
    pl.semaphore_wait(barrier, ndev - 1)
    if first_out is not None:
        first_out()
    recv[me] = buckets_ref[me]

    def send(k, carry):
        d = (me + k) % ndev
        pltpu.make_async_remote_copy(
            src_ref=buckets_ref.at[d],
            dst_ref=recv.at[me],
            send_sem=send_sem.at[d],
            recv_sem=recv_sem.at[me],
            device_id=(mp, d // ngy, d % ngy),
            device_id_type=mesh_id,
        ).start()
        return carry

    lax.fori_loop(1, ndev, send, 0)


def finish_spread(buckets_ref, recv, send_sem, recv_sem, arrived_ref):
    ngy = lax.axis_size("gy")
    ndev = lax.axis_size("gx") * ngy
    me = lax.axis_index("gx") * ngy + lax.axis_index("gy")

    def wait(d, carry):
        @pl.when(d != me)
        def _():
            copy = pltpu.make_async_remote_copy(
                src_ref=buckets_ref.at[d],
                dst_ref=recv.at[d],
                send_sem=send_sem.at[d],
                recv_sem=recv_sem.at[d],
                device_id=(lax.axis_index("mp"), d // ngy, d % ngy),
                device_id_type=pl.DeviceIdType.MESH,
            )
            copy.wait_send()
            copy.wait_recv()

        return carry

    lax.fori_loop(0, ndev, wait, 0)
    arrived_ref[...] = recv[...]


def interval_kernel(coef_ref, wet_ref, u_ref, above_ref, below_ref, buckets_ref,
                    e0n, e0s, e0w, e0e,
                    out_ref, arrived_ref,
                    first, edge1, halo0, halo1, qw_ref, qe_ref, recv,
                    send_sem, recv_sem, hsend, hrecv):
    p = pl.program_id(0)
    i = pl.program_id(1)
    nblk = pl.num_programs(1)
    wet = wet_ref[...]
    rows, cols = wet.shape
    lev = first.shape[0]
    mp = lax.axis_index("mp")
    gx = lax.axis_index("gx")
    gy = lax.axis_index("gy")
    ngx = lax.axis_size("gx")
    ngy = lax.axis_size("gy")
    ndev = ngx * ngy
    me = gx * ngy + gy
    mesh_id = pl.DeviceIdType.MESH
    links = [
        (gx < ngx - 1, (mp, gx + 1, gy), 1, 0),
        (gx > 0, (mp, gx - 1, gy), 0, 1),
        (gy < ngy - 1, (mp, gx, gy + 1), 3, 2),
        (gy > 0, (mp, gx, gy - 1), 2, 3),
    ]
    fills = [gx > 0, gx < ngx - 1, gy > 0, gy < ngy - 1]
    edge0 = [e0n, e0s, e0w, e0e]

    def halo_copy(stage, src, slot, dev):
        srcs = edge0[src] if stage == 0 else edge1.at[src]
        dsts = halo0.at[slot] if stage == 0 else halo1.at[slot]
        return pltpu.make_async_remote_copy(
            src_ref=srcs,
            dst_ref=dsts,
            send_sem=hsend.at[stage, slot],
            recv_sem=hrecv.at[stage, slot],
            device_id=dev,
            device_id_type=mesh_id,
        )

    def send_halos(stage):
        for present, dev, src, slot in links:
            pl.when(present)(halo_copy(stage, src, slot, dev).start)

    def take_halos(stage, dst):
        for present, dev, src, slot in links:
            pl.when(present)(halo_copy(stage, src, slot, dev).wait_send)
        for slot, filled in enumerate(fills):
            _, dev, src, _ = links[slot]
            pl.when(filled)(halo_copy(stage, src, slot, dev).wait_recv)

            @pl.when(jnp.logical_not(filled))
            def _():
                dst[slot] = jnp.zeros_like(dst[slot])

    def bucket_copy(d):
        return pltpu.make_async_remote_copy(
            src_ref=buckets_ref.at[d],
            dst_ref=recv.at[me],
            send_sem=send_sem.at[d],
            recv_sem=recv_sem.at[me],
            device_id=(mp, d // ngy, d % ngy),
            device_id_type=mesh_id,
        )

    def issue(k0, count):
        for n in range(count):
            k = k0 + n

            @pl.when(k < ndev)
            def _():
                bucket_copy((me + k) % ndev).start()

    lane = lax.broadcasted_iota(jnp.int32, qw_ref.shape, 1)
    row = lax.broadcasted_iota(jnp.int32, (rows, cols), 0)
    col = lax.broadcasted_iota(jnp.int32, (rows, cols), 1)
    horiz = coef_ref[0]
    vert = coef_ref[1]

    def step(load, above, below, hn, hs, hw_t, he_t, store):
        for l in range(LB):
            u = load(l)
            prev = load(l - 1) if l > 0 else above
            nxt = load(l + 1) if l < LB - 1 else below
            w = wet * u
            north = jnp.where(row == 0, hn[l:l + 1, :], pltpu.roll(w, 1, 0))
            south = jnp.where(row == rows - 1, hs[l:l + 1, :], pltpu.roll(w, rows - 1, 0))
            west = jnp.where(col == 0, hw_t[:, l:l + 1], pltpu.roll(w, 1, 1))
            east = jnp.where(col == cols - 1, he_t[:, l:l + 1], pltpu.roll(w, cols - 1, 1))
            lateral = north + south + west + east - 4.0 * w
            vertical = prev + nxt - 2.0 * u
            store(l, wet * (u + horiz * lateral + vert * vertical))

    @pl.when((p == 0) & (i == 0))
    def _():
        barrier = pltpu.get_barrier_semaphore()

        def greet(d, carry):
            @pl.when(d != me)
            def _():
                pl.semaphore_signal(barrier, 1, device_id=(mp, d // ngy, d % ngy), device_id_type=mesh_id)

            return carry

        lax.fori_loop(0, ndev, greet, 0)
        pl.semaphore_wait(barrier, ndev - 1)
        send_halos(0)
        recv[me] = buckets_ref[me]
        take_halos(0, halo0)
        qw_ref[...] = jnp.zeros_like(qw_ref)
        qe_ref[...] = jnp.zeros_like(qe_ref)

    @pl.when(p == 0)
    def _():
        issue(1 + 3 * i, 3)
        blk = pl.ds(pl.multiple_of(i * LB, LB), LB)
        hn = halo0[0, blk]
        hs = halo0[1, blk]
        hw_t = jnp.transpose(halo0[2, blk])
        he_t = jnp.transpose(halo0[3, blk])
        above = above_ref[0] * jnp.where(i > 0, 1.0, 0.0)
        below = below_ref[0] * jnp.where(i < nblk - 1, 1.0, 0.0)
        qs = [qw_ref[...], qe_ref[...]]

        def store(l, res):
            first[i * LB + l] = res
            fw = wet * res
            edge1[0, i, l:l + 1, :] = fw[0:1, :]
            edge1[1, i, l:l + 1, :] = fw[rows - 1:rows, :]
            hit = lane == i * LB + l
            qs[0] = jnp.where(hit, fw[:, 0:1], qs[0])
            qs[1] = jnp.where(hit, fw[:, cols - 1:cols], qs[1])

        step(lambda l: u_ref[l], above, below, hn, hs, hw_t, he_t, store)
        qw_ref[...] = qs[0]
        qe_ref[...] = qs[1]

    @pl.when((p == 0) & (i == nblk - 1))
    def _():
        edge1[2] = jnp.transpose(qw_ref[...])[0:lev, :].reshape(nblk, LB, rows)
        edge1[3] = jnp.transpose(qe_ref[...])[0:lev, :].reshape(nblk, LB, rows)
        send_halos(1)

    @pl.when((p == 1) & (i == 0))
    def _():
        take_halos(1, halo1)

        def late(k, carry):
            bucket_copy((me + k) % ndev).start()
            return carry

        lax.fori_loop(min(1 + 3 * nblk, ndev), ndev, late, 0)

    @pl.when(p == 1)
    def _():
        base = i * LB
        above = first[jnp.maximum(base - 1, 0)] * jnp.where(i > 0, 1.0, 0.0)
        below = first[jnp.minimum(base + LB, lev - 1)] * jnp.where(i < nblk - 1, 1.0, 0.0)
        hw_t = jnp.transpose(halo1[2, i])
        he_t = jnp.transpose(halo1[3, i])

        def store(l, res):
            out_ref[l] = res

        step(lambda l: first[base + l], above, below, halo1[0, i], halo1[1, i], hw_t, he_t, store)

    @pl.when((p == 1) & (i == nblk - 1))
    def _():
        def wait(d, carry):
            @pl.when(d != me)
            def _():
                copy = pltpu.make_async_remote_copy(
                    src_ref=buckets_ref.at[d],
                    dst_ref=recv.at[d],
                    send_sem=send_sem.at[d],
                    recv_sem=recv_sem.at[d],
                    device_id=(mp, d // ngy, d % ngy),
                    device_id_type=mesh_id,
                )
                copy.wait_send()
                copy.wait_recv()

            return carry

        lax.fori_loop(0, ndev, wait, 0)
        arrived_ref[...] = recv[...]


def interval(coef, wet, u, buckets, edges):
    lev, rows, cols = u.shape
    nblk = lev // LB
    full2 = lambda shape: pl.BlockSpec(shape, lambda p, i: (0, 0))
    whole = pl.BlockSpec(buckets.shape, lambda p, i: (0, 0, 0, 0))
    held = lambda p, i: i + p * (nblk - 1 - i)
    in_specs = [
        pl.BlockSpec(memory_space=pltpu.SMEM),
        full2((rows, cols)),
        pl.BlockSpec((LB, rows, cols), lambda p, i: (held(p, i), 0, 0)),
        pl.BlockSpec((1, rows, cols), lambda p, i: (jnp.maximum(held(p, i) * LB - 1, 0), 0, 0)),
        pl.BlockSpec((1, rows, cols), lambda p, i: (jnp.minimum(held(p, i) * LB + LB, lev - 1), 0, 0)),
        whole,
    ] + [full2((lev, cols))] * 4
    out_shape = [
        jax.ShapeDtypeStruct((lev, rows, cols), jnp.float32),
        jax.ShapeDtypeStruct(buckets.shape, buckets.dtype),
    ]
    out_specs = [pl.BlockSpec((LB, rows, cols), lambda p, i: (i * p, 0, 0)), whole]
    scratch = [
        pltpu.VMEM((lev, rows, cols), jnp.float32),
        pltpu.VMEM((4, nblk, LB, cols), jnp.float32),
        pltpu.VMEM((4, lev, cols), jnp.float32),
        pltpu.VMEM((4, nblk, LB, cols), jnp.float32),
        pltpu.VMEM((rows, 128), jnp.float32),
        pltpu.VMEM((rows, 128), jnp.float32),
        pltpu.VMEM(buckets.shape, buckets.dtype),
        pltpu.SemaphoreType.DMA((buckets.shape[0],)),
        pltpu.SemaphoreType.DMA((buckets.shape[0],)),
        pltpu.SemaphoreType.DMA((2, 4)),
        pltpu.SemaphoreType.DMA((2, 4)),
    ]
    return pl.pallas_call(
        interval_kernel,
        grid=(2, nblk),
        in_specs=in_specs,
        out_specs=out_specs,
        out_shape=out_shape,
        scratch_shapes=scratch,
        compiler_params=pltpu.CompilerParams(
            dimension_semantics=("arbitrary", "arbitrary"), collective_id=3, has_side_effects=True,
            vmem_limit_bytes=48 * 1024 * 1024,
        ),
        cost_estimate=pl.CostEstimate(flops=60 * u.size, bytes_accessed=12 * u.size, transcendentals=0),
    )(coef, wet, u, u, u, buckets, *edges)


def first_kernel(coef_ref, wet_ref, u_ref, above_ref, below_ref, buckets_ref,
                 e0n, e0s, e0w, e0e,
                 out_ref, en_ref, es_ref, ew_ref, ee_ref, arrived_ref,
                 halo, qw_ref, qe_ref, recv, send_sem, recv_sem, hsend, hrecv):
    i = pl.program_id(0)
    nblk = pl.num_programs(0)
    edge0 = [e0n, e0s, e0w, e0e]
    wet = wet_ref[...]
    rows, cols = wet.shape
    lev = ew_ref.shape[0]
    mp = lax.axis_index("mp")
    gx = lax.axis_index("gx")
    gy = lax.axis_index("gy")
    ngx = lax.axis_size("gx")
    ngy = lax.axis_size("gy")
    mesh_id = pl.DeviceIdType.MESH
    links = [
        (gx < ngx - 1, (mp, gx + 1, gy), 1, 0),
        (gx > 0, (mp, gx - 1, gy), 0, 1),
        (gy < ngy - 1, (mp, gx, gy + 1), 3, 2),
        (gy > 0, (mp, gx, gy - 1), 2, 3),
    ]
    fills = [gx > 0, gx < ngx - 1, gy > 0, gy < ngy - 1]
    copies = [
        pltpu.make_async_remote_copy(
            src_ref=edge0[src],
            dst_ref=halo.at[slot],
            send_sem=hsend.at[slot],
            recv_sem=hrecv.at[slot],
            device_id=dev,
            device_id_type=mesh_id,
        )
        for _, dev, src, slot in links
    ]
    lane = lax.broadcasted_iota(jnp.int32, qw_ref.shape, 1)

    def send_halos():
        for (present, _, _, _), copy in zip(links, copies):
            pl.when(present)(copy.start)

    @pl.when(i == 0)
    def _():
        start_spread(buckets_ref, recv, send_sem, recv_sem, send_halos)
        for (present, _, _, _), copy in zip(links, copies):
            pl.when(present)(copy.wait_send)
        for slot, filled in enumerate(fills):
            pl.when(filled)(copies[slot].wait_recv)

            @pl.when(jnp.logical_not(filled))
            def _():
                halo[slot] = jnp.zeros_like(halo[slot])

        qw_ref[...] = jnp.zeros_like(qw_ref)
        qe_ref[...] = jnp.zeros_like(qe_ref)

    def _():
        horiz = coef_ref[0]
        vert = coef_ref[1]
        row = lax.broadcasted_iota(jnp.int32, (rows, cols), 0)
        col = lax.broadcasted_iota(jnp.int32, (rows, cols), 1)
        hn = halo[0, pl.ds(i * LB, LB)]
        hs = halo[1, pl.ds(i * LB, LB)]
        hw_t = jnp.transpose(halo[2, pl.ds(i * LB, LB)])
        he_t = jnp.transpose(halo[3, pl.ds(i * LB, LB)])
        above = above_ref[0] * jnp.where(i > 0, 1.0, 0.0)
        below = below_ref[0] * jnp.where(i < nblk - 1, 1.0, 0.0)
        qw = qw_ref[...]
        qe = qe_ref[...]
        for l in range(LB):
            u = u_ref[l]
            prev = u_ref[l - 1] if l > 0 else above
            nxt = u_ref[l + 1] if l < LB - 1 else below
            w = wet * u
            north = jnp.where(row == 0, hn[l:l + 1, :], pltpu.roll(w, 1, 0))
            south = jnp.where(row == rows - 1, hs[l:l + 1, :], pltpu.roll(w, rows - 1, 0))
            west = jnp.where(col == 0, hw_t[:, l:l + 1], pltpu.roll(w, 1, 1))
            east = jnp.where(col == cols - 1, he_t[:, l:l + 1], pltpu.roll(w, cols - 1, 1))
            lateral = north + south + west + east - 4.0 * w
            vertical = prev + nxt - 2.0 * u
            res = wet * (u + horiz * lateral + vert * vertical)
            out_ref[l] = res
            fw = wet * res
            en_ref[l:l + 1, :] = fw[0:1, :]
            es_ref[l:l + 1, :] = fw[rows - 1:rows, :]
            hit = lane == i * LB + l
            qw = jnp.where(hit, fw[:, 0:1], qw)
            qe = jnp.where(hit, fw[:, cols - 1:cols], qe)
        qw_ref[...] = qw
        qe_ref[...] = qe

    _()

    @pl.when(i == nblk - 1)
    def _():
        ew_ref[...] = jnp.transpose(qw_ref[...])[0:lev, :]
        ee_ref[...] = jnp.transpose(qe_ref[...])[0:lev, :]
        finish_spread(buckets_ref, recv, send_sem, recv_sem, arrived_ref)


def first_step(coef, wet, u, buckets, edges):
    lev, rows, cols = u.shape
    nblk = lev // LB
    full2 = lambda shape: pl.BlockSpec(shape, lambda i: (0, 0))
    lvl2 = pl.BlockSpec((LB, cols), lambda i: (i, 0))
    whole = pl.BlockSpec(buckets.shape, lambda i: (0, 0, 0, 0))
    in_specs = [
        pl.BlockSpec(memory_space=pltpu.SMEM),
        full2((rows, cols)),
        pl.BlockSpec((LB, rows, cols), lambda i: (i, 0, 0)),
        pl.BlockSpec((1, rows, cols), lambda i: (jnp.maximum(i * LB - 1, 0), 0, 0)),
        pl.BlockSpec((1, rows, cols), lambda i: (jnp.minimum(i * LB + LB, lev - 1), 0, 0)),
        whole,
    ] + [full2((lev, cols))] * 4
    out_shape = [
        jax.ShapeDtypeStruct((lev, rows, cols), jnp.float32),
        jax.ShapeDtypeStruct((lev, cols), jnp.float32),
        jax.ShapeDtypeStruct((lev, cols), jnp.float32),
        jax.ShapeDtypeStruct((lev, rows), jnp.float32),
        jax.ShapeDtypeStruct((lev, rows), jnp.float32),
        jax.ShapeDtypeStruct(buckets.shape, buckets.dtype),
    ]
    out_specs = [
        pl.BlockSpec((LB, rows, cols), lambda i: (i, 0, 0)),
        lvl2, lvl2, full2((lev, rows)), full2((lev, rows)), whole,
    ]
    scratch = [
        pltpu.VMEM((4, lev, cols), jnp.float32),
        pltpu.VMEM((rows, 128), jnp.float32),
        pltpu.VMEM((rows, 128), jnp.float32),
        pltpu.VMEM(buckets.shape, buckets.dtype),
        pltpu.SemaphoreType.DMA((buckets.shape[0],)),
        pltpu.SemaphoreType.DMA((buckets.shape[0],)),
        pltpu.SemaphoreType.DMA((4,)),
        pltpu.SemaphoreType.DMA((4,)),
    ]
    return pl.pallas_call(
        first_kernel,
        grid=(nblk,),
        in_specs=in_specs,
        out_specs=out_specs,
        out_shape=out_shape,
        scratch_shapes=scratch,
        compiler_params=pltpu.CompilerParams(
            dimension_semantics=("arbitrary",), collective_id=2, has_side_effects=True
        ),
        cost_estimate=pl.CostEstimate(flops=30 * u.size, bytes_accessed=12 * u.size, transcendentals=0),
    )(coef, wet, u, u, u, buckets, *edges)


def stencil_kernel(with_edges, with_force, coef_ref, wet_ref, u_ref, above_ref, below_ref,
                   hn_ref, hs_ref, hw_ref, he_ref, *rest):
    if with_force:
        force_ref, rest = rest[0], rest[1:]
    if with_edges:
        buckets_ref, rest = rest[0], rest[1:]
    out_ref = rest[0]
    i = pl.program_id(0)
    nblk = pl.num_programs(0)
    horiz = coef_ref[0]
    vert = coef_ref[1]
    wet = wet_ref[...]
    rows, cols = wet.shape
    row = lax.broadcasted_iota(jnp.int32, (rows, cols), 0)
    col = lax.broadcasted_iota(jnp.int32, (rows, cols), 1)
    hw_t = jnp.transpose(hw_ref[...])
    he_t = jnp.transpose(he_ref[...])
    above = above_ref[0] * jnp.where(i > 0, 1.0, 0.0)
    below = below_ref[0] * jnp.where(i < nblk - 1, 1.0, 0.0)
    if with_edges:
        en_ref, es_ref, ew_ref, ee_ref, arrived_ref, qw_ref, qe_ref, recv, send_sem, recv_sem = rest[1:]

        @pl.when(i == 0)
        def _():
            start_spread(buckets_ref, recv, send_sem, recv_sem)
            qw_ref[...] = jnp.zeros_like(qw_ref)
            qe_ref[...] = jnp.zeros_like(qe_ref)

    if with_edges:
        lane = lax.broadcasted_iota(jnp.int32, qw_ref.shape, 1)
        qw = qw_ref[...]
        qe = qe_ref[...]
    for l in range(LB):
        u = u_ref[l]
        prev = u_ref[l - 1] if l > 0 else above
        nxt = u_ref[l + 1] if l < LB - 1 else below
        w = wet * u
        north = jnp.where(row == 0, hn_ref[l:l + 1, :], pltpu.roll(w, 1, 0))
        south = jnp.where(row == rows - 1, hs_ref[l:l + 1, :], pltpu.roll(w, rows - 1, 0))
        west = jnp.where(col == 0, hw_t[:, l:l + 1], pltpu.roll(w, 1, 1))
        east = jnp.where(col == cols - 1, he_t[:, l:l + 1], pltpu.roll(w, cols - 1, 1))
        lateral = north + south + west + east - 4.0 * w
        vertical = prev + nxt - 2.0 * u
        res = wet * (u + horiz * lateral + vert * vertical)
        if with_force and l == 0:
            res = res + jnp.where(i == 0, 1.0, 0.0) * (force_gain * wet * force_ref[...])
        out_ref[l] = res
        if with_edges:
            fw = wet * res
            en_ref[l:l + 1, :] = fw[0:1, :]
            es_ref[l:l + 1, :] = fw[rows - 1:rows, :]
            hit = lane == i * LB + l
            qw = jnp.where(hit, fw[:, 0:1], qw)
            qe = jnp.where(hit, fw[:, cols - 1:cols], qe)

    if with_edges:
        qw_ref[...] = qw
        qe_ref[...] = qe

        @pl.when(i == nblk - 1)
        def _():
            lev = ew_ref.shape[0]
            ew_ref[...] = jnp.transpose(qw_ref[...])[0:lev, :]
            ee_ref[...] = jnp.transpose(qe_ref[...])[0:lev, :]
            finish_spread(buckets_ref, recv, send_sem, recv_sem, arrived_ref)


def edges_kernel(wet_ref, u_ref, en_ref, es_ref, ew_ref, ee_ref):
    wet = wet_ref[...]
    rows, cols = wet.shape
    fw = wet[None] * u_ref[...]
    for l in range(LB):
        en_ref[l:l + 1, :] = fw[l, 0:1, :]
        es_ref[l:l + 1, :] = fw[l, rows - 1:rows, :]
    pick_r = lax.broadcasted_iota(jnp.int32, (8, cols), 0)
    pick_c = lax.broadcasted_iota(jnp.int32, (8, cols), 1)
    pick = jnp.where(
        ((pick_r == 0) & (pick_c == 0)) | ((pick_r == 1) & (pick_c == cols - 1)), 1.0, 0.0
    ).astype(jnp.float32)
    picked = lax.dot_general(
        pick,
        fw.reshape(LB * rows, cols),
        (((1,), (1,)), ((), ())),
        precision=lax.Precision.HIGHEST,
        preferred_element_type=jnp.float32,
    )
    for l in range(LB):
        ew_ref[l:l + 1, :] = picked[0:1, l * rows:(l + 1) * rows]
        ee_ref[l:l + 1, :] = picked[1:2, l * rows:(l + 1) * rows]


def masked_edges(wet, u):
    lev, rows, cols = u.shape
    lvl2 = pl.BlockSpec((LB, cols), lambda i: (i, 0))
    full2 = lambda shape: pl.BlockSpec(shape, lambda i: (0, 0))
    return pl.pallas_call(
        edges_kernel,
        grid=(lev // LB,),
        in_specs=[full2((rows, cols)), pl.BlockSpec((LB, rows, cols), lambda i: (i, 0, 0))],
        out_specs=[lvl2] * 4,
        out_shape=[jax.ShapeDtypeStruct((lev, cols), jnp.float32)] * 2
        + [jax.ShapeDtypeStruct((lev, rows), jnp.float32)] * 2,
        compiler_params=pltpu.CompilerParams(dimension_semantics=("arbitrary",)),
        cost_estimate=pl.CostEstimate(flops=2 * u.size, bytes_accessed=4 * u.size, transcendentals=0),
    )(wet, u)


def force_kernel(x_ref, wet_ref, f_ref, out_ref):
    out_ref[0] = x_ref[0] + force_gain * wet_ref[...] * f_ref[...]


def add_force(x, wet, f):
    lev, rows, cols = x.shape
    plane = pl.BlockSpec((rows, cols), lambda i: (0, 0))
    level0 = pl.BlockSpec((1, rows, cols), lambda i: (0, 0, 0))
    return pl.pallas_call(
        force_kernel,
        grid=(1,),
        in_specs=[level0, plane, plane],
        out_specs=level0,
        out_shape=jax.ShapeDtypeStruct(x.shape, x.dtype),
        input_output_aliases={0: 0},
    )(x, wet, f)


def stencil_step(coef, wet, u, halos, force=None, buckets=None):
    with_edges = buckets is not None
    lev, rows, cols = u.shape
    nblk = lev // LB
    full2 = lambda shape: pl.BlockSpec(shape, lambda i: (0, 0))
    lvl2 = pl.BlockSpec((LB, cols), lambda i: (i, 0))
    in_specs = [
        pl.BlockSpec(memory_space=pltpu.SMEM),
        full2((rows, cols)),
        pl.BlockSpec((LB, rows, cols), lambda i: (i, 0, 0)),
        pl.BlockSpec((1, rows, cols), lambda i: (jnp.maximum(i * LB - 1, 0), 0, 0)),
        pl.BlockSpec((1, rows, cols), lambda i: (jnp.minimum(i * LB + LB, lev - 1), 0, 0)),
        lvl2, lvl2, lvl2, lvl2,
    ]
    args = [coef, wet, u, u, u] + list(halos)
    if force is not None:
        in_specs.append(full2((rows, cols)))
        args.append(force)
    if with_edges:
        in_specs.append(pl.BlockSpec(buckets.shape, lambda i: (0, 0, 0, 0)))
        args.append(buckets)
    out_shape = [jax.ShapeDtypeStruct((lev, rows, cols), jnp.float32)]
    out_specs = [pl.BlockSpec((LB, rows, cols), lambda i: (i, 0, 0))]
    scratch = []
    params = dict(dimension_semantics=("arbitrary",))
    if with_edges:
        out_shape += [jax.ShapeDtypeStruct((lev, cols), jnp.float32)] * 2
        out_shape += [jax.ShapeDtypeStruct((lev, rows), jnp.float32)] * 2
        out_shape += [jax.ShapeDtypeStruct(buckets.shape, buckets.dtype)]
        out_specs += [lvl2, lvl2, full2((lev, rows)), full2((lev, rows))]
        out_specs += [pl.BlockSpec(buckets.shape, lambda i: (0, 0, 0, 0))]
        scratch = [pltpu.VMEM((rows, 128), jnp.float32)] * 2 + [
            pltpu.VMEM(buckets.shape, buckets.dtype),
            pltpu.SemaphoreType.DMA((buckets.shape[0],)),
            pltpu.SemaphoreType.DMA((buckets.shape[0],)),
        ]
        params.update(collective_id=2, has_side_effects=True)
    return pl.pallas_call(
        functools.partial(stencil_kernel, with_edges, force is not None),
        grid=(nblk,),
        in_specs=in_specs,
        out_specs=out_specs,
        out_shape=out_shape,
        scratch_shapes=scratch,
        compiler_params=pltpu.CompilerParams(**params),
        cost_estimate=pl.CostEstimate(flops=30 * u.size, bytes_accessed=12 * u.size, transcendentals=0),
    )(*args)


def halo_kernel(en_ref, es_ref, ew_ref, ee_ref, hn_ref, hs_ref, hw_ref, he_ref,
                buf, send_sem, recv_sem):
    mp = lax.axis_index("mp")
    gx = lax.axis_index("gx")
    gy = lax.axis_index("gy")
    ngx = lax.axis_size("gx")
    ngy = lax.axis_size("gy")
    mesh_id = pl.DeviceIdType.MESH
    links = [
        (gx < ngx - 1, (mp, gx + 1, gy), es_ref, 0),
        (gx > 0, (mp, gx - 1, gy), en_ref, 1),
        (gy < ngy - 1, (mp, gx, gy + 1), ee_ref, 2),
        (gy > 0, (mp, gx, gy - 1), ew_ref, 3),
    ]
    barrier = pltpu.get_barrier_semaphore()
    count = jnp.int32(0)
    for present, dev, _, _ in links:
        @pl.when(present)
        def _():
            pl.semaphore_signal(barrier, 1, device_id=dev, device_id_type=mesh_id)

        count = count + present.astype(jnp.int32)
    pl.semaphore_wait(barrier, count)

    copies = []
    for present, dev, src, slot in links:
        copy = pltpu.make_async_remote_copy(
            src_ref=src,
            dst_ref=buf.at[slot],
            send_sem=send_sem.at[slot],
            recv_sem=recv_sem.at[slot],
            device_id=dev,
            device_id_type=mesh_id,
        )
        pl.when(present)(copy.start)
        copies.append((present, copy))
    for present, copy in copies:
        pl.when(present)(copy.wait_send)
    fills = [gx > 0, gx < ngx - 1, gy > 0, gy < ngy - 1]
    outs = [hn_ref, hs_ref, hw_ref, he_ref]
    for slot, (filled, out) in enumerate(zip(fills, outs)):
        _, copy = copies[slot]

        @pl.when(filled)
        def _():
            copy.wait_recv()
            out[...] = buf[slot]

        @pl.when(jnp.logical_not(filled))
        def _():
            out[...] = jnp.zeros_like(out)


def exchange(en, es, ew, ee, call):
    shape = jax.ShapeDtypeStruct(en.shape, en.dtype)
    vmem = pl.BlockSpec(memory_space=pltpu.VMEM)
    return pl.pallas_call(
        halo_kernel,
        in_specs=[vmem] * 4,
        out_specs=[vmem] * 4,
        out_shape=[shape] * 4,
        scratch_shapes=[
            pltpu.VMEM((4,) + en.shape, en.dtype),
            pltpu.SemaphoreType.DMA((4,)),
            pltpu.SemaphoreType.DMA((4,)),
        ],
        compiler_params=pltpu.CompilerParams(collective_id=call, has_side_effects=True),
    )(en, es, ew, ee)


def bucket_kernel(inv_ref, lab_ref, contrib_ref, out_ref):
    ndest = out_ref.shape[0]
    ntiles = contrib_ref.shape[0]
    sub = lax.broadcasted_iota(jnp.int32, (KF, CY), 0)

    def body(d, carry):
        labv = jnp.zeros((KF, CY), jnp.float32)
        for c in range(CAP):
            t = inv_ref[d * CAP + c]
            val = contrib_ref[jnp.minimum(t, ntiles - 1)]
            out_ref[d, c] = jnp.where(t < ntiles, val, 0.0)
            labv = jnp.where(sub == c, lab_ref[d * CAP + c].astype(jnp.float32), labv)
        out_ref[d, CAP] = labv
        return carry

    lax.fori_loop(0, ndest, body, 0)


def local(states, surface, land_mask, tile_weights, tile_source, tile_target, tile_row):
    group = lax.axis_index("mp")
    ndev = lax.axis_size("gx") * lax.axis_size("gy")
    state = states[0]
    lev, rows_here, cols_here = state.shape
    wet = jnp.where(
        group == 0, jnp.ones(land_mask.shape, jnp.float32), land_mask.astype(jnp.float32)
    )
    coef = jnp.stack([jnp.where(group == 0, 0.15, 0.12), jnp.where(group == 0, 0.1, 0.15)]).astype(
        jnp.float32
    )

    src = (surface[0] * wet).astype(jnp.bfloat16)
    source = tile_source[0, 0, 0]
    target = tile_target[0, 0, 0, :, 0]
    dest_row = tile_row[0, 0, 0]
    ntiles = source.shape[0]
    picked = jnp.take(src, source, axis=1)
    contrib = jnp.einsum(
        "tji,kti->tkj", tile_weights[0, 0, 0], picked, preferred_element_type=jnp.float32
    )
    onehot = (target[:, None] == jnp.arange(ndev, dtype=jnp.int32)[None, :]).astype(jnp.int32)
    earlier = jnp.cumsum(onehot, axis=0) - onehot
    rank = jnp.sum(earlier * onehot, axis=1)
    slot = target * CAP + rank
    inv = jnp.full((ndev * CAP,), ntiles, jnp.int32).at[slot].set(jnp.arange(ntiles, dtype=jnp.int32))
    labels = jnp.zeros((ndev * CAP,), jnp.int32).at[slot].set(dest_row)
    buckets = pl.pallas_call(
        bucket_kernel,
        in_specs=[
            pl.BlockSpec(memory_space=pltpu.SMEM),
            pl.BlockSpec(memory_space=pltpu.SMEM),
            pl.BlockSpec(memory_space=pltpu.VMEM),
        ],
        out_specs=pl.BlockSpec(memory_space=pltpu.VMEM),
        out_shape=jax.ShapeDtypeStruct((ndev, CAP + 1, KF, CY), jnp.float32),
    )(inv, labels, contrib)
    second, arrived = interval(coef, wet, state, buckets, masked_edges(wet, state))
    got_rows = arrived[:, CAP, :, 0].astype(jnp.int32)
    select = (
        got_rows[:, :, None] == jnp.arange(rows_here, dtype=jnp.int32)[None, None, :]
    ).astype(jnp.float32)
    sent = jnp.einsum(
        "scr,sckj->krj", select, arrived[:, :CAP], precision=lax.Precision.HIGHEST
    )
    received = lax.ppermute(sent, "mp", [(0, 1), (1, 0)])

    second = add_force(second, wet, received[0])
    return (second[None], received[None])


def solution(mesh):
    return jax.shard_map(
        local,
        mesh=mesh,
        in_specs=(
            P("mp", None, "gx", "gy"),
            P("mp", None, "gx", "gy"),
            P("gx", "gy"),
            P("mp", "gx", "gy", None, None, None),
            P("mp", "gx", "gy", None),
            P("mp", "gx", "gy", None, None),
            P("mp", "gx", "gy", None),
        ),
        out_specs=(P("mp", None, "gx", "gy"), P("mp", None, "gx", "gy")),
        check_vma=False,
    )
```

```python
import functools

import jax
import jax.numpy as jnp
from jax import lax
from jax.experimental import pallas as pl
from jax.experimental.pallas import tpu as pltpu
from jax.sharding import PartitionSpec as P

CY = 128
KF = 8
CAP = 8
LB = 8

force_gain = 0.5


def shift_pairs(devices, forward):
    up = [(i, i + 1) for i in range(devices - 1)]
    return up if forward else [(j, i) for i, j in up]


def start_spread(buckets_ref, recv, send_sem, recv_sem, first_out=None):
    mp = lax.axis_index("mp")
    ngy = lax.axis_size("gy")
    ndev = lax.axis_size("gx") * ngy
    me = lax.axis_index("gx") * ngy + lax.axis_index("gy")
    mesh_id = pl.DeviceIdType.MESH
    barrier = pltpu.get_barrier_semaphore()

    def greet(d, carry):
        @pl.when(d != me)
        def _():
            pl.semaphore_signal(barrier, 1, device_id=(mp, d // ngy, d % ngy), device_id_type=mesh_id)

        return carry

    lax.fori_loop(0, ndev, greet, 0)
    pl.semaphore_wait(barrier, ndev - 1)
    if first_out is not None:
        first_out()
    recv[me] = buckets_ref[me]

    def send(k, carry):
        d = (me + k) % ndev
        pltpu.make_async_remote_copy(
            src_ref=buckets_ref.at[d],
            dst_ref=recv.at[me],
            send_sem=send_sem.at[d],
            recv_sem=recv_sem.at[me],
            device_id=(mp, d // ngy, d % ngy),
            device_id_type=mesh_id,
        ).start()
        return carry

    lax.fori_loop(1, ndev, send, 0)


def finish_spread(buckets_ref, recv, send_sem, recv_sem, arrived_ref):
    ngy = lax.axis_size("gy")
    ndev = lax.axis_size("gx") * ngy
    me = lax.axis_index("gx") * ngy + lax.axis_index("gy")

    def wait(d, carry):
        @pl.when(d != me)
        def _():
            copy = pltpu.make_async_remote_copy(
                src_ref=buckets_ref.at[d],
                dst_ref=recv.at[d],
                send_sem=send_sem.at[d],
                recv_sem=recv_sem.at[d],
                device_id=(lax.axis_index("mp"), d // ngy, d % ngy),
                device_id_type=pl.DeviceIdType.MESH,
            )
            copy.wait_send()
            copy.wait_recv()

        return carry

    lax.fori_loop(0, ndev, wait, 0)
    arrived_ref[...] = recv[...]


def interval_kernel(coef_ref, wet_ref, u_ref, above_ref, below_ref, buckets_ref,
                    e0n, e0s, e0w, e0e,
                    out_ref, arrived_ref,
                    first, edge1, halo0, halo1, qw_ref, qe_ref, recv,
                    send_sem, recv_sem, hsend, hrecv):
    p = pl.program_id(0)
    i = pl.program_id(1)
    nblk = pl.num_programs(1)
    wet = wet_ref[...]
    rows, cols = wet.shape
    lev = first.shape[0]
    mp = lax.axis_index("mp")
    gx = lax.axis_index("gx")
    gy = lax.axis_index("gy")
    ngx = lax.axis_size("gx")
    ngy = lax.axis_size("gy")
    ndev = ngx * ngy
    me = gx * ngy + gy
    mesh_id = pl.DeviceIdType.MESH
    links = [
        (gx < ngx - 1, (mp, gx + 1, gy), 1, 0),
        (gx > 0, (mp, gx - 1, gy), 0, 1),
        (gy < ngy - 1, (mp, gx, gy + 1), 3, 2),
        (gy > 0, (mp, gx, gy - 1), 2, 3),
    ]
    fills = [gx > 0, gx < ngx - 1, gy > 0, gy < ngy - 1]
    edge0 = [e0n, e0s, e0w, e0e]

    def halo_copy(stage, src, slot, dev):
        srcs = edge0[src] if stage == 0 else edge1.at[src]
        dsts = halo0.at[slot] if stage == 0 else halo1.at[slot]
        return pltpu.make_async_remote_copy(
            src_ref=srcs,
            dst_ref=dsts,
            send_sem=hsend.at[stage, slot],
            recv_sem=hrecv.at[stage, slot],
            device_id=dev,
            device_id_type=mesh_id,
        )

    def send_halos(stage):
        for present, dev, src, slot in links:
            pl.when(present)(halo_copy(stage, src, slot, dev).start)

    def take_halos(stage, dst):
        for present, dev, src, slot in links:
            pl.when(present)(halo_copy(stage, src, slot, dev).wait_send)
        for slot, filled in enumerate(fills):
            _, dev, src, _ = links[slot]
            pl.when(filled)(halo_copy(stage, src, slot, dev).wait_recv)

            @pl.when(jnp.logical_not(filled))
            def _():
                dst[slot] = jnp.zeros_like(dst[slot])

    def bucket_copy(d):
        return pltpu.make_async_remote_copy(
            src_ref=buckets_ref.at[d],
            dst_ref=recv.at[me],
            send_sem=send_sem.at[d],
            recv_sem=recv_sem.at[me],
            device_id=(mp, d // ngy, d % ngy),
            device_id_type=mesh_id,
        )

    def issue(k0, count):
        for n in range(count):
            k = k0 + n

            @pl.when(k < ndev)
            def _():
                bucket_copy((me + k) % ndev).start()

    lane = lax.broadcasted_iota(jnp.int32, qw_ref.shape, 1)
    row = lax.broadcasted_iota(jnp.int32, (rows, cols), 0)
    col = lax.broadcasted_iota(jnp.int32, (rows, cols), 1)
    horiz = coef_ref[0]
    vert = coef_ref[1]

    def step(load, above, below, hn, hs, hw_t, he_t, store):
        for l in range(LB):
            u = load(l)
            prev = load(l - 1) if l > 0 else above
            nxt = load(l + 1) if l < LB - 1 else below
            w = wet * u
            north = jnp.where(row == 0, hn[l:l + 1, :], pltpu.roll(w, 1, 0))
            south = jnp.where(row == rows - 1, hs[l:l + 1, :], pltpu.roll(w, rows - 1, 0))
            west = jnp.where(col == 0, hw_t[:, l:l + 1], pltpu.roll(w, 1, 1))
            east = jnp.where(col == cols - 1, he_t[:, l:l + 1], pltpu.roll(w, cols - 1, 1))
            lateral = north + south + west + east - 4.0 * w
            vertical = prev + nxt - 2.0 * u
            store(l, wet * (u + horiz * lateral + vert * vertical))

    @pl.when((p == 0) & (i == 0))
    def _():
        barrier = pltpu.get_barrier_semaphore()

        def greet(d, carry):
            @pl.when(d != me)
            def _():
                pl.semaphore_signal(barrier, 1, device_id=(mp, d // ngy, d % ngy), device_id_type=mesh_id)

            return carry

        lax.fori_loop(0, ndev, greet, 0)
        pl.semaphore_wait(barrier, ndev - 1)
        send_halos(0)
        recv[me] = buckets_ref[me]
        take_halos(0, halo0)
        qw_ref[...] = jnp.zeros_like(qw_ref)
        qe_ref[...] = jnp.zeros_like(qe_ref)

    @pl.when(p == 0)
    def _():
        issue(1 + 3 * i, 3)
        blk = pl.ds(pl.multiple_of(i * LB, LB), LB)
        hn = halo0[0, blk]
        hs = halo0[1, blk]
        hw_t = jnp.transpose(halo0[2, blk])
        he_t = jnp.transpose(halo0[3, blk])
        above = above_ref[0] * jnp.where(i > 0, 1.0, 0.0)
        below = below_ref[0] * jnp.where(i < nblk - 1, 1.0, 0.0)
        qs = [qw_ref[...], qe_ref[...]]

        def store(l, res):
            first[i * LB + l] = res
            fw = wet * res
            edge1[0, i, l:l + 1, :] = fw[0:1, :]
            edge1[1, i, l:l + 1, :] = fw[rows - 1:rows, :]
            hit = lane == i * LB + l
            qs[0] = jnp.where(hit, fw[:, 0:1], qs[0])
            qs[1] = jnp.where(hit, fw[:, cols - 1:cols], qs[1])

        step(lambda l: u_ref[l], above, below, hn, hs, hw_t, he_t, store)
        qw_ref[...] = qs[0]
        qe_ref[...] = qs[1]

    @pl.when((p == 0) & (i == nblk - 1))
    def _():
        edge1[2] = jnp.transpose(qw_ref[...])[0:lev, :].reshape(nblk, LB, rows)
        edge1[3] = jnp.transpose(qe_ref[...])[0:lev, :].reshape(nblk, LB, rows)
        send_halos(1)

    @pl.when((p == 1) & (i == 0))
    def _():
        take_halos(1, halo1)

        def late(k, carry):
            bucket_copy((me + k) % ndev).start()
            return carry

        lax.fori_loop(min(1 + 3 * nblk, ndev), ndev, late, 0)

    @pl.when(p == 1)
    def _():
        base = i * LB
        above = first[jnp.maximum(base - 1, 0)] * jnp.where(i > 0, 1.0, 0.0)
        below = first[jnp.minimum(base + LB, lev - 1)] * jnp.where(i < nblk - 1, 1.0, 0.0)
        hw_t = jnp.transpose(halo1[2, i])
        he_t = jnp.transpose(halo1[3, i])

        def store(l, res):
            out_ref[l] = res

        step(lambda l: first[base + l], above, below, halo1[0, i], halo1[1, i], hw_t, he_t, store)

    @pl.when((p == 1) & (i == nblk - 1))
    def _():
        def wait(d, carry):
            @pl.when(d != me)
            def _():
                copy = pltpu.make_async_remote_copy(
                    src_ref=buckets_ref.at[d],
                    dst_ref=recv.at[d],
                    send_sem=send_sem.at[d],
                    recv_sem=recv_sem.at[d],
                    device_id=(mp, d // ngy, d % ngy),
                    device_id_type=mesh_id,
                )
                copy.wait_send()
                copy.wait_recv()

            return carry

        lax.fori_loop(0, ndev, wait, 0)
        arrived_ref[...] = recv[...]


def interval(coef, wet, u, buckets, edges):
    lev, rows, cols = u.shape
    nblk = lev // LB
    full2 = lambda shape: pl.BlockSpec(shape, lambda p, i: (0, 0))
    whole = pl.BlockSpec(buckets.shape, lambda p, i: (0, 0, 0, 0))
    held = lambda p, i: i + p * (nblk - 1 - i)
    in_specs = [
        pl.BlockSpec(memory_space=pltpu.SMEM),
        full2((rows, cols)),
        pl.BlockSpec((LB, rows, cols), lambda p, i: (held(p, i), 0, 0)),
        pl.BlockSpec((1, rows, cols), lambda p, i: (jnp.maximum(held(p, i) * LB - 1, 0), 0, 0)),
        pl.BlockSpec((1, rows, cols), lambda p, i: (jnp.minimum(held(p, i) * LB + LB, lev - 1), 0, 0)),
        whole,
    ] + [full2((lev, cols))] * 4
    out_shape = [
        jax.ShapeDtypeStruct((lev, rows, cols), jnp.float32),
        jax.ShapeDtypeStruct(buckets.shape, buckets.dtype),
    ]
    out_specs = [pl.BlockSpec((LB, rows, cols), lambda p, i: (i * p, 0, 0)), whole]
    scratch = [
        pltpu.VMEM((lev, rows, cols), jnp.float32),
        pltpu.VMEM((4, nblk, LB, cols), jnp.float32),
        pltpu.VMEM((4, lev, cols), jnp.float32),
        pltpu.VMEM((4, nblk, LB, cols), jnp.float32),
        pltpu.VMEM((rows, 128), jnp.float32),
        pltpu.VMEM((rows, 128), jnp.float32),
        pltpu.VMEM(buckets.shape, buckets.dtype),
        pltpu.SemaphoreType.DMA((buckets.shape[0],)),
        pltpu.SemaphoreType.DMA((buckets.shape[0],)),
        pltpu.SemaphoreType.DMA((2, 4)),
        pltpu.SemaphoreType.DMA((2, 4)),
    ]
    return pl.pallas_call(
        interval_kernel,
        grid=(2, nblk),
        in_specs=in_specs,
        out_specs=out_specs,
        out_shape=out_shape,
        scratch_shapes=scratch,
        compiler_params=pltpu.CompilerParams(
            dimension_semantics=("arbitrary", "arbitrary"), collective_id=3, has_side_effects=True,
            vmem_limit_bytes=48 * 1024 * 1024,
        ),
        cost_estimate=pl.CostEstimate(flops=60 * u.size, bytes_accessed=12 * u.size, transcendentals=0),
    )(coef, wet, u, u, u, buckets, *edges)


def first_kernel(coef_ref, wet_ref, u_ref, above_ref, below_ref, buckets_ref,
                 e0n, e0s, e0w, e0e,
                 out_ref, en_ref, es_ref, ew_ref, ee_ref, arrived_ref,
                 halo, qw_ref, qe_ref, recv, send_sem, recv_sem, hsend, hrecv):
    i = pl.program_id(0)
    nblk = pl.num_programs(0)
    edge0 = [e0n, e0s, e0w, e0e]
    wet = wet_ref[...]
    rows, cols = wet.shape
    lev = ew_ref.shape[0]
    mp = lax.axis_index("mp")
    gx = lax.axis_index("gx")
    gy = lax.axis_index("gy")
    ngx = lax.axis_size("gx")
    ngy = lax.axis_size("gy")
    mesh_id = pl.DeviceIdType.MESH
    links = [
        (gx < ngx - 1, (mp, gx + 1, gy), 1, 0),
        (gx > 0, (mp, gx - 1, gy), 0, 1),
        (gy < ngy - 1, (mp, gx, gy + 1), 3, 2),
        (gy > 0, (mp, gx, gy - 1), 2, 3),
    ]
    fills = [gx > 0, gx < ngx - 1, gy > 0, gy < ngy - 1]
    copies = [
        pltpu.make_async_remote_copy(
            src_ref=edge0[src],
            dst_ref=halo.at[slot],
            send_sem=hsend.at[slot],
            recv_sem=hrecv.at[slot],
            device_id=dev,
            device_id_type=mesh_id,
        )
        for _, dev, src, slot in links
    ]
    lane = lax.broadcasted_iota(jnp.int32, qw_ref.shape, 1)

    def send_halos():
        for (present, _, _, _), copy in zip(links, copies):
            pl.when(present)(copy.start)

    @pl.when(i == 0)
    def _():
        start_spread(buckets_ref, recv, send_sem, recv_sem, send_halos)
        for (present, _, _, _), copy in zip(links, copies):
            pl.when(present)(copy.wait_send)
        for slot, filled in enumerate(fills):
            pl.when(filled)(copies[slot].wait_recv)

            @pl.when(jnp.logical_not(filled))
            def _():
                halo[slot] = jnp.zeros_like(halo[slot])

        qw_ref[...] = jnp.zeros_like(qw_ref)
        qe_ref[...] = jnp.zeros_like(qe_ref)

    def _():
        horiz = coef_ref[0]
        vert = coef_ref[1]
        row = lax.broadcasted_iota(jnp.int32, (rows, cols), 0)
        col = lax.broadcasted_iota(jnp.int32, (rows, cols), 1)
        hn = halo[0, pl.ds(i * LB, LB)]
        hs = halo[1, pl.ds(i * LB, LB)]
        hw_t = jnp.transpose(halo[2, pl.ds(i * LB, LB)])
        he_t = jnp.transpose(halo[3, pl.ds(i * LB, LB)])
        above = above_ref[0] * jnp.where(i > 0, 1.0, 0.0)
        below = below_ref[0] * jnp.where(i < nblk - 1, 1.0, 0.0)
        qw = qw_ref[...]
        qe = qe_ref[...]
        for l in range(LB):
            u = u_ref[l]
            prev = u_ref[l - 1] if l > 0 else above
            nxt = u_ref[l + 1] if l < LB - 1 else below
            w = wet * u
            north = jnp.where(row == 0, hn[l:l + 1, :], pltpu.roll(w, 1, 0))
            south = jnp.where(row == rows - 1, hs[l:l + 1, :], pltpu.roll(w, rows - 1, 0))
            west = jnp.where(col == 0, hw_t[:, l:l + 1], pltpu.roll(w, 1, 1))
            east = jnp.where(col == cols - 1, he_t[:, l:l + 1], pltpu.roll(w, cols - 1, 1))
            lateral = north + south + west + east - 4.0 * w
            vertical = prev + nxt - 2.0 * u
            res = wet * (u + horiz * lateral + vert * vertical)
            out_ref[l] = res
            fw = wet * res
            en_ref[l:l + 1, :] = fw[0:1, :]
            es_ref[l:l + 1, :] = fw[rows - 1:rows, :]
            hit = lane == i * LB + l
            qw = jnp.where(hit, fw[:, 0:1], qw)
            qe = jnp.where(hit, fw[:, cols - 1:cols], qe)
        qw_ref[...] = qw
        qe_ref[...] = qe

    _()

    @pl.when(i == nblk - 1)
    def _():
        ew_ref[...] = jnp.transpose(qw_ref[...])[0:lev, :]
        ee_ref[...] = jnp.transpose(qe_ref[...])[0:lev, :]
        finish_spread(buckets_ref, recv, send_sem, recv_sem, arrived_ref)


def first_step(coef, wet, u, buckets, edges):
    lev, rows, cols = u.shape
    nblk = lev // LB
    full2 = lambda shape: pl.BlockSpec(shape, lambda i: (0, 0))
    lvl2 = pl.BlockSpec((LB, cols), lambda i: (i, 0))
    whole = pl.BlockSpec(buckets.shape, lambda i: (0, 0, 0, 0))
    in_specs = [
        pl.BlockSpec(memory_space=pltpu.SMEM),
        full2((rows, cols)),
        pl.BlockSpec((LB, rows, cols), lambda i: (i, 0, 0)),
        pl.BlockSpec((1, rows, cols), lambda i: (jnp.maximum(i * LB - 1, 0), 0, 0)),
        pl.BlockSpec((1, rows, cols), lambda i: (jnp.minimum(i * LB + LB, lev - 1), 0, 0)),
        whole,
    ] + [full2((lev, cols))] * 4
    out_shape = [
        jax.ShapeDtypeStruct((lev, rows, cols), jnp.float32),
        jax.ShapeDtypeStruct((lev, cols), jnp.float32),
        jax.ShapeDtypeStruct((lev, cols), jnp.float32),
        jax.ShapeDtypeStruct((lev, rows), jnp.float32),
        jax.ShapeDtypeStruct((lev, rows), jnp.float32),
        jax.ShapeDtypeStruct(buckets.shape, buckets.dtype),
    ]
    out_specs = [
        pl.BlockSpec((LB, rows, cols), lambda i: (i, 0, 0)),
        lvl2, lvl2, full2((lev, rows)), full2((lev, rows)), whole,
    ]
    scratch = [
        pltpu.VMEM((4, lev, cols), jnp.float32),
        pltpu.VMEM((rows, 128), jnp.float32),
        pltpu.VMEM((rows, 128), jnp.float32),
        pltpu.VMEM(buckets.shape, buckets.dtype),
        pltpu.SemaphoreType.DMA((buckets.shape[0],)),
        pltpu.SemaphoreType.DMA((buckets.shape[0],)),
        pltpu.SemaphoreType.DMA((4,)),
        pltpu.SemaphoreType.DMA((4,)),
    ]
    return pl.pallas_call(
        first_kernel,
        grid=(nblk,),
        in_specs=in_specs,
        out_specs=out_specs,
        out_shape=out_shape,
        scratch_shapes=scratch,
        compiler_params=pltpu.CompilerParams(
            dimension_semantics=("arbitrary",), collective_id=2, has_side_effects=True
        ),
        cost_estimate=pl.CostEstimate(flops=30 * u.size, bytes_accessed=12 * u.size, transcendentals=0),
    )(coef, wet, u, u, u, buckets, *edges)


def stencil_kernel(with_edges, with_force, coef_ref, wet_ref, u_ref, above_ref, below_ref,
                   hn_ref, hs_ref, hw_ref, he_ref, *rest):
    if with_force:
        force_ref, rest = rest[0], rest[1:]
    if with_edges:
        buckets_ref, rest = rest[0], rest[1:]
    out_ref = rest[0]
    i = pl.program_id(0)
    nblk = pl.num_programs(0)
    horiz = coef_ref[0]
    vert = coef_ref[1]
    wet = wet_ref[...]
    rows, cols = wet.shape
    row = lax.broadcasted_iota(jnp.int32, (rows, cols), 0)
    col = lax.broadcasted_iota(jnp.int32, (rows, cols), 1)
    hw_t = jnp.transpose(hw_ref[...])
    he_t = jnp.transpose(he_ref[...])
    above = above_ref[0] * jnp.where(i > 0, 1.0, 0.0)
    below = below_ref[0] * jnp.where(i < nblk - 1, 1.0, 0.0)
    if with_edges:
        en_ref, es_ref, ew_ref, ee_ref, arrived_ref, qw_ref, qe_ref, recv, send_sem, recv_sem = rest[1:]

        @pl.when(i == 0)
        def _():
            start_spread(buckets_ref, recv, send_sem, recv_sem)
            qw_ref[...] = jnp.zeros_like(qw_ref)
            qe_ref[...] = jnp.zeros_like(qe_ref)

    if with_edges:
        lane = lax.broadcasted_iota(jnp.int32, qw_ref.shape, 1)
        qw = qw_ref[...]
        qe = qe_ref[...]
    for l in range(LB):
        u = u_ref[l]
        prev = u_ref[l - 1] if l > 0 else above
        nxt = u_ref[l + 1] if l < LB - 1 else below
        w = wet * u
        north = jnp.where(row == 0, hn_ref[l:l + 1, :], pltpu.roll(w, 1, 0))
        south = jnp.where(row == rows - 1, hs_ref[l:l + 1, :], pltpu.roll(w, rows - 1, 0))
        west = jnp.where(col == 0, hw_t[:, l:l + 1], pltpu.roll(w, 1, 1))
        east = jnp.where(col == cols - 1, he_t[:, l:l + 1], pltpu.roll(w, cols - 1, 1))
        lateral = north + south + west + east - 4.0 * w
        vertical = prev + nxt - 2.0 * u
        res = wet * (u + horiz * lateral + vert * vertical)
        if with_force and l == 0:
            res = res + jnp.where(i == 0, 1.0, 0.0) * (force_gain * wet * force_ref[...])
        out_ref[l] = res
        if with_edges:
            fw = wet * res
            en_ref[l:l + 1, :] = fw[0:1, :]
            es_ref[l:l + 1, :] = fw[rows - 1:rows, :]
            hit = lane == i * LB + l
            qw = jnp.where(hit, fw[:, 0:1], qw)
            qe = jnp.where(hit, fw[:, cols - 1:cols], qe)

    if with_edges:
        qw_ref[...] = qw
        qe_ref[...] = qe

        @pl.when(i == nblk - 1)
        def _():
            lev = ew_ref.shape[0]
            ew_ref[...] = jnp.transpose(qw_ref[...])[0:lev, :]
            ee_ref[...] = jnp.transpose(qe_ref[...])[0:lev, :]
            finish_spread(buckets_ref, recv, send_sem, recv_sem, arrived_ref)


def edges_kernel(wet_ref, u_ref, en_ref, es_ref, ew_ref, ee_ref, qw_ref, qe_ref):
    i = pl.program_id(0)
    nblk = pl.num_programs(0)
    wet = wet_ref[...]
    rows, cols = wet.shape

    @pl.when(i == 0)
    def _():
        qw_ref[...] = jnp.zeros_like(qw_ref)
        qe_ref[...] = jnp.zeros_like(qe_ref)

    lane = lax.broadcasted_iota(jnp.int32, qw_ref.shape, 1)
    qw = qw_ref[...]
    qe = qe_ref[...]
    for l in range(LB):
        fw = wet * u_ref[l]
        en_ref[l:l + 1, :] = fw[0:1, :]
        es_ref[l:l + 1, :] = fw[rows - 1:rows, :]
        hit = lane == i * LB + l
        qw = jnp.where(hit, fw[:, 0:1], qw)
        qe = jnp.where(hit, fw[:, cols - 1:cols], qe)
    qw_ref[...] = qw
    qe_ref[...] = qe

    @pl.when(i == nblk - 1)
    def _():
        lev = ew_ref.shape[0]
        ew_ref[...] = jnp.transpose(qw_ref[...])[0:lev, :]
        ee_ref[...] = jnp.transpose(qe_ref[...])[0:lev, :]


def masked_edges(wet, u):
    lev, rows, cols = u.shape
    lvl2 = pl.BlockSpec((LB, cols), lambda i: (i, 0))
    full2 = lambda shape: pl.BlockSpec(shape, lambda i: (0, 0))
    return pl.pallas_call(
        edges_kernel,
        grid=(lev // LB,),
        in_specs=[full2((rows, cols)), pl.BlockSpec((LB, rows, cols), lambda i: (i, 0, 0))],
        out_specs=[lvl2, lvl2, full2((lev, rows)), full2((lev, rows))],
        out_shape=[jax.ShapeDtypeStruct((lev, cols), jnp.float32)] * 2
        + [jax.ShapeDtypeStruct((lev, rows), jnp.float32)] * 2,
        scratch_shapes=[pltpu.VMEM((rows, 128), jnp.float32)] * 2,
        compiler_params=pltpu.CompilerParams(dimension_semantics=("arbitrary",)),
        cost_estimate=pl.CostEstimate(flops=2 * u.size, bytes_accessed=4 * u.size, transcendentals=0),
    )(wet, u)


def force_kernel(x_ref, wet_ref, f_ref, out_ref):
    out_ref[0] = x_ref[0] + force_gain * wet_ref[...] * f_ref[...]


def add_force(x, wet, f):
    lev, rows, cols = x.shape
    plane = pl.BlockSpec((rows, cols), lambda i: (0, 0))
    level0 = pl.BlockSpec((1, rows, cols), lambda i: (0, 0, 0))
    return pl.pallas_call(
        force_kernel,
        grid=(1,),
        in_specs=[level0, plane, plane],
        out_specs=level0,
        out_shape=jax.ShapeDtypeStruct(x.shape, x.dtype),
        input_output_aliases={0: 0},
    )(x, wet, f)


def stencil_step(coef, wet, u, halos, force=None, buckets=None):
    with_edges = buckets is not None
    lev, rows, cols = u.shape
    nblk = lev // LB
    full2 = lambda shape: pl.BlockSpec(shape, lambda i: (0, 0))
    lvl2 = pl.BlockSpec((LB, cols), lambda i: (i, 0))
    in_specs = [
        pl.BlockSpec(memory_space=pltpu.SMEM),
        full2((rows, cols)),
        pl.BlockSpec((LB, rows, cols), lambda i: (i, 0, 0)),
        pl.BlockSpec((1, rows, cols), lambda i: (jnp.maximum(i * LB - 1, 0), 0, 0)),
        pl.BlockSpec((1, rows, cols), lambda i: (jnp.minimum(i * LB + LB, lev - 1), 0, 0)),
        lvl2, lvl2, lvl2, lvl2,
    ]
    args = [coef, wet, u, u, u] + list(halos)
    if force is not None:
        in_specs.append(full2((rows, cols)))
        args.append(force)
    if with_edges:
        in_specs.append(pl.BlockSpec(buckets.shape, lambda i: (0, 0, 0, 0)))
        args.append(buckets)
    out_shape = [jax.ShapeDtypeStruct((lev, rows, cols), jnp.float32)]
    out_specs = [pl.BlockSpec((LB, rows, cols), lambda i: (i, 0, 0))]
    scratch = []
    params = dict(dimension_semantics=("arbitrary",))
    if with_edges:
        out_shape += [jax.ShapeDtypeStruct((lev, cols), jnp.float32)] * 2
        out_shape += [jax.ShapeDtypeStruct((lev, rows), jnp.float32)] * 2
        out_shape += [jax.ShapeDtypeStruct(buckets.shape, buckets.dtype)]
        out_specs += [lvl2, lvl2, full2((lev, rows)), full2((lev, rows))]
        out_specs += [pl.BlockSpec(buckets.shape, lambda i: (0, 0, 0, 0))]
        scratch = [pltpu.VMEM((rows, 128), jnp.float32)] * 2 + [
            pltpu.VMEM(buckets.shape, buckets.dtype),
            pltpu.SemaphoreType.DMA((buckets.shape[0],)),
            pltpu.SemaphoreType.DMA((buckets.shape[0],)),
        ]
        params.update(collective_id=2, has_side_effects=True)
    return pl.pallas_call(
        functools.partial(stencil_kernel, with_edges, force is not None),
        grid=(nblk,),
        in_specs=in_specs,
        out_specs=out_specs,
        out_shape=out_shape,
        scratch_shapes=scratch,
        compiler_params=pltpu.CompilerParams(**params),
        cost_estimate=pl.CostEstimate(flops=30 * u.size, bytes_accessed=12 * u.size, transcendentals=0),
    )(*args)


def halo_kernel(en_ref, es_ref, ew_ref, ee_ref, hn_ref, hs_ref, hw_ref, he_ref,
                buf, send_sem, recv_sem):
    mp = lax.axis_index("mp")
    gx = lax.axis_index("gx")
    gy = lax.axis_index("gy")
    ngx = lax.axis_size("gx")
    ngy = lax.axis_size("gy")
    mesh_id = pl.DeviceIdType.MESH
    links = [
        (gx < ngx - 1, (mp, gx + 1, gy), es_ref, 0),
        (gx > 0, (mp, gx - 1, gy), en_ref, 1),
        (gy < ngy - 1, (mp, gx, gy + 1), ee_ref, 2),
        (gy > 0, (mp, gx, gy - 1), ew_ref, 3),
    ]
    barrier = pltpu.get_barrier_semaphore()
    count = jnp.int32(0)
    for present, dev, _, _ in links:
        @pl.when(present)
        def _():
            pl.semaphore_signal(barrier, 1, device_id=dev, device_id_type=mesh_id)

        count = count + present.astype(jnp.int32)
    pl.semaphore_wait(barrier, count)

    copies = []
    for present, dev, src, slot in links:
        copy = pltpu.make_async_remote_copy(
            src_ref=src,
            dst_ref=buf.at[slot],
            send_sem=send_sem.at[slot],
            recv_sem=recv_sem.at[slot],
            device_id=dev,
            device_id_type=mesh_id,
        )
        pl.when(present)(copy.start)
        copies.append((present, copy))
    for present, copy in copies:
        pl.when(present)(copy.wait_send)
    fills = [gx > 0, gx < ngx - 1, gy > 0, gy < ngy - 1]
    outs = [hn_ref, hs_ref, hw_ref, he_ref]
    for slot, (filled, out) in enumerate(zip(fills, outs)):
        _, copy = copies[slot]

        @pl.when(filled)
        def _():
            copy.wait_recv()
            out[...] = buf[slot]

        @pl.when(jnp.logical_not(filled))
        def _():
            out[...] = jnp.zeros_like(out)


def exchange(en, es, ew, ee, call):
    shape = jax.ShapeDtypeStruct(en.shape, en.dtype)
    vmem = pl.BlockSpec(memory_space=pltpu.VMEM)
    return pl.pallas_call(
        halo_kernel,
        in_specs=[vmem] * 4,
        out_specs=[vmem] * 4,
        out_shape=[shape] * 4,
        scratch_shapes=[
            pltpu.VMEM((4,) + en.shape, en.dtype),
            pltpu.SemaphoreType.DMA((4,)),
            pltpu.SemaphoreType.DMA((4,)),
        ],
        compiler_params=pltpu.CompilerParams(collective_id=call, has_side_effects=True),
    )(en, es, ew, ee)


def bucket_kernel(slot_ref, row_ref, contrib_ref, out_ref):
    ntiles = contrib_ref.shape[0]
    sub = lax.broadcasted_iota(jnp.int32, (KF, CY), 0)
    out_ref[...] = jnp.zeros_like(out_ref)

    def body(t, carry):
        s = slot_ref[t]
        d = s // CAP
        c = s % CAP
        out_ref[d, c] = contrib_ref[t]
        out_ref[d, CAP] = jnp.where(sub == c, row_ref[t].astype(jnp.float32), out_ref[d, CAP])
        return carry

    lax.fori_loop(0, ntiles, body, 0)


def local(states, surface, land_mask, tile_weights, tile_source, tile_target, tile_row):
    group = lax.axis_index("mp")
    ndev = lax.axis_size("gx") * lax.axis_size("gy")
    state = states[0]
    lev, rows_here, cols_here = state.shape
    wet = jnp.where(
        group == 0, jnp.ones(land_mask.shape, jnp.float32), land_mask.astype(jnp.float32)
    )
    coef = jnp.stack([jnp.where(group == 0, 0.15, 0.12), jnp.where(group == 0, 0.1, 0.15)]).astype(
        jnp.float32
    )

    src = (surface[0] * wet).astype(jnp.bfloat16)
    source = tile_source[0, 0, 0]
    target = tile_target[0, 0, 0, :, 0]
    dest_row = tile_row[0, 0, 0]
    ntiles = source.shape[0]
    picked = jnp.take(src, source, axis=1)
    contrib = jnp.einsum(
        "tji,kti->tkj", tile_weights[0, 0, 0], picked, preferred_element_type=jnp.float32
    )
    onehot = (target[:, None] == jnp.arange(ndev, dtype=jnp.int32)[None, :]).astype(jnp.int32)
    earlier = jnp.cumsum(onehot, axis=0) - onehot
    rank = jnp.sum(earlier * onehot, axis=1)
    slot = target * CAP + rank
    buckets = pl.pallas_call(
        bucket_kernel,
        in_specs=[
            pl.BlockSpec(memory_space=pltpu.SMEM),
            pl.BlockSpec(memory_space=pltpu.SMEM),
            pl.BlockSpec(memory_space=pltpu.VMEM),
        ],
        out_specs=pl.BlockSpec(memory_space=pltpu.VMEM),
        out_shape=jax.ShapeDtypeStruct((ndev, CAP + 1, KF, CY), jnp.float32),
    )(slot, dest_row, contrib)
    second, arrived = interval(coef, wet, state, buckets, masked_edges(wet, state))
    got_rows = arrived[:, CAP, :, 0].astype(jnp.int32)
    select = (
        got_rows[:, :, None] == jnp.arange(rows_here, dtype=jnp.int32)[None, None, :]
    ).astype(jnp.float32)
    sent = jnp.einsum(
        "scr,sckj->krj", select, arrived[:, :CAP], precision=lax.Precision.HIGHEST
    )
    received = lax.ppermute(sent, "mp", [(0, 1), (1, 0)])

    second = add_force(second, wet, received[0])
    return (second[None], received[None])


def solution(mesh):
    return jax.shard_map(
        local,
        mesh=mesh,
        in_specs=(
            P("mp", None, "gx", "gy"),
            P("mp", None, "gx", "gy"),
            P("gx", "gy"),
            P("mp", "gx", "gy", None, None, None),
            P("mp", "gx", "gy", None),
            P("mp", "gx", "gy", None, None),
            P("mp", "gx", "gy", None),
        ),
        out_specs=(P("mp", None, "gx", "gy"), P("mp", None, "gx", "gy")),
        check_vma=False,
    )
```

```python
import functools

import jax
import jax.numpy as jnp
from jax import lax
from jax.experimental import pallas as pl
from jax.experimental.pallas import tpu as pltpu
from jax.sharding import PartitionSpec as P

CY = 128
KF = 8
CAP = 8
LB = 8

force_gain = 0.5


def shift_pairs(devices, forward):
    up = [(i, i + 1) for i in range(devices - 1)]
    return up if forward else [(j, i) for i, j in up]


def start_spread(buckets_ref, recv, send_sem, recv_sem, first_out=None):
    mp = lax.axis_index("mp")
    ngy = lax.axis_size("gy")
    ndev = lax.axis_size("gx") * ngy
    me = lax.axis_index("gx") * ngy + lax.axis_index("gy")
    mesh_id = pl.DeviceIdType.MESH
    barrier = pltpu.get_barrier_semaphore()

    def greet(d, carry):
        @pl.when(d != me)
        def _():
            pl.semaphore_signal(barrier, 1, device_id=(mp, d // ngy, d % ngy), device_id_type=mesh_id)

        return carry

    lax.fori_loop(0, ndev, greet, 0)
    pl.semaphore_wait(barrier, ndev - 1)
    if first_out is not None:
        first_out()
    recv[me] = buckets_ref[me]

    def send(k, carry):
        d = (me + k) % ndev
        pltpu.make_async_remote_copy(
            src_ref=buckets_ref.at[d],
            dst_ref=recv.at[me],
            send_sem=send_sem.at[d],
            recv_sem=recv_sem.at[me],
            device_id=(mp, d // ngy, d % ngy),
            device_id_type=mesh_id,
        ).start()
        return carry

    lax.fori_loop(1, ndev, send, 0)


def finish_spread(buckets_ref, recv, send_sem, recv_sem, arrived_ref):
    ngy = lax.axis_size("gy")
    ndev = lax.axis_size("gx") * ngy
    me = lax.axis_index("gx") * ngy + lax.axis_index("gy")

    def wait(d, carry):
        @pl.when(d != me)
        def _():
            copy = pltpu.make_async_remote_copy(
                src_ref=buckets_ref.at[d],
                dst_ref=recv.at[d],
                send_sem=send_sem.at[d],
                recv_sem=recv_sem.at[d],
                device_id=(lax.axis_index("mp"), d // ngy, d % ngy),
                device_id_type=pl.DeviceIdType.MESH,
            )
            copy.wait_send()
            copy.wait_recv()

        return carry

    lax.fori_loop(0, ndev, wait, 0)
    arrived_ref[...] = recv[...]


def interval_kernel(coef_ref, wet_ref, u_ref, above_ref, below_ref, buckets_ref,
                    e0n, e0s, e0w, e0e,
                    out_ref, arrived_ref,
                    first, edge1, halo0, halo1, qw_ref, qe_ref, recv,
                    send_sem, recv_sem, hsend, hrecv):
    p = pl.program_id(0)
    i = pl.program_id(1)
    nblk = pl.num_programs(1)
    wet = wet_ref[...]
    rows, cols = wet.shape
    lev = first.shape[0]
    mp = lax.axis_index("mp")
    gx = lax.axis_index("gx")
    gy = lax.axis_index("gy")
    ngx = lax.axis_size("gx")
    ngy = lax.axis_size("gy")
    ndev = ngx * ngy
    me = gx * ngy + gy
    mesh_id = pl.DeviceIdType.MESH
    links = [
        (gx < ngx - 1, (mp, gx + 1, gy), 1, 0),
        (gx > 0, (mp, gx - 1, gy), 0, 1),
        (gy < ngy - 1, (mp, gx, gy + 1), 3, 2),
        (gy > 0, (mp, gx, gy - 1), 2, 3),
    ]
    fills = [gx > 0, gx < ngx - 1, gy > 0, gy < ngy - 1]
    edge0 = [e0n, e0s, e0w, e0e]

    def halo_copy(stage, src, slot, dev):
        srcs = edge0[src] if stage == 0 else edge1.at[src]
        dsts = halo0.at[slot] if stage == 0 else halo1.at[slot]
        return pltpu.make_async_remote_copy(
            src_ref=srcs,
            dst_ref=dsts,
            send_sem=hsend.at[stage, slot],
            recv_sem=hrecv.at[stage, slot],
            device_id=dev,
            device_id_type=mesh_id,
        )

    def send_halos(stage):
        for present, dev, src, slot in links:
            pl.when(present)(halo_copy(stage, src, slot, dev).start)

    def take_halos(stage, dst):
        for present, dev, src, slot in links:
            pl.when(present)(halo_copy(stage, src, slot, dev).wait_send)
        for slot, filled in enumerate(fills):
            _, dev, src, _ = links[slot]
            pl.when(filled)(halo_copy(stage, src, slot, dev).wait_recv)

            @pl.when(jnp.logical_not(filled))
            def _():
                dst[slot] = jnp.zeros_like(dst[slot])

    def bucket_copy(d):
        return pltpu.make_async_remote_copy(
            src_ref=buckets_ref.at[d],
            dst_ref=recv.at[me],
            send_sem=send_sem.at[d],
            recv_sem=recv_sem.at[me],
            device_id=(mp, d // ngy, d % ngy),
            device_id_type=mesh_id,
        )

    def issue(k0, count):
        for n in range(count):
            k = k0 + n

            @pl.when(k < ndev)
            def _():
                bucket_copy((me + k) % ndev).start()

    lane = lax.broadcasted_iota(jnp.int32, qw_ref.shape, 1)
    row = lax.broadcasted_iota(jnp.int32, (rows, cols), 0)
    col = lax.broadcasted_iota(jnp.int32, (rows, cols), 1)
    horiz = coef_ref[0]
    vert = coef_ref[1]

    def step(load, above, below, hn, hs, hw_t, he_t, store):
        for l in range(LB):
            u = load(l)
            prev = load(l - 1) if l > 0 else above
            nxt = load(l + 1) if l < LB - 1 else below
            w = wet * u
            north = jnp.where(row == 0, hn[l:l + 1, :], pltpu.roll(w, 1, 0))
            south = jnp.where(row == rows - 1, hs[l:l + 1, :], pltpu.roll(w, rows - 1, 0))
            west = jnp.where(col == 0, hw_t[:, l:l + 1], pltpu.roll(w, 1, 1))
            east = jnp.where(col == cols - 1, he_t[:, l:l + 1], pltpu.roll(w, cols - 1, 1))
            lateral = north + south + west + east - 4.0 * w
            vertical = prev + nxt - 2.0 * u
            store(l, wet * (u + horiz * lateral + vert * vertical))

    @pl.when((p == 0) & (i == 0))
    def _():
        barrier = pltpu.get_barrier_semaphore()

        def greet(d, carry):
            @pl.when(d != me)
            def _():
                pl.semaphore_signal(barrier, 1, device_id=(mp, d // ngy, d % ngy), device_id_type=mesh_id)

            return carry

        lax.fori_loop(0, ndev, greet, 0)
        pl.semaphore_wait(barrier, ndev - 1)
        send_halos(0)
        recv[me] = buckets_ref[me]
        take_halos(0, halo0)
        qw_ref[...] = jnp.zeros_like(qw_ref)
        qe_ref[...] = jnp.zeros_like(qe_ref)

    @pl.when(p == 0)
    def _():
        issue(1 + 3 * i, 3)
        blk = pl.ds(pl.multiple_of(i * LB, LB), LB)
        hn = halo0[0, blk]
        hs = halo0[1, blk]
        hw_t = jnp.transpose(halo0[2, blk])
        he_t = jnp.transpose(halo0[3, blk])
        above = above_ref[0] * jnp.where(i > 0, 1.0, 0.0)
        below = below_ref[0] * jnp.where(i < nblk - 1, 1.0, 0.0)
        qs = [qw_ref[...], qe_ref[...]]

        def store(l, res):
            first[i * LB + l] = res
            fw = wet * res
            edge1[0, i, l:l + 1, :] = fw[0:1, :]
            edge1[1, i, l:l + 1, :] = fw[rows - 1:rows, :]
            hit = lane == i * LB + l
            qs[0] = jnp.where(hit, fw[:, 0:1], qs[0])
            qs[1] = jnp.where(hit, fw[:, cols - 1:cols], qs[1])

        step(lambda l: u_ref[l], above, below, hn, hs, hw_t, he_t, store)
        qw_ref[...] = qs[0]
        qe_ref[...] = qs[1]

    @pl.when((p == 0) & (i == nblk - 1))
    def _():
        edge1[2] = jnp.transpose(qw_ref[...])[0:lev, :].reshape(nblk, LB, rows)
        edge1[3] = jnp.transpose(qe_ref[...])[0:lev, :].reshape(nblk, LB, rows)
        send_halos(1)

    @pl.when((p == 1) & (i == 0))
    def _():
        take_halos(1, halo1)

        def late(k, carry):
            bucket_copy((me + k) % ndev).start()
            return carry

        lax.fori_loop(min(1 + 3 * nblk, ndev), ndev, late, 0)

    @pl.when(p == 1)
    def _():
        base = i * LB
        above = first[jnp.maximum(base - 1, 0)] * jnp.where(i > 0, 1.0, 0.0)
        below = first[jnp.minimum(base + LB, lev - 1)] * jnp.where(i < nblk - 1, 1.0, 0.0)
        hw_t = jnp.transpose(halo1[2, i])
        he_t = jnp.transpose(halo1[3, i])

        def store(l, res):
            out_ref[l] = res

        step(lambda l: first[base + l], above, below, halo1[0, i], halo1[1, i], hw_t, he_t, store)

    @pl.when((p == 1) & (i == nblk - 1))
    def _():
        def wait(d, carry):
            @pl.when(d != me)
            def _():
                copy = pltpu.make_async_remote_copy(
                    src_ref=buckets_ref.at[d],
                    dst_ref=recv.at[d],
                    send_sem=send_sem.at[d],
                    recv_sem=recv_sem.at[d],
                    device_id=(mp, d // ngy, d % ngy),
                    device_id_type=mesh_id,
                )
                copy.wait_send()
                copy.wait_recv()

            return carry

        lax.fori_loop(0, ndev, wait, 0)
        arrived_ref[...] = recv[...]


def interval(coef, wet, u, buckets, edges):
    lev, rows, cols = u.shape
    nblk = lev // LB
    full2 = lambda shape: pl.BlockSpec(shape, lambda p, i: (0, 0))
    whole = pl.BlockSpec(buckets.shape, lambda p, i: (0, 0, 0, 0))
    held = lambda p, i: i + p * (nblk - 1 - i)
    in_specs = [
        pl.BlockSpec(memory_space=pltpu.SMEM),
        full2((rows, cols)),
        pl.BlockSpec((LB, rows, cols), lambda p, i: (held(p, i), 0, 0)),
        pl.BlockSpec((1, rows, cols), lambda p, i: (jnp.maximum(held(p, i) * LB - 1, 0), 0, 0)),
        pl.BlockSpec((1, rows, cols), lambda p, i: (jnp.minimum(held(p, i) * LB + LB, lev - 1), 0, 0)),
        whole,
    ] + [full2((lev, cols))] * 4
    out_shape = [
        jax.ShapeDtypeStruct((lev, rows, cols), jnp.float32),
        jax.ShapeDtypeStruct(buckets.shape, buckets.dtype),
    ]
    out_specs = [pl.BlockSpec((LB, rows, cols), lambda p, i: (i * p, 0, 0)), whole]
    scratch = [
        pltpu.VMEM((lev, rows, cols), jnp.float32),
        pltpu.VMEM((4, nblk, LB, cols), jnp.float32),
        pltpu.VMEM((4, lev, cols), jnp.float32),
        pltpu.VMEM((4, nblk, LB, cols), jnp.float32),
        pltpu.VMEM((rows, 128), jnp.float32),
        pltpu.VMEM((rows, 128), jnp.float32),
        pltpu.VMEM(buckets.shape, buckets.dtype),
        pltpu.SemaphoreType.DMA((buckets.shape[0],)),
        pltpu.SemaphoreType.DMA((buckets.shape[0],)),
        pltpu.SemaphoreType.DMA((2, 4)),
        pltpu.SemaphoreType.DMA((2, 4)),
    ]
    return pl.pallas_call(
        interval_kernel,
        grid=(2, nblk),
        in_specs=in_specs,
        out_specs=out_specs,
        out_shape=out_shape,
        scratch_shapes=scratch,
        compiler_params=pltpu.CompilerParams(
            dimension_semantics=("arbitrary", "arbitrary"), collective_id=3, has_side_effects=True,
            vmem_limit_bytes=48 * 1024 * 1024,
        ),
        cost_estimate=pl.CostEstimate(flops=60 * u.size, bytes_accessed=12 * u.size, transcendentals=0),
    )(coef, wet, u, u, u, buckets, *edges)


def first_kernel(coef_ref, wet_ref, u_ref, above_ref, below_ref, buckets_ref,
                 e0n, e0s, e0w, e0e,
                 out_ref, en_ref, es_ref, ew_ref, ee_ref, arrived_ref,
                 halo, qw_ref, qe_ref, recv, send_sem, recv_sem, hsend, hrecv):
    i = pl.program_id(0)
    nblk = pl.num_programs(0)
    edge0 = [e0n, e0s, e0w, e0e]
    wet = wet_ref[...]
    rows, cols = wet.shape
    lev = ew_ref.shape[0]
    mp = lax.axis_index("mp")
    gx = lax.axis_index("gx")
    gy = lax.axis_index("gy")
    ngx = lax.axis_size("gx")
    ngy = lax.axis_size("gy")
    mesh_id = pl.DeviceIdType.MESH
    links = [
        (gx < ngx - 1, (mp, gx + 1, gy), 1, 0),
        (gx > 0, (mp, gx - 1, gy), 0, 1),
        (gy < ngy - 1, (mp, gx, gy + 1), 3, 2),
        (gy > 0, (mp, gx, gy - 1), 2, 3),
    ]
    fills = [gx > 0, gx < ngx - 1, gy > 0, gy < ngy - 1]
    copies = [
        pltpu.make_async_remote_copy(
            src_ref=edge0[src],
            dst_ref=halo.at[slot],
            send_sem=hsend.at[slot],
            recv_sem=hrecv.at[slot],
            device_id=dev,
            device_id_type=mesh_id,
        )
        for _, dev, src, slot in links
    ]
    lane = lax.broadcasted_iota(jnp.int32, qw_ref.shape, 1)

    def send_halos():
        for (present, _, _, _), copy in zip(links, copies):
            pl.when(present)(copy.start)

    @pl.when(i == 0)
    def _():
        start_spread(buckets_ref, recv, send_sem, recv_sem, send_halos)
        for (present, _, _, _), copy in zip(links, copies):
            pl.when(present)(copy.wait_send)
        for slot, filled in enumerate(fills):
            pl.when(filled)(copies[slot].wait_recv)

            @pl.when(jnp.logical_not(filled))
            def _():
                halo[slot] = jnp.zeros_like(halo[slot])

        qw_ref[...] = jnp.zeros_like(qw_ref)
        qe_ref[...] = jnp.zeros_like(qe_ref)

    def _():
        horiz = coef_ref[0]
        vert = coef_ref[1]
        row = lax.broadcasted_iota(jnp.int32, (rows, cols), 0)
        col = lax.broadcasted_iota(jnp.int32, (rows, cols), 1)
        hn = halo[0, pl.ds(i * LB, LB)]
        hs = halo[1, pl.ds(i * LB, LB)]
        hw_t = jnp.transpose(halo[2, pl.ds(i * LB, LB)])
        he_t = jnp.transpose(halo[3, pl.ds(i * LB, LB)])
        above = above_ref[0] * jnp.where(i > 0, 1.0, 0.0)
        below = below_ref[0] * jnp.where(i < nblk - 1, 1.0, 0.0)
        qw = qw_ref[...]
        qe = qe_ref[...]
        for l in range(LB):
            u = u_ref[l]
            prev = u_ref[l - 1] if l > 0 else above
            nxt = u_ref[l + 1] if l < LB - 1 else below
            w = wet * u
            north = jnp.where(row == 0, hn[l:l + 1, :], pltpu.roll(w, 1, 0))
            south = jnp.where(row == rows - 1, hs[l:l + 1, :], pltpu.roll(w, rows - 1, 0))
            west = jnp.where(col == 0, hw_t[:, l:l + 1], pltpu.roll(w, 1, 1))
            east = jnp.where(col == cols - 1, he_t[:, l:l + 1], pltpu.roll(w, cols - 1, 1))
            lateral = north + south + west + east - 4.0 * w
            vertical = prev + nxt - 2.0 * u
            res = wet * (u + horiz * lateral + vert * vertical)
            out_ref[l] = res
            fw = wet * res
            en_ref[l:l + 1, :] = fw[0:1, :]
            es_ref[l:l + 1, :] = fw[rows - 1:rows, :]
            hit = lane == i * LB + l
            qw = jnp.where(hit, fw[:, 0:1], qw)
            qe = jnp.where(hit, fw[:, cols - 1:cols], qe)
        qw_ref[...] = qw
        qe_ref[...] = qe

    _()

    @pl.when(i == nblk - 1)
    def _():
        ew_ref[...] = jnp.transpose(qw_ref[...])[0:lev, :]
        ee_ref[...] = jnp.transpose(qe_ref[...])[0:lev, :]
        finish_spread(buckets_ref, recv, send_sem, recv_sem, arrived_ref)


def first_step(coef, wet, u, buckets, edges):
    lev, rows, cols = u.shape
    nblk = lev // LB
    full2 = lambda shape: pl.BlockSpec(shape, lambda i: (0, 0))
    lvl2 = pl.BlockSpec((LB, cols), lambda i: (i, 0))
    whole = pl.BlockSpec(buckets.shape, lambda i: (0, 0, 0, 0))
    in_specs = [
        pl.BlockSpec(memory_space=pltpu.SMEM),
        full2((rows, cols)),
        pl.BlockSpec((LB, rows, cols), lambda i: (i, 0, 0)),
        pl.BlockSpec((1, rows, cols), lambda i: (jnp.maximum(i * LB - 1, 0), 0, 0)),
        pl.BlockSpec((1, rows, cols), lambda i: (jnp.minimum(i * LB + LB, lev - 1), 0, 0)),
        whole,
    ] + [full2((lev, cols))] * 4
    out_shape = [
        jax.ShapeDtypeStruct((lev, rows, cols), jnp.float32),
        jax.ShapeDtypeStruct((lev, cols), jnp.float32),
        jax.ShapeDtypeStruct((lev, cols), jnp.float32),
        jax.ShapeDtypeStruct((lev, rows), jnp.float32),
        jax.ShapeDtypeStruct((lev, rows), jnp.float32),
        jax.ShapeDtypeStruct(buckets.shape, buckets.dtype),
    ]
    out_specs = [
        pl.BlockSpec((LB, rows, cols), lambda i: (i, 0, 0)),
        lvl2, lvl2, full2((lev, rows)), full2((lev, rows)), whole,
    ]
    scratch = [
        pltpu.VMEM((4, lev, cols), jnp.float32),
        pltpu.VMEM((rows, 128), jnp.float32),
        pltpu.VMEM((rows, 128), jnp.float32),
        pltpu.VMEM(buckets.shape, buckets.dtype),
        pltpu.SemaphoreType.DMA((buckets.shape[0],)),
        pltpu.SemaphoreType.DMA((buckets.shape[0],)),
        pltpu.SemaphoreType.DMA((4,)),
        pltpu.SemaphoreType.DMA((4,)),
    ]
    return pl.pallas_call(
        first_kernel,
        grid=(nblk,),
        in_specs=in_specs,
        out_specs=out_specs,
        out_shape=out_shape,
        scratch_shapes=scratch,
        compiler_params=pltpu.CompilerParams(
            dimension_semantics=("arbitrary",), collective_id=2, has_side_effects=True
        ),
        cost_estimate=pl.CostEstimate(flops=30 * u.size, bytes_accessed=12 * u.size, transcendentals=0),
    )(coef, wet, u, u, u, buckets, *edges)


def stencil_kernel(with_edges, with_force, coef_ref, wet_ref, u_ref, above_ref, below_ref,
                   hn_ref, hs_ref, hw_ref, he_ref, *rest):
    if with_force:
        force_ref, rest = rest[0], rest[1:]
    if with_edges:
        buckets_ref, rest = rest[0], rest[1:]
    out_ref = rest[0]
    i = pl.program_id(0)
    nblk = pl.num_programs(0)
    horiz = coef_ref[0]
    vert = coef_ref[1]
    wet = wet_ref[...]
    rows, cols = wet.shape
    row = lax.broadcasted_iota(jnp.int32, (rows, cols), 0)
    col = lax.broadcasted_iota(jnp.int32, (rows, cols), 1)
    hw_t = jnp.transpose(hw_ref[...])
    he_t = jnp.transpose(he_ref[...])
    above = above_ref[0] * jnp.where(i > 0, 1.0, 0.0)
    below = below_ref[0] * jnp.where(i < nblk - 1, 1.0, 0.0)
    if with_edges:
        en_ref, es_ref, ew_ref, ee_ref, arrived_ref, qw_ref, qe_ref, recv, send_sem, recv_sem = rest[1:]

        @pl.when(i == 0)
        def _():
            start_spread(buckets_ref, recv, send_sem, recv_sem)
            qw_ref[...] = jnp.zeros_like(qw_ref)
            qe_ref[...] = jnp.zeros_like(qe_ref)

    if with_edges:
        lane = lax.broadcasted_iota(jnp.int32, qw_ref.shape, 1)
        qw = qw_ref[...]
        qe = qe_ref[...]
    for l in range(LB):
        u = u_ref[l]
        prev = u_ref[l - 1] if l > 0 else above
        nxt = u_ref[l + 1] if l < LB - 1 else below
        w = wet * u
        north = jnp.where(row == 0, hn_ref[l:l + 1, :], pltpu.roll(w, 1, 0))
        south = jnp.where(row == rows - 1, hs_ref[l:l + 1, :], pltpu.roll(w, rows - 1, 0))
        west = jnp.where(col == 0, hw_t[:, l:l + 1], pltpu.roll(w, 1, 1))
        east = jnp.where(col == cols - 1, he_t[:, l:l + 1], pltpu.roll(w, cols - 1, 1))
        lateral = north + south + west + east - 4.0 * w
        vertical = prev + nxt - 2.0 * u
        res = wet * (u + horiz * lateral + vert * vertical)
        if with_force and l == 0:
            res = res + jnp.where(i == 0, 1.0, 0.0) * (force_gain * wet * force_ref[...])
        out_ref[l] = res
        if with_edges:
            fw = wet * res
            en_ref[l:l + 1, :] = fw[0:1, :]
            es_ref[l:l + 1, :] = fw[rows - 1:rows, :]
            hit = lane == i * LB + l
            qw = jnp.where(hit, fw[:, 0:1], qw)
            qe = jnp.where(hit, fw[:, cols - 1:cols], qe)

    if with_edges:
        qw_ref[...] = qw
        qe_ref[...] = qe

        @pl.when(i == nblk - 1)
        def _():
            lev = ew_ref.shape[0]
            ew_ref[...] = jnp.transpose(qw_ref[...])[0:lev, :]
            ee_ref[...] = jnp.transpose(qe_ref[...])[0:lev, :]
            finish_spread(buckets_ref, recv, send_sem, recv_sem, arrived_ref)


def edges_kernel(wet_ref, u_ref, en_ref, es_ref, ew_ref, ee_ref, qw_ref, qe_ref):
    i = pl.program_id(0)
    nblk = pl.num_programs(0)
    wet = wet_ref[...]
    rows, cols = wet.shape

    @pl.when(i == 0)
    def _():
        qw_ref[...] = jnp.zeros_like(qw_ref)
        qe_ref[...] = jnp.zeros_like(qe_ref)

    lane = lax.broadcasted_iota(jnp.int32, qw_ref.shape, 1)
    qw = qw_ref[...]
    qe = qe_ref[...]
    for l in range(LB):
        fw = wet * u_ref[l]
        en_ref[l:l + 1, :] = fw[0:1, :]
        es_ref[l:l + 1, :] = fw[rows - 1:rows, :]
        hit = lane == i * LB + l
        qw = jnp.where(hit, fw[:, 0:1], qw)
        qe = jnp.where(hit, fw[:, cols - 1:cols], qe)
    qw_ref[...] = qw
    qe_ref[...] = qe

    @pl.when(i == nblk - 1)
    def _():
        lev = ew_ref.shape[0]
        ew_ref[...] = jnp.transpose(qw_ref[...])[0:lev, :]
        ee_ref[...] = jnp.transpose(qe_ref[...])[0:lev, :]


def masked_edges(wet, u):
    lev, rows, cols = u.shape
    lvl2 = pl.BlockSpec((LB, cols), lambda i: (i, 0))
    full2 = lambda shape: pl.BlockSpec(shape, lambda i: (0, 0))
    return pl.pallas_call(
        edges_kernel,
        grid=(lev // LB,),
        in_specs=[full2((rows, cols)), pl.BlockSpec((LB, rows, cols), lambda i: (i, 0, 0))],
        out_specs=[lvl2, lvl2, full2((lev, rows)), full2((lev, rows))],
        out_shape=[jax.ShapeDtypeStruct((lev, cols), jnp.float32)] * 2
        + [jax.ShapeDtypeStruct((lev, rows), jnp.float32)] * 2,
        scratch_shapes=[pltpu.VMEM((rows, 128), jnp.float32)] * 2,
        compiler_params=pltpu.CompilerParams(dimension_semantics=("arbitrary",)),
        cost_estimate=pl.CostEstimate(flops=2 * u.size, bytes_accessed=4 * u.size, transcendentals=0),
    )(wet, u)


def force_kernel(x_ref, wet_ref, f_ref, out_ref):
    out_ref[0] = x_ref[0] + force_gain * wet_ref[...] * f_ref[...]


def add_force(x, wet, f):
    lev, rows, cols = x.shape
    plane = pl.BlockSpec((rows, cols), lambda i: (0, 0))
    level0 = pl.BlockSpec((1, rows, cols), lambda i: (0, 0, 0))
    return pl.pallas_call(
        force_kernel,
        grid=(1,),
        in_specs=[level0, plane, plane],
        out_specs=level0,
        out_shape=jax.ShapeDtypeStruct(x.shape, x.dtype),
        input_output_aliases={0: 0},
    )(x, wet, f)


def stencil_step(coef, wet, u, halos, force=None, buckets=None):
    with_edges = buckets is not None
    lev, rows, cols = u.shape
    nblk = lev // LB
    full2 = lambda shape: pl.BlockSpec(shape, lambda i: (0, 0))
    lvl2 = pl.BlockSpec((LB, cols), lambda i: (i, 0))
    in_specs = [
        pl.BlockSpec(memory_space=pltpu.SMEM),
        full2((rows, cols)),
        pl.BlockSpec((LB, rows, cols), lambda i: (i, 0, 0)),
        pl.BlockSpec((1, rows, cols), lambda i: (jnp.maximum(i * LB - 1, 0), 0, 0)),
        pl.BlockSpec((1, rows, cols), lambda i: (jnp.minimum(i * LB + LB, lev - 1), 0, 0)),
        lvl2, lvl2, lvl2, lvl2,
    ]
    args = [coef, wet, u, u, u] + list(halos)
    if force is not None:
        in_specs.append(full2((rows, cols)))
        args.append(force)
    if with_edges:
        in_specs.append(pl.BlockSpec(buckets.shape, lambda i: (0, 0, 0, 0)))
        args.append(buckets)
    out_shape = [jax.ShapeDtypeStruct((lev, rows, cols), jnp.float32)]
    out_specs = [pl.BlockSpec((LB, rows, cols), lambda i: (i, 0, 0))]
    scratch = []
    params = dict(dimension_semantics=("arbitrary",))
    if with_edges:
        out_shape += [jax.ShapeDtypeStruct((lev, cols), jnp.float32)] * 2
        out_shape += [jax.ShapeDtypeStruct((lev, rows), jnp.float32)] * 2
        out_shape += [jax.ShapeDtypeStruct(buckets.shape, buckets.dtype)]
        out_specs += [lvl2, lvl2, full2((lev, rows)), full2((lev, rows))]
        out_specs += [pl.BlockSpec(buckets.shape, lambda i: (0, 0, 0, 0))]
        scratch = [pltpu.VMEM((rows, 128), jnp.float32)] * 2 + [
            pltpu.VMEM(buckets.shape, buckets.dtype),
            pltpu.SemaphoreType.DMA((buckets.shape[0],)),
            pltpu.SemaphoreType.DMA((buckets.shape[0],)),
        ]
        params.update(collective_id=2, has_side_effects=True)
    return pl.pallas_call(
        functools.partial(stencil_kernel, with_edges, force is not None),
        grid=(nblk,),
        in_specs=in_specs,
        out_specs=out_specs,
        out_shape=out_shape,
        scratch_shapes=scratch,
        compiler_params=pltpu.CompilerParams(**params),
        cost_estimate=pl.CostEstimate(flops=30 * u.size, bytes_accessed=12 * u.size, transcendentals=0),
    )(*args)


def halo_kernel(en_ref, es_ref, ew_ref, ee_ref, hn_ref, hs_ref, hw_ref, he_ref,
                buf, send_sem, recv_sem):
    mp = lax.axis_index("mp")
    gx = lax.axis_index("gx")
    gy = lax.axis_index("gy")
    ngx = lax.axis_size("gx")
    ngy = lax.axis_size("gy")
    mesh_id = pl.DeviceIdType.MESH
    links = [
        (gx < ngx - 1, (mp, gx + 1, gy), es_ref, 0),
        (gx > 0, (mp, gx - 1, gy), en_ref, 1),
        (gy < ngy - 1, (mp, gx, gy + 1), ee_ref, 2),
        (gy > 0, (mp, gx, gy - 1), ew_ref, 3),
    ]
    barrier = pltpu.get_barrier_semaphore()
    count = jnp.int32(0)
    for present, dev, _, _ in links:
        @pl.when(present)
        def _():
            pl.semaphore_signal(barrier, 1, device_id=dev, device_id_type=mesh_id)

        count = count + present.astype(jnp.int32)
    pl.semaphore_wait(barrier, count)

    copies = []
    for present, dev, src, slot in links:
        copy = pltpu.make_async_remote_copy(
            src_ref=src,
            dst_ref=buf.at[slot],
            send_sem=send_sem.at[slot],
            recv_sem=recv_sem.at[slot],
            device_id=dev,
            device_id_type=mesh_id,
        )
        pl.when(present)(copy.start)
        copies.append((present, copy))
    for present, copy in copies:
        pl.when(present)(copy.wait_send)
    fills = [gx > 0, gx < ngx - 1, gy > 0, gy < ngy - 1]
    outs = [hn_ref, hs_ref, hw_ref, he_ref]
    for slot, (filled, out) in enumerate(zip(fills, outs)):
        _, copy = copies[slot]

        @pl.when(filled)
        def _():
            copy.wait_recv()
            out[...] = buf[slot]

        @pl.when(jnp.logical_not(filled))
        def _():
            out[...] = jnp.zeros_like(out)


def exchange(en, es, ew, ee, call):
    shape = jax.ShapeDtypeStruct(en.shape, en.dtype)
    vmem = pl.BlockSpec(memory_space=pltpu.VMEM)
    return pl.pallas_call(
        halo_kernel,
        in_specs=[vmem] * 4,
        out_specs=[vmem] * 4,
        out_shape=[shape] * 4,
        scratch_shapes=[
            pltpu.VMEM((4,) + en.shape, en.dtype),
            pltpu.SemaphoreType.DMA((4,)),
            pltpu.SemaphoreType.DMA((4,)),
        ],
        compiler_params=pltpu.CompilerParams(collective_id=call, has_side_effects=True),
    )(en, es, ew, ee)


def bucket_kernel(target_ref, row_ref, contrib_ref, out_ref, count_ref):
    ntiles = contrib_ref.shape[0]
    ndest = out_ref.shape[0]
    sub = lax.broadcasted_iota(jnp.int32, (KF, CY), 0)
    out_ref[...] = jnp.zeros_like(out_ref)

    def clear(d, carry):
        count_ref[d] = 0
        return carry

    lax.fori_loop(0, ndest, clear, 0)

    def body(t, carry):
        d = target_ref[t]
        c = count_ref[d]
        count_ref[d] = c + 1
        out_ref[d, c] = contrib_ref[t]
        out_ref[d, CAP] = jnp.where(sub == c, row_ref[t].astype(jnp.float32), out_ref[d, CAP])
        return carry

    lax.fori_loop(0, ntiles, body, 0)


def local(states, surface, land_mask, tile_weights, tile_source, tile_target, tile_row):
    group = lax.axis_index("mp")
    ndev = lax.axis_size("gx") * lax.axis_size("gy")
    state = states[0]
    lev, rows_here, cols_here = state.shape
    wet = jnp.where(
        group == 0, jnp.ones(land_mask.shape, jnp.float32), land_mask.astype(jnp.float32)
    )
    coef = jnp.stack([jnp.where(group == 0, 0.15, 0.12), jnp.where(group == 0, 0.1, 0.15)]).astype(
        jnp.float32
    )

    src = (surface[0] * wet).astype(jnp.bfloat16)
    source = tile_source[0, 0, 0]
    target = tile_target[0, 0, 0, :, 0]
    dest_row = tile_row[0, 0, 0]
    ntiles = source.shape[0]
    picked = jnp.take(src, source, axis=1)
    contrib = jnp.einsum(
        "tji,kti->tkj", tile_weights[0, 0, 0], picked, preferred_element_type=jnp.float32
    )
    buckets = pl.pallas_call(
        bucket_kernel,
        in_specs=[
            pl.BlockSpec(memory_space=pltpu.SMEM),
            pl.BlockSpec(memory_space=pltpu.SMEM),
            pl.BlockSpec(memory_space=pltpu.VMEM),
        ],
        out_specs=pl.BlockSpec(memory_space=pltpu.VMEM),
        out_shape=jax.ShapeDtypeStruct((ndev, CAP + 1, KF, CY), jnp.float32),
        scratch_shapes=[pltpu.SMEM((ndev,), jnp.int32)],
    )(target, dest_row, contrib)
    second, arrived = interval(coef, wet, state, buckets, masked_edges(wet, state))
    got_rows = arrived[:, CAP, :, 0].astype(jnp.int32)
    select = (
        got_rows[:, :, None] == jnp.arange(rows_here, dtype=jnp.int32)[None, None, :]
    ).astype(jnp.float32)
    sent = jnp.einsum(
        "scr,sckj->krj", select, arrived[:, :CAP], precision=lax.Precision.HIGHEST
    )
    received = lax.ppermute(sent, "mp", [(0, 1), (1, 0)])

    second = add_force(second, wet, received[0])
    return (second[None], received[None])


def solution(mesh):
    return jax.shard_map(
        local,
        mesh=mesh,
        in_specs=(
            P("mp", None, "gx", "gy"),
            P("mp", None, "gx", "gy"),
            P("gx", "gy"),
            P("mp", "gx", "gy", None, None, None),
            P("mp", "gx", "gy", None),
            P("mp", "gx", "gy", None, None),
            P("mp", "gx", "gy", None),
        ),
        out_specs=(P("mp", None, "gx", "gy"), P("mp", None, "gx", "gy")),
        check_vma=False,
    )
```

```python
import functools

import jax
import jax.numpy as jnp
from jax import lax
from jax.experimental import pallas as pl
from jax.experimental.pallas import tpu as pltpu
from jax.sharding import PartitionSpec as P

CY = 128
KF = 8
CAP = 8
LB = 8

force_gain = 0.5


def shift_pairs(devices, forward):
    up = [(i, i + 1) for i in range(devices - 1)]
    return up if forward else [(j, i) for i, j in up]


def start_spread(buckets_ref, recv, send_sem, recv_sem, first_out=None):
    mp = lax.axis_index("mp")
    ngy = lax.axis_size("gy")
    ndev = lax.axis_size("gx") * ngy
    me = lax.axis_index("gx") * ngy + lax.axis_index("gy")
    mesh_id = pl.DeviceIdType.MESH
    barrier = pltpu.get_barrier_semaphore()

    def greet(d, carry):
        @pl.when(d != me)
        def _():
            pl.semaphore_signal(barrier, 1, device_id=(mp, d // ngy, d % ngy), device_id_type=mesh_id)

        return carry

    lax.fori_loop(0, ndev, greet, 0)
    pl.semaphore_wait(barrier, ndev - 1)
    if first_out is not None:
        first_out()
    recv[me] = buckets_ref[me]

    def send(k, carry):
        d = (me + k) % ndev
        pltpu.make_async_remote_copy(
            src_ref=buckets_ref.at[d],
            dst_ref=recv.at[me],
            send_sem=send_sem.at[d],
            recv_sem=recv_sem.at[me],
            device_id=(mp, d // ngy, d % ngy),
            device_id_type=mesh_id,
        ).start()
        return carry

    lax.fori_loop(1, ndev, send, 0)


def finish_spread(buckets_ref, recv, send_sem, recv_sem, arrived_ref):
    ngy = lax.axis_size("gy")
    ndev = lax.axis_size("gx") * ngy
    me = lax.axis_index("gx") * ngy + lax.axis_index("gy")

    def wait(d, carry):
        @pl.when(d != me)
        def _():
            copy = pltpu.make_async_remote_copy(
                src_ref=buckets_ref.at[d],
                dst_ref=recv.at[d],
                send_sem=send_sem.at[d],
                recv_sem=recv_sem.at[d],
                device_id=(lax.axis_index("mp"), d // ngy, d % ngy),
                device_id_type=pl.DeviceIdType.MESH,
            )
            copy.wait_send()
            copy.wait_recv()

        return carry

    lax.fori_loop(0, ndev, wait, 0)
    arrived_ref[...] = recv[...]


def interval_kernel(coef_ref, wet_ref, u_ref, above_ref, below_ref, buckets_ref,
                    e0n, e0s, e0w, e0e,
                    out_ref, arrived_ref,
                    first, edge1, halo0, halo1, qw_ref, qe_ref, recv,
                    send_sem, recv_sem, hsend, hrecv):
    p = pl.program_id(0)
    i = pl.program_id(1)
    nblk = pl.num_programs(1)
    wet = wet_ref[...]
    rows, cols = wet.shape
    lev = first.shape[0]
    mp = lax.axis_index("mp")
    gx = lax.axis_index("gx")
    gy = lax.axis_index("gy")
    ngx = lax.axis_size("gx")
    ngy = lax.axis_size("gy")
    ndev = ngx * ngy
    me = gx * ngy + gy
    mesh_id = pl.DeviceIdType.MESH
    links = [
        (gx < ngx - 1, (mp, gx + 1, gy), 1, 0),
        (gx > 0, (mp, gx - 1, gy), 0, 1),
        (gy < ngy - 1, (mp, gx, gy + 1), 3, 2),
        (gy > 0, (mp, gx, gy - 1), 2, 3),
    ]
    fills = [gx > 0, gx < ngx - 1, gy > 0, gy < ngy - 1]
    edge0 = [e0n, e0s, e0w, e0e]

    def halo_copy(stage, src, slot, dev):
        srcs = edge0[src] if stage == 0 else edge1.at[src]
        dsts = halo0.at[slot] if stage == 0 else halo1.at[slot]
        return pltpu.make_async_remote_copy(
            src_ref=srcs,
            dst_ref=dsts,
            send_sem=hsend.at[stage, slot],
            recv_sem=hrecv.at[stage, slot],
            device_id=dev,
            device_id_type=mesh_id,
        )

    def send_halos(stage):
        for present, dev, src, slot in links:
            pl.when(present)(halo_copy(stage, src, slot, dev).start)

    def take_halos(stage, dst):
        for present, dev, src, slot in links:
            pl.when(present)(halo_copy(stage, src, slot, dev).wait_send)
        for slot, filled in enumerate(fills):
            _, dev, src, _ = links[slot]
            pl.when(filled)(halo_copy(stage, src, slot, dev).wait_recv)

            @pl.when(jnp.logical_not(filled))
            def _():
                dst[slot] = jnp.zeros_like(dst[slot])

    def bucket_copy(d):
        return pltpu.make_async_remote_copy(
            src_ref=buckets_ref.at[d],
            dst_ref=recv.at[me],
            send_sem=send_sem.at[d],
            recv_sem=recv_sem.at[me],
            device_id=(mp, d // ngy, d % ngy),
            device_id_type=mesh_id,
        )

    def issue(k0, count):
        for n in range(count):
            k = k0 + n

            @pl.when(k < ndev)
            def _():
                bucket_copy((me + k) % ndev).start()

    lane = lax.broadcasted_iota(jnp.int32, qw_ref.shape, 1)
    row = lax.broadcasted_iota(jnp.int32, (rows, cols), 0)
    col = lax.broadcasted_iota(jnp.int32, (rows, cols), 1)
    horiz = coef_ref[0]
    vert = coef_ref[1]

    def step(load, above, below, hn, hs, hw_t, he_t, store):
        for l in range(LB):
            u = load(l)
            prev = load(l - 1) if l > 0 else above
            nxt = load(l + 1) if l < LB - 1 else below
            w = wet * u
            north = jnp.where(row == 0, hn[l:l + 1, :], pltpu.roll(w, 1, 0))
            south = jnp.where(row == rows - 1, hs[l:l + 1, :], pltpu.roll(w, rows - 1, 0))
            west = jnp.where(col == 0, hw_t[:, l:l + 1], pltpu.roll(w, 1, 1))
            east = jnp.where(col == cols - 1, he_t[:, l:l + 1], pltpu.roll(w, cols - 1, 1))
            lateral = north + south + west + east - 4.0 * w
            vertical = prev + nxt - 2.0 * u
            store(l, wet * (u + horiz * lateral + vert * vertical))

    @pl.when((p == 0) & (i == 0))
    def _():
        barrier = pltpu.get_barrier_semaphore()

        def greet(d, carry):
            @pl.when(d != me)
            def _():
                pl.semaphore_signal(barrier, 1, device_id=(mp, d // ngy, d % ngy), device_id_type=mesh_id)

            return carry

        lax.fori_loop(0, ndev, greet, 0)
        pl.semaphore_wait(barrier, ndev - 1)
        send_halos(0)
        recv[me] = buckets_ref[me]
        take_halos(0, halo0)
        qw_ref[...] = jnp.zeros_like(qw_ref)
        qe_ref[...] = jnp.zeros_like(qe_ref)

    @pl.when(p == 0)
    def _():
        issue(1 + 3 * i, 3)
        blk = pl.ds(pl.multiple_of(i * LB, LB), LB)
        hn = halo0[0, blk]
        hs = halo0[1, blk]
        hw_t = jnp.transpose(halo0[2, blk])
        he_t = jnp.transpose(halo0[3, blk])
        above = above_ref[0] * jnp.where(i > 0, 1.0, 0.0)
        below = below_ref[0] * jnp.where(i < nblk - 1, 1.0, 0.0)
        qs = [qw_ref[...], qe_ref[...]]

        def store(l, res):
            first[i * LB + l] = res
            fw = wet * res
            edge1[0, i, l:l + 1, :] = fw[0:1, :]
            edge1[1, i, l:l + 1, :] = fw[rows - 1:rows, :]
            hit = lane == i * LB + l
            qs[0] = jnp.where(hit, fw[:, 0:1], qs[0])
            qs[1] = jnp.where(hit, fw[:, cols - 1:cols], qs[1])

        step(lambda l: u_ref[l], above, below, hn, hs, hw_t, he_t, store)
        qw_ref[...] = qs[0]
        qe_ref[...] = qs[1]

    @pl.when((p == 0) & (i == nblk - 1))
    def _():
        edge1[2] = jnp.transpose(qw_ref[...])[0:lev, :].reshape(nblk, LB, rows)
        edge1[3] = jnp.transpose(qe_ref[...])[0:lev, :].reshape(nblk, LB, rows)
        send_halos(1)

    @pl.when((p == 1) & (i == 0))
    def _():
        take_halos(1, halo1)

        def late(k, carry):
            bucket_copy((me + k) % ndev).start()
            return carry

        lax.fori_loop(min(1 + 3 * nblk, ndev), ndev, late, 0)

    @pl.when(p == 1)
    def _():
        base = i * LB
        above = first[jnp.maximum(base - 1, 0)] * jnp.where(i > 0, 1.0, 0.0)
        below = first[jnp.minimum(base + LB, lev - 1)] * jnp.where(i < nblk - 1, 1.0, 0.0)
        hw_t = jnp.transpose(halo1[2, i])
        he_t = jnp.transpose(halo1[3, i])

        def store(l, res):
            out_ref[l] = res

        step(lambda l: first[base + l], above, below, halo1[0, i], halo1[1, i], hw_t, he_t, store)

    @pl.when((p == 1) & (i == nblk - 1))
    def _():
        def wait(d, carry):
            @pl.when(d != me)
            def _():
                copy = pltpu.make_async_remote_copy(
                    src_ref=buckets_ref.at[d],
                    dst_ref=recv.at[d],
                    send_sem=send_sem.at[d],
                    recv_sem=recv_sem.at[d],
                    device_id=(mp, d // ngy, d % ngy),
                    device_id_type=mesh_id,
                )
                copy.wait_send()
                copy.wait_recv()

            return carry

        lax.fori_loop(0, ndev, wait, 0)
        arrived_ref[...] = recv[...]


def interval(coef, wet, u, buckets, edges):
    lev, rows, cols = u.shape
    nblk = lev // LB
    full2 = lambda shape: pl.BlockSpec(shape, lambda p, i: (0, 0))
    whole = pl.BlockSpec(buckets.shape, lambda p, i: (0, 0, 0, 0))
    held = lambda p, i: i + p * (nblk - 1 - i)
    in_specs = [
        pl.BlockSpec(memory_space=pltpu.SMEM),
        full2((rows, cols)),
        pl.BlockSpec((LB, rows, cols), lambda p, i: (held(p, i), 0, 0)),
        pl.BlockSpec((1, rows, cols), lambda p, i: (jnp.maximum(held(p, i) * LB - 1, 0), 0, 0)),
        pl.BlockSpec((1, rows, cols), lambda p, i: (jnp.minimum(held(p, i) * LB + LB, lev - 1), 0, 0)),
        whole,
    ] + [full2((lev, cols))] * 4
    out_shape = [
        jax.ShapeDtypeStruct((lev, rows, cols), jnp.float32),
        jax.ShapeDtypeStruct(buckets.shape, buckets.dtype),
    ]
    out_specs = [pl.BlockSpec((LB, rows, cols), lambda p, i: (i * p, 0, 0)), whole]
    scratch = [
        pltpu.VMEM((lev, rows, cols), jnp.float32),
        pltpu.VMEM((4, nblk, LB, cols), jnp.float32),
        pltpu.VMEM((4, lev, cols), jnp.float32),
        pltpu.VMEM((4, nblk, LB, cols), jnp.float32),
        pltpu.VMEM((rows, 128), jnp.float32),
        pltpu.VMEM((rows, 128), jnp.float32),
        pltpu.VMEM(buckets.shape, buckets.dtype),
        pltpu.SemaphoreType.DMA((buckets.shape[0],)),
        pltpu.SemaphoreType.DMA((buckets.shape[0],)),
        pltpu.SemaphoreType.DMA((2, 4)),
        pltpu.SemaphoreType.DMA((2, 4)),
    ]
    return pl.pallas_call(
        interval_kernel,
        grid=(2, nblk),
        in_specs=in_specs,
        out_specs=out_specs,
        out_shape=out_shape,
        scratch_shapes=scratch,
        compiler_params=pltpu.CompilerParams(
            dimension_semantics=("arbitrary", "arbitrary"), collective_id=3, has_side_effects=True,
            vmem_limit_bytes=48 * 1024 * 1024,
        ),
        cost_estimate=pl.CostEstimate(flops=60 * u.size, bytes_accessed=12 * u.size, transcendentals=0),
    )(coef, wet, u, u, u, buckets, *edges)


def first_kernel(coef_ref, wet_ref, u_ref, above_ref, below_ref, buckets_ref,
                 e0n, e0s, e0w, e0e,
                 out_ref, en_ref, es_ref, ew_ref, ee_ref, arrived_ref,
                 halo, qw_ref, qe_ref, recv, send_sem, recv_sem, hsend, hrecv):
    i = pl.program_id(0)
    nblk = pl.num_programs(0)
    edge0 = [e0n, e0s, e0w, e0e]
    wet = wet_ref[...]
    rows, cols = wet.shape
    lev = ew_ref.shape[0]
    mp = lax.axis_index("mp")
    gx = lax.axis_index("gx")
    gy = lax.axis_index("gy")
    ngx = lax.axis_size("gx")
    ngy = lax.axis_size("gy")
    mesh_id = pl.DeviceIdType.MESH
    links = [
        (gx < ngx - 1, (mp, gx + 1, gy), 1, 0),
        (gx > 0, (mp, gx - 1, gy), 0, 1),
        (gy < ngy - 1, (mp, gx, gy + 1), 3, 2),
        (gy > 0, (mp, gx, gy - 1), 2, 3),
    ]
    fills = [gx > 0, gx < ngx - 1, gy > 0, gy < ngy - 1]
    copies = [
        pltpu.make_async_remote_copy(
            src_ref=edge0[src],
            dst_ref=halo.at[slot],
            send_sem=hsend.at[slot],
            recv_sem=hrecv.at[slot],
            device_id=dev,
            device_id_type=mesh_id,
        )
        for _, dev, src, slot in links
    ]
    lane = lax.broadcasted_iota(jnp.int32, qw_ref.shape, 1)

    def send_halos():
        for (present, _, _, _), copy in zip(links, copies):
            pl.when(present)(copy.start)

    @pl.when(i == 0)
    def _():
        start_spread(buckets_ref, recv, send_sem, recv_sem, send_halos)
        for (present, _, _, _), copy in zip(links, copies):
            pl.when(present)(copy.wait_send)
        for slot, filled in enumerate(fills):
            pl.when(filled)(copies[slot].wait_recv)

            @pl.when(jnp.logical_not(filled))
            def _():
                halo[slot] = jnp.zeros_like(halo[slot])

        qw_ref[...] = jnp.zeros_like(qw_ref)
        qe_ref[...] = jnp.zeros_like(qe_ref)

    def _():
        horiz = coef_ref[0]
        vert = coef_ref[1]
        row = lax.broadcasted_iota(jnp.int32, (rows, cols), 0)
        col = lax.broadcasted_iota(jnp.int32, (rows, cols), 1)
        hn = halo[0, pl.ds(i * LB, LB)]
        hs = halo[1, pl.ds(i * LB, LB)]
        hw_t = jnp.transpose(halo[2, pl.ds(i * LB, LB)])
        he_t = jnp.transpose(halo[3, pl.ds(i * LB, LB)])
        above = above_ref[0] * jnp.where(i > 0, 1.0, 0.0)
        below = below_ref[0] * jnp.where(i < nblk - 1, 1.0, 0.0)
        qw = qw_ref[...]
        qe = qe_ref[...]
        for l in range(LB):
            u = u_ref[l]
            prev = u_ref[l - 1] if l > 0 else above
            nxt = u_ref[l + 1] if l < LB - 1 else below
            w = wet * u
            north = jnp.where(row == 0, hn[l:l + 1, :], pltpu.roll(w, 1, 0))
            south = jnp.where(row == rows - 1, hs[l:l + 1, :], pltpu.roll(w, rows - 1, 0))
            west = jnp.where(col == 0, hw_t[:, l:l + 1], pltpu.roll(w, 1, 1))
            east = jnp.where(col == cols - 1, he_t[:, l:l + 1], pltpu.roll(w, cols - 1, 1))
            lateral = north + south + west + east - 4.0 * w
            vertical = prev + nxt - 2.0 * u
            res = wet * (u + horiz * lateral + vert * vertical)
            out_ref[l] = res
            fw = wet * res
            en_ref[l:l + 1, :] = fw[0:1, :]
            es_ref[l:l + 1, :] = fw[rows - 1:rows, :]
            hit = lane == i * LB + l
            qw = jnp.where(hit, fw[:, 0:1], qw)
            qe = jnp.where(hit, fw[:, cols - 1:cols], qe)
        qw_ref[...] = qw
        qe_ref[...] = qe

    _()

    @pl.when(i == nblk - 1)
    def _():
        ew_ref[...] = jnp.transpose(qw_ref[...])[0:lev, :]
        ee_ref[...] = jnp.transpose(qe_ref[...])[0:lev, :]
        finish_spread(buckets_ref, recv, send_sem, recv_sem, arrived_ref)


def first_step(coef, wet, u, buckets, edges):
    lev, rows, cols = u.shape
    nblk = lev // LB
    full2 = lambda shape: pl.BlockSpec(shape, lambda i: (0, 0))
    lvl2 = pl.BlockSpec((LB, cols), lambda i: (i, 0))
    whole = pl.BlockSpec(buckets.shape, lambda i: (0, 0, 0, 0))
    in_specs = [
        pl.BlockSpec(memory_space=pltpu.SMEM),
        full2((rows, cols)),
        pl.BlockSpec((LB, rows, cols), lambda i: (i, 0, 0)),
        pl.BlockSpec((1, rows, cols), lambda i: (jnp.maximum(i * LB - 1, 0), 0, 0)),
        pl.BlockSpec((1, rows, cols), lambda i: (jnp.minimum(i * LB + LB, lev - 1), 0, 0)),
        whole,
    ] + [full2((lev, cols))] * 4
    out_shape = [
        jax.ShapeDtypeStruct((lev, rows, cols), jnp.float32),
        jax.ShapeDtypeStruct((lev, cols), jnp.float32),
        jax.ShapeDtypeStruct((lev, cols), jnp.float32),
        jax.ShapeDtypeStruct((lev, rows), jnp.float32),
        jax.ShapeDtypeStruct((lev, rows), jnp.float32),
        jax.ShapeDtypeStruct(buckets.shape, buckets.dtype),
    ]
    out_specs = [
        pl.BlockSpec((LB, rows, cols), lambda i: (i, 0, 0)),
        lvl2, lvl2, full2((lev, rows)), full2((lev, rows)), whole,
    ]
    scratch = [
        pltpu.VMEM((4, lev, cols), jnp.float32),
        pltpu.VMEM((rows, 128), jnp.float32),
        pltpu.VMEM((rows, 128), jnp.float32),
        pltpu.VMEM(buckets.shape, buckets.dtype),
        pltpu.SemaphoreType.DMA((buckets.shape[0],)),
        pltpu.SemaphoreType.DMA((buckets.shape[0],)),
        pltpu.SemaphoreType.DMA((4,)),
        pltpu.SemaphoreType.DMA((4,)),
    ]
    return pl.pallas_call(
        first_kernel,
        grid=(nblk,),
        in_specs=in_specs,
        out_specs=out_specs,
        out_shape=out_shape,
        scratch_shapes=scratch,
        compiler_params=pltpu.CompilerParams(
            dimension_semantics=("arbitrary",), collective_id=2, has_side_effects=True
        ),
        cost_estimate=pl.CostEstimate(flops=30 * u.size, bytes_accessed=12 * u.size, transcendentals=0),
    )(coef, wet, u, u, u, buckets, *edges)


def stencil_kernel(with_edges, with_force, coef_ref, wet_ref, u_ref, above_ref, below_ref,
                   hn_ref, hs_ref, hw_ref, he_ref, *rest):
    if with_force:
        force_ref, rest = rest[0], rest[1:]
    if with_edges:
        buckets_ref, rest = rest[0], rest[1:]
    out_ref = rest[0]
    i = pl.program_id(0)
    nblk = pl.num_programs(0)
    horiz = coef_ref[0]
    vert = coef_ref[1]
    wet = wet_ref[...]
    rows, cols = wet.shape
    row = lax.broadcasted_iota(jnp.int32, (rows, cols), 0)
    col = lax.broadcasted_iota(jnp.int32, (rows, cols), 1)
    hw_t = jnp.transpose(hw_ref[...])
    he_t = jnp.transpose(he_ref[...])
    above = above_ref[0] * jnp.where(i > 0, 1.0, 0.0)
    below = below_ref[0] * jnp.where(i < nblk - 1, 1.0, 0.0)
    if with_edges:
        en_ref, es_ref, ew_ref, ee_ref, arrived_ref, qw_ref, qe_ref, recv, send_sem, recv_sem = rest[1:]

        @pl.when(i == 0)
        def _():
            start_spread(buckets_ref, recv, send_sem, recv_sem)
            qw_ref[...] = jnp.zeros_like(qw_ref)
            qe_ref[...] = jnp.zeros_like(qe_ref)

    if with_edges:
        lane = lax.broadcasted_iota(jnp.int32, qw_ref.shape, 1)
        qw = qw_ref[...]
        qe = qe_ref[...]
    for l in range(LB):
        u = u_ref[l]
        prev = u_ref[l - 1] if l > 0 else above
        nxt = u_ref[l + 1] if l < LB - 1 else below
        w = wet * u
        north = jnp.where(row == 0, hn_ref[l:l + 1, :], pltpu.roll(w, 1, 0))
        south = jnp.where(row == rows - 1, hs_ref[l:l + 1, :], pltpu.roll(w, rows - 1, 0))
        west = jnp.where(col == 0, hw_t[:, l:l + 1], pltpu.roll(w, 1, 1))
        east = jnp.where(col == cols - 1, he_t[:, l:l + 1], pltpu.roll(w, cols - 1, 1))
        lateral = north + south + west + east - 4.0 * w
        vertical = prev + nxt - 2.0 * u
        res = wet * (u + horiz * lateral + vert * vertical)
        if with_force and l == 0:
            res = res + jnp.where(i == 0, 1.0, 0.0) * (force_gain * wet * force_ref[...])
        out_ref[l] = res
        if with_edges:
            fw = wet * res
            en_ref[l:l + 1, :] = fw[0:1, :]
            es_ref[l:l + 1, :] = fw[rows - 1:rows, :]
            hit = lane == i * LB + l
            qw = jnp.where(hit, fw[:, 0:1], qw)
            qe = jnp.where(hit, fw[:, cols - 1:cols], qe)

    if with_edges:
        qw_ref[...] = qw
        qe_ref[...] = qe

        @pl.when(i == nblk - 1)
        def _():
            lev = ew_ref.shape[0]
            ew_ref[...] = jnp.transpose(qw_ref[...])[0:lev, :]
            ee_ref[...] = jnp.transpose(qe_ref[...])[0:lev, :]
            finish_spread(buckets_ref, recv, send_sem, recv_sem, arrived_ref)


def edges_kernel(wet_ref, u_ref, en_ref, es_ref, ew_ref, ee_ref, qw_ref, qe_ref):
    i = pl.program_id(0)
    nblk = pl.num_programs(0)
    wet = wet_ref[...]
    rows, cols = wet.shape

    @pl.when(i == 0)
    def _():
        qw_ref[...] = jnp.zeros_like(qw_ref)
        qe_ref[...] = jnp.zeros_like(qe_ref)

    lane = lax.broadcasted_iota(jnp.int32, qw_ref.shape, 1)
    qw = qw_ref[...]
    qe = qe_ref[...]
    for l in range(LB):
        fw = wet * u_ref[l]
        en_ref[l:l + 1, :] = fw[0:1, :]
        es_ref[l:l + 1, :] = fw[rows - 1:rows, :]
        hit = lane == i * LB + l
        qw = jnp.where(hit, fw[:, 0:1], qw)
        qe = jnp.where(hit, fw[:, cols - 1:cols], qe)
    qw_ref[...] = qw
    qe_ref[...] = qe

    @pl.when(i == nblk - 1)
    def _():
        lev = ew_ref.shape[0]
        ew_ref[...] = jnp.transpose(qw_ref[...])[0:lev, :]
        ee_ref[...] = jnp.transpose(qe_ref[...])[0:lev, :]


def masked_edges(wet, u):
    lev, rows, cols = u.shape
    lvl2 = pl.BlockSpec((LB, cols), lambda i: (i, 0))
    full2 = lambda shape: pl.BlockSpec(shape, lambda i: (0, 0))
    return pl.pallas_call(
        edges_kernel,
        grid=(lev // LB,),
        in_specs=[full2((rows, cols)), pl.BlockSpec((LB, rows, cols), lambda i: (i, 0, 0))],
        out_specs=[lvl2, lvl2, full2((lev, rows)), full2((lev, rows))],
        out_shape=[jax.ShapeDtypeStruct((lev, cols), jnp.float32)] * 2
        + [jax.ShapeDtypeStruct((lev, rows), jnp.float32)] * 2,
        scratch_shapes=[pltpu.VMEM((rows, 128), jnp.float32)] * 2,
        compiler_params=pltpu.CompilerParams(dimension_semantics=("arbitrary",)),
        cost_estimate=pl.CostEstimate(flops=2 * u.size, bytes_accessed=4 * u.size, transcendentals=0),
    )(wet, u)


def force_kernel(x_ref, wet_ref, f_ref, out_ref):
    out_ref[0] = x_ref[0] + force_gain * wet_ref[...] * f_ref[...]


def add_force(x, wet, f):
    lev, rows, cols = x.shape
    plane = pl.BlockSpec((rows, cols), lambda i: (0, 0))
    level0 = pl.BlockSpec((1, rows, cols), lambda i: (0, 0, 0))
    return pl.pallas_call(
        force_kernel,
        grid=(1,),
        in_specs=[level0, plane, plane],
        out_specs=level0,
        out_shape=jax.ShapeDtypeStruct(x.shape, x.dtype),
        input_output_aliases={0: 0},
    )(x, wet, f)


def stencil_step(coef, wet, u, halos, force=None, buckets=None):
    with_edges = buckets is not None
    lev, rows, cols = u.shape
    nblk = lev // LB
    full2 = lambda shape: pl.BlockSpec(shape, lambda i: (0, 0))
    lvl2 = pl.BlockSpec((LB, cols), lambda i: (i, 0))
    in_specs = [
        pl.BlockSpec(memory_space=pltpu.SMEM),
        full2((rows, cols)),
        pl.BlockSpec((LB, rows, cols), lambda i: (i, 0, 0)),
        pl.BlockSpec((1, rows, cols), lambda i: (jnp.maximum(i * LB - 1, 0), 0, 0)),
        pl.BlockSpec((1, rows, cols), lambda i: (jnp.minimum(i * LB + LB, lev - 1), 0, 0)),
        lvl2, lvl2, lvl2, lvl2,
    ]
    args = [coef, wet, u, u, u] + list(halos)
    if force is not None:
        in_specs.append(full2((rows, cols)))
        args.append(force)
    if with_edges:
        in_specs.append(pl.BlockSpec(buckets.shape, lambda i: (0, 0, 0, 0)))
        args.append(buckets)
    out_shape = [jax.ShapeDtypeStruct((lev, rows, cols), jnp.float32)]
    out_specs = [pl.BlockSpec((LB, rows, cols), lambda i: (i, 0, 0))]
    scratch = []
    params = dict(dimension_semantics=("arbitrary",))
    if with_edges:
        out_shape += [jax.ShapeDtypeStruct((lev, cols), jnp.float32)] * 2
        out_shape += [jax.ShapeDtypeStruct((lev, rows), jnp.float32)] * 2
        out_shape += [jax.ShapeDtypeStruct(buckets.shape, buckets.dtype)]
        out_specs += [lvl2, lvl2, full2((lev, rows)), full2((lev, rows))]
        out_specs += [pl.BlockSpec(buckets.shape, lambda i: (0, 0, 0, 0))]
        scratch = [pltpu.VMEM((rows, 128), jnp.float32)] * 2 + [
            pltpu.VMEM(buckets.shape, buckets.dtype),
            pltpu.SemaphoreType.DMA((buckets.shape[0],)),
            pltpu.SemaphoreType.DMA((buckets.shape[0],)),
        ]
        params.update(collective_id=2, has_side_effects=True)
    return pl.pallas_call(
        functools.partial(stencil_kernel, with_edges, force is not None),
        grid=(nblk,),
        in_specs=in_specs,
        out_specs=out_specs,
        out_shape=out_shape,
        scratch_shapes=scratch,
        compiler_params=pltpu.CompilerParams(**params),
        cost_estimate=pl.CostEstimate(flops=30 * u.size, bytes_accessed=12 * u.size, transcendentals=0),
    )(*args)


def halo_kernel(en_ref, es_ref, ew_ref, ee_ref, hn_ref, hs_ref, hw_ref, he_ref,
                buf, send_sem, recv_sem):
    mp = lax.axis_index("mp")
    gx = lax.axis_index("gx")
    gy = lax.axis_index("gy")
    ngx = lax.axis_size("gx")
    ngy = lax.axis_size("gy")
    mesh_id = pl.DeviceIdType.MESH
    links = [
        (gx < ngx - 1, (mp, gx + 1, gy), es_ref, 0),
        (gx > 0, (mp, gx - 1, gy), en_ref, 1),
        (gy < ngy - 1, (mp, gx, gy + 1), ee_ref, 2),
        (gy > 0, (mp, gx, gy - 1), ew_ref, 3),
    ]
    barrier = pltpu.get_barrier_semaphore()
    count = jnp.int32(0)
    for present, dev, _, _ in links:
        @pl.when(present)
        def _():
            pl.semaphore_signal(barrier, 1, device_id=dev, device_id_type=mesh_id)

        count = count + present.astype(jnp.int32)
    pl.semaphore_wait(barrier, count)

    copies = []
    for present, dev, src, slot in links:
        copy = pltpu.make_async_remote_copy(
            src_ref=src,
            dst_ref=buf.at[slot],
            send_sem=send_sem.at[slot],
            recv_sem=recv_sem.at[slot],
            device_id=dev,
            device_id_type=mesh_id,
        )
        pl.when(present)(copy.start)
        copies.append((present, copy))
    for present, copy in copies:
        pl.when(present)(copy.wait_send)
    fills = [gx > 0, gx < ngx - 1, gy > 0, gy < ngy - 1]
    outs = [hn_ref, hs_ref, hw_ref, he_ref]
    for slot, (filled, out) in enumerate(zip(fills, outs)):
        _, copy = copies[slot]

        @pl.when(filled)
        def _():
            copy.wait_recv()
            out[...] = buf[slot]

        @pl.when(jnp.logical_not(filled))
        def _():
            out[...] = jnp.zeros_like(out)


def exchange(en, es, ew, ee, call):
    shape = jax.ShapeDtypeStruct(en.shape, en.dtype)
    vmem = pl.BlockSpec(memory_space=pltpu.VMEM)
    return pl.pallas_call(
        halo_kernel,
        in_specs=[vmem] * 4,
        out_specs=[vmem] * 4,
        out_shape=[shape] * 4,
        scratch_shapes=[
            pltpu.VMEM((4,) + en.shape, en.dtype),
            pltpu.SemaphoreType.DMA((4,)),
            pltpu.SemaphoreType.DMA((4,)),
        ],
        compiler_params=pltpu.CompilerParams(collective_id=call, has_side_effects=True),
    )(en, es, ew, ee)


def bucket_kernel(target_ref, row_ref, contrib_ref, out_ref, count_ref):
    ntiles = contrib_ref.shape[0]
    ndest = out_ref.shape[0]
    sub = lax.broadcasted_iota(jnp.int32, (KF, CY), 0)
    out_ref[...] = jnp.zeros_like(out_ref)

    def clear(d, carry):
        count_ref[d] = 0
        return carry

    lax.fori_loop(0, ndest, clear, 0)

    def body(t, carry):
        d = target_ref[t]
        c = count_ref[d]
        count_ref[d] = c + 1
        out_ref[d, c] = contrib_ref[t]
        out_ref[d, CAP] = jnp.where(sub == c, row_ref[t].astype(jnp.float32), out_ref[d, CAP])
        return carry

    lax.fori_loop(0, ntiles, body, 0, unroll=8)


def local(states, surface, land_mask, tile_weights, tile_source, tile_target, tile_row):
    group = lax.axis_index("mp")
    ndev = lax.axis_size("gx") * lax.axis_size("gy")
    state = states[0]
    lev, rows_here, cols_here = state.shape
    wet = jnp.where(
        group == 0, jnp.ones(land_mask.shape, jnp.float32), land_mask.astype(jnp.float32)
    )
    coef = jnp.stack([jnp.where(group == 0, 0.15, 0.12), jnp.where(group == 0, 0.1, 0.15)]).astype(
        jnp.float32
    )

    src = (surface[0] * wet).astype(jnp.bfloat16)
    source = tile_source[0, 0, 0]
    target = tile_target[0, 0, 0, :, 0]
    dest_row = tile_row[0, 0, 0]
    ntiles = source.shape[0]
    picked = jnp.take(src, source, axis=1)
    contrib = jnp.einsum(
        "tji,kti->tkj", tile_weights[0, 0, 0], picked, preferred_element_type=jnp.float32
    )
    buckets = pl.pallas_call(
        bucket_kernel,
        in_specs=[
            pl.BlockSpec(memory_space=pltpu.SMEM),
            pl.BlockSpec(memory_space=pltpu.SMEM),
            pl.BlockSpec(memory_space=pltpu.VMEM),
        ],
        out_specs=pl.BlockSpec(memory_space=pltpu.VMEM),
        out_shape=jax.ShapeDtypeStruct((ndev, CAP + 1, KF, CY), jnp.float32),
        scratch_shapes=[pltpu.SMEM((ndev,), jnp.int32)],
    )(target, dest_row, contrib)
    second, arrived = interval(coef, wet, state, buckets, masked_edges(wet, state))
    got_rows = arrived[:, CAP, :, 0].astype(jnp.int32)
    select = (
        got_rows[:, :, None] == jnp.arange(rows_here, dtype=jnp.int32)[None, None, :]
    ).astype(jnp.float32)
    sent = jnp.einsum(
        "scr,sckj->krj", select, arrived[:, :CAP], precision=lax.Precision.HIGHEST
    )
    received = lax.ppermute(sent, "mp", [(0, 1), (1, 0)])

    second = add_force(second, wet, received[0])
    return (second[None], received[None])


def solution(mesh):
    return jax.shard_map(
        local,
        mesh=mesh,
        in_specs=(
            P("mp", None, "gx", "gy"),
            P("mp", None, "gx", "gy"),
            P("gx", "gy"),
            P("mp", "gx", "gy", None, None, None),
            P("mp", "gx", "gy", None),
            P("mp", "gx", "gy", None, None),
            P("mp", "gx", "gy", None),
        ),
        out_specs=(P("mp", None, "gx", "gy"), P("mp", None, "gx", "gy")),
        check_vma=False,
    )
```

```python
import functools

import jax
import jax.numpy as jnp
from jax import lax
from jax.experimental import pallas as pl
from jax.experimental.pallas import tpu as pltpu
from jax.sharding import PartitionSpec as P

CY = 128
KF = 8
CAP = 8
LB = 8
EB = 16

force_gain = 0.5


def shift_pairs(devices, forward):
    up = [(i, i + 1) for i in range(devices - 1)]
    return up if forward else [(j, i) for i, j in up]


def start_spread(buckets_ref, recv, send_sem, recv_sem, first_out=None):
    mp = lax.axis_index("mp")
    ngy = lax.axis_size("gy")
    ndev = lax.axis_size("gx") * ngy
    me = lax.axis_index("gx") * ngy + lax.axis_index("gy")
    mesh_id = pl.DeviceIdType.MESH
    barrier = pltpu.get_barrier_semaphore()

    def greet(d, carry):
        @pl.when(d != me)
        def _():
            pl.semaphore_signal(barrier, 1, device_id=(mp, d // ngy, d % ngy), device_id_type=mesh_id)

        return carry

    lax.fori_loop(0, ndev, greet, 0)
    pl.semaphore_wait(barrier, ndev - 1)
    if first_out is not None:
        first_out()
    recv[me] = buckets_ref[me]

    def send(k, carry):
        d = (me + k) % ndev
        pltpu.make_async_remote_copy(
            src_ref=buckets_ref.at[d],
            dst_ref=recv.at[me],
            send_sem=send_sem.at[d],
            recv_sem=recv_sem.at[me],
            device_id=(mp, d // ngy, d % ngy),
            device_id_type=mesh_id,
        ).start()
        return carry

    lax.fori_loop(1, ndev, send, 0)


def finish_spread(buckets_ref, recv, send_sem, recv_sem, arrived_ref):
    ngy = lax.axis_size("gy")
    ndev = lax.axis_size("gx") * ngy
    me = lax.axis_index("gx") * ngy + lax.axis_index("gy")

    def wait(d, carry):
        @pl.when(d != me)
        def _():
            copy = pltpu.make_async_remote_copy(
                src_ref=buckets_ref.at[d],
                dst_ref=recv.at[d],
                send_sem=send_sem.at[d],
                recv_sem=recv_sem.at[d],
                device_id=(lax.axis_index("mp"), d // ngy, d % ngy),
                device_id_type=pl.DeviceIdType.MESH,
            )
            copy.wait_send()
            copy.wait_recv()

        return carry

    lax.fori_loop(0, ndev, wait, 0)
    arrived_ref[...] = recv[...]


def interval_kernel(coef_ref, wet_ref, u_ref, above_ref, below_ref, buckets_ref,
                    e0n, e0s, e0w, e0e,
                    out_ref, arrived_ref,
                    first, edge1, halo0, halo1, qw_ref, qe_ref, recv,
                    send_sem, recv_sem, hsend, hrecv):
    p = pl.program_id(0)
    i = pl.program_id(1)
    nblk = pl.num_programs(1)
    wet = wet_ref[...]
    rows, cols = wet.shape
    lev = first.shape[0]
    mp = lax.axis_index("mp")
    gx = lax.axis_index("gx")
    gy = lax.axis_index("gy")
    ngx = lax.axis_size("gx")
    ngy = lax.axis_size("gy")
    ndev = ngx * ngy
    me = gx * ngy + gy
    mesh_id = pl.DeviceIdType.MESH
    links = [
        (gx < ngx - 1, (mp, gx + 1, gy), 1, 0),
        (gx > 0, (mp, gx - 1, gy), 0, 1),
        (gy < ngy - 1, (mp, gx, gy + 1), 3, 2),
        (gy > 0, (mp, gx, gy - 1), 2, 3),
    ]
    fills = [gx > 0, gx < ngx - 1, gy > 0, gy < ngy - 1]
    edge0 = [e0n, e0s, e0w, e0e]

    def halo_copy(stage, src, slot, dev):
        srcs = edge0[src] if stage == 0 else edge1.at[src]
        dsts = halo0.at[slot] if stage == 0 else halo1.at[slot]
        return pltpu.make_async_remote_copy(
            src_ref=srcs,
            dst_ref=dsts,
            send_sem=hsend.at[stage, slot],
            recv_sem=hrecv.at[stage, slot],
            device_id=dev,
            device_id_type=mesh_id,
        )

    def send_halos(stage):
        for present, dev, src, slot in links:
            pl.when(present)(halo_copy(stage, src, slot, dev).start)

    def take_halos(stage, dst):
        for present, dev, src, slot in links:
            pl.when(present)(halo_copy(stage, src, slot, dev).wait_send)
        for slot, filled in enumerate(fills):
            _, dev, src, _ = links[slot]
            pl.when(filled)(halo_copy(stage, src, slot, dev).wait_recv)

            @pl.when(jnp.logical_not(filled))
            def _():
                dst[slot] = jnp.zeros_like(dst[slot])

    def bucket_copy(d):
        return pltpu.make_async_remote_copy(
            src_ref=buckets_ref.at[d],
            dst_ref=recv.at[me],
            send_sem=send_sem.at[d],
            recv_sem=recv_sem.at[me],
            device_id=(mp, d // ngy, d % ngy),
            device_id_type=mesh_id,
        )

    def issue(k0, count):
        for n in range(count):
            k = k0 + n

            @pl.when(k < ndev)
            def _():
                bucket_copy((me + k) % ndev).start()

    lane = lax.broadcasted_iota(jnp.int32, qw_ref.shape, 1)
    row = lax.broadcasted_iota(jnp.int32, (rows, cols), 0)
    col = lax.broadcasted_iota(jnp.int32, (rows, cols), 1)
    horiz = coef_ref[0]
    vert = coef_ref[1]

    def step(load, above, below, hn, hs, hw_t, he_t, store):
        for l in range(LB):
            u = load(l)
            prev = load(l - 1) if l > 0 else above
            nxt = load(l + 1) if l < LB - 1 else below
            w = wet * u
            north = jnp.where(row == 0, hn[l:l + 1, :], pltpu.roll(w, 1, 0))
            south = jnp.where(row == rows - 1, hs[l:l + 1, :], pltpu.roll(w, rows - 1, 0))
            west = jnp.where(col == 0, hw_t[:, l:l + 1], pltpu.roll(w, 1, 1))
            east = jnp.where(col == cols - 1, he_t[:, l:l + 1], pltpu.roll(w, cols - 1, 1))
            lateral = north + south + west + east - 4.0 * w
            vertical = prev + nxt - 2.0 * u
            store(l, wet * (u + horiz * lateral + vert * vertical))

    @pl.when((p == 0) & (i == 0))
    def _():
        barrier = pltpu.get_barrier_semaphore()

        def greet(d, carry):
            @pl.when(d != me)
            def _():
                pl.semaphore_signal(barrier, 1, device_id=(mp, d // ngy, d % ngy), device_id_type=mesh_id)

            return carry

        lax.fori_loop(0, ndev, greet, 0)
        pl.semaphore_wait(barrier, ndev - 1)
        send_halos(0)
        recv[me] = buckets_ref[me]
        take_halos(0, halo0)
        qw_ref[...] = jnp.zeros_like(qw_ref)
        qe_ref[...] = jnp.zeros_like(qe_ref)

    @pl.when(p == 0)
    def _():
        issue(1 + 3 * i, 3)
        blk = pl.ds(pl.multiple_of(i * LB, LB), LB)
        hn = halo0[0, blk]
        hs = halo0[1, blk]
        hw_t = jnp.transpose(halo0[2, blk])
        he_t = jnp.transpose(halo0[3, blk])
        above = above_ref[0] * jnp.where(i > 0, 1.0, 0.0)
        below = below_ref[0] * jnp.where(i < nblk - 1, 1.0, 0.0)
        qs = [qw_ref[...], qe_ref[...]]

        def store(l, res):
            first[i * LB + l] = res
            fw = wet * res
            edge1[0, i, l:l + 1, :] = fw[0:1, :]
            edge1[1, i, l:l + 1, :] = fw[rows - 1:rows, :]
            hit = lane == i * LB + l
            qs[0] = jnp.where(hit, fw[:, 0:1], qs[0])
            qs[1] = jnp.where(hit, fw[:, cols - 1:cols], qs[1])

        step(lambda l: u_ref[l], above, below, hn, hs, hw_t, he_t, store)
        qw_ref[...] = qs[0]
        qe_ref[...] = qs[1]

    @pl.when((p == 0) & (i == nblk - 1))
    def _():
        edge1[2] = jnp.transpose(qw_ref[...])[0:lev, :].reshape(nblk, LB, rows)
        edge1[3] = jnp.transpose(qe_ref[...])[0:lev, :].reshape(nblk, LB, rows)
        send_halos(1)

    @pl.when((p == 1) & (i == 0))
    def _():
        take_halos(1, halo1)

        def late(k, carry):
            bucket_copy((me + k) % ndev).start()
            return carry

        lax.fori_loop(min(1 + 3 * nblk, ndev), ndev, late, 0)

    @pl.when(p == 1)
    def _():
        base = i * LB
        above = first[jnp.maximum(base - 1, 0)] * jnp.where(i > 0, 1.0, 0.0)
        below = first[jnp.minimum(base + LB, lev - 1)] * jnp.where(i < nblk - 1, 1.0, 0.0)
        hw_t = jnp.transpose(halo1[2, i])
        he_t = jnp.transpose(halo1[3, i])

        def store(l, res):
            out_ref[l] = res

        step(lambda l: first[base + l], above, below, halo1[0, i], halo1[1, i], hw_t, he_t, store)

    @pl.when((p == 1) & (i == nblk - 1))
    def _():
        def wait(d, carry):
            @pl.when(d != me)
            def _():
                copy = pltpu.make_async_remote_copy(
                    src_ref=buckets_ref.at[d],
                    dst_ref=recv.at[d],
                    send_sem=send_sem.at[d],
                    recv_sem=recv_sem.at[d],
                    device_id=(mp, d // ngy, d % ngy),
                    device_id_type=mesh_id,
                )
                copy.wait_send()
                copy.wait_recv()

            return carry

        lax.fori_loop(0, ndev, wait, 0)
        arrived_ref[...] = recv[...]


def interval(coef, wet, u, buckets, edges):
    lev, rows, cols = u.shape
    nblk = lev // LB
    full2 = lambda shape: pl.BlockSpec(shape, lambda p, i: (0, 0))
    whole = pl.BlockSpec(buckets.shape, lambda p, i: (0, 0, 0, 0))
    held = lambda p, i: i + p * (nblk - 1 - i)
    in_specs = [
        pl.BlockSpec(memory_space=pltpu.SMEM),
        full2((rows, cols)),
        pl.BlockSpec((LB, rows, cols), lambda p, i: (held(p, i), 0, 0)),
        pl.BlockSpec((1, rows, cols), lambda p, i: (jnp.maximum(held(p, i) * LB - 1, 0), 0, 0)),
        pl.BlockSpec((1, rows, cols), lambda p, i: (jnp.minimum(held(p, i) * LB + LB, lev - 1), 0, 0)),
        whole,
    ] + [full2((lev, cols))] * 4
    out_shape = [
        jax.ShapeDtypeStruct((lev, rows, cols), jnp.float32),
        jax.ShapeDtypeStruct(buckets.shape, buckets.dtype),
    ]
    out_specs = [pl.BlockSpec((LB, rows, cols), lambda p, i: (i * p, 0, 0)), whole]
    scratch = [
        pltpu.VMEM((lev, rows, cols), jnp.float32),
        pltpu.VMEM((4, nblk, LB, cols), jnp.float32),
        pltpu.VMEM((4, lev, cols), jnp.float32),
        pltpu.VMEM((4, nblk, LB, cols), jnp.float32),
        pltpu.VMEM((rows, 128), jnp.float32),
        pltpu.VMEM((rows, 128), jnp.float32),
        pltpu.VMEM(buckets.shape, buckets.dtype),
        pltpu.SemaphoreType.DMA((buckets.shape[0],)),
        pltpu.SemaphoreType.DMA((buckets.shape[0],)),
        pltpu.SemaphoreType.DMA((2, 4)),
        pltpu.SemaphoreType.DMA((2, 4)),
    ]
    return pl.pallas_call(
        interval_kernel,
        grid=(2, nblk),
        in_specs=in_specs,
        out_specs=out_specs,
        out_shape=out_shape,
        scratch_shapes=scratch,
        compiler_params=pltpu.CompilerParams(
            dimension_semantics=("arbitrary", "arbitrary"), collective_id=3, has_side_effects=True,
            vmem_limit_bytes=48 * 1024 * 1024,
        ),
        cost_estimate=pl.CostEstimate(flops=60 * u.size, bytes_accessed=12 * u.size, transcendentals=0),
    )(coef, wet, u, u, u, buckets, *edges)


def first_kernel(coef_ref, wet_ref, u_ref, above_ref, below_ref, buckets_ref,
                 e0n, e0s, e0w, e0e,
                 out_ref, en_ref, es_ref, ew_ref, ee_ref, arrived_ref,
                 halo, qw_ref, qe_ref, recv, send_sem, recv_sem, hsend, hrecv):
    i = pl.program_id(0)
    nblk = pl.num_programs(0)
    edge0 = [e0n, e0s, e0w, e0e]
    wet = wet_ref[...]
    rows, cols = wet.shape
    lev = ew_ref.shape[0]
    mp = lax.axis_index("mp")
    gx = lax.axis_index("gx")
    gy = lax.axis_index("gy")
    ngx = lax.axis_size("gx")
    ngy = lax.axis_size("gy")
    mesh_id = pl.DeviceIdType.MESH
    links = [
        (gx < ngx - 1, (mp, gx + 1, gy), 1, 0),
        (gx > 0, (mp, gx - 1, gy), 0, 1),
        (gy < ngy - 1, (mp, gx, gy + 1), 3, 2),
        (gy > 0, (mp, gx, gy - 1), 2, 3),
    ]
    fills = [gx > 0, gx < ngx - 1, gy > 0, gy < ngy - 1]
    copies = [
        pltpu.make_async_remote_copy(
            src_ref=edge0[src],
            dst_ref=halo.at[slot],
            send_sem=hsend.at[slot],
            recv_sem=hrecv.at[slot],
            device_id=dev,
            device_id_type=mesh_id,
        )
        for _, dev, src, slot in links
    ]
    lane = lax.broadcasted_iota(jnp.int32, qw_ref.shape, 1)

    def send_halos():
        for (present, _, _, _), copy in zip(links, copies):
            pl.when(present)(copy.start)

    @pl.when(i == 0)
    def _():
        start_spread(buckets_ref, recv, send_sem, recv_sem, send_halos)
        for (present, _, _, _), copy in zip(links, copies):
            pl.when(present)(copy.wait_send)
        for slot, filled in enumerate(fills):
            pl.when(filled)(copies[slot].wait_recv)

            @pl.when(jnp.logical_not(filled))
            def _():
                halo[slot] = jnp.zeros_like(halo[slot])

        qw_ref[...] = jnp.zeros_like(qw_ref)
        qe_ref[...] = jnp.zeros_like(qe_ref)

    def _():
        horiz = coef_ref[0]
        vert = coef_ref[1]
        row = lax.broadcasted_iota(jnp.int32, (rows, cols), 0)
        col = lax.broadcasted_iota(jnp.int32, (rows, cols), 1)
        hn = halo[0, pl.ds(i * LB, LB)]
        hs = halo[1, pl.ds(i * LB, LB)]
        hw_t = jnp.transpose(halo[2, pl.ds(i * LB, LB)])
        he_t = jnp.transpose(halo[3, pl.ds(i * LB, LB)])
        above = above_ref[0] * jnp.where(i > 0, 1.0, 0.0)
        below = below_ref[0] * jnp.where(i < nblk - 1, 1.0, 0.0)
        qw = qw_ref[...]
        qe = qe_ref[...]
        for l in range(LB):
            u = u_ref[l]
            prev = u_ref[l - 1] if l > 0 else above
            nxt = u_ref[l + 1] if l < LB - 1 else below
            w = wet * u
            north = jnp.where(row == 0, hn[l:l + 1, :], pltpu.roll(w, 1, 0))
            south = jnp.where(row == rows - 1, hs[l:l + 1, :], pltpu.roll(w, rows - 1, 0))
            west = jnp.where(col == 0, hw_t[:, l:l + 1], pltpu.roll(w, 1, 1))
            east = jnp.where(col == cols - 1, he_t[:, l:l + 1], pltpu.roll(w, cols - 1, 1))
            lateral = north + south + west + east - 4.0 * w
            vertical = prev + nxt - 2.0 * u
            res = wet * (u + horiz * lateral + vert * vertical)
            out_ref[l] = res
            fw = wet * res
            en_ref[l:l + 1, :] = fw[0:1, :]
            es_ref[l:l + 1, :] = fw[rows - 1:rows, :]
            hit = lane == i * LB + l
            qw = jnp.where(hit, fw[:, 0:1], qw)
            qe = jnp.where(hit, fw[:, cols - 1:cols], qe)
        qw_ref[...] = qw
        qe_ref[...] = qe

    _()

    @pl.when(i == nblk - 1)
    def _():
        ew_ref[...] = jnp.transpose(qw_ref[...])[0:lev, :]
        ee_ref[...] = jnp.transpose(qe_ref[...])[0:lev, :]
        finish_spread(buckets_ref, recv, send_sem, recv_sem, arrived_ref)


def first_step(coef, wet, u, buckets, edges):
    lev, rows, cols = u.shape
    nblk = lev // LB
    full2 = lambda shape: pl.BlockSpec(shape, lambda i: (0, 0))
    lvl2 = pl.BlockSpec((LB, cols), lambda i: (i, 0))
    whole = pl.BlockSpec(buckets.shape, lambda i: (0, 0, 0, 0))
    in_specs = [
        pl.BlockSpec(memory_space=pltpu.SMEM),
        full2((rows, cols)),
        pl.BlockSpec((LB, rows, cols), lambda i: (i, 0, 0)),
        pl.BlockSpec((1, rows, cols), lambda i: (jnp.maximum(i * LB - 1, 0), 0, 0)),
        pl.BlockSpec((1, rows, cols), lambda i: (jnp.minimum(i * LB + LB, lev - 1), 0, 0)),
        whole,
    ] + [full2((lev, cols))] * 4
    out_shape = [
        jax.ShapeDtypeStruct((lev, rows, cols), jnp.float32),
        jax.ShapeDtypeStruct((lev, cols), jnp.float32),
        jax.ShapeDtypeStruct((lev, cols), jnp.float32),
        jax.ShapeDtypeStruct((lev, rows), jnp.float32),
        jax.ShapeDtypeStruct((lev, rows), jnp.float32),
        jax.ShapeDtypeStruct(buckets.shape, buckets.dtype),
    ]
    out_specs = [
        pl.BlockSpec((LB, rows, cols), lambda i: (i, 0, 0)),
        lvl2, lvl2, full2((lev, rows)), full2((lev, rows)), whole,
    ]
    scratch = [
        pltpu.VMEM((4, lev, cols), jnp.float32),
        pltpu.VMEM((rows, 128), jnp.float32),
        pltpu.VMEM((rows, 128), jnp.float32),
        pltpu.VMEM(buckets.shape, buckets.dtype),
        pltpu.SemaphoreType.DMA((buckets.shape[0],)),
        pltpu.SemaphoreType.DMA((buckets.shape[0],)),
        pltpu.SemaphoreType.DMA((4,)),
        pltpu.SemaphoreType.DMA((4,)),
    ]
    return pl.pallas_call(
        first_kernel,
        grid=(nblk,),
        in_specs=in_specs,
        out_specs=out_specs,
        out_shape=out_shape,
        scratch_shapes=scratch,
        compiler_params=pltpu.CompilerParams(
            dimension_semantics=("arbitrary",), collective_id=2, has_side_effects=True
        ),
        cost_estimate=pl.CostEstimate(flops=30 * u.size, bytes_accessed=12 * u.size, transcendentals=0),
    )(coef, wet, u, u, u, buckets, *edges)


def stencil_kernel(with_edges, with_force, coef_ref, wet_ref, u_ref, above_ref, below_ref,
                   hn_ref, hs_ref, hw_ref, he_ref, *rest):
    if with_force:
        force_ref, rest = rest[0], rest[1:]
    if with_edges:
        buckets_ref, rest = rest[0], rest[1:]
    out_ref = rest[0]
    i = pl.program_id(0)
    nblk = pl.num_programs(0)
    horiz = coef_ref[0]
    vert = coef_ref[1]
    wet = wet_ref[...]
    rows, cols = wet.shape
    row = lax.broadcasted_iota(jnp.int32, (rows, cols), 0)
    col = lax.broadcasted_iota(jnp.int32, (rows, cols), 1)
    hw_t = jnp.transpose(hw_ref[...])
    he_t = jnp.transpose(he_ref[...])
    above = above_ref[0] * jnp.where(i > 0, 1.0, 0.0)
    below = below_ref[0] * jnp.where(i < nblk - 1, 1.0, 0.0)
    if with_edges:
        en_ref, es_ref, ew_ref, ee_ref, arrived_ref, qw_ref, qe_ref, recv, send_sem, recv_sem = rest[1:]

        @pl.when(i == 0)
        def _():
            start_spread(buckets_ref, recv, send_sem, recv_sem)
            qw_ref[...] = jnp.zeros_like(qw_ref)
            qe_ref[...] = jnp.zeros_like(qe_ref)

    if with_edges:
        lane = lax.broadcasted_iota(jnp.int32, qw_ref.shape, 1)
        qw = qw_ref[...]
        qe = qe_ref[...]
    for l in range(LB):
        u = u_ref[l]
        prev = u_ref[l - 1] if l > 0 else above
        nxt = u_ref[l + 1] if l < LB - 1 else below
        w = wet * u
        north = jnp.where(row == 0, hn_ref[l:l + 1, :], pltpu.roll(w, 1, 0))
        south = jnp.where(row == rows - 1, hs_ref[l:l + 1, :], pltpu.roll(w, rows - 1, 0))
        west = jnp.where(col == 0, hw_t[:, l:l + 1], pltpu.roll(w, 1, 1))
        east = jnp.where(col == cols - 1, he_t[:, l:l + 1], pltpu.roll(w, cols - 1, 1))
        lateral = north + south + west + east - 4.0 * w
        vertical = prev + nxt - 2.0 * u
        res = wet * (u + horiz * lateral + vert * vertical)
        if with_force and l == 0:
            res = res + jnp.where(i == 0, 1.0, 0.0) * (force_gain * wet * force_ref[...])
        out_ref[l] = res
        if with_edges:
            fw = wet * res
            en_ref[l:l + 1, :] = fw[0:1, :]
            es_ref[l:l + 1, :] = fw[rows - 1:rows, :]
            hit = lane == i * LB + l
            qw = jnp.where(hit, fw[:, 0:1], qw)
            qe = jnp.where(hit, fw[:, cols - 1:cols], qe)

    if with_edges:
        qw_ref[...] = qw
        qe_ref[...] = qe

        @pl.when(i == nblk - 1)
        def _():
            lev = ew_ref.shape[0]
            ew_ref[...] = jnp.transpose(qw_ref[...])[0:lev, :]
            ee_ref[...] = jnp.transpose(qe_ref[...])[0:lev, :]
            finish_spread(buckets_ref, recv, send_sem, recv_sem, arrived_ref)


def edges_kernel(wet_ref, u_ref, en_ref, es_ref, ew_ref, ee_ref, qw_ref, qe_ref):
    i = pl.program_id(0)
    nblk = pl.num_programs(0)
    wet = wet_ref[...]
    rows, cols = wet.shape

    @pl.when(i == 0)
    def _():
        qw_ref[...] = jnp.zeros_like(qw_ref)
        qe_ref[...] = jnp.zeros_like(qe_ref)

    lane = lax.broadcasted_iota(jnp.int32, qw_ref.shape, 1)
    qw = qw_ref[...]
    qe = qe_ref[...]
    for l in range(EB):
        fw = wet * u_ref[l]
        en_ref[l:l + 1, :] = fw[0:1, :]
        es_ref[l:l + 1, :] = fw[rows - 1:rows, :]
        hit = lane == i * EB + l
        qw = jnp.where(hit, fw[:, 0:1], qw)
        qe = jnp.where(hit, fw[:, cols - 1:cols], qe)
    qw_ref[...] = qw
    qe_ref[...] = qe

    @pl.when(i == nblk - 1)
    def _():
        lev = ew_ref.shape[0]
        ew_ref[...] = jnp.transpose(qw_ref[...])[0:lev, :]
        ee_ref[...] = jnp.transpose(qe_ref[...])[0:lev, :]


def masked_edges(wet, u):
    lev, rows, cols = u.shape
    lvl2 = pl.BlockSpec((EB, cols), lambda i: (i, 0))
    full2 = lambda shape: pl.BlockSpec(shape, lambda i: (0, 0))
    return pl.pallas_call(
        edges_kernel,
        grid=(lev // EB,),
        in_specs=[full2((rows, cols)), pl.BlockSpec((EB, rows, cols), lambda i: (i, 0, 0))],
        out_specs=[lvl2, lvl2, full2((lev, rows)), full2((lev, rows))],
        out_shape=[jax.ShapeDtypeStruct((lev, cols), jnp.float32)] * 2
        + [jax.ShapeDtypeStruct((lev, rows), jnp.float32)] * 2,
        scratch_shapes=[pltpu.VMEM((rows, 128), jnp.float32)] * 2,
        compiler_params=pltpu.CompilerParams(dimension_semantics=("arbitrary",)),
        cost_estimate=pl.CostEstimate(flops=2 * u.size, bytes_accessed=4 * u.size, transcendentals=0),
    )(wet, u)


def force_kernel(x_ref, wet_ref, f_ref, out_ref):
    out_ref[0] = x_ref[0] + force_gain * wet_ref[...] * f_ref[...]


def add_force(x, wet, f):
    lev, rows, cols = x.shape
    plane = pl.BlockSpec((rows, cols), lambda i: (0, 0))
    level0 = pl.BlockSpec((1, rows, cols), lambda i: (0, 0, 0))
    return pl.pallas_call(
        force_kernel,
        grid=(1,),
        in_specs=[level0, plane, plane],
        out_specs=level0,
        out_shape=jax.ShapeDtypeStruct(x.shape, x.dtype),
        input_output_aliases={0: 0},
    )(x, wet, f)


def stencil_step(coef, wet, u, halos, force=None, buckets=None):
    with_edges = buckets is not None
    lev, rows, cols = u.shape
    nblk = lev // LB
    full2 = lambda shape: pl.BlockSpec(shape, lambda i: (0, 0))
    lvl2 = pl.BlockSpec((LB, cols), lambda i: (i, 0))
    in_specs = [
        pl.BlockSpec(memory_space=pltpu.SMEM),
        full2((rows, cols)),
        pl.BlockSpec((LB, rows, cols), lambda i: (i, 0, 0)),
        pl.BlockSpec((1, rows, cols), lambda i: (jnp.maximum(i * LB - 1, 0), 0, 0)),
        pl.BlockSpec((1, rows, cols), lambda i: (jnp.minimum(i * LB + LB, lev - 1), 0, 0)),
        lvl2, lvl2, lvl2, lvl2,
    ]
    args = [coef, wet, u, u, u] + list(halos)
    if force is not None:
        in_specs.append(full2((rows, cols)))
        args.append(force)
    if with_edges:
        in_specs.append(pl.BlockSpec(buckets.shape, lambda i: (0, 0, 0, 0)))
        args.append(buckets)
    out_shape = [jax.ShapeDtypeStruct((lev, rows, cols), jnp.float32)]
    out_specs = [pl.BlockSpec((LB, rows, cols), lambda i: (i, 0, 0))]
    scratch = []
    params = dict(dimension_semantics=("arbitrary",))
    if with_edges:
        out_shape += [jax.ShapeDtypeStruct((lev, cols), jnp.float32)] * 2
        out_shape += [jax.ShapeDtypeStruct((lev, rows), jnp.float32)] * 2
        out_shape += [jax.ShapeDtypeStruct(buckets.shape, buckets.dtype)]
        out_specs += [lvl2, lvl2, full2((lev, rows)), full2((lev, rows))]
        out_specs += [pl.BlockSpec(buckets.shape, lambda i: (0, 0, 0, 0))]
        scratch = [pltpu.VMEM((rows, 128), jnp.float32)] * 2 + [
            pltpu.VMEM(buckets.shape, buckets.dtype),
            pltpu.SemaphoreType.DMA((buckets.shape[0],)),
            pltpu.SemaphoreType.DMA((buckets.shape[0],)),
        ]
        params.update(collective_id=2, has_side_effects=True)
    return pl.pallas_call(
        functools.partial(stencil_kernel, with_edges, force is not None),
        grid=(nblk,),
        in_specs=in_specs,
        out_specs=out_specs,
        out_shape=out_shape,
        scratch_shapes=scratch,
        compiler_params=pltpu.CompilerParams(**params),
        cost_estimate=pl.CostEstimate(flops=30 * u.size, bytes_accessed=12 * u.size, transcendentals=0),
    )(*args)


def halo_kernel(en_ref, es_ref, ew_ref, ee_ref, hn_ref, hs_ref, hw_ref, he_ref,
                buf, send_sem, recv_sem):
    mp = lax.axis_index("mp")
    gx = lax.axis_index("gx")
    gy = lax.axis_index("gy")
    ngx = lax.axis_size("gx")
    ngy = lax.axis_size("gy")
    mesh_id = pl.DeviceIdType.MESH
    links = [
        (gx < ngx - 1, (mp, gx + 1, gy), es_ref, 0),
        (gx > 0, (mp, gx - 1, gy), en_ref, 1),
        (gy < ngy - 1, (mp, gx, gy + 1), ee_ref, 2),
        (gy > 0, (mp, gx, gy - 1), ew_ref, 3),
    ]
    barrier = pltpu.get_barrier_semaphore()
    count = jnp.int32(0)
    for present, dev, _, _ in links:
        @pl.when(present)
        def _():
            pl.semaphore_signal(barrier, 1, device_id=dev, device_id_type=mesh_id)

        count = count + present.astype(jnp.int32)
    pl.semaphore_wait(barrier, count)

    copies = []
    for present, dev, src, slot in links:
        copy = pltpu.make_async_remote_copy(
            src_ref=src,
            dst_ref=buf.at[slot],
            send_sem=send_sem.at[slot],
            recv_sem=recv_sem.at[slot],
            device_id=dev,
            device_id_type=mesh_id,
        )
        pl.when(present)(copy.start)
        copies.append((present, copy))
    for present, copy in copies:
        pl.when(present)(copy.wait_send)
    fills = [gx > 0, gx < ngx - 1, gy > 0, gy < ngy - 1]
    outs = [hn_ref, hs_ref, hw_ref, he_ref]
    for slot, (filled, out) in enumerate(zip(fills, outs)):
        _, copy = copies[slot]

        @pl.when(filled)
        def _():
            copy.wait_recv()
            out[...] = buf[slot]

        @pl.when(jnp.logical_not(filled))
        def _():
            out[...] = jnp.zeros_like(out)


def exchange(en, es, ew, ee, call):
    shape = jax.ShapeDtypeStruct(en.shape, en.dtype)
    vmem = pl.BlockSpec(memory_space=pltpu.VMEM)
    return pl.pallas_call(
        halo_kernel,
        in_specs=[vmem] * 4,
        out_specs=[vmem] * 4,
        out_shape=[shape] * 4,
        scratch_shapes=[
            pltpu.VMEM((4,) + en.shape, en.dtype),
            pltpu.SemaphoreType.DMA((4,)),
            pltpu.SemaphoreType.DMA((4,)),
        ],
        compiler_params=pltpu.CompilerParams(collective_id=call, has_side_effects=True),
    )(en, es, ew, ee)


def bucket_kernel(target_ref, row_ref, contrib_ref, out_ref, count_ref):
    ntiles = contrib_ref.shape[0]
    ndest = out_ref.shape[0]
    sub = lax.broadcasted_iota(jnp.int32, (KF, CY), 0)
    out_ref[...] = jnp.zeros_like(out_ref)

    def clear(d, carry):
        count_ref[d] = 0
        return carry

    lax.fori_loop(0, ndest, clear, 0)

    def body(t, carry):
        d = target_ref[t]
        c = count_ref[d]
        count_ref[d] = c + 1
        out_ref[d, c] = contrib_ref[t]
        out_ref[d, CAP] = jnp.where(sub == c, row_ref[t].astype(jnp.float32), out_ref[d, CAP])
        return carry

    lax.fori_loop(0, ntiles, body, 0, unroll=8)


def local(states, surface, land_mask, tile_weights, tile_source, tile_target, tile_row):
    group = lax.axis_index("mp")
    ndev = lax.axis_size("gx") * lax.axis_size("gy")
    state = states[0]
    lev, rows_here, cols_here = state.shape
    wet = jnp.where(
        group == 0, jnp.ones(land_mask.shape, jnp.float32), land_mask.astype(jnp.float32)
    )
    coef = jnp.stack([jnp.where(group == 0, 0.15, 0.12), jnp.where(group == 0, 0.1, 0.15)]).astype(
        jnp.float32
    )

    src = (surface[0] * wet).astype(jnp.bfloat16)
    source = tile_source[0, 0, 0]
    target = tile_target[0, 0, 0, :, 0]
    dest_row = tile_row[0, 0, 0]
    ntiles = source.shape[0]
    picked = jnp.take(src, source, axis=1)
    contrib = jnp.einsum(
        "tji,kti->tkj", tile_weights[0, 0, 0], picked, preferred_element_type=jnp.float32
    )
    buckets = pl.pallas_call(
        bucket_kernel,
        in_specs=[
            pl.BlockSpec(memory_space=pltpu.SMEM),
            pl.BlockSpec(memory_space=pltpu.SMEM),
            pl.BlockSpec(memory_space=pltpu.VMEM),
        ],
        out_specs=pl.BlockSpec(memory_space=pltpu.VMEM),
        out_shape=jax.ShapeDtypeStruct((ndev, CAP + 1, KF, CY), jnp.float32),
        scratch_shapes=[pltpu.SMEM((ndev,), jnp.int32)],
    )(target, dest_row, contrib)
    second, arrived = interval(coef, wet, state, buckets, masked_edges(wet, state))
    got_rows = arrived[:, CAP, :, 0].astype(jnp.int32)
    select = (
        got_rows[:, :, None] == jnp.arange(rows_here, dtype=jnp.int32)[None, None, :]
    ).astype(jnp.float32)
    sent = jnp.einsum(
        "scr,sckj->krj", select, arrived[:, :CAP], precision=lax.Precision.HIGHEST
    )
    received = lax.ppermute(sent, "mp", [(0, 1), (1, 0)])

    second = add_force(second, wet, received[0])
    return (second[None], received[None])


def solution(mesh):
    return jax.shard_map(
        local,
        mesh=mesh,
        in_specs=(
            P("mp", None, "gx", "gy"),
            P("mp", None, "gx", "gy"),
            P("gx", "gy"),
            P("mp", "gx", "gy", None, None, None),
            P("mp", "gx", "gy", None),
            P("mp", "gx", "gy", None, None),
            P("mp", "gx", "gy", None),
        ),
        out_specs=(P("mp", None, "gx", "gy"), P("mp", None, "gx", "gy")),
        check_vma=False,
    )
```

```python
import functools

import jax
import jax.numpy as jnp
from jax import lax
from jax.experimental import pallas as pl
from jax.experimental.pallas import tpu as pltpu
from jax.sharding import PartitionSpec as P

CY = 128
KF = 8
CAP = 8
LB = 8
EB = 32

force_gain = 0.5


def shift_pairs(devices, forward):
    up = [(i, i + 1) for i in range(devices - 1)]
    return up if forward else [(j, i) for i, j in up]


def start_spread(buckets_ref, recv, send_sem, recv_sem, first_out=None):
    mp = lax.axis_index("mp")
    ngy = lax.axis_size("gy")
    ndev = lax.axis_size("gx") * ngy
    me = lax.axis_index("gx") * ngy + lax.axis_index("gy")
    mesh_id = pl.DeviceIdType.MESH
    barrier = pltpu.get_barrier_semaphore()

    def greet(d, carry):
        @pl.when(d != me)
        def _():
            pl.semaphore_signal(barrier, 1, device_id=(mp, d // ngy, d % ngy), device_id_type=mesh_id)

        return carry

    lax.fori_loop(0, ndev, greet, 0)
    pl.semaphore_wait(barrier, ndev - 1)
    if first_out is not None:
        first_out()
    recv[me] = buckets_ref[me]

    def send(k, carry):
        d = (me + k) % ndev
        pltpu.make_async_remote_copy(
            src_ref=buckets_ref.at[d],
            dst_ref=recv.at[me],
            send_sem=send_sem.at[d],
            recv_sem=recv_sem.at[me],
            device_id=(mp, d // ngy, d % ngy),
            device_id_type=mesh_id,
        ).start()
        return carry

    lax.fori_loop(1, ndev, send, 0)


def finish_spread(buckets_ref, recv, send_sem, recv_sem, arrived_ref):
    ngy = lax.axis_size("gy")
    ndev = lax.axis_size("gx") * ngy
    me = lax.axis_index("gx") * ngy + lax.axis_index("gy")

    def wait(d, carry):
        @pl.when(d != me)
        def _():
            copy = pltpu.make_async_remote_copy(
                src_ref=buckets_ref.at[d],
                dst_ref=recv.at[d],
                send_sem=send_sem.at[d],
                recv_sem=recv_sem.at[d],
                device_id=(lax.axis_index("mp"), d // ngy, d % ngy),
                device_id_type=pl.DeviceIdType.MESH,
            )
            copy.wait_send()
            copy.wait_recv()

        return carry

    lax.fori_loop(0, ndev, wait, 0)
    arrived_ref[...] = recv[...]


def interval_kernel(coef_ref, wet_ref, u_ref, above_ref, below_ref, buckets_ref,
                    e0n, e0s, e0w, e0e,
                    out_ref, arrived_ref,
                    first, edge1, halo0, halo1, qw_ref, qe_ref, recv,
                    send_sem, recv_sem, hsend, hrecv):
    p = pl.program_id(0)
    i = pl.program_id(1)
    nblk = pl.num_programs(1)
    wet = wet_ref[...]
    rows, cols = wet.shape
    lev = first.shape[0]
    mp = lax.axis_index("mp")
    gx = lax.axis_index("gx")
    gy = lax.axis_index("gy")
    ngx = lax.axis_size("gx")
    ngy = lax.axis_size("gy")
    ndev = ngx * ngy
    me = gx * ngy + gy
    mesh_id = pl.DeviceIdType.MESH
    links = [
        (gx < ngx - 1, (mp, gx + 1, gy), 1, 0),
        (gx > 0, (mp, gx - 1, gy), 0, 1),
        (gy < ngy - 1, (mp, gx, gy + 1), 3, 2),
        (gy > 0, (mp, gx, gy - 1), 2, 3),
    ]
    fills = [gx > 0, gx < ngx - 1, gy > 0, gy < ngy - 1]
    edge0 = [e0n, e0s, e0w, e0e]

    def halo_copy(stage, src, slot, dev):
        srcs = edge0[src] if stage == 0 else edge1.at[src]
        dsts = halo0.at[slot] if stage == 0 else halo1.at[slot]
        return pltpu.make_async_remote_copy(
            src_ref=srcs,
            dst_ref=dsts,
            send_sem=hsend.at[stage, slot],
            recv_sem=hrecv.at[stage, slot],
            device_id=dev,
            device_id_type=mesh_id,
        )

    def send_halos(stage):
        for present, dev, src, slot in links:
            pl.when(present)(halo_copy(stage, src, slot, dev).start)

    def take_halos(stage, dst):
        for present, dev, src, slot in links:
            pl.when(present)(halo_copy(stage, src, slot, dev).wait_send)
        for slot, filled in enumerate(fills):
            _, dev, src, _ = links[slot]
            pl.when(filled)(halo_copy(stage, src, slot, dev).wait_recv)

            @pl.when(jnp.logical_not(filled))
            def _():
                dst[slot] = jnp.zeros_like(dst[slot])

    def bucket_copy(d):
        return pltpu.make_async_remote_copy(
            src_ref=buckets_ref.at[d],
            dst_ref=recv.at[me],
            send_sem=send_sem.at[d],
            recv_sem=recv_sem.at[me],
            device_id=(mp, d // ngy, d % ngy),
            device_id_type=mesh_id,
        )

    def issue(k0, count):
        for n in range(count):
            k = k0 + n

            @pl.when(k < ndev)
            def _():
                bucket_copy((me + k) % ndev).start()

    lane = lax.broadcasted_iota(jnp.int32, qw_ref.shape, 1)
    row = lax.broadcasted_iota(jnp.int32, (rows, cols), 0)
    col = lax.broadcasted_iota(jnp.int32, (rows, cols), 1)
    horiz = coef_ref[0]
    vert = coef_ref[1]

    def step(load, above, below, hn, hs, hw_t, he_t, store):
        for l in range(LB):
            u = load(l)
            prev = load(l - 1) if l > 0 else above
            nxt = load(l + 1) if l < LB - 1 else below
            w = wet * u
            north = jnp.where(row == 0, hn[l:l + 1, :], pltpu.roll(w, 1, 0))
            south = jnp.where(row == rows - 1, hs[l:l + 1, :], pltpu.roll(w, rows - 1, 0))
            west = jnp.where(col == 0, hw_t[:, l:l + 1], pltpu.roll(w, 1, 1))
            east = jnp.where(col == cols - 1, he_t[:, l:l + 1], pltpu.roll(w, cols - 1, 1))
            lateral = north + south + west + east - 4.0 * w
            vertical = prev + nxt - 2.0 * u
            store(l, wet * (u + horiz * lateral + vert * vertical))

    @pl.when((p == 0) & (i == 0))
    def _():
        barrier = pltpu.get_barrier_semaphore()

        def greet(d, carry):
            @pl.when(d != me)
            def _():
                pl.semaphore_signal(barrier, 1, device_id=(mp, d // ngy, d % ngy), device_id_type=mesh_id)

            return carry

        lax.fori_loop(0, ndev, greet, 0)
        pl.semaphore_wait(barrier, ndev - 1)
        send_halos(0)
        recv[me] = buckets_ref[me]
        take_halos(0, halo0)
        qw_ref[...] = jnp.zeros_like(qw_ref)
        qe_ref[...] = jnp.zeros_like(qe_ref)

    @pl.when(p == 0)
    def _():
        issue(1 + 3 * i, 3)
        blk = pl.ds(pl.multiple_of(i * LB, LB), LB)
        hn = halo0[0, blk]
        hs = halo0[1, blk]
        hw_t = jnp.transpose(halo0[2, blk])
        he_t = jnp.transpose(halo0[3, blk])
        above = above_ref[0] * jnp.where(i > 0, 1.0, 0.0)
        below = below_ref[0] * jnp.where(i < nblk - 1, 1.0, 0.0)
        qs = [qw_ref[...], qe_ref[...]]

        def store(l, res):
            first[i * LB + l] = res
            fw = wet * res
            edge1[0, i, l:l + 1, :] = fw[0:1, :]
            edge1[1, i, l:l + 1, :] = fw[rows - 1:rows, :]
            hit = lane == i * LB + l
            qs[0] = jnp.where(hit, fw[:, 0:1], qs[0])
            qs[1] = jnp.where(hit, fw[:, cols - 1:cols], qs[1])

        step(lambda l: u_ref[l], above, below, hn, hs, hw_t, he_t, store)
        qw_ref[...] = qs[0]
        qe_ref[...] = qs[1]

    @pl.when((p == 0) & (i == nblk - 1))
    def _():
        edge1[2] = jnp.transpose(qw_ref[...])[0:lev, :].reshape(nblk, LB, rows)
        edge1[3] = jnp.transpose(qe_ref[...])[0:lev, :].reshape(nblk, LB, rows)
        send_halos(1)

    @pl.when((p == 1) & (i == 0))
    def _():
        take_halos(1, halo1)

        def late(k, carry):
            bucket_copy((me + k) % ndev).start()
            return carry

        lax.fori_loop(min(1 + 3 * nblk, ndev), ndev, late, 0)

    @pl.when(p == 1)
    def _():
        base = i * LB
        above = first[jnp.maximum(base - 1, 0)] * jnp.where(i > 0, 1.0, 0.0)
        below = first[jnp.minimum(base + LB, lev - 1)] * jnp.where(i < nblk - 1, 1.0, 0.0)
        hw_t = jnp.transpose(halo1[2, i])
        he_t = jnp.transpose(halo1[3, i])

        def store(l, res):
            out_ref[l] = res

        step(lambda l: first[base + l], above, below, halo1[0, i], halo1[1, i], hw_t, he_t, store)

    @pl.when((p == 1) & (i == nblk - 1))
    def _():
        def wait(d, carry):
            @pl.when(d != me)
            def _():
                copy = pltpu.make_async_remote_copy(
                    src_ref=buckets_ref.at[d],
                    dst_ref=recv.at[d],
                    send_sem=send_sem.at[d],
                    recv_sem=recv_sem.at[d],
                    device_id=(mp, d // ngy, d % ngy),
                    device_id_type=mesh_id,
                )
                copy.wait_send()
                copy.wait_recv()

            return carry

        lax.fori_loop(0, ndev, wait, 0)
        arrived_ref[...] = recv[...]


def interval(coef, wet, u, buckets, edges):
    lev, rows, cols = u.shape
    nblk = lev // LB
    full2 = lambda shape: pl.BlockSpec(shape, lambda p, i: (0, 0))
    whole = pl.BlockSpec(buckets.shape, lambda p, i: (0, 0, 0, 0))
    held = lambda p, i: i + p * (nblk - 1 - i)
    in_specs = [
        pl.BlockSpec(memory_space=pltpu.SMEM),
        full2((rows, cols)),
        pl.BlockSpec((LB, rows, cols), lambda p, i: (held(p, i), 0, 0)),
        pl.BlockSpec((1, rows, cols), lambda p, i: (jnp.maximum(held(p, i) * LB - 1, 0), 0, 0)),
        pl.BlockSpec((1, rows, cols), lambda p, i: (jnp.minimum(held(p, i) * LB + LB, lev - 1), 0, 0)),
        whole,
    ] + [full2((lev, cols))] * 4
    out_shape = [
        jax.ShapeDtypeStruct((lev, rows, cols), jnp.float32),
        jax.ShapeDtypeStruct(buckets.shape, buckets.dtype),
    ]
    out_specs = [pl.BlockSpec((LB, rows, cols), lambda p, i: (i * p, 0, 0)), whole]
    scratch = [
        pltpu.VMEM((lev, rows, cols), jnp.float32),
        pltpu.VMEM((4, nblk, LB, cols), jnp.float32),
        pltpu.VMEM((4, lev, cols), jnp.float32),
        pltpu.VMEM((4, nblk, LB, cols), jnp.float32),
        pltpu.VMEM((rows, 128), jnp.float32),
        pltpu.VMEM((rows, 128), jnp.float32),
        pltpu.VMEM(buckets.shape, buckets.dtype),
        pltpu.SemaphoreType.DMA((buckets.shape[0],)),
        pltpu.SemaphoreType.DMA((buckets.shape[0],)),
        pltpu.SemaphoreType.DMA((2, 4)),
        pltpu.SemaphoreType.DMA((2, 4)),
    ]
    return pl.pallas_call(
        interval_kernel,
        grid=(2, nblk),
        in_specs=in_specs,
        out_specs=out_specs,
        out_shape=out_shape,
        scratch_shapes=scratch,
        compiler_params=pltpu.CompilerParams(
            dimension_semantics=("arbitrary", "arbitrary"), collective_id=3, has_side_effects=True,
            vmem_limit_bytes=48 * 1024 * 1024,
        ),
        cost_estimate=pl.CostEstimate(flops=60 * u.size, bytes_accessed=12 * u.size, transcendentals=0),
    )(coef, wet, u, u, u, buckets, *edges)


def first_kernel(coef_ref, wet_ref, u_ref, above_ref, below_ref, buckets_ref,
                 e0n, e0s, e0w, e0e,
                 out_ref, en_ref, es_ref, ew_ref, ee_ref, arrived_ref,
                 halo, qw_ref, qe_ref, recv, send_sem, recv_sem, hsend, hrecv):
    i = pl.program_id(0)
    nblk = pl.num_programs(0)
    edge0 = [e0n, e0s, e0w, e0e]
    wet = wet_ref[...]
    rows, cols = wet.shape
    lev = ew_ref.shape[0]
    mp = lax.axis_index("mp")
    gx = lax.axis_index("gx")
    gy = lax.axis_index("gy")
    ngx = lax.axis_size("gx")
    ngy = lax.axis_size("gy")
    mesh_id = pl.DeviceIdType.MESH
    links = [
        (gx < ngx - 1, (mp, gx + 1, gy), 1, 0),
        (gx > 0, (mp, gx - 1, gy), 0, 1),
        (gy < ngy - 1, (mp, gx, gy + 1), 3, 2),
        (gy > 0, (mp, gx, gy - 1), 2, 3),
    ]
    fills = [gx > 0, gx < ngx - 1, gy > 0, gy < ngy - 1]
    copies = [
        pltpu.make_async_remote_copy(
            src_ref=edge0[src],
            dst_ref=halo.at[slot],
            send_sem=hsend.at[slot],
            recv_sem=hrecv.at[slot],
            device_id=dev,
            device_id_type=mesh_id,
        )
        for _, dev, src, slot in links
    ]
    lane = lax.broadcasted_iota(jnp.int32, qw_ref.shape, 1)

    def send_halos():
        for (present, _, _, _), copy in zip(links, copies):
            pl.when(present)(copy.start)

    @pl.when(i == 0)
    def _():
        start_spread(buckets_ref, recv, send_sem, recv_sem, send_halos)
        for (present, _, _, _), copy in zip(links, copies):
            pl.when(present)(copy.wait_send)
        for slot, filled in enumerate(fills):
            pl.when(filled)(copies[slot].wait_recv)

            @pl.when(jnp.logical_not(filled))
            def _():
                halo[slot] = jnp.zeros_like(halo[slot])

        qw_ref[...] = jnp.zeros_like(qw_ref)
        qe_ref[...] = jnp.zeros_like(qe_ref)

    def _():
        horiz = coef_ref[0]
        vert = coef_ref[1]
        row = lax.broadcasted_iota(jnp.int32, (rows, cols), 0)
        col = lax.broadcasted_iota(jnp.int32, (rows, cols), 1)
        hn = halo[0, pl.ds(i * LB, LB)]
        hs = halo[1, pl.ds(i * LB, LB)]
        hw_t = jnp.transpose(halo[2, pl.ds(i * LB, LB)])
        he_t = jnp.transpose(halo[3, pl.ds(i * LB, LB)])
        above = above_ref[0] * jnp.where(i > 0, 1.0, 0.0)
        below = below_ref[0] * jnp.where(i < nblk - 1, 1.0, 0.0)
        qw = qw_ref[...]
        qe = qe_ref[...]
        for l in range(LB):
            u = u_ref[l]
            prev = u_ref[l - 1] if l > 0 else above
            nxt = u_ref[l + 1] if l < LB - 1 else below
            w = wet * u
            north = jnp.where(row == 0, hn[l:l + 1, :], pltpu.roll(w, 1, 0))
            south = jnp.where(row == rows - 1, hs[l:l + 1, :], pltpu.roll(w, rows - 1, 0))
            west = jnp.where(col == 0, hw_t[:, l:l + 1], pltpu.roll(w, 1, 1))
            east = jnp.where(col == cols - 1, he_t[:, l:l + 1], pltpu.roll(w, cols - 1, 1))
            lateral = north + south + west + east - 4.0 * w
            vertical = prev + nxt - 2.0 * u
            res = wet * (u + horiz * lateral + vert * vertical)
            out_ref[l] = res
            fw = wet * res
            en_ref[l:l + 1, :] = fw[0:1, :]
            es_ref[l:l + 1, :] = fw[rows - 1:rows, :]
            hit = lane == i * LB + l
            qw = jnp.where(hit, fw[:, 0:1], qw)
            qe = jnp.where(hit, fw[:, cols - 1:cols], qe)
        qw_ref[...] = qw
        qe_ref[...] = qe

    _()

    @pl.when(i == nblk - 1)
    def _():
        ew_ref[...] = jnp.transpose(qw_ref[...])[0:lev, :]
        ee_ref[...] = jnp.transpose(qe_ref[...])[0:lev, :]
        finish_spread(buckets_ref, recv, send_sem, recv_sem, arrived_ref)


def first_step(coef, wet, u, buckets, edges):
    lev, rows, cols = u.shape
    nblk = lev // LB
    full2 = lambda shape: pl.BlockSpec(shape, lambda i: (0, 0))
    lvl2 = pl.BlockSpec((LB, cols), lambda i: (i, 0))
    whole = pl.BlockSpec(buckets.shape, lambda i: (0, 0, 0, 0))
    in_specs = [
        pl.BlockSpec(memory_space=pltpu.SMEM),
        full2((rows, cols)),
        pl.BlockSpec((LB, rows, cols), lambda i: (i, 0, 0)),
        pl.BlockSpec((1, rows, cols), lambda i: (jnp.maximum(i * LB - 1, 0), 0, 0)),
        pl.BlockSpec((1, rows, cols), lambda i: (jnp.minimum(i * LB + LB, lev - 1), 0, 0)),
        whole,
    ] + [full2((lev, cols))] * 4
    out_shape = [
        jax.ShapeDtypeStruct((lev, rows, cols), jnp.float32),
        jax.ShapeDtypeStruct((lev, cols), jnp.float32),
        jax.ShapeDtypeStruct((lev, cols), jnp.float32),
        jax.ShapeDtypeStruct((lev, rows), jnp.float32),
        jax.ShapeDtypeStruct((lev, rows), jnp.float32),
        jax.ShapeDtypeStruct(buckets.shape, buckets.dtype),
    ]
    out_specs = [
        pl.BlockSpec((LB, rows, cols), lambda i: (i, 0, 0)),
        lvl2, lvl2, full2((lev, rows)), full2((lev, rows)), whole,
    ]
    scratch = [
        pltpu.VMEM((4, lev, cols), jnp.float32),
        pltpu.VMEM((rows, 128), jnp.float32),
        pltpu.VMEM((rows, 128), jnp.float32),
        pltpu.VMEM(buckets.shape, buckets.dtype),
        pltpu.SemaphoreType.DMA((buckets.shape[0],)),
        pltpu.SemaphoreType.DMA((buckets.shape[0],)),
        pltpu.SemaphoreType.DMA((4,)),
        pltpu.SemaphoreType.DMA((4,)),
    ]
    return pl.pallas_call(
        first_kernel,
        grid=(nblk,),
        in_specs=in_specs,
        out_specs=out_specs,
        out_shape=out_shape,
        scratch_shapes=scratch,
        compiler_params=pltpu.CompilerParams(
            dimension_semantics=("arbitrary",), collective_id=2, has_side_effects=True
        ),
        cost_estimate=pl.CostEstimate(flops=30 * u.size, bytes_accessed=12 * u.size, transcendentals=0),
    )(coef, wet, u, u, u, buckets, *edges)


def stencil_kernel(with_edges, with_force, coef_ref, wet_ref, u_ref, above_ref, below_ref,
                   hn_ref, hs_ref, hw_ref, he_ref, *rest):
    if with_force:
        force_ref, rest = rest[0], rest[1:]
    if with_edges:
        buckets_ref, rest = rest[0], rest[1:]
    out_ref = rest[0]
    i = pl.program_id(0)
    nblk = pl.num_programs(0)
    horiz = coef_ref[0]
    vert = coef_ref[1]
    wet = wet_ref[...]
    rows, cols = wet.shape
    row = lax.broadcasted_iota(jnp.int32, (rows, cols), 0)
    col = lax.broadcasted_iota(jnp.int32, (rows, cols), 1)
    hw_t = jnp.transpose(hw_ref[...])
    he_t = jnp.transpose(he_ref[...])
    above = above_ref[0] * jnp.where(i > 0, 1.0, 0.0)
    below = below_ref[0] * jnp.where(i < nblk - 1, 1.0, 0.0)
    if with_edges:
        en_ref, es_ref, ew_ref, ee_ref, arrived_ref, qw_ref, qe_ref, recv, send_sem, recv_sem = rest[1:]

        @pl.when(i == 0)
        def _():
            start_spread(buckets_ref, recv, send_sem, recv_sem)
            qw_ref[...] = jnp.zeros_like(qw_ref)
            qe_ref[...] = jnp.zeros_like(qe_ref)

    if with_edges:
        lane = lax.broadcasted_iota(jnp.int32, qw_ref.shape, 1)
        qw = qw_ref[...]
        qe = qe_ref[...]
    for l in range(LB):
        u = u_ref[l]
        prev = u_ref[l - 1] if l > 0 else above
        nxt = u_ref[l + 1] if l < LB - 1 else below
        w = wet * u
        north = jnp.where(row == 0, hn_ref[l:l + 1, :], pltpu.roll(w, 1, 0))
        south = jnp.where(row == rows - 1, hs_ref[l:l + 1, :], pltpu.roll(w, rows - 1, 0))
        west = jnp.where(col == 0, hw_t[:, l:l + 1], pltpu.roll(w, 1, 1))
        east = jnp.where(col == cols - 1, he_t[:, l:l + 1], pltpu.roll(w, cols - 1, 1))
        lateral = north + south + west + east - 4.0 * w
        vertical = prev + nxt - 2.0 * u
        res = wet * (u + horiz * lateral + vert * vertical)
        if with_force and l == 0:
            res = res + jnp.where(i == 0, 1.0, 0.0) * (force_gain * wet * force_ref[...])
        out_ref[l] = res
        if with_edges:
            fw = wet * res
            en_ref[l:l + 1, :] = fw[0:1, :]
            es_ref[l:l + 1, :] = fw[rows - 1:rows, :]
            hit = lane == i * LB + l
            qw = jnp.where(hit, fw[:, 0:1], qw)
            qe = jnp.where(hit, fw[:, cols - 1:cols], qe)

    if with_edges:
        qw_ref[...] = qw
        qe_ref[...] = qe

        @pl.when(i == nblk - 1)
        def _():
            lev = ew_ref.shape[0]
            ew_ref[...] = jnp.transpose(qw_ref[...])[0:lev, :]
            ee_ref[...] = jnp.transpose(qe_ref[...])[0:lev, :]
            finish_spread(buckets_ref, recv, send_sem, recv_sem, arrived_ref)


def edges_kernel(wet_ref, u_ref, en_ref, es_ref, ew_ref, ee_ref, qw_ref, qe_ref):
    i = pl.program_id(0)
    nblk = pl.num_programs(0)
    wet = wet_ref[...]
    rows, cols = wet.shape

    @pl.when(i == 0)
    def _():
        qw_ref[...] = jnp.zeros_like(qw_ref)
        qe_ref[...] = jnp.zeros_like(qe_ref)

    lane = lax.broadcasted_iota(jnp.int32, qw_ref.shape, 1)
    qw = qw_ref[...]
    qe = qe_ref[...]
    for l in range(EB):
        fw = wet * u_ref[l]
        en_ref[l:l + 1, :] = fw[0:1, :]
        es_ref[l:l + 1, :] = fw[rows - 1:rows, :]
        hit = lane == i * EB + l
        qw = jnp.where(hit, fw[:, 0:1], qw)
        qe = jnp.where(hit, fw[:, cols - 1:cols], qe)
    qw_ref[...] = qw
    qe_ref[...] = qe

    @pl.when(i == nblk - 1)
    def _():
        lev = ew_ref.shape[0]
        ew_ref[...] = jnp.transpose(qw_ref[...])[0:lev, :]
        ee_ref[...] = jnp.transpose(qe_ref[...])[0:lev, :]


def masked_edges(wet, u):
    lev, rows, cols = u.shape
    lvl2 = pl.BlockSpec((EB, cols), lambda i: (i, 0))
    full2 = lambda shape: pl.BlockSpec(shape, lambda i: (0, 0))
    return pl.pallas_call(
        edges_kernel,
        grid=(lev // EB,),
        in_specs=[full2((rows, cols)), pl.BlockSpec((EB, rows, cols), lambda i: (i, 0, 0))],
        out_specs=[lvl2, lvl2, full2((lev, rows)), full2((lev, rows))],
        out_shape=[jax.ShapeDtypeStruct((lev, cols), jnp.float32)] * 2
        + [jax.ShapeDtypeStruct((lev, rows), jnp.float32)] * 2,
        scratch_shapes=[pltpu.VMEM((rows, 128), jnp.float32)] * 2,
        compiler_params=pltpu.CompilerParams(dimension_semantics=("arbitrary",)),
        cost_estimate=pl.CostEstimate(flops=2 * u.size, bytes_accessed=4 * u.size, transcendentals=0),
    )(wet, u)


def force_kernel(x_ref, wet_ref, f_ref, out_ref):
    out_ref[0] = x_ref[0] + force_gain * wet_ref[...] * f_ref[...]


def add_force(x, wet, f):
    lev, rows, cols = x.shape
    plane = pl.BlockSpec((rows, cols), lambda i: (0, 0))
    level0 = pl.BlockSpec((1, rows, cols), lambda i: (0, 0, 0))
    return pl.pallas_call(
        force_kernel,
        grid=(1,),
        in_specs=[level0, plane, plane],
        out_specs=level0,
        out_shape=jax.ShapeDtypeStruct(x.shape, x.dtype),
        input_output_aliases={0: 0},
    )(x, wet, f)


def stencil_step(coef, wet, u, halos, force=None, buckets=None):
    with_edges = buckets is not None
    lev, rows, cols = u.shape
    nblk = lev // LB
    full2 = lambda shape: pl.BlockSpec(shape, lambda i: (0, 0))
    lvl2 = pl.BlockSpec((LB, cols), lambda i: (i, 0))
    in_specs = [
        pl.BlockSpec(memory_space=pltpu.SMEM),
        full2((rows, cols)),
        pl.BlockSpec((LB, rows, cols), lambda i: (i, 0, 0)),
        pl.BlockSpec((1, rows, cols), lambda i: (jnp.maximum(i * LB - 1, 0), 0, 0)),
        pl.BlockSpec((1, rows, cols), lambda i: (jnp.minimum(i * LB + LB, lev - 1), 0, 0)),
        lvl2, lvl2, lvl2, lvl2,
    ]
    args = [coef, wet, u, u, u] + list(halos)
    if force is not None:
        in_specs.append(full2((rows, cols)))
        args.append(force)
    if with_edges:
        in_specs.append(pl.BlockSpec(buckets.shape, lambda i: (0, 0, 0, 0)))
        args.append(buckets)
    out_shape = [jax.ShapeDtypeStruct((lev, rows, cols), jnp.float32)]
    out_specs = [pl.BlockSpec((LB, rows, cols), lambda i: (i, 0, 0))]
    scratch = []
    params = dict(dimension_semantics=("arbitrary",))
    if with_edges:
        out_shape += [jax.ShapeDtypeStruct((lev, cols), jnp.float32)] * 2
        out_shape += [jax.ShapeDtypeStruct((lev, rows), jnp.float32)] * 2
        out_shape += [jax.ShapeDtypeStruct(buckets.shape, buckets.dtype)]
        out_specs += [lvl2, lvl2, full2((lev, rows)), full2((lev, rows))]
        out_specs += [pl.BlockSpec(buckets.shape, lambda i: (0, 0, 0, 0))]
        scratch = [pltpu.VMEM((rows, 128), jnp.float32)] * 2 + [
            pltpu.VMEM(buckets.shape, buckets.dtype),
            pltpu.SemaphoreType.DMA((buckets.shape[0],)),
            pltpu.SemaphoreType.DMA((buckets.shape[0],)),
        ]
        params.update(collective_id=2, has_side_effects=True)
    return pl.pallas_call(
        functools.partial(stencil_kernel, with_edges, force is not None),
        grid=(nblk,),
        in_specs=in_specs,
        out_specs=out_specs,
        out_shape=out_shape,
        scratch_shapes=scratch,
        compiler_params=pltpu.CompilerParams(**params),
        cost_estimate=pl.CostEstimate(flops=30 * u.size, bytes_accessed=12 * u.size, transcendentals=0),
    )(*args)


def halo_kernel(en_ref, es_ref, ew_ref, ee_ref, hn_ref, hs_ref, hw_ref, he_ref,
                buf, send_sem, recv_sem):
    mp = lax.axis_index("mp")
    gx = lax.axis_index("gx")
    gy = lax.axis_index("gy")
    ngx = lax.axis_size("gx")
    ngy = lax.axis_size("gy")
    mesh_id = pl.DeviceIdType.MESH
    links = [
        (gx < ngx - 1, (mp, gx + 1, gy), es_ref, 0),
        (gx > 0, (mp, gx - 1, gy), en_ref, 1),
        (gy < ngy - 1, (mp, gx, gy + 1), ee_ref, 2),
        (gy > 0, (mp, gx, gy - 1), ew_ref, 3),
    ]
    barrier = pltpu.get_barrier_semaphore()
    count = jnp.int32(0)
    for present, dev, _, _ in links:
        @pl.when(present)
        def _():
            pl.semaphore_signal(barrier, 1, device_id=dev, device_id_type=mesh_id)

        count = count + present.astype(jnp.int32)
    pl.semaphore_wait(barrier, count)

    copies = []
    for present, dev, src, slot in links:
        copy = pltpu.make_async_remote_copy(
            src_ref=src,
            dst_ref=buf.at[slot],
            send_sem=send_sem.at[slot],
            recv_sem=recv_sem.at[slot],
            device_id=dev,
            device_id_type=mesh_id,
        )
        pl.when(present)(copy.start)
        copies.append((present, copy))
    for present, copy in copies:
        pl.when(present)(copy.wait_send)
    fills = [gx > 0, gx < ngx - 1, gy > 0, gy < ngy - 1]
    outs = [hn_ref, hs_ref, hw_ref, he_ref]
    for slot, (filled, out) in enumerate(zip(fills, outs)):
        _, copy = copies[slot]

        @pl.when(filled)
        def _():
            copy.wait_recv()
            out[...] = buf[slot]

        @pl.when(jnp.logical_not(filled))
        def _():
            out[...] = jnp.zeros_like(out)


def exchange(en, es, ew, ee, call):
    shape = jax.ShapeDtypeStruct(en.shape, en.dtype)
    vmem = pl.BlockSpec(memory_space=pltpu.VMEM)
    return pl.pallas_call(
        halo_kernel,
        in_specs=[vmem] * 4,
        out_specs=[vmem] * 4,
        out_shape=[shape] * 4,
        scratch_shapes=[
            pltpu.VMEM((4,) + en.shape, en.dtype),
            pltpu.SemaphoreType.DMA((4,)),
            pltpu.SemaphoreType.DMA((4,)),
        ],
        compiler_params=pltpu.CompilerParams(collective_id=call, has_side_effects=True),
    )(en, es, ew, ee)


def bucket_kernel(target_ref, row_ref, contrib_ref, out_ref, count_ref):
    ntiles = contrib_ref.shape[0]
    ndest = out_ref.shape[0]
    sub = lax.broadcasted_iota(jnp.int32, (KF, CY), 0)
    out_ref[...] = jnp.zeros_like(out_ref)

    def clear(d, carry):
        count_ref[d] = 0
        return carry

    lax.fori_loop(0, ndest, clear, 0)

    def body(t, carry):
        d = target_ref[t]
        c = count_ref[d]
        count_ref[d] = c + 1
        out_ref[d, c] = contrib_ref[t]
        out_ref[d, CAP] = jnp.where(sub == c, row_ref[t].astype(jnp.float32), out_ref[d, CAP])
        return carry

    lax.fori_loop(0, ntiles, body, 0, unroll=8)


def local(states, surface, land_mask, tile_weights, tile_source, tile_target, tile_row):
    group = lax.axis_index("mp")
    ndev = lax.axis_size("gx") * lax.axis_size("gy")
    state = states[0]
    lev, rows_here, cols_here = state.shape
    wet = jnp.where(
        group == 0, jnp.ones(land_mask.shape, jnp.float32), land_mask.astype(jnp.float32)
    )
    coef = jnp.stack([jnp.where(group == 0, 0.15, 0.12), jnp.where(group == 0, 0.1, 0.15)]).astype(
        jnp.float32
    )

    src = (surface[0] * wet).astype(jnp.bfloat16)
    source = tile_source[0, 0, 0]
    target = tile_target[0, 0, 0, :, 0]
    dest_row = tile_row[0, 0, 0]
    ntiles = source.shape[0]
    picked = jnp.take(src, source, axis=1)
    contrib = jnp.einsum(
        "tji,kti->tkj", tile_weights[0, 0, 0], picked, preferred_element_type=jnp.float32
    )
    buckets = pl.pallas_call(
        bucket_kernel,
        in_specs=[
            pl.BlockSpec(memory_space=pltpu.SMEM),
            pl.BlockSpec(memory_space=pltpu.SMEM),
            pl.BlockSpec(memory_space=pltpu.VMEM),
        ],
        out_specs=pl.BlockSpec(memory_space=pltpu.VMEM),
        out_shape=jax.ShapeDtypeStruct((ndev, CAP + 1, KF, CY), jnp.float32),
        scratch_shapes=[pltpu.SMEM((ndev,), jnp.int32)],
    )(target, dest_row, contrib)
    second, arrived = interval(coef, wet, state, buckets, masked_edges(wet, state))
    got_rows = arrived[:, CAP, :, 0].astype(jnp.int32)
    select = (
        got_rows[:, :, None] == jnp.arange(rows_here, dtype=jnp.int32)[None, None, :]
    ).astype(jnp.float32)
    sent = jnp.einsum(
        "scr,sckj->krj", select, arrived[:, :CAP], precision=lax.Precision.HIGHEST
    )
    received = lax.ppermute(sent, "mp", [(0, 1), (1, 0)])

    second = add_force(second, wet, received[0])
    return (second[None], received[None])


def solution(mesh):
    return jax.shard_map(
        local,
        mesh=mesh,
        in_specs=(
            P("mp", None, "gx", "gy"),
            P("mp", None, "gx", "gy"),
            P("gx", "gy"),
            P("mp", "gx", "gy", None, None, None),
            P("mp", "gx", "gy", None),
            P("mp", "gx", "gy", None, None),
            P("mp", "gx", "gy", None),
        ),
        out_specs=(P("mp", None, "gx", "gy"), P("mp", None, "gx", "gy")),
        check_vma=False,
    )
```

```python
import functools

import jax
import jax.numpy as jnp
from jax import lax
from jax.experimental import pallas as pl
from jax.experimental.pallas import tpu as pltpu
from jax.sharding import PartitionSpec as P

CY = 128
KF = 8
CAP = 8
LB = 8
EB = 32

force_gain = 0.5


def shift_pairs(devices, forward):
    up = [(i, i + 1) for i in range(devices - 1)]
    return up if forward else [(j, i) for i, j in up]


def start_spread(buckets_ref, recv, send_sem, recv_sem, first_out=None):
    mp = lax.axis_index("mp")
    ngy = lax.axis_size("gy")
    ndev = lax.axis_size("gx") * ngy
    me = lax.axis_index("gx") * ngy + lax.axis_index("gy")
    mesh_id = pl.DeviceIdType.MESH
    barrier = pltpu.get_barrier_semaphore()

    def greet(d, carry):
        @pl.when(d != me)
        def _():
            pl.semaphore_signal(barrier, 1, device_id=(mp, d // ngy, d % ngy), device_id_type=mesh_id)

        return carry

    lax.fori_loop(0, ndev, greet, 0)
    pl.semaphore_wait(barrier, ndev - 1)
    if first_out is not None:
        first_out()
    recv[me] = buckets_ref[me]

    def send(k, carry):
        d = (me + k) % ndev
        pltpu.make_async_remote_copy(
            src_ref=buckets_ref.at[d],
            dst_ref=recv.at[me],
            send_sem=send_sem.at[d],
            recv_sem=recv_sem.at[me],
            device_id=(mp, d // ngy, d % ngy),
            device_id_type=mesh_id,
        ).start()
        return carry

    lax.fori_loop(1, ndev, send, 0)


def finish_spread(buckets_ref, recv, send_sem, recv_sem, arrived_ref):
    ngy = lax.axis_size("gy")
    ndev = lax.axis_size("gx") * ngy
    me = lax.axis_index("gx") * ngy + lax.axis_index("gy")

    def wait(d, carry):
        @pl.when(d != me)
        def _():
            copy = pltpu.make_async_remote_copy(
                src_ref=buckets_ref.at[d],
                dst_ref=recv.at[d],
                send_sem=send_sem.at[d],
                recv_sem=recv_sem.at[d],
                device_id=(lax.axis_index("mp"), d // ngy, d % ngy),
                device_id_type=pl.DeviceIdType.MESH,
            )
            copy.wait_send()
            copy.wait_recv()

        return carry

    lax.fori_loop(0, ndev, wait, 0)
    arrived_ref[...] = recv[...]


def interval_kernel(coef_ref, wet_ref, u_ref, above_ref, below_ref, buckets_ref,
                    e0n, e0s, e0w, e0e,
                    out_ref, arrived_ref,
                    first, edge1, halo0, halo1, qw_ref, qe_ref, recv,
                    send_sem, recv_sem, hsend, hrecv):
    p = pl.program_id(0)
    i = pl.program_id(1)
    nblk = pl.num_programs(1)
    wet = wet_ref[...]
    rows, cols = wet.shape
    lev = first.shape[0]
    mp = lax.axis_index("mp")
    gx = lax.axis_index("gx")
    gy = lax.axis_index("gy")
    ngx = lax.axis_size("gx")
    ngy = lax.axis_size("gy")
    ndev = ngx * ngy
    me = gx * ngy + gy
    mesh_id = pl.DeviceIdType.MESH
    links = [
        (gx < ngx - 1, (mp, gx + 1, gy), 1, 0),
        (gx > 0, (mp, gx - 1, gy), 0, 1),
        (gy < ngy - 1, (mp, gx, gy + 1), 3, 2),
        (gy > 0, (mp, gx, gy - 1), 2, 3),
    ]
    fills = [gx > 0, gx < ngx - 1, gy > 0, gy < ngy - 1]
    edge0 = [e0n, e0s, e0w, e0e]

    def halo_copy(stage, src, slot, dev):
        srcs = edge0[src] if stage == 0 else edge1.at[src]
        dsts = halo0.at[slot] if stage == 0 else halo1.at[slot]
        return pltpu.make_async_remote_copy(
            src_ref=srcs,
            dst_ref=dsts,
            send_sem=hsend.at[stage, slot],
            recv_sem=hrecv.at[stage, slot],
            device_id=dev,
            device_id_type=mesh_id,
        )

    def send_halos(stage):
        for present, dev, src, slot in links:
            pl.when(present)(halo_copy(stage, src, slot, dev).start)

    def take_halos(stage, dst):
        for present, dev, src, slot in links:
            pl.when(present)(halo_copy(stage, src, slot, dev).wait_send)
        for slot, filled in enumerate(fills):
            _, dev, src, _ = links[slot]
            pl.when(filled)(halo_copy(stage, src, slot, dev).wait_recv)

            @pl.when(jnp.logical_not(filled))
            def _():
                dst[slot] = jnp.zeros_like(dst[slot])

    def bucket_copy(d):
        return pltpu.make_async_remote_copy(
            src_ref=buckets_ref.at[d],
            dst_ref=recv.at[me],
            send_sem=send_sem.at[d],
            recv_sem=recv_sem.at[me],
            device_id=(mp, d // ngy, d % ngy),
            device_id_type=mesh_id,
        )

    def issue(k0, count):
        for n in range(count):
            k = k0 + n

            @pl.when(k < ndev)
            def _():
                bucket_copy((me + k) % ndev).start()

    lane = lax.broadcasted_iota(jnp.int32, qw_ref.shape, 1)
    row = lax.broadcasted_iota(jnp.int32, (rows, cols), 0)
    col = lax.broadcasted_iota(jnp.int32, (rows, cols), 1)
    horiz = coef_ref[0]
    vert = coef_ref[1]

    def step(load, above, below, hn, hs, hw_t, he_t, store):
        for l in range(LB):
            u = load(l)
            prev = load(l - 1) if l > 0 else above
            nxt = load(l + 1) if l < LB - 1 else below
            w = wet * u
            north = jnp.where(row == 0, hn[l:l + 1, :], pltpu.roll(w, 1, 0))
            south = jnp.where(row == rows - 1, hs[l:l + 1, :], pltpu.roll(w, rows - 1, 0))
            west = jnp.where(col == 0, hw_t[:, l:l + 1], pltpu.roll(w, 1, 1))
            east = jnp.where(col == cols - 1, he_t[:, l:l + 1], pltpu.roll(w, cols - 1, 1))
            lateral = north + south + west + east - 4.0 * w
            vertical = prev + nxt - 2.0 * u
            store(l, wet * (u + horiz * lateral + vert * vertical))

    @pl.when((p == 0) & (i == 0))
    def _():
        barrier = pltpu.get_barrier_semaphore()

        def greet(d, carry):
            @pl.when(d != me)
            def _():
                pl.semaphore_signal(barrier, 1, device_id=(mp, d // ngy, d % ngy), device_id_type=mesh_id)

            return carry

        lax.fori_loop(0, ndev, greet, 0)
        pl.semaphore_wait(barrier, ndev - 1)
        send_halos(0)
        recv[me] = buckets_ref[me]
        take_halos(0, halo0)
        qw_ref[...] = jnp.zeros_like(qw_ref)
        qe_ref[...] = jnp.zeros_like(qe_ref)

    @pl.when(p == 0)
    def _():
        issue(1 + 4 * i, 4)
        blk = pl.ds(pl.multiple_of(i * LB, LB), LB)
        hn = halo0[0, blk]
        hs = halo0[1, blk]
        hw_t = jnp.transpose(halo0[2, blk])
        he_t = jnp.transpose(halo0[3, blk])
        above = above_ref[0] * jnp.where(i > 0, 1.0, 0.0)
        below = below_ref[0] * jnp.where(i < nblk - 1, 1.0, 0.0)
        qs = [qw_ref[...], qe_ref[...]]

        def store(l, res):
            first[i * LB + l] = res
            fw = wet * res
            edge1[0, i, l:l + 1, :] = fw[0:1, :]
            edge1[1, i, l:l + 1, :] = fw[rows - 1:rows, :]
            hit = lane == i * LB + l
            qs[0] = jnp.where(hit, fw[:, 0:1], qs[0])
            qs[1] = jnp.where(hit, fw[:, cols - 1:cols], qs[1])

        step(lambda l: u_ref[l], above, below, hn, hs, hw_t, he_t, store)
        qw_ref[...] = qs[0]
        qe_ref[...] = qs[1]

    @pl.when((p == 0) & (i == nblk - 1))
    def _():
        edge1[2] = jnp.transpose(qw_ref[...])[0:lev, :].reshape(nblk, LB, rows)
        edge1[3] = jnp.transpose(qe_ref[...])[0:lev, :].reshape(nblk, LB, rows)
        send_halos(1)

    @pl.when((p == 1) & (i == 0))
    def _():
        take_halos(1, halo1)

        def late(k, carry):
            bucket_copy((me + k) % ndev).start()
            return carry

        lax.fori_loop(min(1 + 4 * nblk, ndev), ndev, late, 0)

    @pl.when(p == 1)
    def _():
        base = i * LB
        above = first[jnp.maximum(base - 1, 0)] * jnp.where(i > 0, 1.0, 0.0)
        below = first[jnp.minimum(base + LB, lev - 1)] * jnp.where(i < nblk - 1, 1.0, 0.0)
        hw_t = jnp.transpose(halo1[2, i])
        he_t = jnp.transpose(halo1[3, i])

        def store(l, res):
            out_ref[l] = res

        step(lambda l: first[base + l], above, below, halo1[0, i], halo1[1, i], hw_t, he_t, store)

    @pl.when((p == 1) & (i == nblk - 1))
    def _():
        def wait(d, carry):
            @pl.when(d != me)
            def _():
                copy = pltpu.make_async_remote_copy(
                    src_ref=buckets_ref.at[d],
                    dst_ref=recv.at[d],
                    send_sem=send_sem.at[d],
                    recv_sem=recv_sem.at[d],
                    device_id=(mp, d // ngy, d % ngy),
                    device_id_type=mesh_id,
                )
                copy.wait_send()
                copy.wait_recv()

            return carry

        lax.fori_loop(0, ndev, wait, 0)
        arrived_ref[...] = recv[...]


def interval(coef, wet, u, buckets, edges):
    lev, rows, cols = u.shape
    nblk = lev // LB
    full2 = lambda shape: pl.BlockSpec(shape, lambda p, i: (0, 0))
    whole = pl.BlockSpec(buckets.shape, lambda p, i: (0, 0, 0, 0))
    held = lambda p, i: i + p * (nblk - 1 - i)
    in_specs = [
        pl.BlockSpec(memory_space=pltpu.SMEM),
        full2((rows, cols)),
        pl.BlockSpec((LB, rows, cols), lambda p, i: (held(p, i), 0, 0)),
        pl.BlockSpec((1, rows, cols), lambda p, i: (jnp.maximum(held(p, i) * LB - 1, 0), 0, 0)),
        pl.BlockSpec((1, rows, cols), lambda p, i: (jnp.minimum(held(p, i) * LB + LB, lev - 1), 0, 0)),
        whole,
    ] + [full2((lev, cols))] * 4
    out_shape = [
        jax.ShapeDtypeStruct((lev, rows, cols), jnp.float32),
        jax.ShapeDtypeStruct(buckets.shape, buckets.dtype),
    ]
    out_specs = [pl.BlockSpec((LB, rows, cols), lambda p, i: (i * p, 0, 0)), whole]
    scratch = [
        pltpu.VMEM((lev, rows, cols), jnp.float32),
        pltpu.VMEM((4, nblk, LB, cols), jnp.float32),
        pltpu.VMEM((4, lev, cols), jnp.float32),
        pltpu.VMEM((4, nblk, LB, cols), jnp.float32),
        pltpu.VMEM((rows, 128), jnp.float32),
        pltpu.VMEM((rows, 128), jnp.float32),
        pltpu.VMEM(buckets.shape, buckets.dtype),
        pltpu.SemaphoreType.DMA((buckets.shape[0],)),
        pltpu.SemaphoreType.DMA((buckets.shape[0],)),
        pltpu.SemaphoreType.DMA((2, 4)),
        pltpu.SemaphoreType.DMA((2, 4)),
    ]
    return pl.pallas_call(
        interval_kernel,
        grid=(2, nblk),
        in_specs=in_specs,
        out_specs=out_specs,
        out_shape=out_shape,
        scratch_shapes=scratch,
        compiler_params=pltpu.CompilerParams(
            dimension_semantics=("arbitrary", "arbitrary"), collective_id=3, has_side_effects=True,
            vmem_limit_bytes=48 * 1024 * 1024,
        ),
        cost_estimate=pl.CostEstimate(flops=60 * u.size, bytes_accessed=12 * u.size, transcendentals=0),
    )(coef, wet, u, u, u, buckets, *edges)


def first_kernel(coef_ref, wet_ref, u_ref, above_ref, below_ref, buckets_ref,
                 e0n, e0s, e0w, e0e,
                 out_ref, en_ref, es_ref, ew_ref, ee_ref, arrived_ref,
                 halo, qw_ref, qe_ref, recv, send_sem, recv_sem, hsend, hrecv):
    i = pl.program_id(0)
    nblk = pl.num_programs(0)
    edge0 = [e0n, e0s, e0w, e0e]
    wet = wet_ref[...]
    rows, cols = wet.shape
    lev = ew_ref.shape[0]
    mp = lax.axis_index("mp")
    gx = lax.axis_index("gx")
    gy = lax.axis_index("gy")
    ngx = lax.axis_size("gx")
    ngy = lax.axis_size("gy")
    mesh_id = pl.DeviceIdType.MESH
    links = [
        (gx < ngx - 1, (mp, gx + 1, gy), 1, 0),
        (gx > 0, (mp, gx - 1, gy), 0, 1),
        (gy < ngy - 1, (mp, gx, gy + 1), 3, 2),
        (gy > 0, (mp, gx, gy - 1), 2, 3),
    ]
    fills = [gx > 0, gx < ngx - 1, gy > 0, gy < ngy - 1]
    copies = [
        pltpu.make_async_remote_copy(
            src_ref=edge0[src],
            dst_ref=halo.at[slot],
            send_sem=hsend.at[slot],
            recv_sem=hrecv.at[slot],
            device_id=dev,
            device_id_type=mesh_id,
        )
        for _, dev, src, slot in links
    ]
    lane = lax.broadcasted_iota(jnp.int32, qw_ref.shape, 1)

    def send_halos():
        for (present, _, _, _), copy in zip(links, copies):
            pl.when(present)(copy.start)

    @pl.when(i == 0)
    def _():
        start_spread(buckets_ref, recv, send_sem, recv_sem, send_halos)
        for (present, _, _, _), copy in zip(links, copies):
            pl.when(present)(copy.wait_send)
        for slot, filled in enumerate(fills):
            pl.when(filled)(copies[slot].wait_recv)

            @pl.when(jnp.logical_not(filled))
            def _():
                halo[slot] = jnp.zeros_like(halo[slot])

        qw_ref[...] = jnp.zeros_like(qw_ref)
        qe_ref[...] = jnp.zeros_like(qe_ref)

    def _():
        horiz = coef_ref[0]
        vert = coef_ref[1]
        row = lax.broadcasted_iota(jnp.int32, (rows, cols), 0)
        col = lax.broadcasted_iota(jnp.int32, (rows, cols), 1)
        hn = halo[0, pl.ds(i * LB, LB)]
        hs = halo[1, pl.ds(i * LB, LB)]
        hw_t = jnp.transpose(halo[2, pl.ds(i * LB, LB)])
        he_t = jnp.transpose(halo[3, pl.ds(i * LB, LB)])
        above = above_ref[0] * jnp.where(i > 0, 1.0, 0.0)
        below = below_ref[0] * jnp.where(i < nblk - 1, 1.0, 0.0)
        qw = qw_ref[...]
        qe = qe_ref[...]
        for l in range(LB):
            u = u_ref[l]
            prev = u_ref[l - 1] if l > 0 else above
            nxt = u_ref[l + 1] if l < LB - 1 else below
            w = wet * u
            north = jnp.where(row == 0, hn[l:l + 1, :], pltpu.roll(w, 1, 0))
            south = jnp.where(row == rows - 1, hs[l:l + 1, :], pltpu.roll(w, rows - 1, 0))
            west = jnp.where(col == 0, hw_t[:, l:l + 1], pltpu.roll(w, 1, 1))
            east = jnp.where(col == cols - 1, he_t[:, l:l + 1], pltpu.roll(w, cols - 1, 1))
            lateral = north + south + west + east - 4.0 * w
            vertical = prev + nxt - 2.0 * u
            res = wet * (u + horiz * lateral + vert * vertical)
            out_ref[l] = res
            fw = wet * res
            en_ref[l:l + 1, :] = fw[0:1, :]
            es_ref[l:l + 1, :] = fw[rows - 1:rows, :]
            hit = lane == i * LB + l
            qw = jnp.where(hit, fw[:, 0:1], qw)
            qe = jnp.where(hit, fw[:, cols - 1:cols], qe)
        qw_ref[...] = qw
        qe_ref[...] = qe

    _()

    @pl.when(i == nblk - 1)
    def _():
        ew_ref[...] = jnp.transpose(qw_ref[...])[0:lev, :]
        ee_ref[...] = jnp.transpose(qe_ref[...])[0:lev, :]
        finish_spread(buckets_ref, recv, send_sem, recv_sem, arrived_ref)


def first_step(coef, wet, u, buckets, edges):
    lev, rows, cols = u.shape
    nblk = lev // LB
    full2 = lambda shape: pl.BlockSpec(shape, lambda i: (0, 0))
    lvl2 = pl.BlockSpec((LB, cols), lambda i: (i, 0))
    whole = pl.BlockSpec(buckets.shape, lambda i: (0, 0, 0, 0))
    in_specs = [
        pl.BlockSpec(memory_space=pltpu.SMEM),
        full2((rows, cols)),
        pl.BlockSpec((LB, rows, cols), lambda i: (i, 0, 0)),
        pl.BlockSpec((1, rows, cols), lambda i: (jnp.maximum(i * LB - 1, 0), 0, 0)),
        pl.BlockSpec((1, rows, cols), lambda i: (jnp.minimum(i * LB + LB, lev - 1), 0, 0)),
        whole,
    ] + [full2((lev, cols))] * 4
    out_shape = [
        jax.ShapeDtypeStruct((lev, rows, cols), jnp.float32),
        jax.ShapeDtypeStruct((lev, cols), jnp.float32),
        jax.ShapeDtypeStruct((lev, cols), jnp.float32),
        jax.ShapeDtypeStruct((lev, rows), jnp.float32),
        jax.ShapeDtypeStruct((lev, rows), jnp.float32),
        jax.ShapeDtypeStruct(buckets.shape, buckets.dtype),
    ]
    out_specs = [
        pl.BlockSpec((LB, rows, cols), lambda i: (i, 0, 0)),
        lvl2, lvl2, full2((lev, rows)), full2((lev, rows)), whole,
    ]
    scratch = [
        pltpu.VMEM((4, lev, cols), jnp.float32),
        pltpu.VMEM((rows, 128), jnp.float32),
        pltpu.VMEM((rows, 128), jnp.float32),
        pltpu.VMEM(buckets.shape, buckets.dtype),
        pltpu.SemaphoreType.DMA((buckets.shape[0],)),
        pltpu.SemaphoreType.DMA((buckets.shape[0],)),
        pltpu.SemaphoreType.DMA((4,)),
        pltpu.SemaphoreType.DMA((4,)),
    ]
    return pl.pallas_call(
        first_kernel,
        grid=(nblk,),
        in_specs=in_specs,
        out_specs=out_specs,
        out_shape=out_shape,
        scratch_shapes=scratch,
        compiler_params=pltpu.CompilerParams(
            dimension_semantics=("arbitrary",), collective_id=2, has_side_effects=True
        ),
        cost_estimate=pl.CostEstimate(flops=30 * u.size, bytes_accessed=12 * u.size, transcendentals=0),
    )(coef, wet, u, u, u, buckets, *edges)


def stencil_kernel(with_edges, with_force, coef_ref, wet_ref, u_ref, above_ref, below_ref,
                   hn_ref, hs_ref, hw_ref, he_ref, *rest):
    if with_force:
        force_ref, rest = rest[0], rest[1:]
    if with_edges:
        buckets_ref, rest = rest[0], rest[1:]
    out_ref = rest[0]
    i = pl.program_id(0)
    nblk = pl.num_programs(0)
    horiz = coef_ref[0]
    vert = coef_ref[1]
    wet = wet_ref[...]
    rows, cols = wet.shape
    row = lax.broadcasted_iota(jnp.int32, (rows, cols), 0)
    col = lax.broadcasted_iota(jnp.int32, (rows, cols), 1)
    hw_t = jnp.transpose(hw_ref[...])
    he_t = jnp.transpose(he_ref[...])
    above = above_ref[0] * jnp.where(i > 0, 1.0, 0.0)
    below = below_ref[0] * jnp.where(i < nblk - 1, 1.0, 0.0)
    if with_edges:
        en_ref, es_ref, ew_ref, ee_ref, arrived_ref, qw_ref, qe_ref, recv, send_sem, recv_sem = rest[1:]

        @pl.when(i == 0)
        def _():
            start_spread(buckets_ref, recv, send_sem, recv_sem)
            qw_ref[...] = jnp.zeros_like(qw_ref)
            qe_ref[...] = jnp.zeros_like(qe_ref)

    if with_edges:
        lane = lax.broadcasted_iota(jnp.int32, qw_ref.shape, 1)
        qw = qw_ref[...]
        qe = qe_ref[...]
    for l in range(LB):
        u = u_ref[l]
        prev = u_ref[l - 1] if l > 0 else above
        nxt = u_ref[l + 1] if l < LB - 1 else below
        w = wet * u
        north = jnp.where(row == 0, hn_ref[l:l + 1, :], pltpu.roll(w, 1, 0))
        south = jnp.where(row == rows - 1, hs_ref[l:l + 1, :], pltpu.roll(w, rows - 1, 0))
        west = jnp.where(col == 0, hw_t[:, l:l + 1], pltpu.roll(w, 1, 1))
        east = jnp.where(col == cols - 1, he_t[:, l:l + 1], pltpu.roll(w, cols - 1, 1))
        lateral = north + south + west + east - 4.0 * w
        vertical = prev + nxt - 2.0 * u
        res = wet * (u + horiz * lateral + vert * vertical)
        if with_force and l == 0:
            res = res + jnp.where(i == 0, 1.0, 0.0) * (force_gain * wet * force_ref[...])
        out_ref[l] = res
        if with_edges:
            fw = wet * res
            en_ref[l:l + 1, :] = fw[0:1, :]
            es_ref[l:l + 1, :] = fw[rows - 1:rows, :]
            hit = lane == i * LB + l
            qw = jnp.where(hit, fw[:, 0:1], qw)
            qe = jnp.where(hit, fw[:, cols - 1:cols], qe)

    if with_edges:
        qw_ref[...] = qw
        qe_ref[...] = qe

        @pl.when(i == nblk - 1)
        def _():
            lev = ew_ref.shape[0]
            ew_ref[...] = jnp.transpose(qw_ref[...])[0:lev, :]
            ee_ref[...] = jnp.transpose(qe_ref[...])[0:lev, :]
            finish_spread(buckets_ref, recv, send_sem, recv_sem, arrived_ref)


def edges_kernel(wet_ref, u_ref, en_ref, es_ref, ew_ref, ee_ref, qw_ref, qe_ref):
    i = pl.program_id(0)
    nblk = pl.num_programs(0)
    wet = wet_ref[...]
    rows, cols = wet.shape

    @pl.when(i == 0)
    def _():
        qw_ref[...] = jnp.zeros_like(qw_ref)
        qe_ref[...] = jnp.zeros_like(qe_ref)

    lane = lax.broadcasted_iota(jnp.int32, qw_ref.shape, 1)
    qw = qw_ref[...]
    qe = qe_ref[...]
    for l in range(EB):
        fw = wet * u_ref[l]
        en_ref[l:l + 1, :] = fw[0:1, :]
        es_ref[l:l + 1, :] = fw[rows - 1:rows, :]
        hit = lane == i * EB + l
        qw = jnp.where(hit, fw[:, 0:1], qw)
        qe = jnp.where(hit, fw[:, cols - 1:cols], qe)
    qw_ref[...] = qw
    qe_ref[...] = qe

    @pl.when(i == nblk - 1)
    def _():
        lev = ew_ref.shape[0]
        ew_ref[...] = jnp.transpose(qw_ref[...])[0:lev, :]
        ee_ref[...] = jnp.transpose(qe_ref[...])[0:lev, :]


def masked_edges(wet, u):
    lev, rows, cols = u.shape
    lvl2 = pl.BlockSpec((EB, cols), lambda i: (i, 0))
    full2 = lambda shape: pl.BlockSpec(shape, lambda i: (0, 0))
    return pl.pallas_call(
        edges_kernel,
        grid=(lev // EB,),
        in_specs=[full2((rows, cols)), pl.BlockSpec((EB, rows, cols), lambda i: (i, 0, 0))],
        out_specs=[lvl2, lvl2, full2((lev, rows)), full2((lev, rows))],
        out_shape=[jax.ShapeDtypeStruct((lev, cols), jnp.float32)] * 2
        + [jax.ShapeDtypeStruct((lev, rows), jnp.float32)] * 2,
        scratch_shapes=[pltpu.VMEM((rows, 128), jnp.float32)] * 2,
        compiler_params=pltpu.CompilerParams(dimension_semantics=("arbitrary",)),
        cost_estimate=pl.CostEstimate(flops=2 * u.size, bytes_accessed=4 * u.size, transcendentals=0),
    )(wet, u)


def force_kernel(x_ref, wet_ref, f_ref, out_ref):
    out_ref[0] = x_ref[0] + force_gain * wet_ref[...] * f_ref[...]


def add_force(x, wet, f):
    lev, rows, cols = x.shape
    plane = pl.BlockSpec((rows, cols), lambda i: (0, 0))
    level0 = pl.BlockSpec((1, rows, cols), lambda i: (0, 0, 0))
    return pl.pallas_call(
        force_kernel,
        grid=(1,),
        in_specs=[level0, plane, plane],
        out_specs=level0,
        out_shape=jax.ShapeDtypeStruct(x.shape, x.dtype),
        input_output_aliases={0: 0},
    )(x, wet, f)


def stencil_step(coef, wet, u, halos, force=None, buckets=None):
    with_edges = buckets is not None
    lev, rows, cols = u.shape
    nblk = lev // LB
    full2 = lambda shape: pl.BlockSpec(shape, lambda i: (0, 0))
    lvl2 = pl.BlockSpec((LB, cols), lambda i: (i, 0))
    in_specs = [
        pl.BlockSpec(memory_space=pltpu.SMEM),
        full2((rows, cols)),
        pl.BlockSpec((LB, rows, cols), lambda i: (i, 0, 0)),
        pl.BlockSpec((1, rows, cols), lambda i: (jnp.maximum(i * LB - 1, 0), 0, 0)),
        pl.BlockSpec((1, rows, cols), lambda i: (jnp.minimum(i * LB + LB, lev - 1), 0, 0)),
        lvl2, lvl2, lvl2, lvl2,
    ]
    args = [coef, wet, u, u, u] + list(halos)
    if force is not None:
        in_specs.append(full2((rows, cols)))
        args.append(force)
    if with_edges:
        in_specs.append(pl.BlockSpec(buckets.shape, lambda i: (0, 0, 0, 0)))
        args.append(buckets)
    out_shape = [jax.ShapeDtypeStruct((lev, rows, cols), jnp.float32)]
    out_specs = [pl.BlockSpec((LB, rows, cols), lambda i: (i, 0, 0))]
    scratch = []
    params = dict(dimension_semantics=("arbitrary",))
    if with_edges:
        out_shape += [jax.ShapeDtypeStruct((lev, cols), jnp.float32)] * 2
        out_shape += [jax.ShapeDtypeStruct((lev, rows), jnp.float32)] * 2
        out_shape += [jax.ShapeDtypeStruct(buckets.shape, buckets.dtype)]
        out_specs += [lvl2, lvl2, full2((lev, rows)), full2((lev, rows))]
        out_specs += [pl.BlockSpec(buckets.shape, lambda i: (0, 0, 0, 0))]
        scratch = [pltpu.VMEM((rows, 128), jnp.float32)] * 2 + [
            pltpu.VMEM(buckets.shape, buckets.dtype),
            pltpu.SemaphoreType.DMA((buckets.shape[0],)),
            pltpu.SemaphoreType.DMA((buckets.shape[0],)),
        ]
        params.update(collective_id=2, has_side_effects=True)
    return pl.pallas_call(
        functools.partial(stencil_kernel, with_edges, force is not None),
        grid=(nblk,),
        in_specs=in_specs,
        out_specs=out_specs,
        out_shape=out_shape,
        scratch_shapes=scratch,
        compiler_params=pltpu.CompilerParams(**params),
        cost_estimate=pl.CostEstimate(flops=30 * u.size, bytes_accessed=12 * u.size, transcendentals=0),
    )(*args)


def halo_kernel(en_ref, es_ref, ew_ref, ee_ref, hn_ref, hs_ref, hw_ref, he_ref,
                buf, send_sem, recv_sem):
    mp = lax.axis_index("mp")
    gx = lax.axis_index("gx")
    gy = lax.axis_index("gy")
    ngx = lax.axis_size("gx")
    ngy = lax.axis_size("gy")
    mesh_id = pl.DeviceIdType.MESH
    links = [
        (gx < ngx - 1, (mp, gx + 1, gy), es_ref, 0),
        (gx > 0, (mp, gx - 1, gy), en_ref, 1),
        (gy < ngy - 1, (mp, gx, gy + 1), ee_ref, 2),
        (gy > 0, (mp, gx, gy - 1), ew_ref, 3),
    ]
    barrier = pltpu.get_barrier_semaphore()
    count = jnp.int32(0)
    for present, dev, _, _ in links:
        @pl.when(present)
        def _():
            pl.semaphore_signal(barrier, 1, device_id=dev, device_id_type=mesh_id)

        count = count + present.astype(jnp.int32)
    pl.semaphore_wait(barrier, count)

    copies = []
    for present, dev, src, slot in links:
        copy = pltpu.make_async_remote_copy(
            src_ref=src,
            dst_ref=buf.at[slot],
            send_sem=send_sem.at[slot],
            recv_sem=recv_sem.at[slot],
            device_id=dev,
            device_id_type=mesh_id,
        )
        pl.when(present)(copy.start)
        copies.append((present, copy))
    for present, copy in copies:
        pl.when(present)(copy.wait_send)
    fills = [gx > 0, gx < ngx - 1, gy > 0, gy < ngy - 1]
    outs = [hn_ref, hs_ref, hw_ref, he_ref]
    for slot, (filled, out) in enumerate(zip(fills, outs)):
        _, copy = copies[slot]

        @pl.when(filled)
        def _():
            copy.wait_recv()
            out[...] = buf[slot]

        @pl.when(jnp.logical_not(filled))
        def _():
            out[...] = jnp.zeros_like(out)


def exchange(en, es, ew, ee, call):
    shape = jax.ShapeDtypeStruct(en.shape, en.dtype)
    vmem = pl.BlockSpec(memory_space=pltpu.VMEM)
    return pl.pallas_call(
        halo_kernel,
        in_specs=[vmem] * 4,
        out_specs=[vmem] * 4,
        out_shape=[shape] * 4,
        scratch_shapes=[
            pltpu.VMEM((4,) + en.shape, en.dtype),
            pltpu.SemaphoreType.DMA((4,)),
            pltpu.SemaphoreType.DMA((4,)),
        ],
        compiler_params=pltpu.CompilerParams(collective_id=call, has_side_effects=True),
    )(en, es, ew, ee)


def bucket_kernel(target_ref, row_ref, contrib_ref, out_ref, count_ref):
    ntiles = contrib_ref.shape[0]
    ndest = out_ref.shape[0]
    sub = lax.broadcasted_iota(jnp.int32, (KF, CY), 0)
    out_ref[...] = jnp.zeros_like(out_ref)

    def clear(d, carry):
        count_ref[d] = 0
        return carry

    lax.fori_loop(0, ndest, clear, 0)

    def body(t, carry):
        d = target_ref[t]
        c = count_ref[d]
        count_ref[d] = c + 1
        out_ref[d, c] = contrib_ref[t]
        out_ref[d, CAP] = jnp.where(sub == c, row_ref[t].astype(jnp.float32), out_ref[d, CAP])
        return carry

    lax.fori_loop(0, ntiles, body, 0, unroll=8)


def local(states, surface, land_mask, tile_weights, tile_source, tile_target, tile_row):
    group = lax.axis_index("mp")
    ndev = lax.axis_size("gx") * lax.axis_size("gy")
    state = states[0]
    lev, rows_here, cols_here = state.shape
    wet = jnp.where(
        group == 0, jnp.ones(land_mask.shape, jnp.float32), land_mask.astype(jnp.float32)
    )
    coef = jnp.stack([jnp.where(group == 0, 0.15, 0.12), jnp.where(group == 0, 0.1, 0.15)]).astype(
        jnp.float32
    )

    src = (surface[0] * wet).astype(jnp.bfloat16)
    source = tile_source[0, 0, 0]
    target = tile_target[0, 0, 0, :, 0]
    dest_row = tile_row[0, 0, 0]
    ntiles = source.shape[0]
    picked = jnp.take(src, source, axis=1)
    contrib = jnp.einsum(
        "tji,kti->tkj", tile_weights[0, 0, 0], picked, preferred_element_type=jnp.float32
    )
    buckets = pl.pallas_call(
        bucket_kernel,
        in_specs=[
            pl.BlockSpec(memory_space=pltpu.SMEM),
            pl.BlockSpec(memory_space=pltpu.SMEM),
            pl.BlockSpec(memory_space=pltpu.VMEM),
        ],
        out_specs=pl.BlockSpec(memory_space=pltpu.VMEM),
        out_shape=jax.ShapeDtypeStruct((ndev, CAP + 1, KF, CY), jnp.float32),
        scratch_shapes=[pltpu.SMEM((ndev,), jnp.int32)],
    )(target, dest_row, contrib)
    second, arrived = interval(coef, wet, state, buckets, masked_edges(wet, state))
    got_rows = arrived[:, CAP, :, 0].astype(jnp.int32)
    select = (
        got_rows[:, :, None] == jnp.arange(rows_here, dtype=jnp.int32)[None, None, :]
    ).astype(jnp.float32)
    sent = jnp.einsum(
        "scr,sckj->krj", select, arrived[:, :CAP], precision=lax.Precision.HIGHEST
    )
    received = lax.ppermute(sent, "mp", [(0, 1), (1, 0)])

    second = add_force(second, wet, received[0])
    return (second[None], received[None])


def solution(mesh):
    return jax.shard_map(
        local,
        mesh=mesh,
        in_specs=(
            P("mp", None, "gx", "gy"),
            P("mp", None, "gx", "gy"),
            P("gx", "gy"),
            P("mp", "gx", "gy", None, None, None),
            P("mp", "gx", "gy", None),
            P("mp", "gx", "gy", None, None),
            P("mp", "gx", "gy", None),
        ),
        out_specs=(P("mp", None, "gx", "gy"), P("mp", None, "gx", "gy")),
        check_vma=False,
    )
```

```python
import functools

import jax
import jax.numpy as jnp
from jax import lax
from jax.experimental import pallas as pl
from jax.experimental.pallas import tpu as pltpu
from jax.sharding import PartitionSpec as P

CY = 128
KF = 8
CAP = 8
LB = 16
EB = 32

force_gain = 0.5


def shift_pairs(devices, forward):
    up = [(i, i + 1) for i in range(devices - 1)]
    return up if forward else [(j, i) for i, j in up]


def start_spread(buckets_ref, recv, send_sem, recv_sem, first_out=None):
    mp = lax.axis_index("mp")
    ngy = lax.axis_size("gy")
    ndev = lax.axis_size("gx") * ngy
    me = lax.axis_index("gx") * ngy + lax.axis_index("gy")
    mesh_id = pl.DeviceIdType.MESH
    barrier = pltpu.get_barrier_semaphore()

    def greet(d, carry):
        @pl.when(d != me)
        def _():
            pl.semaphore_signal(barrier, 1, device_id=(mp, d // ngy, d % ngy), device_id_type=mesh_id)

        return carry

    lax.fori_loop(0, ndev, greet, 0)
    pl.semaphore_wait(barrier, ndev - 1)
    if first_out is not None:
        first_out()
    recv[me] = buckets_ref[me]

    def send(k, carry):
        d = (me + k) % ndev
        pltpu.make_async_remote_copy(
            src_ref=buckets_ref.at[d],
            dst_ref=recv.at[me],
            send_sem=send_sem.at[d],
            recv_sem=recv_sem.at[me],
            device_id=(mp, d // ngy, d % ngy),
            device_id_type=mesh_id,
        ).start()
        return carry

    lax.fori_loop(1, ndev, send, 0)


def finish_spread(buckets_ref, recv, send_sem, recv_sem, arrived_ref):
    ngy = lax.axis_size("gy")
    ndev = lax.axis_size("gx") * ngy
    me = lax.axis_index("gx") * ngy + lax.axis_index("gy")

    def wait(d, carry):
        @pl.when(d != me)
        def _():
            copy = pltpu.make_async_remote_copy(
                src_ref=buckets_ref.at[d],
                dst_ref=recv.at[d],
                send_sem=send_sem.at[d],
                recv_sem=recv_sem.at[d],
                device_id=(lax.axis_index("mp"), d // ngy, d % ngy),
                device_id_type=pl.DeviceIdType.MESH,
            )
            copy.wait_send()
            copy.wait_recv()

        return carry

    lax.fori_loop(0, ndev, wait, 0)
    arrived_ref[...] = recv[...]


def interval_kernel(coef_ref, wet_ref, u_ref, above_ref, below_ref, buckets_ref,
                    e0n, e0s, e0w, e0e,
                    out_ref, arrived_ref,
                    first, edge1, halo0, halo1, qw_ref, qe_ref, recv,
                    send_sem, recv_sem, hsend, hrecv):
    p = pl.program_id(0)
    i = pl.program_id(1)
    nblk = pl.num_programs(1)
    wet = wet_ref[...]
    rows, cols = wet.shape
    lev = first.shape[0]
    mp = lax.axis_index("mp")
    gx = lax.axis_index("gx")
    gy = lax.axis_index("gy")
    ngx = lax.axis_size("gx")
    ngy = lax.axis_size("gy")
    ndev = ngx * ngy
    me = gx * ngy + gy
    mesh_id = pl.DeviceIdType.MESH
    links = [
        (gx < ngx - 1, (mp, gx + 1, gy), 1, 0),
        (gx > 0, (mp, gx - 1, gy), 0, 1),
        (gy < ngy - 1, (mp, gx, gy + 1), 3, 2),
        (gy > 0, (mp, gx, gy - 1), 2, 3),
    ]
    fills = [gx > 0, gx < ngx - 1, gy > 0, gy < ngy - 1]
    edge0 = [e0n, e0s, e0w, e0e]

    def halo_copy(stage, src, slot, dev):
        srcs = edge0[src] if stage == 0 else edge1.at[src]
        dsts = halo0.at[slot] if stage == 0 else halo1.at[slot]
        return pltpu.make_async_remote_copy(
            src_ref=srcs,
            dst_ref=dsts,
            send_sem=hsend.at[stage, slot],
            recv_sem=hrecv.at[stage, slot],
            device_id=dev,
            device_id_type=mesh_id,
        )

    def send_halos(stage):
        for present, dev, src, slot in links:
            pl.when(present)(halo_copy(stage, src, slot, dev).start)

    def take_halos(stage, dst):
        for present, dev, src, slot in links:
            pl.when(present)(halo_copy(stage, src, slot, dev).wait_send)
        for slot, filled in enumerate(fills):
            _, dev, src, _ = links[slot]
            pl.when(filled)(halo_copy(stage, src, slot, dev).wait_recv)

            @pl.when(jnp.logical_not(filled))
            def _():
                dst[slot] = jnp.zeros_like(dst[slot])

    def bucket_copy(d):
        return pltpu.make_async_remote_copy(
            src_ref=buckets_ref.at[d],
            dst_ref=recv.at[me],
            send_sem=send_sem.at[d],
            recv_sem=recv_sem.at[me],
            device_id=(mp, d // ngy, d % ngy),
            device_id_type=mesh_id,
        )

    def issue(k0, count):
        for n in range(count):
            k = k0 + n

            @pl.when(k < ndev)
            def _():
                bucket_copy((me + k) % ndev).start()

    lane = lax.broadcasted_iota(jnp.int32, qw_ref.shape, 1)
    row = lax.broadcasted_iota(jnp.int32, (rows, cols), 0)
    col = lax.broadcasted_iota(jnp.int32, (rows, cols), 1)
    horiz = coef_ref[0]
    vert = coef_ref[1]

    def step(load, above, below, hn, hs, hw_t, he_t, store):
        for l in range(LB):
            u = load(l)
            prev = load(l - 1) if l > 0 else above
            nxt = load(l + 1) if l < LB - 1 else below
            w = wet * u
            north = jnp.where(row == 0, hn[l:l + 1, :], pltpu.roll(w, 1, 0))
            south = jnp.where(row == rows - 1, hs[l:l + 1, :], pltpu.roll(w, rows - 1, 0))
            west = jnp.where(col == 0, hw_t[:, l:l + 1], pltpu.roll(w, 1, 1))
            east = jnp.where(col == cols - 1, he_t[:, l:l + 1], pltpu.roll(w, cols - 1, 1))
            lateral = north + south + west + east - 4.0 * w
            vertical = prev + nxt - 2.0 * u
            store(l, wet * (u + horiz * lateral + vert * vertical))

    @pl.when((p == 0) & (i == 0))
    def _():
        barrier = pltpu.get_barrier_semaphore()

        def greet(d, carry):
            @pl.when(d != me)
            def _():
                pl.semaphore_signal(barrier, 1, device_id=(mp, d // ngy, d % ngy), device_id_type=mesh_id)

            return carry

        lax.fori_loop(0, ndev, greet, 0)
        pl.semaphore_wait(barrier, ndev - 1)
        send_halos(0)
        recv[me] = buckets_ref[me]
        take_halos(0, halo0)
        qw_ref[...] = jnp.zeros_like(qw_ref)
        qe_ref[...] = jnp.zeros_like(qe_ref)

    @pl.when(p == 0)
    def _():
        issue(1 + (3 * LB // 8) * i, 3 * LB // 8)
        blk = pl.ds(pl.multiple_of(i * LB, LB), LB)
        hn = halo0[0, blk]
        hs = halo0[1, blk]
        hw_t = jnp.transpose(halo0[2, blk])
        he_t = jnp.transpose(halo0[3, blk])
        above = above_ref[0] * jnp.where(i > 0, 1.0, 0.0)
        below = below_ref[0] * jnp.where(i < nblk - 1, 1.0, 0.0)
        qs = [qw_ref[...], qe_ref[...]]

        def store(l, res):
            first[i * LB + l] = res
            fw = wet * res
            edge1[0, i, l:l + 1, :] = fw[0:1, :]
            edge1[1, i, l:l + 1, :] = fw[rows - 1:rows, :]
            hit = lane == i * LB + l
            qs[0] = jnp.where(hit, fw[:, 0:1], qs[0])
            qs[1] = jnp.where(hit, fw[:, cols - 1:cols], qs[1])

        step(lambda l: u_ref[l], above, below, hn, hs, hw_t, he_t, store)
        qw_ref[...] = qs[0]
        qe_ref[...] = qs[1]

    @pl.when((p == 0) & (i == nblk - 1))
    def _():
        edge1[2] = jnp.transpose(qw_ref[...])[0:lev, :].reshape(nblk, LB, rows)
        edge1[3] = jnp.transpose(qe_ref[...])[0:lev, :].reshape(nblk, LB, rows)
        send_halos(1)

    @pl.when((p == 1) & (i == 0))
    def _():
        take_halos(1, halo1)

        def late(k, carry):
            bucket_copy((me + k) % ndev).start()
            return carry

        lax.fori_loop(min(1 + (3 * LB // 8) * nblk, ndev), ndev, late, 0)

    @pl.when(p == 1)
    def _():
        base = i * LB
        above = first[jnp.maximum(base - 1, 0)] * jnp.where(i > 0, 1.0, 0.0)
        below = first[jnp.minimum(base + LB, lev - 1)] * jnp.where(i < nblk - 1, 1.0, 0.0)
        hw_t = jnp.transpose(halo1[2, i])
        he_t = jnp.transpose(halo1[3, i])

        def store(l, res):
            out_ref[l] = res

        step(lambda l: first[base + l], above, below, halo1[0, i], halo1[1, i], hw_t, he_t, store)

    @pl.when((p == 1) & (i == nblk - 1))
    def _():
        def wait(d, carry):
            @pl.when(d != me)
            def _():
                copy = pltpu.make_async_remote_copy(
                    src_ref=buckets_ref.at[d],
                    dst_ref=recv.at[d],
                    send_sem=send_sem.at[d],
                    recv_sem=recv_sem.at[d],
                    device_id=(mp, d // ngy, d % ngy),
                    device_id_type=mesh_id,
                )
                copy.wait_send()
                copy.wait_recv()

            return carry

        lax.fori_loop(0, ndev, wait, 0)
        arrived_ref[...] = recv[...]


def interval(coef, wet, u, buckets, edges):
    lev, rows, cols = u.shape
    nblk = lev // LB
    full2 = lambda shape: pl.BlockSpec(shape, lambda p, i: (0, 0))
    whole = pl.BlockSpec(buckets.shape, lambda p, i: (0, 0, 0, 0))
    held = lambda p, i: i + p * (nblk - 1 - i)
    in_specs = [
        pl.BlockSpec(memory_space=pltpu.SMEM),
        full2((rows, cols)),
        pl.BlockSpec((LB, rows, cols), lambda p, i: (held(p, i), 0, 0)),
        pl.BlockSpec((1, rows, cols), lambda p, i: (jnp.maximum(held(p, i) * LB - 1, 0), 0, 0)),
        pl.BlockSpec((1, rows, cols), lambda p, i: (jnp.minimum(held(p, i) * LB + LB, lev - 1), 0, 0)),
        whole,
    ] + [full2((lev, cols))] * 4
    out_shape = [
        jax.ShapeDtypeStruct((lev, rows, cols), jnp.float32),
        jax.ShapeDtypeStruct(buckets.shape, buckets.dtype),
    ]
    out_specs = [pl.BlockSpec((LB, rows, cols), lambda p, i: (i * p, 0, 0)), whole]
    scratch = [
        pltpu.VMEM((lev, rows, cols), jnp.float32),
        pltpu.VMEM((4, nblk, LB, cols), jnp.float32),
        pltpu.VMEM((4, lev, cols), jnp.float32),
        pltpu.VMEM((4, nblk, LB, cols), jnp.float32),
        pltpu.VMEM((rows, 128), jnp.float32),
        pltpu.VMEM((rows, 128), jnp.float32),
        pltpu.VMEM(buckets.shape, buckets.dtype),
        pltpu.SemaphoreType.DMA((buckets.shape[0],)),
        pltpu.SemaphoreType.DMA((buckets.shape[0],)),
        pltpu.SemaphoreType.DMA((2, 4)),
        pltpu.SemaphoreType.DMA((2, 4)),
    ]
    return pl.pallas_call(
        interval_kernel,
        grid=(2, nblk),
        in_specs=in_specs,
        out_specs=out_specs,
        out_shape=out_shape,
        scratch_shapes=scratch,
        compiler_params=pltpu.CompilerParams(
            dimension_semantics=("arbitrary", "arbitrary"), collective_id=3, has_side_effects=True,
            vmem_limit_bytes=48 * 1024 * 1024,
        ),
        cost_estimate=pl.CostEstimate(flops=60 * u.size, bytes_accessed=12 * u.size, transcendentals=0),
    )(coef, wet, u, u, u, buckets, *edges)


def first_kernel(coef_ref, wet_ref, u_ref, above_ref, below_ref, buckets_ref,
                 e0n, e0s, e0w, e0e,
                 out_ref, en_ref, es_ref, ew_ref, ee_ref, arrived_ref,
                 halo, qw_ref, qe_ref, recv, send_sem, recv_sem, hsend, hrecv):
    i = pl.program_id(0)
    nblk = pl.num_programs(0)
    edge0 = [e0n, e0s, e0w, e0e]
    wet = wet_ref[...]
    rows, cols = wet.shape
    lev = ew_ref.shape[0]
    mp = lax.axis_index("mp")
    gx = lax.axis_index("gx")
    gy = lax.axis_index("gy")
    ngx = lax.axis_size("gx")
    ngy = lax.axis_size("gy")
    mesh_id = pl.DeviceIdType.MESH
    links = [
        (gx < ngx - 1, (mp, gx + 1, gy), 1, 0),
        (gx > 0, (mp, gx - 1, gy), 0, 1),
        (gy < ngy - 1, (mp, gx, gy + 1), 3, 2),
        (gy > 0, (mp, gx, gy - 1), 2, 3),
    ]
    fills = [gx > 0, gx < ngx - 1, gy > 0, gy < ngy - 1]
    copies = [
        pltpu.make_async_remote_copy(
            src_ref=edge0[src],
            dst_ref=halo.at[slot],
            send_sem=hsend.at[slot],
            recv_sem=hrecv.at[slot],
            device_id=dev,
            device_id_type=mesh_id,
        )
        for _, dev, src, slot in links
    ]
    lane = lax.broadcasted_iota(jnp.int32, qw_ref.shape, 1)

    def send_halos():
        for (present, _, _, _), copy in zip(links, copies):
            pl.when(present)(copy.start)

    @pl.when(i == 0)
    def _():
        start_spread(buckets_ref, recv, send_sem, recv_sem, send_halos)
        for (present, _, _, _), copy in zip(links, copies):
            pl.when(present)(copy.wait_send)
        for slot, filled in enumerate(fills):
            pl.when(filled)(copies[slot].wait_recv)

            @pl.when(jnp.logical_not(filled))
            def _():
                halo[slot] = jnp.zeros_like(halo[slot])

        qw_ref[...] = jnp.zeros_like(qw_ref)
        qe_ref[...] = jnp.zeros_like(qe_ref)

    def _():
        horiz = coef_ref[0]
        vert = coef_ref[1]
        row = lax.broadcasted_iota(jnp.int32, (rows, cols), 0)
        col = lax.broadcasted_iota(jnp.int32, (rows, cols), 1)
        hn = halo[0, pl.ds(i * LB, LB)]
        hs = halo[1, pl.ds(i * LB, LB)]
        hw_t = jnp.transpose(halo[2, pl.ds(i * LB, LB)])
        he_t = jnp.transpose(halo[3, pl.ds(i * LB, LB)])
        above = above_ref[0] * jnp.where(i > 0, 1.0, 0.0)
        below = below_ref[0] * jnp.where(i < nblk - 1, 1.0, 0.0)
        qw = qw_ref[...]
        qe = qe_ref[...]
        for l in range(LB):
            u = u_ref[l]
            prev = u_ref[l - 1] if l > 0 else above
            nxt = u_ref[l + 1] if l < LB - 1 else below
            w = wet * u
            north = jnp.where(row == 0, hn[l:l + 1, :], pltpu.roll(w, 1, 0))
            south = jnp.where(row == rows - 1, hs[l:l + 1, :], pltpu.roll(w, rows - 1, 0))
            west = jnp.where(col == 0, hw_t[:, l:l + 1], pltpu.roll(w, 1, 1))
            east = jnp.where(col == cols - 1, he_t[:, l:l + 1], pltpu.roll(w, cols - 1, 1))
            lateral = north + south + west + east - 4.0 * w
            vertical = prev + nxt - 2.0 * u
            res = wet * (u + horiz * lateral + vert * vertical)
            out_ref[l] = res
            fw = wet * res
            en_ref[l:l + 1, :] = fw[0:1, :]
            es_ref[l:l + 1, :] = fw[rows - 1:rows, :]
            hit = lane == i * LB + l
            qw = jnp.where(hit, fw[:, 0:1], qw)
            qe = jnp.where(hit, fw[:, cols - 1:cols], qe)
        qw_ref[...] = qw
        qe_ref[...] = qe

    _()

    @pl.when(i == nblk - 1)
    def _():
        ew_ref[...] = jnp.transpose(qw_ref[...])[0:lev, :]
        ee_ref[...] = jnp.transpose(qe_ref[...])[0:lev, :]
        finish_spread(buckets_ref, recv, send_sem, recv_sem, arrived_ref)


def first_step(coef, wet, u, buckets, edges):
    lev, rows, cols = u.shape
    nblk = lev // LB
    full2 = lambda shape: pl.BlockSpec(shape, lambda i: (0, 0))
    lvl2 = pl.BlockSpec((LB, cols), lambda i: (i, 0))
    whole = pl.BlockSpec(buckets.shape, lambda i: (0, 0, 0, 0))
    in_specs = [
        pl.BlockSpec(memory_space=pltpu.SMEM),
        full2((rows, cols)),
        pl.BlockSpec((LB, rows, cols), lambda i: (i, 0, 0)),
        pl.BlockSpec((1, rows, cols), lambda i: (jnp.maximum(i * LB - 1, 0), 0, 0)),
        pl.BlockSpec((1, rows, cols), lambda i: (jnp.minimum(i * LB + LB, lev - 1), 0, 0)),
        whole,
    ] + [full2((lev, cols))] * 4
    out_shape = [
        jax.ShapeDtypeStruct((lev, rows, cols), jnp.float32),
        jax.ShapeDtypeStruct((lev, cols), jnp.float32),
        jax.ShapeDtypeStruct((lev, cols), jnp.float32),
        jax.ShapeDtypeStruct((lev, rows), jnp.float32),
        jax.ShapeDtypeStruct((lev, rows), jnp.float32),
        jax.ShapeDtypeStruct(buckets.shape, buckets.dtype),
    ]
    out_specs = [
        pl.BlockSpec((LB, rows, cols), lambda i: (i, 0, 0)),
        lvl2, lvl2, full2((lev, rows)), full2((lev, rows)), whole,
    ]
    scratch = [
        pltpu.VMEM((4, lev, cols), jnp.float32),
        pltpu.VMEM((rows, 128), jnp.float32),
        pltpu.VMEM((rows, 128), jnp.float32),
        pltpu.VMEM(buckets.shape, buckets.dtype),
        pltpu.SemaphoreType.DMA((buckets.shape[0],)),
        pltpu.SemaphoreType.DMA((buckets.shape[0],)),
        pltpu.SemaphoreType.DMA((4,)),
        pltpu.SemaphoreType.DMA((4,)),
    ]
    return pl.pallas_call(
        first_kernel,
        grid=(nblk,),
        in_specs=in_specs,
        out_specs=out_specs,
        out_shape=out_shape,
        scratch_shapes=scratch,
        compiler_params=pltpu.CompilerParams(
            dimension_semantics=("arbitrary",), collective_id=2, has_side_effects=True
        ),
        cost_estimate=pl.CostEstimate(flops=30 * u.size, bytes_accessed=12 * u.size, transcendentals=0),
    )(coef, wet, u, u, u, buckets, *edges)


def stencil_kernel(with_edges, with_force, coef_ref, wet_ref, u_ref, above_ref, below_ref,
                   hn_ref, hs_ref, hw_ref, he_ref, *rest):
    if with_force:
        force_ref, rest = rest[0], rest[1:]
    if with_edges:
        buckets_ref, rest = rest[0], rest[1:]
    out_ref = rest[0]
    i = pl.program_id(0)
    nblk = pl.num_programs(0)
    horiz = coef_ref[0]
    vert = coef_ref[1]
    wet = wet_ref[...]
    rows, cols = wet.shape
    row = lax.broadcasted_iota(jnp.int32, (rows, cols), 0)
    col = lax.broadcasted_iota(jnp.int32, (rows, cols), 1)
    hw_t = jnp.transpose(hw_ref[...])
    he_t = jnp.transpose(he_ref[...])
    above = above_ref[0] * jnp.where(i > 0, 1.0, 0.0)
    below = below_ref[0] * jnp.where(i < nblk - 1, 1.0, 0.0)
    if with_edges:
        en_ref, es_ref, ew_ref, ee_ref, arrived_ref, qw_ref, qe_ref, recv, send_sem, recv_sem = rest[1:]

        @pl.when(i == 0)
        def _():
            start_spread(buckets_ref, recv, send_sem, recv_sem)
            qw_ref[...] = jnp.zeros_like(qw_ref)
            qe_ref[...] = jnp.zeros_like(qe_ref)

    if with_edges:
        lane = lax.broadcasted_iota(jnp.int32, qw_ref.shape, 1)
        qw = qw_ref[...]
        qe = qe_ref[...]
    for l in range(LB):
        u = u_ref[l]
        prev = u_ref[l - 1] if l > 0 else above
        nxt = u_ref[l + 1] if l < LB - 1 else below
        w = wet * u
        north = jnp.where(row == 0, hn_ref[l:l + 1, :], pltpu.roll(w, 1, 0))
        south = jnp.where(row == rows - 1, hs_ref[l:l + 1, :], pltpu.roll(w, rows - 1, 0))
        west = jnp.where(col == 0, hw_t[:, l:l + 1], pltpu.roll(w, 1, 1))
        east = jnp.where(col == cols - 1, he_t[:, l:l + 1], pltpu.roll(w, cols - 1, 1))
        lateral = north + south + west + east - 4.0 * w
        vertical = prev + nxt - 2.0 * u
        res = wet * (u + horiz * lateral + vert * vertical)
        if with_force and l == 0:
            res = res + jnp.where(i == 0, 1.0, 0.0) * (force_gain * wet * force_ref[...])
        out_ref[l] = res
        if with_edges:
            fw = wet * res
            en_ref[l:l + 1, :] = fw[0:1, :]
            es_ref[l:l + 1, :] = fw[rows - 1:rows, :]
            hit = lane == i * LB + l
            qw = jnp.where(hit, fw[:, 0:1], qw)
            qe = jnp.where(hit, fw[:, cols - 1:cols], qe)

    if with_edges:
        qw_ref[...] = qw
        qe_ref[...] = qe

        @pl.when(i == nblk - 1)
        def _():
            lev = ew_ref.shape[0]
            ew_ref[...] = jnp.transpose(qw_ref[...])[0:lev, :]
            ee_ref[...] = jnp.transpose(qe_ref[...])[0:lev, :]
            finish_spread(buckets_ref, recv, send_sem, recv_sem, arrived_ref)


def edges_kernel(wet_ref, u_ref, en_ref, es_ref, ew_ref, ee_ref, qw_ref, qe_ref):
    i = pl.program_id(0)
    nblk = pl.num_programs(0)
    wet = wet_ref[...]
    rows, cols = wet.shape

    @pl.when(i == 0)
    def _():
        qw_ref[...] = jnp.zeros_like(qw_ref)
        qe_ref[...] = jnp.zeros_like(qe_ref)

    lane = lax.broadcasted_iota(jnp.int32, qw_ref.shape, 1)
    qw = qw_ref[...]
    qe = qe_ref[...]
    for l in range(EB):
        fw = wet * u_ref[l]
        en_ref[l:l + 1, :] = fw[0:1, :]
        es_ref[l:l + 1, :] = fw[rows - 1:rows, :]
        hit = lane == i * EB + l
        qw = jnp.where(hit, fw[:, 0:1], qw)
        qe = jnp.where(hit, fw[:, cols - 1:cols], qe)
    qw_ref[...] = qw
    qe_ref[...] = qe

    @pl.when(i == nblk - 1)
    def _():
        lev = ew_ref.shape[0]
        ew_ref[...] = jnp.transpose(qw_ref[...])[0:lev, :]
        ee_ref[...] = jnp.transpose(qe_ref[...])[0:lev, :]


def masked_edges(wet, u):
    lev, rows, cols = u.shape
    lvl2 = pl.BlockSpec((EB, cols), lambda i: (i, 0))
    full2 = lambda shape: pl.BlockSpec(shape, lambda i: (0, 0))
    return pl.pallas_call(
        edges_kernel,
        grid=(lev // EB,),
        in_specs=[full2((rows, cols)), pl.BlockSpec((EB, rows, cols), lambda i: (i, 0, 0))],
        out_specs=[lvl2, lvl2, full2((lev, rows)), full2((lev, rows))],
        out_shape=[jax.ShapeDtypeStruct((lev, cols), jnp.float32)] * 2
        + [jax.ShapeDtypeStruct((lev, rows), jnp.float32)] * 2,
        scratch_shapes=[pltpu.VMEM((rows, 128), jnp.float32)] * 2,
        compiler_params=pltpu.CompilerParams(dimension_semantics=("arbitrary",)),
        cost_estimate=pl.CostEstimate(flops=2 * u.size, bytes_accessed=4 * u.size, transcendentals=0),
    )(wet, u)


def force_kernel(x_ref, wet_ref, f_ref, out_ref):
    out_ref[0] = x_ref[0] + force_gain * wet_ref[...] * f_ref[...]


def add_force(x, wet, f):
    lev, rows, cols = x.shape
    plane = pl.BlockSpec((rows, cols), lambda i: (0, 0))
    level0 = pl.BlockSpec((1, rows, cols), lambda i: (0, 0, 0))
    return pl.pallas_call(
        force_kernel,
        grid=(1,),
        in_specs=[level0, plane, plane],
        out_specs=level0,
        out_shape=jax.ShapeDtypeStruct(x.shape, x.dtype),
        input_output_aliases={0: 0},
    )(x, wet, f)


def stencil_step(coef, wet, u, halos, force=None, buckets=None):
    with_edges = buckets is not None
    lev, rows, cols = u.shape
    nblk = lev // LB
    full2 = lambda shape: pl.BlockSpec(shape, lambda i: (0, 0))
    lvl2 = pl.BlockSpec((LB, cols), lambda i: (i, 0))
    in_specs = [
        pl.BlockSpec(memory_space=pltpu.SMEM),
        full2((rows, cols)),
        pl.BlockSpec((LB, rows, cols), lambda i: (i, 0, 0)),
        pl.BlockSpec((1, rows, cols), lambda i: (jnp.maximum(i * LB - 1, 0), 0, 0)),
        pl.BlockSpec((1, rows, cols), lambda i: (jnp.minimum(i * LB + LB, lev - 1), 0, 0)),
        lvl2, lvl2, lvl2, lvl2,
    ]
    args = [coef, wet, u, u, u] + list(halos)
    if force is not None:
        in_specs.append(full2((rows, cols)))
        args.append(force)
    if with_edges:
        in_specs.append(pl.BlockSpec(buckets.shape, lambda i: (0, 0, 0, 0)))
        args.append(buckets)
    out_shape = [jax.ShapeDtypeStruct((lev, rows, cols), jnp.float32)]
    out_specs = [pl.BlockSpec((LB, rows, cols), lambda i: (i, 0, 0))]
    scratch = []
    params = dict(dimension_semantics=("arbitrary",))
    if with_edges:
        out_shape += [jax.ShapeDtypeStruct((lev, cols), jnp.float32)] * 2
        out_shape += [jax.ShapeDtypeStruct((lev, rows), jnp.float32)] * 2
        out_shape += [jax.ShapeDtypeStruct(buckets.shape, buckets.dtype)]
        out_specs += [lvl2, lvl2, full2((lev, rows)), full2((lev, rows))]
        out_specs += [pl.BlockSpec(buckets.shape, lambda i: (0, 0, 0, 0))]
        scratch = [pltpu.VMEM((rows, 128), jnp.float32)] * 2 + [
            pltpu.VMEM(buckets.shape, buckets.dtype),
            pltpu.SemaphoreType.DMA((buckets.shape[0],)),
            pltpu.SemaphoreType.DMA((buckets.shape[0],)),
        ]
        params.update(collective_id=2, has_side_effects=True)
    return pl.pallas_call(
        functools.partial(stencil_kernel, with_edges, force is not None),
        grid=(nblk,),
        in_specs=in_specs,
        out_specs=out_specs,
        out_shape=out_shape,
        scratch_shapes=scratch,
        compiler_params=pltpu.CompilerParams(**params),
        cost_estimate=pl.CostEstimate(flops=30 * u.size, bytes_accessed=12 * u.size, transcendentals=0),
    )(*args)


def halo_kernel(en_ref, es_ref, ew_ref, ee_ref, hn_ref, hs_ref, hw_ref, he_ref,
                buf, send_sem, recv_sem):
    mp = lax.axis_index("mp")
    gx = lax.axis_index("gx")
    gy = lax.axis_index("gy")
    ngx = lax.axis_size("gx")
    ngy = lax.axis_size("gy")
    mesh_id = pl.DeviceIdType.MESH
    links = [
        (gx < ngx - 1, (mp, gx + 1, gy), es_ref, 0),
        (gx > 0, (mp, gx - 1, gy), en_ref, 1),
        (gy < ngy - 1, (mp, gx, gy + 1), ee_ref, 2),
        (gy > 0, (mp, gx, gy - 1), ew_ref, 3),
    ]
    barrier = pltpu.get_barrier_semaphore()
    count = jnp.int32(0)
    for present, dev, _, _ in links:
        @pl.when(present)
        def _():
            pl.semaphore_signal(barrier, 1, device_id=dev, device_id_type=mesh_id)

        count = count + present.astype(jnp.int32)
    pl.semaphore_wait(barrier, count)

    copies = []
    for present, dev, src, slot in links:
        copy = pltpu.make_async_remote_copy(
            src_ref=src,
            dst_ref=buf.at[slot],
            send_sem=send_sem.at[slot],
            recv_sem=recv_sem.at[slot],
            device_id=dev,
            device_id_type=mesh_id,
        )
        pl.when(present)(copy.start)
        copies.append((present, copy))
    for present, copy in copies:
        pl.when(present)(copy.wait_send)
    fills = [gx > 0, gx < ngx - 1, gy > 0, gy < ngy - 1]
    outs = [hn_ref, hs_ref, hw_ref, he_ref]
    for slot, (filled, out) in enumerate(zip(fills, outs)):
        _, copy = copies[slot]

        @pl.when(filled)
        def _():
            copy.wait_recv()
            out[...] = buf[slot]

        @pl.when(jnp.logical_not(filled))
        def _():
            out[...] = jnp.zeros_like(out)


def exchange(en, es, ew, ee, call):
    shape = jax.ShapeDtypeStruct(en.shape, en.dtype)
    vmem = pl.BlockSpec(memory_space=pltpu.VMEM)
    return pl.pallas_call(
        halo_kernel,
        in_specs=[vmem] * 4,
        out_specs=[vmem] * 4,
        out_shape=[shape] * 4,
        scratch_shapes=[
            pltpu.VMEM((4,) + en.shape, en.dtype),
            pltpu.SemaphoreType.DMA((4,)),
            pltpu.SemaphoreType.DMA((4,)),
        ],
        compiler_params=pltpu.CompilerParams(collective_id=call, has_side_effects=True),
    )(en, es, ew, ee)


def bucket_kernel(target_ref, row_ref, contrib_ref, out_ref, count_ref):
    ntiles = contrib_ref.shape[0]
    ndest = out_ref.shape[0]
    sub = lax.broadcasted_iota(jnp.int32, (KF, CY), 0)
    out_ref[...] = jnp.zeros_like(out_ref)

    def clear(d, carry):
        count_ref[d] = 0
        return carry

    lax.fori_loop(0, ndest, clear, 0)

    def body(t, carry):
        d = target_ref[t]
        c = count_ref[d]
        count_ref[d] = c + 1
        out_ref[d, c] = contrib_ref[t]
        out_ref[d, CAP] = jnp.where(sub == c, row_ref[t].astype(jnp.float32), out_ref[d, CAP])
        return carry

    lax.fori_loop(0, ntiles, body, 0, unroll=8)


def local(states, surface, land_mask, tile_weights, tile_source, tile_target, tile_row):
    group = lax.axis_index("mp")
    ndev = lax.axis_size("gx") * lax.axis_size("gy")
    state = states[0]
    lev, rows_here, cols_here = state.shape
    wet = jnp.where(
        group == 0, jnp.ones(land_mask.shape, jnp.float32), land_mask.astype(jnp.float32)
    )
    coef = jnp.stack([jnp.where(group == 0, 0.15, 0.12), jnp.where(group == 0, 0.1, 0.15)]).astype(
        jnp.float32
    )

    src = (surface[0] * wet).astype(jnp.bfloat16)
    source = tile_source[0, 0, 0]
    target = tile_target[0, 0, 0, :, 0]
    dest_row = tile_row[0, 0, 0]
    ntiles = source.shape[0]
    picked = jnp.take(src, source, axis=1)
    contrib = jnp.einsum(
        "tji,kti->tkj", tile_weights[0, 0, 0], picked, preferred_element_type=jnp.float32
    )
    buckets = pl.pallas_call(
        bucket_kernel,
        in_specs=[
            pl.BlockSpec(memory_space=pltpu.SMEM),
            pl.BlockSpec(memory_space=pltpu.SMEM),
            pl.BlockSpec(memory_space=pltpu.VMEM),
        ],
        out_specs=pl.BlockSpec(memory_space=pltpu.VMEM),
        out_shape=jax.ShapeDtypeStruct((ndev, CAP + 1, KF, CY), jnp.float32),
        scratch_shapes=[pltpu.SMEM((ndev,), jnp.int32)],
    )(target, dest_row, contrib)
    second, arrived = interval(coef, wet, state, buckets, masked_edges(wet, state))
    got_rows = arrived[:, CAP, :, 0].astype(jnp.int32)
    select = (
        got_rows[:, :, None] == jnp.arange(rows_here, dtype=jnp.int32)[None, None, :]
    ).astype(jnp.float32)
    sent = jnp.einsum(
        "scr,sckj->krj", select, arrived[:, :CAP], precision=lax.Precision.HIGHEST
    )
    received = lax.ppermute(sent, "mp", [(0, 1), (1, 0)])

    second = add_force(second, wet, received[0])
    return (second[None], received[None])


def solution(mesh):
    return jax.shard_map(
        local,
        mesh=mesh,
        in_specs=(
            P("mp", None, "gx", "gy"),
            P("mp", None, "gx", "gy"),
            P("gx", "gy"),
            P("mp", "gx", "gy", None, None, None),
            P("mp", "gx", "gy", None),
            P("mp", "gx", "gy", None, None),
            P("mp", "gx", "gy", None),
        ),
        out_specs=(P("mp", None, "gx", "gy"), P("mp", None, "gx", "gy")),
        check_vma=False,
    )
```

```python
import functools

import jax
import jax.numpy as jnp
from jax import lax
from jax.experimental import pallas as pl
from jax.experimental.pallas import tpu as pltpu
from jax.sharding import PartitionSpec as P

CY = 128
KF = 8
CAP = 8
LB = 32
EB = 32

force_gain = 0.5


def shift_pairs(devices, forward):
    up = [(i, i + 1) for i in range(devices - 1)]
    return up if forward else [(j, i) for i, j in up]


def start_spread(buckets_ref, recv, send_sem, recv_sem, first_out=None):
    mp = lax.axis_index("mp")
    ngy = lax.axis_size("gy")
    ndev = lax.axis_size("gx") * ngy
    me = lax.axis_index("gx") * ngy + lax.axis_index("gy")
    mesh_id = pl.DeviceIdType.MESH
    barrier = pltpu.get_barrier_semaphore()

    def greet(d, carry):
        @pl.when(d != me)
        def _():
            pl.semaphore_signal(barrier, 1, device_id=(mp, d // ngy, d % ngy), device_id_type=mesh_id)

        return carry

    lax.fori_loop(0, ndev, greet, 0)
    pl.semaphore_wait(barrier, ndev - 1)
    if first_out is not None:
        first_out()
    recv[me] = buckets_ref[me]

    def send(k, carry):
        d = (me + k) % ndev
        pltpu.make_async_remote_copy(
            src_ref=buckets_ref.at[d],
            dst_ref=recv.at[me],
            send_sem=send_sem.at[d],
            recv_sem=recv_sem.at[me],
            device_id=(mp, d // ngy, d % ngy),
            device_id_type=mesh_id,
        ).start()
        return carry

    lax.fori_loop(1, ndev, send, 0)


def finish_spread(buckets_ref, recv, send_sem, recv_sem, arrived_ref):
    ngy = lax.axis_size("gy")
    ndev = lax.axis_size("gx") * ngy
    me = lax.axis_index("gx") * ngy + lax.axis_index("gy")

    def wait(d, carry):
        @pl.when(d != me)
        def _():
            copy = pltpu.make_async_remote_copy(
                src_ref=buckets_ref.at[d],
                dst_ref=recv.at[d],
                send_sem=send_sem.at[d],
                recv_sem=recv_sem.at[d],
                device_id=(lax.axis_index("mp"), d // ngy, d % ngy),
                device_id_type=pl.DeviceIdType.MESH,
            )
            copy.wait_send()
            copy.wait_recv()

        return carry

    lax.fori_loop(0, ndev, wait, 0)
    arrived_ref[...] = recv[...]


def interval_kernel(coef_ref, wet_ref, u_ref, above_ref, below_ref, buckets_ref,
                    e0n, e0s, e0w, e0e,
                    out_ref, arrived_ref,
                    first, edge1, halo0, halo1, qw_ref, qe_ref, recv,
                    send_sem, recv_sem, hsend, hrecv):
    p = pl.program_id(0)
    i = pl.program_id(1)
    nblk = pl.num_programs(1)
    wet = wet_ref[...]
    rows, cols = wet.shape
    lev = first.shape[0]
    mp = lax.axis_index("mp")
    gx = lax.axis_index("gx")
    gy = lax.axis_index("gy")
    ngx = lax.axis_size("gx")
    ngy = lax.axis_size("gy")
    ndev = ngx * ngy
    me = gx * ngy + gy
    mesh_id = pl.DeviceIdType.MESH
    links = [
        (gx < ngx - 1, (mp, gx + 1, gy), 1, 0),
        (gx > 0, (mp, gx - 1, gy), 0, 1),
        (gy < ngy - 1, (mp, gx, gy + 1), 3, 2),
        (gy > 0, (mp, gx, gy - 1), 2, 3),
    ]
    fills = [gx > 0, gx < ngx - 1, gy > 0, gy < ngy - 1]
    edge0 = [e0n, e0s, e0w, e0e]

    def halo_copy(stage, src, slot, dev):
        srcs = edge0[src] if stage == 0 else edge1.at[src]
        dsts = halo0.at[slot] if stage == 0 else halo1.at[slot]
        return pltpu.make_async_remote_copy(
            src_ref=srcs,
            dst_ref=dsts,
            send_sem=hsend.at[stage, slot],
            recv_sem=hrecv.at[stage, slot],
            device_id=dev,
            device_id_type=mesh_id,
        )

    def send_halos(stage):
        for present, dev, src, slot in links:
            pl.when(present)(halo_copy(stage, src, slot, dev).start)

    def take_halos(stage, dst):
        for present, dev, src, slot in links:
            pl.when(present)(halo_copy(stage, src, slot, dev).wait_send)
        for slot, filled in enumerate(fills):
            _, dev, src, _ = links[slot]
            pl.when(filled)(halo_copy(stage, src, slot, dev).wait_recv)

            @pl.when(jnp.logical_not(filled))
            def _():
                dst[slot] = jnp.zeros_like(dst[slot])

    def bucket_copy(d):
        return pltpu.make_async_remote_copy(
            src_ref=buckets_ref.at[d],
            dst_ref=recv.at[me],
            send_sem=send_sem.at[d],
            recv_sem=recv_sem.at[me],
            device_id=(mp, d // ngy, d % ngy),
            device_id_type=mesh_id,
        )

    def issue(k0, count):
        for n in range(count):
            k = k0 + n

            @pl.when(k < ndev)
            def _():
                bucket_copy((me + k) % ndev).start()

    lane = lax.broadcasted_iota(jnp.int32, qw_ref.shape, 1)
    row = lax.broadcasted_iota(jnp.int32, (rows, cols), 0)
    col = lax.broadcasted_iota(jnp.int32, (rows, cols), 1)
    horiz = coef_ref[0]
    vert = coef_ref[1]

    def step(load, above, below, hn, hs, hw_t, he_t, store):
        for l in range(LB):
            u = load(l)
            prev = load(l - 1) if l > 0 else above
            nxt = load(l + 1) if l < LB - 1 else below
            w = wet * u
            north = jnp.where(row == 0, hn[l:l + 1, :], pltpu.roll(w, 1, 0))
            south = jnp.where(row == rows - 1, hs[l:l + 1, :], pltpu.roll(w, rows - 1, 0))
            west = jnp.where(col == 0, hw_t[:, l:l + 1], pltpu.roll(w, 1, 1))
            east = jnp.where(col == cols - 1, he_t[:, l:l + 1], pltpu.roll(w, cols - 1, 1))
            lateral = north + south + west + east - 4.0 * w
            vertical = prev + nxt - 2.0 * u
            store(l, wet * (u + horiz * lateral + vert * vertical))

    @pl.when((p == 0) & (i == 0))
    def _():
        barrier = pltpu.get_barrier_semaphore()

        def greet(d, carry):
            @pl.when(d != me)
            def _():
                pl.semaphore_signal(barrier, 1, device_id=(mp, d // ngy, d % ngy), device_id_type=mesh_id)

            return carry

        lax.fori_loop(0, ndev, greet, 0)
        pl.semaphore_wait(barrier, ndev - 1)
        send_halos(0)
        recv[me] = buckets_ref[me]
        take_halos(0, halo0)
        qw_ref[...] = jnp.zeros_like(qw_ref)
        qe_ref[...] = jnp.zeros_like(qe_ref)

    @pl.when(p == 0)
    def _():
        issue(1 + (3 * LB // 8) * i, 3 * LB // 8)
        blk = pl.ds(pl.multiple_of(i * LB, LB), LB)
        hn = halo0[0, blk]
        hs = halo0[1, blk]
        hw_t = jnp.transpose(halo0[2, blk])
        he_t = jnp.transpose(halo0[3, blk])
        above = above_ref[0] * jnp.where(i > 0, 1.0, 0.0)
        below = below_ref[0] * jnp.where(i < nblk - 1, 1.0, 0.0)
        qs = [qw_ref[...], qe_ref[...]]

        def store(l, res):
            first[i * LB + l] = res
            fw = wet * res
            edge1[0, i, l:l + 1, :] = fw[0:1, :]
            edge1[1, i, l:l + 1, :] = fw[rows - 1:rows, :]
            hit = lane == i * LB + l
            qs[0] = jnp.where(hit, fw[:, 0:1], qs[0])
            qs[1] = jnp.where(hit, fw[:, cols - 1:cols], qs[1])

        step(lambda l: u_ref[l], above, below, hn, hs, hw_t, he_t, store)
        qw_ref[...] = qs[0]
        qe_ref[...] = qs[1]

    @pl.when((p == 0) & (i == nblk - 1))
    def _():
        edge1[2] = jnp.transpose(qw_ref[...])[0:lev, :].reshape(nblk, LB, rows)
        edge1[3] = jnp.transpose(qe_ref[...])[0:lev, :].reshape(nblk, LB, rows)
        send_halos(1)

    @pl.when((p == 1) & (i == 0))
    def _():
        take_halos(1, halo1)

        def late(k, carry):
            bucket_copy((me + k) % ndev).start()
            return carry

        lax.fori_loop(min(1 + (3 * LB // 8) * nblk, ndev), ndev, late, 0)

    @pl.when(p == 1)
    def _():
        base = i * LB
        above = first[jnp.maximum(base - 1, 0)] * jnp.where(i > 0, 1.0, 0.0)
        below = first[jnp.minimum(base + LB, lev - 1)] * jnp.where(i < nblk - 1, 1.0, 0.0)
        hw_t = jnp.transpose(halo1[2, i])
        he_t = jnp.transpose(halo1[3, i])

        def store(l, res):
            out_ref[l] = res

        step(lambda l: first[base + l], above, below, halo1[0, i], halo1[1, i], hw_t, he_t, store)

    @pl.when((p == 1) & (i == nblk - 1))
    def _():
        def wait(d, carry):
            @pl.when(d != me)
            def _():
                copy = pltpu.make_async_remote_copy(
                    src_ref=buckets_ref.at[d],
                    dst_ref=recv.at[d],
                    send_sem=send_sem.at[d],
                    recv_sem=recv_sem.at[d],
                    device_id=(mp, d // ngy, d % ngy),
                    device_id_type=mesh_id,
                )
                copy.wait_send()
                copy.wait_recv()

            return carry

        lax.fori_loop(0, ndev, wait, 0)
        arrived_ref[...] = recv[...]


def interval(coef, wet, u, buckets, edges):
    lev, rows, cols = u.shape
    nblk = lev // LB
    full2 = lambda shape: pl.BlockSpec(shape, lambda p, i: (0, 0))
    whole = pl.BlockSpec(buckets.shape, lambda p, i: (0, 0, 0, 0))
    held = lambda p, i: i + p * (nblk - 1 - i)
    in_specs = [
        pl.BlockSpec(memory_space=pltpu.SMEM),
        full2((rows, cols)),
        pl.BlockSpec((LB, rows, cols), lambda p, i: (held(p, i), 0, 0)),
        pl.BlockSpec((1, rows, cols), lambda p, i: (jnp.maximum(held(p, i) * LB - 1, 0), 0, 0)),
        pl.BlockSpec((1, rows, cols), lambda p, i: (jnp.minimum(held(p, i) * LB + LB, lev - 1), 0, 0)),
        whole,
    ] + [full2((lev, cols))] * 4
    out_shape = [
        jax.ShapeDtypeStruct((lev, rows, cols), jnp.float32),
        jax.ShapeDtypeStruct(buckets.shape, buckets.dtype),
    ]
    out_specs = [pl.BlockSpec((LB, rows, cols), lambda p, i: (i * p, 0, 0)), whole]
    scratch = [
        pltpu.VMEM((lev, rows, cols), jnp.float32),
        pltpu.VMEM((4, nblk, LB, cols), jnp.float32),
        pltpu.VMEM((4, lev, cols), jnp.float32),
        pltpu.VMEM((4, nblk, LB, cols), jnp.float32),
        pltpu.VMEM((rows, 128), jnp.float32),
        pltpu.VMEM((rows, 128), jnp.float32),
        pltpu.VMEM(buckets.shape, buckets.dtype),
        pltpu.SemaphoreType.DMA((buckets.shape[0],)),
        pltpu.SemaphoreType.DMA((buckets.shape[0],)),
        pltpu.SemaphoreType.DMA((2, 4)),
        pltpu.SemaphoreType.DMA((2, 4)),
    ]
    return pl.pallas_call(
        interval_kernel,
        grid=(2, nblk),
        in_specs=in_specs,
        out_specs=out_specs,
        out_shape=out_shape,
        scratch_shapes=scratch,
        compiler_params=pltpu.CompilerParams(
            dimension_semantics=("arbitrary", "arbitrary"), collective_id=3, has_side_effects=True,
            vmem_limit_bytes=48 * 1024 * 1024,
        ),
        cost_estimate=pl.CostEstimate(flops=60 * u.size, bytes_accessed=12 * u.size, transcendentals=0),
    )(coef, wet, u, u, u, buckets, *edges)


def first_kernel(coef_ref, wet_ref, u_ref, above_ref, below_ref, buckets_ref,
                 e0n, e0s, e0w, e0e,
                 out_ref, en_ref, es_ref, ew_ref, ee_ref, arrived_ref,
                 halo, qw_ref, qe_ref, recv, send_sem, recv_sem, hsend, hrecv):
    i = pl.program_id(0)
    nblk = pl.num_programs(0)
    edge0 = [e0n, e0s, e0w, e0e]
    wet = wet_ref[...]
    rows, cols = wet.shape
    lev = ew_ref.shape[0]
    mp = lax.axis_index("mp")
    gx = lax.axis_index("gx")
    gy = lax.axis_index("gy")
    ngx = lax.axis_size("gx")
    ngy = lax.axis_size("gy")
    mesh_id = pl.DeviceIdType.MESH
    links = [
        (gx < ngx - 1, (mp, gx + 1, gy), 1, 0),
        (gx > 0, (mp, gx - 1, gy), 0, 1),
        (gy < ngy - 1, (mp, gx, gy + 1), 3, 2),
        (gy > 0, (mp, gx, gy - 1), 2, 3),
    ]
    fills = [gx > 0, gx < ngx - 1, gy > 0, gy < ngy - 1]
    copies = [
        pltpu.make_async_remote_copy(
            src_ref=edge0[src],
            dst_ref=halo.at[slot],
            send_sem=hsend.at[slot],
            recv_sem=hrecv.at[slot],
            device_id=dev,
            device_id_type=mesh_id,
        )
        for _, dev, src, slot in links
    ]
    lane = lax.broadcasted_iota(jnp.int32, qw_ref.shape, 1)

    def send_halos():
        for (present, _, _, _), copy in zip(links, copies):
            pl.when(present)(copy.start)

    @pl.when(i == 0)
    def _():
        start_spread(buckets_ref, recv, send_sem, recv_sem, send_halos)
        for (present, _, _, _), copy in zip(links, copies):
            pl.when(present)(copy.wait_send)
        for slot, filled in enumerate(fills):
            pl.when(filled)(copies[slot].wait_recv)

            @pl.when(jnp.logical_not(filled))
            def _():
                halo[slot] = jnp.zeros_like(halo[slot])

        qw_ref[...] = jnp.zeros_like(qw_ref)
        qe_ref[...] = jnp.zeros_like(qe_ref)

    def _():
        horiz = coef_ref[0]
        vert = coef_ref[1]
        row = lax.broadcasted_iota(jnp.int32, (rows, cols), 0)
        col = lax.broadcasted_iota(jnp.int32, (rows, cols), 1)
        hn = halo[0, pl.ds(i * LB, LB)]
        hs = halo[1, pl.ds(i * LB, LB)]
        hw_t = jnp.transpose(halo[2, pl.ds(i * LB, LB)])
        he_t = jnp.transpose(halo[3, pl.ds(i * LB, LB)])
        above = above_ref[0] * jnp.where(i > 0, 1.0, 0.0)
        below = below_ref[0] * jnp.where(i < nblk - 1, 1.0, 0.0)
        qw = qw_ref[...]
        qe = qe_ref[...]
        for l in range(LB):
            u = u_ref[l]
            prev = u_ref[l - 1] if l > 0 else above
            nxt = u_ref[l + 1] if l < LB - 1 else below
            w = wet * u
            north = jnp.where(row == 0, hn[l:l + 1, :], pltpu.roll(w, 1, 0))
            south = jnp.where(row == rows - 1, hs[l:l + 1, :], pltpu.roll(w, rows - 1, 0))
            west = jnp.where(col == 0, hw_t[:, l:l + 1], pltpu.roll(w, 1, 1))
            east = jnp.where(col == cols - 1, he_t[:, l:l + 1], pltpu.roll(w, cols - 1, 1))
            lateral = north + south + west + east - 4.0 * w
            vertical = prev + nxt - 2.0 * u
            res = wet * (u + horiz * lateral + vert * vertical)
            out_ref[l] = res
            fw = wet * res
            en_ref[l:l + 1, :] = fw[0:1, :]
            es_ref[l:l + 1, :] = fw[rows - 1:rows, :]
            hit = lane == i * LB + l
            qw = jnp.where(hit, fw[:, 0:1], qw)
            qe = jnp.where(hit, fw[:, cols - 1:cols], qe)
        qw_ref[...] = qw
        qe_ref[...] = qe

    _()

    @pl.when(i == nblk - 1)
    def _():
        ew_ref[...] = jnp.transpose(qw_ref[...])[0:lev, :]
        ee_ref[...] = jnp.transpose(qe_ref[...])[0:lev, :]
        finish_spread(buckets_ref, recv, send_sem, recv_sem, arrived_ref)


def first_step(coef, wet, u, buckets, edges):
    lev, rows, cols = u.shape
    nblk = lev // LB
    full2 = lambda shape: pl.BlockSpec(shape, lambda i: (0, 0))
    lvl2 = pl.BlockSpec((LB, cols), lambda i: (i, 0))
    whole = pl.BlockSpec(buckets.shape, lambda i: (0, 0, 0, 0))
    in_specs = [
        pl.BlockSpec(memory_space=pltpu.SMEM),
        full2((rows, cols)),
        pl.BlockSpec((LB, rows, cols), lambda i: (i, 0, 0)),
        pl.BlockSpec((1, rows, cols), lambda i: (jnp.maximum(i * LB - 1, 0), 0, 0)),
        pl.BlockSpec((1, rows, cols), lambda i: (jnp.minimum(i * LB + LB, lev - 1), 0, 0)),
        whole,
    ] + [full2((lev, cols))] * 4
    out_shape = [
        jax.ShapeDtypeStruct((lev, rows, cols), jnp.float32),
        jax.ShapeDtypeStruct((lev, cols), jnp.float32),
        jax.ShapeDtypeStruct((lev, cols), jnp.float32),
        jax.ShapeDtypeStruct((lev, rows), jnp.float32),
        jax.ShapeDtypeStruct((lev, rows), jnp.float32),
        jax.ShapeDtypeStruct(buckets.shape, buckets.dtype),
    ]
    out_specs = [
        pl.BlockSpec((LB, rows, cols), lambda i: (i, 0, 0)),
        lvl2, lvl2, full2((lev, rows)), full2((lev, rows)), whole,
    ]
    scratch = [
        pltpu.VMEM((4, lev, cols), jnp.float32),
        pltpu.VMEM((rows, 128), jnp.float32),
        pltpu.VMEM((rows, 128), jnp.float32),
        pltpu.VMEM(buckets.shape, buckets.dtype),
        pltpu.SemaphoreType.DMA((buckets.shape[0],)),
        pltpu.SemaphoreType.DMA((buckets.shape[0],)),
        pltpu.SemaphoreType.DMA((4,)),
        pltpu.SemaphoreType.DMA((4,)),
    ]
    return pl.pallas_call(
        first_kernel,
        grid=(nblk,),
        in_specs=in_specs,
        out_specs=out_specs,
        out_shape=out_shape,
        scratch_shapes=scratch,
        compiler_params=pltpu.CompilerParams(
            dimension_semantics=("arbitrary",), collective_id=2, has_side_effects=True
        ),
        cost_estimate=pl.CostEstimate(flops=30 * u.size, bytes_accessed=12 * u.size, transcendentals=0),
    )(coef, wet, u, u, u, buckets, *edges)


def stencil_kernel(with_edges, with_force, coef_ref, wet_ref, u_ref, above_ref, below_ref,
                   hn_ref, hs_ref, hw_ref, he_ref, *rest):
    if with_force:
        force_ref, rest = rest[0], rest[1:]
    if with_edges:
        buckets_ref, rest = rest[0], rest[1:]
    out_ref = rest[0]
    i = pl.program_id(0)
    nblk = pl.num_programs(0)
    horiz = coef_ref[0]
    vert = coef_ref[1]
    wet = wet_ref[...]
    rows, cols = wet.shape
    row = lax.broadcasted_iota(jnp.int32, (rows, cols), 0)
    col = lax.broadcasted_iota(jnp.int32, (rows, cols), 1)
    hw_t = jnp.transpose(hw_ref[...])
    he_t = jnp.transpose(he_ref[...])
    above = above_ref[0] * jnp.where(i > 0, 1.0, 0.0)
    below = below_ref[0] * jnp.where(i < nblk - 1, 1.0, 0.0)
    if with_edges:
        en_ref, es_ref, ew_ref, ee_ref, arrived_ref, qw_ref, qe_ref, recv, send_sem, recv_sem = rest[1:]

        @pl.when(i == 0)
        def _():
            start_spread(buckets_ref, recv, send_sem, recv_sem)
            qw_ref[...] = jnp.zeros_like(qw_ref)
            qe_ref[...] = jnp.zeros_like(qe_ref)

    if with_edges:
        lane = lax.broadcasted_iota(jnp.int32, qw_ref.shape, 1)
        qw = qw_ref[...]
        qe = qe_ref[...]
    for l in range(LB):
        u = u_ref[l]
        prev = u_ref[l - 1] if l > 0 else above
        nxt = u_ref[l + 1] if l < LB - 1 else below
        w = wet * u
        north = jnp.where(row == 0, hn_ref[l:l + 1, :], pltpu.roll(w, 1, 0))
        south = jnp.where(row == rows - 1, hs_ref[l:l + 1, :], pltpu.roll(w, rows - 1, 0))
        west = jnp.where(col == 0, hw_t[:, l:l + 1], pltpu.roll(w, 1, 1))
        east = jnp.where(col == cols - 1, he_t[:, l:l + 1], pltpu.roll(w, cols - 1, 1))
        lateral = north + south + west + east - 4.0 * w
        vertical = prev + nxt - 2.0 * u
        res = wet * (u + horiz * lateral + vert * vertical)
        if with_force and l == 0:
            res = res + jnp.where(i == 0, 1.0, 0.0) * (force_gain * wet * force_ref[...])
        out_ref[l] = res
        if with_edges:
            fw = wet * res
            en_ref[l:l + 1, :] = fw[0:1, :]
            es_ref[l:l + 1, :] = fw[rows - 1:rows, :]
            hit = lane == i * LB + l
            qw = jnp.where(hit, fw[:, 0:1], qw)
            qe = jnp.where(hit, fw[:, cols - 1:cols], qe)

    if with_edges:
        qw_ref[...] = qw
        qe_ref[...] = qe

        @pl.when(i == nblk - 1)
        def _():
            lev = ew_ref.shape[0]
            ew_ref[...] = jnp.transpose(qw_ref[...])[0:lev, :]
            ee_ref[...] = jnp.transpose(qe_ref[...])[0:lev, :]
            finish_spread(buckets_ref, recv, send_sem, recv_sem, arrived_ref)


def edges_kernel(wet_ref, u_ref, en_ref, es_ref, ew_ref, ee_ref, qw_ref, qe_ref):
    i = pl.program_id(0)
    nblk = pl.num_programs(0)
    wet = wet_ref[...]
    rows, cols = wet.shape

    @pl.when(i == 0)
    def _():
        qw_ref[...] = jnp.zeros_like(qw_ref)
        qe_ref[...] = jnp.zeros_like(qe_ref)

    lane = lax.broadcasted_iota(jnp.int32, qw_ref.shape, 1)
    qw = qw_ref[...]
    qe = qe_ref[...]
    for l in range(EB):
        fw = wet * u_ref[l]
        en_ref[l:l + 1, :] = fw[0:1, :]
        es_ref[l:l + 1, :] = fw[rows - 1:rows, :]
        hit = lane == i * EB + l
        qw = jnp.where(hit, fw[:, 0:1], qw)
        qe = jnp.where(hit, fw[:, cols - 1:cols], qe)
    qw_ref[...] = qw
    qe_ref[...] = qe

    @pl.when(i == nblk - 1)
    def _():
        lev = ew_ref.shape[0]
        ew_ref[...] = jnp.transpose(qw_ref[...])[0:lev, :]
        ee_ref[...] = jnp.transpose(qe_ref[...])[0:lev, :]


def masked_edges(wet, u):
    lev, rows, cols = u.shape
    lvl2 = pl.BlockSpec((EB, cols), lambda i: (i, 0))
    full2 = lambda shape: pl.BlockSpec(shape, lambda i: (0, 0))
    return pl.pallas_call(
        edges_kernel,
        grid=(lev // EB,),
        in_specs=[full2((rows, cols)), pl.BlockSpec((EB, rows, cols), lambda i: (i, 0, 0))],
        out_specs=[lvl2, lvl2, full2((lev, rows)), full2((lev, rows))],
        out_shape=[jax.ShapeDtypeStruct((lev, cols), jnp.float32)] * 2
        + [jax.ShapeDtypeStruct((lev, rows), jnp.float32)] * 2,
        scratch_shapes=[pltpu.VMEM((rows, 128), jnp.float32)] * 2,
        compiler_params=pltpu.CompilerParams(dimension_semantics=("arbitrary",)),
        cost_estimate=pl.CostEstimate(flops=2 * u.size, bytes_accessed=4 * u.size, transcendentals=0),
    )(wet, u)


def force_kernel(x_ref, wet_ref, f_ref, out_ref):
    out_ref[0] = x_ref[0] + force_gain * wet_ref[...] * f_ref[...]


def add_force(x, wet, f):
    lev, rows, cols = x.shape
    plane = pl.BlockSpec((rows, cols), lambda i: (0, 0))
    level0 = pl.BlockSpec((1, rows, cols), lambda i: (0, 0, 0))
    return pl.pallas_call(
        force_kernel,
        grid=(1,),
        in_specs=[level0, plane, plane],
        out_specs=level0,
        out_shape=jax.ShapeDtypeStruct(x.shape, x.dtype),
        input_output_aliases={0: 0},
    )(x, wet, f)


def stencil_step(coef, wet, u, halos, force=None, buckets=None):
    with_edges = buckets is not None
    lev, rows, cols = u.shape
    nblk = lev // LB
    full2 = lambda shape: pl.BlockSpec(shape, lambda i: (0, 0))
    lvl2 = pl.BlockSpec((LB, cols), lambda i: (i, 0))
    in_specs = [
        pl.BlockSpec(memory_space=pltpu.SMEM),
        full2((rows, cols)),
        pl.BlockSpec((LB, rows, cols), lambda i: (i, 0, 0)),
        pl.BlockSpec((1, rows, cols), lambda i: (jnp.maximum(i * LB - 1, 0), 0, 0)),
        pl.BlockSpec((1, rows, cols), lambda i: (jnp.minimum(i * LB + LB, lev - 1), 0, 0)),
        lvl2, lvl2, lvl2, lvl2,
    ]
    args = [coef, wet, u, u, u] + list(halos)
    if force is not None:
        in_specs.append(full2((rows, cols)))
        args.append(force)
    if with_edges:
        in_specs.append(pl.BlockSpec(buckets.shape, lambda i: (0, 0, 0, 0)))
        args.append(buckets)
    out_shape = [jax.ShapeDtypeStruct((lev, rows, cols), jnp.float32)]
    out_specs = [pl.BlockSpec((LB, rows, cols), lambda i: (i, 0, 0))]
    scratch = []
    params = dict(dimension_semantics=("arbitrary",))
    if with_edges:
        out_shape += [jax.ShapeDtypeStruct((lev, cols), jnp.float32)] * 2
        out_shape += [jax.ShapeDtypeStruct((lev, rows), jnp.float32)] * 2
        out_shape += [jax.ShapeDtypeStruct(buckets.shape, buckets.dtype)]
        out_specs += [lvl2, lvl2, full2((lev, rows)), full2((lev, rows))]
        out_specs += [pl.BlockSpec(buckets.shape, lambda i: (0, 0, 0, 0))]
        scratch = [pltpu.VMEM((rows, 128), jnp.float32)] * 2 + [
            pltpu.VMEM(buckets.shape, buckets.dtype),
            pltpu.SemaphoreType.DMA((buckets.shape[0],)),
            pltpu.SemaphoreType.DMA((buckets.shape[0],)),
        ]
        params.update(collective_id=2, has_side_effects=True)
    return pl.pallas_call(
        functools.partial(stencil_kernel, with_edges, force is not None),
        grid=(nblk,),
        in_specs=in_specs,
        out_specs=out_specs,
        out_shape=out_shape,
        scratch_shapes=scratch,
        compiler_params=pltpu.CompilerParams(**params),
        cost_estimate=pl.CostEstimate(flops=30 * u.size, bytes_accessed=12 * u.size, transcendentals=0),
    )(*args)


def halo_kernel(en_ref, es_ref, ew_ref, ee_ref, hn_ref, hs_ref, hw_ref, he_ref,
                buf, send_sem, recv_sem):
    mp = lax.axis_index("mp")
    gx = lax.axis_index("gx")
    gy = lax.axis_index("gy")
    ngx = lax.axis_size("gx")
    ngy = lax.axis_size("gy")
    mesh_id = pl.DeviceIdType.MESH
    links = [
        (gx < ngx - 1, (mp, gx + 1, gy), es_ref, 0),
        (gx > 0, (mp, gx - 1, gy), en_ref, 1),
        (gy < ngy - 1, (mp, gx, gy + 1), ee_ref, 2),
        (gy > 0, (mp, gx, gy - 1), ew_ref, 3),
    ]
    barrier = pltpu.get_barrier_semaphore()
    count = jnp.int32(0)
    for present, dev, _, _ in links:
        @pl.when(present)
        def _():
            pl.semaphore_signal(barrier, 1, device_id=dev, device_id_type=mesh_id)

        count = count + present.astype(jnp.int32)
    pl.semaphore_wait(barrier, count)

    copies = []
    for present, dev, src, slot in links:
        copy = pltpu.make_async_remote_copy(
            src_ref=src,
            dst_ref=buf.at[slot],
            send_sem=send_sem.at[slot],
            recv_sem=recv_sem.at[slot],
            device_id=dev,
            device_id_type=mesh_id,
        )
        pl.when(present)(copy.start)
        copies.append((present, copy))
    for present, copy in copies:
        pl.when(present)(copy.wait_send)
    fills = [gx > 0, gx < ngx - 1, gy > 0, gy < ngy - 1]
    outs = [hn_ref, hs_ref, hw_ref, he_ref]
    for slot, (filled, out) in enumerate(zip(fills, outs)):
        _, copy = copies[slot]

        @pl.when(filled)
        def _():
            copy.wait_recv()
            out[...] = buf[slot]

        @pl.when(jnp.logical_not(filled))
        def _():
            out[...] = jnp.zeros_like(out)


def exchange(en, es, ew, ee, call):
    shape = jax.ShapeDtypeStruct(en.shape, en.dtype)
    vmem = pl.BlockSpec(memory_space=pltpu.VMEM)
    return pl.pallas_call(
        halo_kernel,
        in_specs=[vmem] * 4,
        out_specs=[vmem] * 4,
        out_shape=[shape] * 4,
        scratch_shapes=[
            pltpu.VMEM((4,) + en.shape, en.dtype),
            pltpu.SemaphoreType.DMA((4,)),
            pltpu.SemaphoreType.DMA((4,)),
        ],
        compiler_params=pltpu.CompilerParams(collective_id=call, has_side_effects=True),
    )(en, es, ew, ee)


def bucket_kernel(target_ref, row_ref, contrib_ref, out_ref, count_ref):
    ntiles = contrib_ref.shape[0]
    ndest = out_ref.shape[0]
    sub = lax.broadcasted_iota(jnp.int32, (KF, CY), 0)
    out_ref[...] = jnp.zeros_like(out_ref)

    def clear(d, carry):
        count_ref[d] = 0
        return carry

    lax.fori_loop(0, ndest, clear, 0)

    def body(t, carry):
        d = target_ref[t]
        c = count_ref[d]
        count_ref[d] = c + 1
        out_ref[d, c] = contrib_ref[t]
        out_ref[d, CAP] = jnp.where(sub == c, row_ref[t].astype(jnp.float32), out_ref[d, CAP])
        return carry

    lax.fori_loop(0, ntiles, body, 0, unroll=8)


def local(states, surface, land_mask, tile_weights, tile_source, tile_target, tile_row):
    group = lax.axis_index("mp")
    ndev = lax.axis_size("gx") * lax.axis_size("gy")
    state = states[0]
    lev, rows_here, cols_here = state.shape
    wet = jnp.where(
        group == 0, jnp.ones(land_mask.shape, jnp.float32), land_mask.astype(jnp.float32)
    )
    coef = jnp.stack([jnp.where(group == 0, 0.15, 0.12), jnp.where(group == 0, 0.1, 0.15)]).astype(
        jnp.float32
    )

    src = (surface[0] * wet).astype(jnp.bfloat16)
    source = tile_source[0, 0, 0]
    target = tile_target[0, 0, 0, :, 0]
    dest_row = tile_row[0, 0, 0]
    ntiles = source.shape[0]
    picked = jnp.take(src, source, axis=1)
    contrib = jnp.einsum(
        "tji,kti->tkj", tile_weights[0, 0, 0], picked, preferred_element_type=jnp.float32
    )
    buckets = pl.pallas_call(
        bucket_kernel,
        in_specs=[
            pl.BlockSpec(memory_space=pltpu.SMEM),
            pl.BlockSpec(memory_space=pltpu.SMEM),
            pl.BlockSpec(memory_space=pltpu.VMEM),
        ],
        out_specs=pl.BlockSpec(memory_space=pltpu.VMEM),
        out_shape=jax.ShapeDtypeStruct((ndev, CAP + 1, KF, CY), jnp.float32),
        scratch_shapes=[pltpu.SMEM((ndev,), jnp.int32)],
    )(target, dest_row, contrib)
    second, arrived = interval(coef, wet, state, buckets, masked_edges(wet, state))
    got_rows = arrived[:, CAP, :, 0].astype(jnp.int32)
    select = (
        got_rows[:, :, None] == jnp.arange(rows_here, dtype=jnp.int32)[None, None, :]
    ).astype(jnp.float32)
    sent = jnp.einsum(
        "scr,sckj->krj", select, arrived[:, :CAP], precision=lax.Precision.HIGHEST
    )
    received = lax.ppermute(sent, "mp", [(0, 1), (1, 0)])

    second = add_force(second, wet, received[0])
    return (second[None], received[None])


def solution(mesh):
    return jax.shard_map(
        local,
        mesh=mesh,
        in_specs=(
            P("mp", None, "gx", "gy"),
            P("mp", None, "gx", "gy"),
            P("gx", "gy"),
            P("mp", "gx", "gy", None, None, None),
            P("mp", "gx", "gy", None),
            P("mp", "gx", "gy", None, None),
            P("mp", "gx", "gy", None),
        ),
        out_specs=(P("mp", None, "gx", "gy"), P("mp", None, "gx", "gy")),
        check_vma=False,
    )
```

```python
import functools

import jax
import jax.numpy as jnp
from jax import lax
from jax.experimental import pallas as pl
from jax.experimental.pallas import tpu as pltpu
from jax.sharding import PartitionSpec as P

CY = 128
KF = 8
CAP = 8
LB = 16
EB = 32

force_gain = 0.5


def shift_pairs(devices, forward):
    up = [(i, i + 1) for i in range(devices - 1)]
    return up if forward else [(j, i) for i, j in up]


def start_spread(buckets_ref, recv, send_sem, recv_sem, first_out=None):
    mp = lax.axis_index("mp")
    ngy = lax.axis_size("gy")
    ndev = lax.axis_size("gx") * ngy
    me = lax.axis_index("gx") * ngy + lax.axis_index("gy")
    mesh_id = pl.DeviceIdType.MESH
    barrier = pltpu.get_barrier_semaphore()

    def greet(d, carry):
        @pl.when(d != me)
        def _():
            pl.semaphore_signal(barrier, 1, device_id=(mp, d // ngy, d % ngy), device_id_type=mesh_id)

        return carry

    lax.fori_loop(0, ndev, greet, 0)
    pl.semaphore_wait(barrier, ndev - 1)
    if first_out is not None:
        first_out()
    recv[me] = buckets_ref[me]

    def send(k, carry):
        d = (me + k) % ndev
        pltpu.make_async_remote_copy(
            src_ref=buckets_ref.at[d],
            dst_ref=recv.at[me],
            send_sem=send_sem.at[d],
            recv_sem=recv_sem.at[me],
            device_id=(mp, d // ngy, d % ngy),
            device_id_type=mesh_id,
        ).start()
        return carry

    lax.fori_loop(1, ndev, send, 0)


def finish_spread(buckets_ref, recv, send_sem, recv_sem, arrived_ref):
    ngy = lax.axis_size("gy")
    ndev = lax.axis_size("gx") * ngy
    me = lax.axis_index("gx") * ngy + lax.axis_index("gy")

    def wait(d, carry):
        @pl.when(d != me)
        def _():
            copy = pltpu.make_async_remote_copy(
                src_ref=buckets_ref.at[d],
                dst_ref=recv.at[d],
                send_sem=send_sem.at[d],
                recv_sem=recv_sem.at[d],
                device_id=(lax.axis_index("mp"), d // ngy, d % ngy),
                device_id_type=pl.DeviceIdType.MESH,
            )
            copy.wait_send()
            copy.wait_recv()

        return carry

    lax.fori_loop(0, ndev, wait, 0)
    arrived_ref[...] = recv[...]


def interval_kernel(coef_ref, wet_ref, u_ref, above_ref, below_ref, buckets_ref,
                    e0n, e0s, e0w, e0e,
                    out_ref, arrived_ref,
                    first, edge1, halo0, halo1, qw_ref, qe_ref, recv,
                    send_sem, recv_sem, hsend, hrecv):
    p = pl.program_id(0)
    i = pl.program_id(1)
    nblk = pl.num_programs(1)
    wet = wet_ref[...]
    rows, cols = wet.shape
    lev = first.shape[0]
    mp = lax.axis_index("mp")
    gx = lax.axis_index("gx")
    gy = lax.axis_index("gy")
    ngx = lax.axis_size("gx")
    ngy = lax.axis_size("gy")
    ndev = ngx * ngy
    me = gx * ngy + gy
    mesh_id = pl.DeviceIdType.MESH
    links = [
        (gx < ngx - 1, (mp, gx + 1, gy), 1, 0),
        (gx > 0, (mp, gx - 1, gy), 0, 1),
        (gy < ngy - 1, (mp, gx, gy + 1), 3, 2),
        (gy > 0, (mp, gx, gy - 1), 2, 3),
    ]
    fills = [gx > 0, gx < ngx - 1, gy > 0, gy < ngy - 1]
    edge0 = [e0n, e0s, e0w, e0e]

    def halo_copy(stage, src, slot, dev):
        srcs = edge0[src] if stage == 0 else edge1.at[src]
        dsts = halo0.at[slot] if stage == 0 else halo1.at[slot]
        return pltpu.make_async_remote_copy(
            src_ref=srcs,
            dst_ref=dsts,
            send_sem=hsend.at[stage, slot],
            recv_sem=hrecv.at[stage, slot],
            device_id=dev,
            device_id_type=mesh_id,
        )

    def send_halos(stage):
        for present, dev, src, slot in links:
            pl.when(present)(halo_copy(stage, src, slot, dev).start)

    def take_halos(stage, dst):
        for present, dev, src, slot in links:
            pl.when(present)(halo_copy(stage, src, slot, dev).wait_send)
        for slot, filled in enumerate(fills):
            _, dev, src, _ = links[slot]
            pl.when(filled)(halo_copy(stage, src, slot, dev).wait_recv)

            @pl.when(jnp.logical_not(filled))
            def _():
                dst[slot] = jnp.zeros_like(dst[slot])

    def bucket_copy(d):
        return pltpu.make_async_remote_copy(
            src_ref=buckets_ref.at[d],
            dst_ref=recv.at[me],
            send_sem=send_sem.at[d],
            recv_sem=recv_sem.at[me],
            device_id=(mp, d // ngy, d % ngy),
            device_id_type=mesh_id,
        )

    def issue(k0, count):
        for n in range(count):
            k = k0 + n

            @pl.when(k < ndev)
            def _():
                bucket_copy((me + k) % ndev).start()

    lane = lax.broadcasted_iota(jnp.int32, qw_ref.shape, 1)
    row = lax.broadcasted_iota(jnp.int32, (rows, cols), 0)
    col = lax.broadcasted_iota(jnp.int32, (rows, cols), 1)
    horiz = coef_ref[0]
    vert = coef_ref[1]

    def step(load, above, below, hn, hs, hw_t, he_t, store):
        for l in range(LB):
            u = load(l)
            prev = load(l - 1) if l > 0 else above
            nxt = load(l + 1) if l < LB - 1 else below
            w = wet * u
            north = jnp.where(row == 0, hn[l:l + 1, :], pltpu.roll(w, 1, 0))
            south = jnp.where(row == rows - 1, hs[l:l + 1, :], pltpu.roll(w, rows - 1, 0))
            west = jnp.where(col == 0, hw_t[:, l:l + 1], pltpu.roll(w, 1, 1))
            east = jnp.where(col == cols - 1, he_t[:, l:l + 1], pltpu.roll(w, cols - 1, 1))
            lateral = north + south + west + east - 4.0 * w
            vertical = prev + nxt - 2.0 * u
            store(l, wet * (u + horiz * lateral + vert * vertical))

    @pl.when((p == 0) & (i == 0))
    def _():
        barrier = pltpu.get_barrier_semaphore()

        def greet(d, carry):
            @pl.when(d != me)
            def _():
                pl.semaphore_signal(barrier, 1, device_id=(mp, d // ngy, d % ngy), device_id_type=mesh_id)

            return carry

        lax.fori_loop(0, ndev, greet, 0)
        pl.semaphore_wait(barrier, ndev - 1)
        send_halos(0)
        recv[me] = buckets_ref[me]
        take_halos(0, halo0)
        qw_ref[...] = jnp.zeros_like(qw_ref)
        qe_ref[...] = jnp.zeros_like(qe_ref)

    @pl.when(p == 0)
    def _():
        issue(1 + (3 * LB // 8) * i, 3 * LB // 8)
        blk = pl.ds(pl.multiple_of(i * LB, LB), LB)
        hn = halo0[0, blk]
        hs = halo0[1, blk]
        hw_t = jnp.transpose(halo0[2, blk])
        he_t = jnp.transpose(halo0[3, blk])
        above = above_ref[0] * jnp.where(i > 0, 1.0, 0.0)
        below = below_ref[0] * jnp.where(i < nblk - 1, 1.0, 0.0)
        qs = [qw_ref[...], qe_ref[...]]

        def store(l, res):
            first[i * LB + l] = res
            fw = wet * res
            edge1[0, i, l:l + 1, :] = fw[0:1, :]
            edge1[1, i, l:l + 1, :] = fw[rows - 1:rows, :]
            hit = lane == i * LB + l
            qs[0] = jnp.where(hit, fw[:, 0:1], qs[0])
            qs[1] = jnp.where(hit, fw[:, cols - 1:cols], qs[1])

        step(lambda l: u_ref[l], above, below, hn, hs, hw_t, he_t, store)
        qw_ref[...] = qs[0]
        qe_ref[...] = qs[1]

    @pl.when((p == 0) & (i == nblk - 1))
    def _():
        edge1[2] = jnp.transpose(qw_ref[...])[0:lev, :].reshape(nblk, LB, rows)
        edge1[3] = jnp.transpose(qe_ref[...])[0:lev, :].reshape(nblk, LB, rows)
        send_halos(1)

    @pl.when((p == 1) & (i == 0))
    def _():
        take_halos(1, halo1)

        def late(k, carry):
            bucket_copy((me + k) % ndev).start()
            return carry

        lax.fori_loop(min(1 + (3 * LB // 8) * nblk, ndev), ndev, late, 0)

    @pl.when(p == 1)
    def _():
        base = i * LB
        above = first[jnp.maximum(base - 1, 0)] * jnp.where(i > 0, 1.0, 0.0)
        below = first[jnp.minimum(base + LB, lev - 1)] * jnp.where(i < nblk - 1, 1.0, 0.0)
        hw_t = jnp.transpose(halo1[2, i])
        he_t = jnp.transpose(halo1[3, i])

        def store(l, res):
            out_ref[l] = res

        step(lambda l: first[base + l], above, below, halo1[0, i], halo1[1, i], hw_t, he_t, store)

    @pl.when((p == 1) & (i == nblk - 1))
    def _():
        def wait(d, carry):
            @pl.when(d != me)
            def _():
                copy = pltpu.make_async_remote_copy(
                    src_ref=buckets_ref.at[d],
                    dst_ref=recv.at[d],
                    send_sem=send_sem.at[d],
                    recv_sem=recv_sem.at[d],
                    device_id=(mp, d // ngy, d % ngy),
                    device_id_type=mesh_id,
                )
                copy.wait_send()
                copy.wait_recv()

            return carry

        lax.fori_loop(0, ndev, wait, 0)
        arrived_ref[...] = recv[...]


def interval(coef, wet, u, buckets, edges):
    lev, rows, cols = u.shape
    nblk = lev // LB
    full2 = lambda shape: pl.BlockSpec(shape, lambda p, i: (0, 0))
    whole = pl.BlockSpec(buckets.shape, lambda p, i: (0, 0, 0, 0))
    held = lambda p, i: i + p * (nblk - 1 - i)
    in_specs = [
        pl.BlockSpec(memory_space=pltpu.SMEM),
        full2((rows, cols)),
        pl.BlockSpec((LB, rows, cols), lambda p, i: (held(p, i), 0, 0)),
        pl.BlockSpec((1, rows, cols), lambda p, i: (jnp.maximum(held(p, i) * LB - 1, 0), 0, 0)),
        pl.BlockSpec((1, rows, cols), lambda p, i: (jnp.minimum(held(p, i) * LB + LB, lev - 1), 0, 0)),
        whole,
    ] + [full2((lev, cols))] * 4
    out_shape = [
        jax.ShapeDtypeStruct((lev, rows, cols), jnp.float32),
        jax.ShapeDtypeStruct(buckets.shape, buckets.dtype),
    ]
    out_specs = [pl.BlockSpec((LB, rows, cols), lambda p, i: (i * p, 0, 0)), whole]
    scratch = [
        pltpu.VMEM((lev, rows, cols), jnp.float32),
        pltpu.VMEM((4, nblk, LB, cols), jnp.float32),
        pltpu.VMEM((4, lev, cols), jnp.float32),
        pltpu.VMEM((4, nblk, LB, cols), jnp.float32),
        pltpu.VMEM((rows, 128), jnp.float32),
        pltpu.VMEM((rows, 128), jnp.float32),
        pltpu.VMEM(buckets.shape, buckets.dtype),
        pltpu.SemaphoreType.DMA((buckets.shape[0],)),
        pltpu.SemaphoreType.DMA((buckets.shape[0],)),
        pltpu.SemaphoreType.DMA((2, 4)),
        pltpu.SemaphoreType.DMA((2, 4)),
    ]
    return pl.pallas_call(
        interval_kernel,
        grid=(2, nblk),
        in_specs=in_specs,
        out_specs=out_specs,
        out_shape=out_shape,
        scratch_shapes=scratch,
        compiler_params=pltpu.CompilerParams(
            dimension_semantics=("arbitrary", "arbitrary"), collective_id=3, has_side_effects=True,
            vmem_limit_bytes=48 * 1024 * 1024,
        ),
        cost_estimate=pl.CostEstimate(flops=60 * u.size, bytes_accessed=12 * u.size, transcendentals=0),
    )(coef, wet, u, u, u, buckets, *edges)


def first_kernel(coef_ref, wet_ref, u_ref, above_ref, below_ref, buckets_ref,
                 e0n, e0s, e0w, e0e,
                 out_ref, en_ref, es_ref, ew_ref, ee_ref, arrived_ref,
                 halo, qw_ref, qe_ref, recv, send_sem, recv_sem, hsend, hrecv):
    i = pl.program_id(0)
    nblk = pl.num_programs(0)
    edge0 = [e0n, e0s, e0w, e0e]
    wet = wet_ref[...]
    rows, cols = wet.shape
    lev = ew_ref.shape[0]
    mp = lax.axis_index("mp")
    gx = lax.axis_index("gx")
    gy = lax.axis_index("gy")
    ngx = lax.axis_size("gx")
    ngy = lax.axis_size("gy")
    mesh_id = pl.DeviceIdType.MESH
    links = [
        (gx < ngx - 1, (mp, gx + 1, gy), 1, 0),
        (gx > 0, (mp, gx - 1, gy), 0, 1),
        (gy < ngy - 1, (mp, gx, gy + 1), 3, 2),
        (gy > 0, (mp, gx, gy - 1), 2, 3),
    ]
    fills = [gx > 0, gx < ngx - 1, gy > 0, gy < ngy - 1]
    copies = [
        pltpu.make_async_remote_copy(
            src_ref=edge0[src],
            dst_ref=halo.at[slot],
            send_sem=hsend.at[slot],
            recv_sem=hrecv.at[slot],
            device_id=dev,
            device_id_type=mesh_id,
        )
        for _, dev, src, slot in links
    ]
    lane = lax.broadcasted_iota(jnp.int32, qw_ref.shape, 1)

    def send_halos():
        for (present, _, _, _), copy in zip(links, copies):
            pl.when(present)(copy.start)

    @pl.when(i == 0)
    def _():
        start_spread(buckets_ref, recv, send_sem, recv_sem, send_halos)
        for (present, _, _, _), copy in zip(links, copies):
            pl.when(present)(copy.wait_send)
        for slot, filled in enumerate(fills):
            pl.when(filled)(copies[slot].wait_recv)

            @pl.when(jnp.logical_not(filled))
            def _():
                halo[slot] = jnp.zeros_like(halo[slot])

        qw_ref[...] = jnp.zeros_like(qw_ref)
        qe_ref[...] = jnp.zeros_like(qe_ref)

    def _():
        horiz = coef_ref[0]
        vert = coef_ref[1]
        row = lax.broadcasted_iota(jnp.int32, (rows, cols), 0)
        col = lax.broadcasted_iota(jnp.int32, (rows, cols), 1)
        hn = halo[0, pl.ds(i * LB, LB)]
        hs = halo[1, pl.ds(i * LB, LB)]
        hw_t = jnp.transpose(halo[2, pl.ds(i * LB, LB)])
        he_t = jnp.transpose(halo[3, pl.ds(i * LB, LB)])
        above = above_ref[0] * jnp.where(i > 0, 1.0, 0.0)
        below = below_ref[0] * jnp.where(i < nblk - 1, 1.0, 0.0)
        qw = qw_ref[...]
        qe = qe_ref[...]
        for l in range(LB):
            u = u_ref[l]
            prev = u_ref[l - 1] if l > 0 else above
            nxt = u_ref[l + 1] if l < LB - 1 else below
            w = wet * u
            north = jnp.where(row == 0, hn[l:l + 1, :], pltpu.roll(w, 1, 0))
            south = jnp.where(row == rows - 1, hs[l:l + 1, :], pltpu.roll(w, rows - 1, 0))
            west = jnp.where(col == 0, hw_t[:, l:l + 1], pltpu.roll(w, 1, 1))
            east = jnp.where(col == cols - 1, he_t[:, l:l + 1], pltpu.roll(w, cols - 1, 1))
            lateral = north + south + west + east - 4.0 * w
            vertical = prev + nxt - 2.0 * u
            res = wet * (u + horiz * lateral + vert * vertical)
            out_ref[l] = res
            fw = wet * res
            en_ref[l:l + 1, :] = fw[0:1, :]
            es_ref[l:l + 1, :] = fw[rows - 1:rows, :]
            hit = lane == i * LB + l
            qw = jnp.where(hit, fw[:, 0:1], qw)
            qe = jnp.where(hit, fw[:, cols - 1:cols], qe)
        qw_ref[...] = qw
        qe_ref[...] = qe

    _()

    @pl.when(i == nblk - 1)
    def _():
        ew_ref[...] = jnp.transpose(qw_ref[...])[0:lev, :]
        ee_ref[...] = jnp.transpose(qe_ref[...])[0:lev, :]
        finish_spread(buckets_ref, recv, send_sem, recv_sem, arrived_ref)


def first_step(coef, wet, u, buckets, edges):
    lev, rows, cols = u.shape
    nblk = lev // LB
    full2 = lambda shape: pl.BlockSpec(shape, lambda i: (0, 0))
    lvl2 = pl.BlockSpec((LB, cols), lambda i: (i, 0))
    whole = pl.BlockSpec(buckets.shape, lambda i: (0, 0, 0, 0))
    in_specs = [
        pl.BlockSpec(memory_space=pltpu.SMEM),
        full2((rows, cols)),
        pl.BlockSpec((LB, rows, cols), lambda i: (i, 0, 0)),
        pl.BlockSpec((1, rows, cols), lambda i: (jnp.maximum(i * LB - 1, 0), 0, 0)),
        pl.BlockSpec((1, rows, cols), lambda i: (jnp.minimum(i * LB + LB, lev - 1), 0, 0)),
        whole,
    ] + [full2((lev, cols))] * 4
    out_shape = [
        jax.ShapeDtypeStruct((lev, rows, cols), jnp.float32),
        jax.ShapeDtypeStruct((lev, cols), jnp.float32),
        jax.ShapeDtypeStruct((lev, cols), jnp.float32),
        jax.ShapeDtypeStruct((lev, rows), jnp.float32),
        jax.ShapeDtypeStruct((lev, rows), jnp.float32),
        jax.ShapeDtypeStruct(buckets.shape, buckets.dtype),
    ]
    out_specs = [
        pl.BlockSpec((LB, rows, cols), lambda i: (i, 0, 0)),
        lvl2, lvl2, full2((lev, rows)), full2((lev, rows)), whole,
    ]
    scratch = [
        pltpu.VMEM((4, lev, cols), jnp.float32),
        pltpu.VMEM((rows, 128), jnp.float32),
        pltpu.VMEM((rows, 128), jnp.float32),
        pltpu.VMEM(buckets.shape, buckets.dtype),
        pltpu.SemaphoreType.DMA((buckets.shape[0],)),
        pltpu.SemaphoreType.DMA((buckets.shape[0],)),
        pltpu.SemaphoreType.DMA((4,)),
        pltpu.SemaphoreType.DMA((4,)),
    ]
    return pl.pallas_call(
        first_kernel,
        grid=(nblk,),
        in_specs=in_specs,
        out_specs=out_specs,
        out_shape=out_shape,
        scratch_shapes=scratch,
        compiler_params=pltpu.CompilerParams(
            dimension_semantics=("arbitrary",), collective_id=2, has_side_effects=True
        ),
        cost_estimate=pl.CostEstimate(flops=30 * u.size, bytes_accessed=12 * u.size, transcendentals=0),
    )(coef, wet, u, u, u, buckets, *edges)


def stencil_kernel(with_edges, with_force, coef_ref, wet_ref, u_ref, above_ref, below_ref,
                   hn_ref, hs_ref, hw_ref, he_ref, *rest):
    if with_force:
        force_ref, rest = rest[0], rest[1:]
    if with_edges:
        buckets_ref, rest = rest[0], rest[1:]
    out_ref = rest[0]
    i = pl.program_id(0)
    nblk = pl.num_programs(0)
    horiz = coef_ref[0]
    vert = coef_ref[1]
    wet = wet_ref[...]
    rows, cols = wet.shape
    row = lax.broadcasted_iota(jnp.int32, (rows, cols), 0)
    col = lax.broadcasted_iota(jnp.int32, (rows, cols), 1)
    hw_t = jnp.transpose(hw_ref[...])
    he_t = jnp.transpose(he_ref[...])
    above = above_ref[0] * jnp.where(i > 0, 1.0, 0.0)
    below = below_ref[0] * jnp.where(i < nblk - 1, 1.0, 0.0)
    if with_edges:
        en_ref, es_ref, ew_ref, ee_ref, arrived_ref, qw_ref, qe_ref, recv, send_sem, recv_sem = rest[1:]

        @pl.when(i == 0)
        def _():
            start_spread(buckets_ref, recv, send_sem, recv_sem)
            qw_ref[...] = jnp.zeros_like(qw_ref)
            qe_ref[...] = jnp.zeros_like(qe_ref)

    if with_edges:
        lane = lax.broadcasted_iota(jnp.int32, qw_ref.shape, 1)
        qw = qw_ref[...]
        qe = qe_ref[...]
    for l in range(LB):
        u = u_ref[l]
        prev = u_ref[l - 1] if l > 0 else above
        nxt = u_ref[l + 1] if l < LB - 1 else below
        w = wet * u
        north = jnp.where(row == 0, hn_ref[l:l + 1, :], pltpu.roll(w, 1, 0))
        south = jnp.where(row == rows - 1, hs_ref[l:l + 1, :], pltpu.roll(w, rows - 1, 0))
        west = jnp.where(col == 0, hw_t[:, l:l + 1], pltpu.roll(w, 1, 1))
        east = jnp.where(col == cols - 1, he_t[:, l:l + 1], pltpu.roll(w, cols - 1, 1))
        lateral = north + south + west + east - 4.0 * w
        vertical = prev + nxt - 2.0 * u
        res = wet * (u + horiz * lateral + vert * vertical)
        if with_force and l == 0:
            res = res + jnp.where(i == 0, 1.0, 0.0) * (force_gain * wet * force_ref[...])
        out_ref[l] = res
        if with_edges:
            fw = wet * res
            en_ref[l:l + 1, :] = fw[0:1, :]
            es_ref[l:l + 1, :] = fw[rows - 1:rows, :]
            hit = lane == i * LB + l
            qw = jnp.where(hit, fw[:, 0:1], qw)
            qe = jnp.where(hit, fw[:, cols - 1:cols], qe)

    if with_edges:
        qw_ref[...] = qw
        qe_ref[...] = qe

        @pl.when(i == nblk - 1)
        def _():
            lev = ew_ref.shape[0]
            ew_ref[...] = jnp.transpose(qw_ref[...])[0:lev, :]
            ee_ref[...] = jnp.transpose(qe_ref[...])[0:lev, :]
            finish_spread(buckets_ref, recv, send_sem, recv_sem, arrived_ref)


def edges_kernel(wet_ref, u_ref, en_ref, es_ref, ew_ref, ee_ref, qw_ref, qe_ref):
    i = pl.program_id(0)
    nblk = pl.num_programs(0)
    wet = wet_ref[...]
    rows, cols = wet.shape

    @pl.when(i == 0)
    def _():
        qw_ref[...] = jnp.zeros_like(qw_ref)
        qe_ref[...] = jnp.zeros_like(qe_ref)

    lane = lax.broadcasted_iota(jnp.int32, qw_ref.shape, 1)
    qw = qw_ref[...]
    qe = qe_ref[...]
    for l in range(EB):
        fw = wet * u_ref[l]
        en_ref[l:l + 1, :] = fw[0:1, :]
        es_ref[l:l + 1, :] = fw[rows - 1:rows, :]
        hit = lane == i * EB + l
        qw = jnp.where(hit, fw[:, 0:1], qw)
        qe = jnp.where(hit, fw[:, cols - 1:cols], qe)
    qw_ref[...] = qw
    qe_ref[...] = qe

    @pl.when(i == nblk - 1)
    def _():
        lev = ew_ref.shape[0]
        ew_ref[...] = jnp.transpose(qw_ref[...])[0:lev, :]
        ee_ref[...] = jnp.transpose(qe_ref[...])[0:lev, :]


def masked_edges(wet, u):
    lev, rows, cols = u.shape
    lvl2 = pl.BlockSpec((EB, cols), lambda i: (i, 0))
    full2 = lambda shape: pl.BlockSpec(shape, lambda i: (0, 0))
    return pl.pallas_call(
        edges_kernel,
        grid=(lev // EB,),
        in_specs=[full2((rows, cols)), pl.BlockSpec((EB, rows, cols), lambda i: (i, 0, 0))],
        out_specs=[lvl2, lvl2, full2((lev, rows)), full2((lev, rows))],
        out_shape=[jax.ShapeDtypeStruct((lev, cols), jnp.float32)] * 2
        + [jax.ShapeDtypeStruct((lev, rows), jnp.float32)] * 2,
        scratch_shapes=[pltpu.VMEM((rows, 128), jnp.float32)] * 2,
        compiler_params=pltpu.CompilerParams(dimension_semantics=("arbitrary",)),
        cost_estimate=pl.CostEstimate(flops=2 * u.size, bytes_accessed=4 * u.size, transcendentals=0),
    )(wet, u)


def force_kernel(x_ref, wet_ref, f_ref, out_ref):
    out_ref[0] = x_ref[0] + force_gain * wet_ref[...] * f_ref[...]


def add_force(x, wet, f):
    lev, rows, cols = x.shape
    plane = pl.BlockSpec((rows, cols), lambda i: (0, 0))
    level0 = pl.BlockSpec((1, rows, cols), lambda i: (0, 0, 0))
    return pl.pallas_call(
        force_kernel,
        grid=(1,),
        in_specs=[level0, plane, plane],
        out_specs=level0,
        out_shape=jax.ShapeDtypeStruct(x.shape, x.dtype),
        input_output_aliases={0: 0},
    )(x, wet, f)


def stencil_step(coef, wet, u, halos, force=None, buckets=None):
    with_edges = buckets is not None
    lev, rows, cols = u.shape
    nblk = lev // LB
    full2 = lambda shape: pl.BlockSpec(shape, lambda i: (0, 0))
    lvl2 = pl.BlockSpec((LB, cols), lambda i: (i, 0))
    in_specs = [
        pl.BlockSpec(memory_space=pltpu.SMEM),
        full2((rows, cols)),
        pl.BlockSpec((LB, rows, cols), lambda i: (i, 0, 0)),
        pl.BlockSpec((1, rows, cols), lambda i: (jnp.maximum(i * LB - 1, 0), 0, 0)),
        pl.BlockSpec((1, rows, cols), lambda i: (jnp.minimum(i * LB + LB, lev - 1), 0, 0)),
        lvl2, lvl2, lvl2, lvl2,
    ]
    args = [coef, wet, u, u, u] + list(halos)
    if force is not None:
        in_specs.append(full2((rows, cols)))
        args.append(force)
    if with_edges:
        in_specs.append(pl.BlockSpec(buckets.shape, lambda i: (0, 0, 0, 0)))
        args.append(buckets)
    out_shape = [jax.ShapeDtypeStruct((lev, rows, cols), jnp.float32)]
    out_specs = [pl.BlockSpec((LB, rows, cols), lambda i: (i, 0, 0))]
    scratch = []
    params = dict(dimension_semantics=("arbitrary",))
    if with_edges:
        out_shape += [jax.ShapeDtypeStruct((lev, cols), jnp.float32)] * 2
        out_shape += [jax.ShapeDtypeStruct((lev, rows), jnp.float32)] * 2
        out_shape += [jax.ShapeDtypeStruct(buckets.shape, buckets.dtype)]
        out_specs += [lvl2, lvl2, full2((lev, rows)), full2((lev, rows))]
        out_specs += [pl.BlockSpec(buckets.shape, lambda i: (0, 0, 0, 0))]
        scratch = [pltpu.VMEM((rows, 128), jnp.float32)] * 2 + [
            pltpu.VMEM(buckets.shape, buckets.dtype),
            pltpu.SemaphoreType.DMA((buckets.shape[0],)),
            pltpu.SemaphoreType.DMA((buckets.shape[0],)),
        ]
        params.update(collective_id=2, has_side_effects=True)
    return pl.pallas_call(
        functools.partial(stencil_kernel, with_edges, force is not None),
        grid=(nblk,),
        in_specs=in_specs,
        out_specs=out_specs,
        out_shape=out_shape,
        scratch_shapes=scratch,
        compiler_params=pltpu.CompilerParams(**params),
        cost_estimate=pl.CostEstimate(flops=30 * u.size, bytes_accessed=12 * u.size, transcendentals=0),
    )(*args)


def halo_kernel(en_ref, es_ref, ew_ref, ee_ref, hn_ref, hs_ref, hw_ref, he_ref,
                buf, send_sem, recv_sem):
    mp = lax.axis_index("mp")
    gx = lax.axis_index("gx")
    gy = lax.axis_index("gy")
    ngx = lax.axis_size("gx")
    ngy = lax.axis_size("gy")
    mesh_id = pl.DeviceIdType.MESH
    links = [
        (gx < ngx - 1, (mp, gx + 1, gy), es_ref, 0),
        (gx > 0, (mp, gx - 1, gy), en_ref, 1),
        (gy < ngy - 1, (mp, gx, gy + 1), ee_ref, 2),
        (gy > 0, (mp, gx, gy - 1), ew_ref, 3),
    ]
    barrier = pltpu.get_barrier_semaphore()
    count = jnp.int32(0)
    for present, dev, _, _ in links:
        @pl.when(present)
        def _():
            pl.semaphore_signal(barrier, 1, device_id=dev, device_id_type=mesh_id)

        count = count + present.astype(jnp.int32)
    pl.semaphore_wait(barrier, count)

    copies = []
    for present, dev, src, slot in links:
        copy = pltpu.make_async_remote_copy(
            src_ref=src,
            dst_ref=buf.at[slot],
            send_sem=send_sem.at[slot],
            recv_sem=recv_sem.at[slot],
            device_id=dev,
            device_id_type=mesh_id,
        )
        pl.when(present)(copy.start)
        copies.append((present, copy))
    for present, copy in copies:
        pl.when(present)(copy.wait_send)
    fills = [gx > 0, gx < ngx - 1, gy > 0, gy < ngy - 1]
    outs = [hn_ref, hs_ref, hw_ref, he_ref]
    for slot, (filled, out) in enumerate(zip(fills, outs)):
        _, copy = copies[slot]

        @pl.when(filled)
        def _():
            copy.wait_recv()
            out[...] = buf[slot]

        @pl.when(jnp.logical_not(filled))
        def _():
            out[...] = jnp.zeros_like(out)


def exchange(en, es, ew, ee, call):
    shape = jax.ShapeDtypeStruct(en.shape, en.dtype)
    vmem = pl.BlockSpec(memory_space=pltpu.VMEM)
    return pl.pallas_call(
        halo_kernel,
        in_specs=[vmem] * 4,
        out_specs=[vmem] * 4,
        out_shape=[shape] * 4,
        scratch_shapes=[
            pltpu.VMEM((4,) + en.shape, en.dtype),
            pltpu.SemaphoreType.DMA((4,)),
            pltpu.SemaphoreType.DMA((4,)),
        ],
        compiler_params=pltpu.CompilerParams(collective_id=call, has_side_effects=True),
    )(en, es, ew, ee)


def bucket_kernel(target_ref, row_ref, contrib_ref, out_ref, count_ref):
    ntiles = contrib_ref.shape[0]
    ndest = out_ref.shape[0]
    sub = lax.broadcasted_iota(jnp.int32, (KF, CY), 0)
    out_ref[...] = jnp.zeros_like(out_ref)

    def clear(d, carry):
        count_ref[d] = 0
        return carry

    lax.fori_loop(0, ndest, clear, 0)

    def body(t, carry):
        d = target_ref[t]
        c = count_ref[d]
        count_ref[d] = c + 1
        out_ref[d, c] = contrib_ref[t]
        out_ref[d, CAP] = jnp.where(sub == c, row_ref[t].astype(jnp.float32), out_ref[d, CAP])
        return carry

    lax.fori_loop(0, ntiles, body, 0, unroll=16)


def local(states, surface, land_mask, tile_weights, tile_source, tile_target, tile_row):
    group = lax.axis_index("mp")
    ndev = lax.axis_size("gx") * lax.axis_size("gy")
    state = states[0]
    lev, rows_here, cols_here = state.shape
    wet = jnp.where(
        group == 0, jnp.ones(land_mask.shape, jnp.float32), land_mask.astype(jnp.float32)
    )
    coef = jnp.stack([jnp.where(group == 0, 0.15, 0.12), jnp.where(group == 0, 0.1, 0.15)]).astype(
        jnp.float32
    )

    src = (surface[0] * wet).astype(jnp.bfloat16)
    source = tile_source[0, 0, 0]
    target = tile_target[0, 0, 0, :, 0]
    dest_row = tile_row[0, 0, 0]
    ntiles = source.shape[0]
    picked = jnp.take(src, source, axis=1)
    contrib = jnp.einsum(
        "tji,kti->tkj", tile_weights[0, 0, 0], picked, preferred_element_type=jnp.float32
    )
    buckets = pl.pallas_call(
        bucket_kernel,
        in_specs=[
            pl.BlockSpec(memory_space=pltpu.SMEM),
            pl.BlockSpec(memory_space=pltpu.SMEM),
            pl.BlockSpec(memory_space=pltpu.VMEM),
        ],
        out_specs=pl.BlockSpec(memory_space=pltpu.VMEM),
        out_shape=jax.ShapeDtypeStruct((ndev, CAP + 1, KF, CY), jnp.float32),
        scratch_shapes=[pltpu.SMEM((ndev,), jnp.int32)],
    )(target, dest_row, contrib)
    second, arrived = interval(coef, wet, state, buckets, masked_edges(wet, state))
    got_rows = arrived[:, CAP, :, 0].astype(jnp.int32)
    select = (
        got_rows[:, :, None] == jnp.arange(rows_here, dtype=jnp.int32)[None, None, :]
    ).astype(jnp.float32)
    sent = jnp.einsum(
        "scr,sckj->krj", select, arrived[:, :CAP], precision=lax.Precision.HIGHEST
    )
    received = lax.ppermute(sent, "mp", [(0, 1), (1, 0)])

    second = add_force(second, wet, received[0])
    return (second[None], received[None])


def solution(mesh):
    return jax.shard_map(
        local,
        mesh=mesh,
        in_specs=(
            P("mp", None, "gx", "gy"),
            P("mp", None, "gx", "gy"),
            P("gx", "gy"),
            P("mp", "gx", "gy", None, None, None),
            P("mp", "gx", "gy", None),
            P("mp", "gx", "gy", None, None),
            P("mp", "gx", "gy", None),
        ),
        out_specs=(P("mp", None, "gx", "gy"), P("mp", None, "gx", "gy")),
        check_vma=False,
    )
```
